32 devices in a mesh: seq: 4 (over z), ctx: 8 (over y, x, core).
Axes of the slice: x: 2, y: 2, z: 4, core: 2. Of those that a mesh axis runs over, the one named last changes fastest.
Arguments:
- inputs: bfloat16 [2, 4, 512, 1536], P(None, 'seq', 'ctx'), may hold values from -6 to 6
- out_grad: bfloat16 [2, 4, 512, 1536], P(None, 'seq', 'ctx'), may hold values from -6 to 6
- pair_index: int32 [2, 8], replicated, may hold values from 0 to 7, each once within a row
- norm_gain: bfloat16 [1536], P(('seq', 'ctx')), may hold values from 0.5 to 1.5
- query_weight: bfloat16 [1536, 1536], P(('seq', 'ctx')), may hold values from -0.15625 to 0.15625
- key_weight: bfloat16 [1536, 1536], P(('seq', 'ctx')), may hold values from -0.15625 to 0.15625
- value_weight: bfloat16 [1536, 1536], P(('seq', 'ctx')), may hold values from -0.15625 to 0.15625
- score_kernel: float32 [16, 6, 11], replicated, may hold values from -1 to 1
- head_mixing: float32 [16, 2], replicated, may hold values from 0.3 to 1
- group_gain: bfloat16 [1536], P(('seq', 'ctx')), may hold values from 0.5 to 1.5
- output_weight: bfloat16 [1536, 1536], P(('seq', 'ctx')), may hold values from -0.15625 to 0.15625
- second_gain: bfloat16 [1536], P(('seq', 'ctx')), may hold values from 0.5 to 1.5
- gate_weight: bfloat16 [1536, 4096], P(('seq', 'ctx')), may hold values from -0.15625 to 0.15625
- up_weight: bfloat16 [1536, 4096], P(('seq', 'ctx')), may hold values from -0.15625 to 0.15625
- down_weight: bfloat16 [4096, 1536], P(('seq', 'ctx')), may hold values from -0.09375 to 0.09375
Outputs:
- layer_out: bfloat16 [2, 4, 512, 1536], P(None, 'seq', 'ctx')
- input_grad: bfloat16 [2, 4, 512, 1536], P(None, 'seq', 'ctx')
- norm_gain_grad: float32 [1536], P(('seq', 'ctx'))
- query_weight_grad: float32 [1536, 1536], P(('seq', 'ctx'))
- key_weight_grad: float32 [1536, 1536], P(('seq', 'ctx'))
- value_weight_grad: float32 [1536, 1536], P(('seq', 'ctx'))
- score_kernel_grad: float32 [16, 6, 11], replicated
- head_mixing_grad: float32 [16, 2], replicated
- group_gain_grad: float32 [1536], P(('seq', 'ctx'))
- output_weight_grad: float32 [1536, 1536], P(('seq', 'ctx'))
- second_gain_grad: float32 [1536], P(('seq', 'ctx'))
- gate_weight_grad: float32 [1536, 4096], P(('seq', 'ctx'))
- up_weight_grad: float32 [1536, 4096], P(('seq', 'ctx'))
- down_weight_grad: float32 [4096, 1536], P(('seq', 'ctx'))
The draws below stay inside these ranges and needn't reach their ends.
Inputs may be any that keep to these rules, and one draw needn't show every extreme that they name: `pair_index`: each row names every number of 0 to 7 once.
All inputs are finite; a program needn't handle non-finite values.
Results may differ from the reference program's by a relative error of at most 0.025.
Values may be sent and summed in bfloat16 or wider, within the bound.
A program may use at most 320 MiB of HBM per device.

```python
import jax
import jax.numpy as jnp
from jax import lax

D = 1536
HEADS = 16
HEAD_DIM = 96
FF = 4096
QC = 6
KC = 11
MICRO = 2
BLK = 32
SEQS = 4
SEQ_LEN = 512
BLOCKS = 16
N_CTX = 8


def strengthened(array, key, source, target, blocks, factor):
    def block_of(axis_at):
        return (jnp.arange(array.shape[axis_at]) // (array.shape[axis_at] // blocks)).reshape((-1,) + (1,) * (array.ndim - 1 - axis_at))

    one_side = jax.random.permutation(key, blocks)[block_of(target)]
    other_side = (block_of(target) + blocks // 2) % blocks
    return jnp.where((block_of(source) == one_side) | (block_of(source) == other_side), factor * array, array)


def block_levels(own_key, dims, pieces, low, top_value):
    level = 1.0
    for dim, shards_of in pieces:
        steps = jax.random.uniform(jax.random.fold_in(jax.random.fold_in(own_key, 6), dim), (shards_of,), jnp.float32, low / len(pieces), top_value / len(pieces))
        level = level * jnp.repeat(jnp.exp(steps), dims[dim] // shards_of).reshape((-1,) + (1,) * (len(dims) - 1 - dim))
    return level


def noise(stream_key, shape, width, bound, shards=(), kind=jnp.bfloat16):
    values = width * jax.random.normal(stream_key, shape, jnp.float32)
    if shards:
        values = values * block_levels(stream_key, shape, shards, -0.22, 0.18)
    return jnp.clip(values, -bound, bound).astype(kind)


def gaussian_with(stream_key, shape, spread, limit, cuts, heavy, kind=jnp.bfloat16):
    array = spread * jax.random.normal(stream_key, shape, jnp.float32)
    if cuts:
        array = array * block_levels(stream_key, shape, cuts, -0.22, 0.18)
    return jnp.clip(strengthened(array, jax.random.fold_in(stream_key, 3), *heavy), -limit, limit).astype(kind)


def setup_inputs(seed: int = 0) -> dict:
    streams_of = jax.random.split(jax.random.key(seed), 16)
    return {
        "inputs": gaussian_with(streams_of[0], (MICRO, SEQS, SEQ_LEN, D), 1.0, 6.0, ((1, 4), (2, 8)), (2, 3, 8, 2.0)),
        "out_grad": noise(streams_of[1], (MICRO, SEQS, SEQ_LEN, D), 1.0, 6.0, ((1, 4), (2, 8))),
        "pair_index": jax.vmap(lambda own: jax.random.permutation(own, N_CTX))(jax.random.split(streams_of[2], MICRO)).reshape((MICRO, N_CTX)).astype(jnp.int32),
        "norm_gain": jnp.clip(1.0 + 0.1 * jax.random.normal(streams_of[3], (D,), jnp.float32), 0.5, 1.5).astype(jnp.bfloat16),
        "query_weight": noise(streams_of[4], (D, D), D ** -0.5, 0.15625, ((0, 32),)),
        "key_weight": noise(streams_of[5], (D, D), D ** -0.5, 0.15625, ((0, 32),)),
        "value_weight": noise(streams_of[6], (D, D), D ** -0.5, 0.15625, ((0, 32),)),
        "score_kernel": noise(streams_of[7], (HEADS, QC, KC), 0.25, 1.0, (), jnp.float32),
        "head_mixing": jnp.clip(jax.random.uniform(streams_of[8], (HEADS, 2), jnp.float32, 0.3, 1.0), 0.3, 1.0),
        "group_gain": jnp.clip(1.0 + 0.1 * jax.random.normal(streams_of[9], (D,), jnp.float32), 0.5, 1.5).astype(jnp.bfloat16),
        "output_weight": noise(streams_of[10], (D, D), D ** -0.5, 0.15625, ((0, 32),)),
        "second_gain": jnp.clip(1.0 + 0.1 * jax.random.normal(streams_of[11], (D,), jnp.float32), 0.5, 1.5).astype(jnp.bfloat16),
        "gate_weight": noise(streams_of[12], (D, FF), D ** -0.5, 0.15625, ((0, 32),)),
        "up_weight": noise(streams_of[13], (D, FF), D ** -0.5, 0.15625, ((0, 32),)),
        "down_weight": noise(streams_of[14], (FF, D), FF ** -0.5, 0.09375, ((0, 32),)),
    }


@jax.custom_vjp
def low(v):
    return lax.optimization_barrier(v.astype(jnp.bfloat16)).astype(jnp.float32)

@jax.custom_vjp
def low_back(v):
    return v

def low_keep(v):
    return (low(v), None)

def low_pass(kept, grad):
    return (grad,)

def back_keep(v):
    return (v, None)

def back_low(kept, grad):
    return (low(grad),)
low.defvjp(low_keep, low_pass)
low_back.defvjp(back_keep, back_low)
EPSILON = 1e-05
NEGATIVE = -1e+30
PRECISE = lax.Precision.HIGHEST

def matmul(left, right):
    return jnp.dot(left, right, precision=PRECISE, preferred_element_type=jnp.float32)

def rescale(values, gain):
    return values * lax.rsqrt(lax.optimization_barrier(jnp.mean(values * values, axis=-1, keepdims=True)) + EPSILON) * gain

def block_heads(block_index, query_pad, key_pad, value_all, kernel, mixing):
    halo_rows = QC - 1
    key_reach = (KC - 1) // 2
    ext_rows = BLK + halo_rows
    query_ext = lax.dynamic_slice_in_dim(query_pad, block_index * BLK, ext_rows, 0)
    scores = jnp.einsum('rhd,khd->hrk', query_ext, key_pad, precision=PRECISE) * HEAD_DIM ** (-0.5)
    scores = jnp.concatenate([low_back(scores[:, :halo_rows]), low_back(scores[:, halo_rows:])], axis=1)
    row_pos = block_index * BLK - halo_rows + jnp.arange(ext_rows, dtype=jnp.int32)
    key_pos = jnp.arange(SEQ_LEN + 2 * key_reach, dtype=jnp.int32) - key_reach
    keep_mask = (key_pos[None, :] <= row_pos[:, None]) & (key_pos[None, :] >= 0)
    zeroed = jnp.where(keep_mask[None], scores, 0.0)
    logits = jnp.zeros((HEADS, BLK, SEQ_LEN), jnp.float32)
    for row_tap in range(QC):
        for key_tap in range(KC):
            column = 2 * key_reach - key_tap
            logits = logits + kernel[:, row_tap, key_tap][:, None, None] * zeroed[:, halo_rows - row_tap:halo_rows - row_tap + BLK, column:column + SEQ_LEN]
    own_pos = block_index * BLK + jnp.arange(BLK, dtype=jnp.int32)
    valid_mask = jnp.arange(SEQ_LEN, dtype=jnp.int32)[None, :] <= own_pos[:, None]
    logits = jnp.where(valid_mask[None], logits, NEGATIVE)
    probability = low(jax.nn.softmax(logits, axis=-1))
    groups = HEADS // 2
    paired = probability.reshape(groups, 2, BLK, SEQ_LEN)
    value_pairs = value_all.reshape(SEQ_LEN, groups, 2 * HEAD_DIM)
    mixed_in = low_back(jnp.einsum('gpik,kgc->gpic', paired, value_pairs, precision=PRECISE))
    mixed_in = mixed_in.reshape(groups, 2, BLK, 2, HEAD_DIM)
    mix_table = mixing.reshape(groups, 2, 2)
    heads_out = jnp.einsum('gqp,gpiqd->igqd', mix_table, mixed_in, precision=PRECISE)
    return heads_out.reshape(BLK, HEADS * HEAD_DIM)

def forward_layer(tokens, norm_gain, query_weight, key_weight, value_weight, score_kernel, head_mixing, group_gain, output_weight, second_gain, gate_weight, up_weight, down_weight):
    hidden = low(rescale(tokens, norm_gain))
    query_proj = low_back(low(matmul(hidden, query_weight)))
    key_proj = low_back(low(matmul(hidden, key_weight)))
    value_proj = low_back(low(matmul(hidden, value_weight)))
    halo_rows = QC - 1
    key_reach = (KC - 1) // 2
    query_heads = query_proj.reshape(SEQ_LEN, HEADS, HEAD_DIM)
    query_pad = jnp.concatenate([jnp.zeros((halo_rows, HEADS, HEAD_DIM), jnp.float32), query_heads], axis=0)
    key_pad = jnp.pad(key_proj.reshape(SEQ_LEN, HEADS, HEAD_DIM), ((key_reach, key_reach), (0, 0), (0, 0)))
    value_heads = value_proj.reshape(SEQ_LEN, HEADS, HEAD_DIM)

    def mapped(block_index):
        return block_heads(block_index, query_pad, key_pad, value_heads, score_kernel, head_mixing)
    blocks_out = lax.map(jax.checkpoint(mapped), jnp.arange(BLOCKS, dtype=jnp.int32))
    heads_out = blocks_out.reshape(SEQ_LEN, HEADS, HEAD_DIM)
    normed = heads_out * lax.rsqrt(lax.optimization_barrier(jnp.mean(heads_out * heads_out, axis=-1, keepdims=True)) + EPSILON)
    normed_out = low(normed.reshape(SEQ_LEN, HEADS * HEAD_DIM) * group_gain)
    attended = low_back(matmul(normed_out, output_weight))
    residual = tokens + attended
    second_hidden = low(rescale(residual, second_gain))
    gate_proj = low_back(matmul(second_hidden, gate_weight))
    up_proj = low_back(matmul(second_hidden, up_weight))
    activated = low(jax.nn.silu(gate_proj) * up_proj)
    return residual + low_back(matmul(activated, down_weight))

def reference(inputs, out_grad, pair_index, norm_gain, query_weight, key_weight, value_weight, score_kernel, head_mixing, group_gain, output_weight, second_gain, gate_weight, up_weight, down_weight):
    weight_list = tuple((item.astype(jnp.float32) for item in (norm_gain, query_weight, key_weight, value_weight, score_kernel, head_mixing, group_gain, output_weight, second_gain, gate_weight, up_weight, down_weight)))
    slot_ids = jnp.arange(BLOCKS, dtype=jnp.int32)
    flat_inputs = inputs.reshape(MICRO * SEQS, SEQ_LEN, D)
    flat_grads = out_grad.reshape(MICRO * SEQS, SEQ_LEN, D)
    flat_pairs = jnp.repeat(pair_index, SEQS, axis=0).astype(jnp.int32)

    def per_sequence(carried, element):
        seq_rows, seq_grads, pairs_row = element
        owner_pair = pairs_row[slot_ids // 2]
        block_of_slot = jnp.where(slot_ids % 2 == 0, owner_pair, BLOCKS - 1 - owner_pair).astype(jnp.int32)
        slot_of_block = jnp.argsort(block_of_slot).astype(jnp.int32)
        natural = seq_rows.reshape(BLOCKS, BLK, D)[slot_of_block].reshape(SEQ_LEN, D).astype(jnp.float32)
        cotangent = seq_grads.reshape(BLOCKS, BLK, D)[slot_of_block].reshape(SEQ_LEN, D).astype(jnp.float32)
        forward_out, pullback = jax.vjp(forward_layer, natural, *weight_list)
        gradients = pullback(cotangent)
        dealt_out = forward_out.reshape(BLOCKS, BLK, D)[block_of_slot].reshape(SEQ_LEN, D).astype(jnp.bfloat16)
        dealt_grad = gradients[0].reshape(BLOCKS, BLK, D)[block_of_slot].reshape(SEQ_LEN, D).astype(jnp.bfloat16)
        carried = tuple((total + part for total, part in zip(carried, gradients[1:])))
        return (carried, (dealt_out, dealt_grad))
    initial = tuple((jnp.zeros_like(item) for item in weight_list))
    sums, (dealt_outs, dealt_grads) = lax.scan(per_sequence, initial, (flat_inputs, flat_grads, flat_pairs))
    layer_out = dealt_outs.reshape(MICRO, SEQS, SEQ_LEN, D)
    input_grad = dealt_grads.reshape(MICRO, SEQS, SEQ_LEN, D)
    return (layer_out, input_grad, sums[0], sums[1], sums[2], sums[3], sums[4], sums[5], sums[6], sums[7], sums[8], sums[9], sums[10], sums[11])
```

```python
import functools

import jax
import jax.numpy as jnp
from jax import lax
from jax.experimental import pallas as pl
from jax.experimental.pallas import tpu as pltpu
from jax.sharding import PartitionSpec as P

EPSILON = 1e-05
NEGATIVE = -1e30
F32 = jnp.float32
BF16 = jnp.bfloat16
TILE = 128


def nt(left, right):
    return lax.dot_general(left, right, (((1,), (1,)), ((), ())), preferred_element_type=F32)


def tn(left, right):
    return lax.dot_general(left, right, (((0,), (0,)), ((), ())), preferred_element_type=F32)


def nn(left, right):
    return lax.dot_general(left, right, (((1,), (0,)), ((), ())), preferred_element_type=F32)


def natural_rows(blk_ref, m, blk, seq):
    return [pl.multiple_of(blk_ref[m, b] * blk, blk) for b in range(seq // blk)]


def head_lanes(width):
    return lax.broadcasted_iota(jnp.int32, (1, width), 1) < width // 2


def load_heads(blk_ref, m, blk, seq, q_ref, k_ref, v_ref, qm, kf, ks, vn):
    width = q_ref.shape[1]
    first = head_lanes(width)
    kf[0:8, :] = jnp.zeros((8, width), F32)
    kf[seq : seq + TILE + 8, :] = jnp.zeros((TILE + 8, width), F32)
    for b, row in enumerate(natural_rows(blk_ref, m, blk, seq)):
        here = pl.ds(blk * b, blk)
        q = q_ref[pl.ds(row, blk), :].astype(F32)
        qm[0, here, :] = jnp.where(first, q, 0.0).astype(BF16)
        qm[1, here, :] = jnp.where(first, 0.0, q).astype(BF16)
        kf[pl.ds(blk * b + 5, blk), :] = k_ref[pl.ds(row, blk), :].astype(F32)
        vn[here, :] = v_ref[pl.ds(row, blk), :]
    ks[...] = kf[0 : seq + TILE, :].astype(BF16)


def scores(qm, ks, h, rb, upto, scale):
    rows = pl.ds(TILE * rb, TILE)
    raw = nt(qm[h, rows, :], ks[0 : TILE * upto, :]) * scale
    key = lax.broadcasted_iota(jnp.int32, raw.shape, 1) - 5
    row = lax.broadcasted_iota(jnp.int32, raw.shape, 0) + TILE * rb
    return jnp.where((key >= 0) & (key <= row), raw, 0.0)


def head_factor(values, first, dim):
    squares = values * values
    own = jnp.sum(jnp.where(first, squares, 0.0), axis=1, keepdims=True)
    other = jnp.sum(jnp.where(first, 0.0, squares), axis=1, keepdims=True)
    return jnp.where(
        first, lax.rsqrt(own / dim + EPSILON), lax.rsqrt(other / dim + EPSILON)
    )


def forward_kernel(
    seq, blk, rows_tap, keys_tap, scale,
    blk_ref, ker_ref, mix_ref, gain_ref, q_ref, k_ref, v_ref,
    z_ref, y_ref, p_ref,
    qm, kf, ks, vn, shi, slo, thi, tlo, run, logit,
):
    m = pl.program_id(0)
    width = q_ref.shape[1]
    first = head_lanes(width)
    tiles = seq // TILE

    @pl.when(m == 0)
    def _():
        shi[...] = jnp.zeros(shi.shape, BF16)
        slo[...] = jnp.zeros(slo.shape, BF16)
        away = lax.broadcasted_iota(jnp.int32, (2 * TILE, TILE), 0) - lax.broadcasted_iota(
            jnp.int32, (2 * TILE, TILE), 1
        )
        for h in range(2):
            for a in range(rows_tap):
                band = jnp.zeros((2 * TILE, TILE), F32)
                for t in range(keys_tap):
                    band = jnp.where(away == keys_tap - 1 - t, ker_ref[h, a, t], band)
                high = band.astype(BF16)
                thi[h, :, TILE * a : TILE * (a + 1)] = high
                tlo[h, :, TILE * a : TILE * (a + 1)] = (band - high.astype(F32)).astype(BF16)

    load_heads(blk_ref, m, blk, seq, q_ref, k_ref, v_ref, qm, kf, ks, vn)
    for h in range(2):
        for rb in range(tiles):
            upto = min(rb + 2, tiles + 1)
            zeroed = scores(qm, ks, h, rb, upto, scale)
            high = zeroed.astype(BF16)
            shi[pl.ds(16 + TILE * rb, TILE), 0 : TILE * upto] = high
            slo[pl.ds(16 + TILE * rb, TILE), 0 : TILE * upto] = (zeroed - high.astype(F32)).astype(BF16)
        for b in range(tiles):
            count = seq - TILE * b
            rows = pl.ds(TILE * b, count + 16)
            lanes = pl.ds(TILE * b, 2 * TILE)
            high, low = shi[rows, lanes], slo[rows, lanes]
            run[0 : count + 16, :] = nn(high, thi[h]) + nn(low, thi[h]) + nn(high, tlo[h])
            total = run[16 : 16 + count, 0:TILE]
            for a in range(1, rows_tap):
                total = total + run[pl.ds(16 - a, count), TILE * a : TILE * (a + 1)]
            logit[pl.ds(TILE * b, count), TILE * b : TILE * (b + 1)] = total
        for rb in range(tiles):
            rows = pl.ds(TILE * rb, TILE)
            wide = TILE * (rb + 1)
            value = logit[rows, 0:wide]
            key = lax.broadcasted_iota(jnp.int32, value.shape, 1)
            row = lax.broadcasted_iota(jnp.int32, value.shape, 0) + TILE * rb
            value = jnp.where(key <= row, value, NEGATIVE)
            weight = jnp.exp(value - jnp.max(value, axis=1, keepdims=True))
            weight = weight / jnp.sum(weight, axis=1, keepdims=True)
            lowered = weight.astype(BF16)
            p_ref[0, h, rows, 0:wide] = lowered
            y_ref[0, h, rows, :] = nn(lowered, vn[0:wide, :])
    out = mix_ref[0:1, :] * y_ref[0, 0] + mix_ref[1:2, :] * y_ref[0, 1]
    normed = out * head_factor(out, first, width // 2)
    final = (normed * gain_ref[...]).astype(BF16)
    for b, row in enumerate(natural_rows(blk_ref, m, blk, seq)):
        z_ref[pl.ds(row, blk), :] = final[blk * b : blk * (b + 1), :]


def backward_kernel(
    seq, blk, rows_tap, keys_tap, scale,
    blk_ref, ker_ref, mix_ref, gain_ref, q_ref, k_ref, v_ref, zg_ref, y_ref, p_ref,
    ql_ref, kl_ref, vl_ref, gg_ref, hm_ref, kg_ref,
    qm, kf, ks, vn, sb, up, zn, yl, cg, cs, eb, qa, ka, acc,
):
    m = pl.program_id(0)
    width = q_ref.shape[1]
    first = head_lanes(width)
    tiles = seq // TILE
    wide_u = 3 * TILE
    span = keys_tap - 1
    lanes_all = rows_tap * TILE

    @pl.when(m == 0)
    def _():
        gg_ref[...] = jnp.zeros(gg_ref.shape, F32)
        hm_ref[...] = jnp.zeros(hm_ref.shape, F32)
        acc[...] = jnp.zeros(acc.shape, F32)
        cg[...] = jnp.zeros(cg.shape, F32)
        cs[...] = jnp.zeros(cs.shape, BF16)
        eb[...] = jnp.zeros(eb.shape, BF16)
        sb[...] = jnp.zeros(sb.shape, BF16)
        away = lax.broadcasted_iota(jnp.int32, (wide_u, 2 * TILE), 0) - lax.broadcasted_iota(
            jnp.int32, (wide_u, 2 * TILE), 1
        )
        for h in range(2):
            for a in range(rows_tap):
                band = jnp.zeros((wide_u, 2 * TILE), F32)
                for t in range(keys_tap):
                    band = jnp.where(away == TILE - span + t, ker_ref[h, a, t], band)
                up[h, wide_u * a : wide_u * (a + 1), :] = band.astype(BF16)

    load_heads(blk_ref, m, blk, seq, q_ref, k_ref, v_ref, qm, kf, ks, vn)
    places = natural_rows(blk_ref, m, blk, seq)
    for b, row in enumerate(places):
        zn[pl.ds(blk * b, blk), :] = zg_ref[pl.ds(row, blk), :].astype(F32)
    dim = width // 2
    y0, y1 = y_ref[0, 0], y_ref[0, 1]
    out = mix_ref[0:1, :] * y0 + mix_ref[1:2, :] * y1
    factor = head_factor(out, first, dim)
    normed = out * factor
    upstream = zn[...]
    gg_ref[...] += jnp.sum(upstream * normed, axis=0, keepdims=True)
    scaled = upstream * gain_ref[...]
    both = scaled * normed
    own = jnp.sum(jnp.where(first, both, 0.0), axis=1, keepdims=True) / dim
    other = jnp.sum(jnp.where(first, 0.0, both), axis=1, keepdims=True) / dim
    out_grad = factor * (scaled - normed * jnp.where(first, own, other))
    hm_ref[0:1, :] += jnp.sum(out_grad * y0, axis=0, keepdims=True)
    hm_ref[1:2, :] += jnp.sum(out_grad * y1, axis=0, keepdims=True)
    yl[0] = (mix_ref[0:1, :] * out_grad).astype(BF16)
    yl[1] = (mix_ref[1:2, :] * out_grad).astype(BF16)

    for b in range(tiles):
        rows = pl.ds(TILE * b, seq - TILE * b)
        lanes = pl.ds(TILE * b, TILE)
        part = tn(p_ref[0, 0, rows, lanes], yl[0, rows, :]) + tn(p_ref[0, 1, rows, lanes], yl[1, rows, :])
        part = part.astype(BF16)
        for i in range(TILE // blk):
            vl_ref[pl.ds(places[b * (TILE // blk) + i], blk), :] = part[blk * i : blk * (i + 1), :]

    ka[...] = jnp.zeros(ka.shape, F32)
    for h in range(2):
        for rb in range(tiles):
            rows = pl.ds(TILE * rb, TILE)
            upto = min(rb + 2, tiles + 1)
            sb[rows, 0 : TILE * upto] = scores(qm, ks, h, rb, upto, scale).astype(BF16)
            wide = TILE * (rb + 1)
            prob = p_ref[0, h, rows, 0:wide].astype(F32)
            grad = nt(yl[h, rows, :], vn[0:wide, :])
            both = prob * grad
            cg[rows, 0:wide] = both - prob * jnp.sum(both, axis=1, keepdims=True)
        for b in range(tiles):
            start = max(0, TILE * b - 16)
            count = seq - start
            for a in range(rows_tap):
                cs[pl.ds(start, count), pl.ds(lanes_all * b + TILE * a, TILE)] = cg[
                    pl.ds(start + a, count), TILE * b : TILE * (b + 1)
                ].astype(BF16)
            acc[h] += tn(
                sb[pl.ds(start, count), pl.ds(TILE * b, 2 * TILE)],
                cs[pl.ds(start, count), pl.ds(lanes_all * b, lanes_all)],
            )
        for b in range(0, tiles + 1, 2):
            start = max(0, TILE * b - 16)
            count = seq - start
            columns = min(2, tiles + 1 - b)
            left, right = [], []
            for a in range(rows_tap):
                for piece in range(columns + 1):
                    block = b - 1 + piece
                    if 0 <= block < tiles:
                        left.append(cs[pl.ds(start, count), pl.ds(lanes_all * block + TILE * a, TILE)])
                        right.append(
                            up[h, pl.ds(wide_u * a + TILE * piece, TILE), 0 : TILE * columns]
                        )
            grad = nn(jnp.concatenate(left, axis=1), jnp.concatenate(right, axis=0))
            key = lax.broadcasted_iota(jnp.int32, grad.shape, 1) + TILE * b - 5
            row = lax.broadcasted_iota(jnp.int32, grad.shape, 0) + start
            low = jnp.where((key >= 0) & (key <= row), grad, 0.0).astype(BF16)
            eb[pl.ds(start, count), pl.ds(TILE * b, TILE * columns)] = low
            ka[pl.ds(TILE * b, TILE * columns), :] += tn(low, qm[h, pl.ds(start, count), :])
        for rb in range(tiles):
            rows = pl.ds(TILE * rb, TILE)
            upto = min(rb + 2, tiles + 1)
            part = nn(eb[rows, 0 : TILE * upto], ks[0 : TILE * upto, :]) * scale
            if h == 0:
                qa[rows, :] = part
            else:
                qa[rows, :] = jnp.where(first, qa[rows, :], part)
    for b, row in enumerate(places):
        ql_ref[pl.ds(row, blk), :] = qa[pl.ds(blk * b, blk), :].astype(BF16)
        kl_ref[pl.ds(row, blk), :] = (ka[pl.ds(blk * b + 5, blk), :] * scale).astype(BF16)

    @pl.when(m == pl.num_programs(0) - 1)
    def _():
        away = lax.broadcasted_iota(jnp.int32, (2 * TILE, TILE), 0) - lax.broadcasted_iota(
            jnp.int32, (2 * TILE, TILE), 1
        )
        for h in range(2):
            for a in range(rows_tap):
                table = acc[h, :, TILE * a : TILE * (a + 1)]
                for t in range(keys_tap):
                    at = a * keys_tap + t
                    kg_ref[h, at : at + 1, :] = jnp.sum(
                        jnp.where(away == span - t, table, 0.0), axis=0, keepdims=True
                    )


def whole(shape):
    return pl.BlockSpec(shape, lambda m: (0,) * len(shape))


def pair_forward(blk_table, ker, mix, gain, q, k, v, micro, seq, blk, scale):
    width = q.shape[1]
    rows_tap, keys_tap = ker.shape[1:]
    smem = pl.BlockSpec(memory_space=pltpu.SMEM)
    per = lambda shape: pl.BlockSpec((1,) + shape, lambda m: (m,) + (0,) * len(shape))
    return pl.pallas_call(
        functools.partial(forward_kernel, seq, blk, rows_tap, keys_tap, scale),
        name="pair_forward",
        grid=(micro,),
        out_shape=(
            jax.ShapeDtypeStruct(q.shape, BF16),
            jax.ShapeDtypeStruct((micro, 2, seq, width), F32),
            jax.ShapeDtypeStruct((micro, 2, seq, seq), BF16),
        ),
        in_specs=[smem, smem, whole(mix.shape), whole(gain.shape)] + [whole(q.shape)] * 3,
        out_specs=(whole(q.shape), per((2, seq, width)), per((2, seq, seq))),
        scratch_shapes=[
            pltpu.VMEM((2, seq, width), BF16),
            pltpu.VMEM((seq + TILE + 8, width), F32),
            pltpu.VMEM((seq + TILE, width), BF16),
            pltpu.VMEM((seq, width), BF16),
            pltpu.VMEM((seq + 16, seq + TILE), BF16),
            pltpu.VMEM((seq + 16, seq + TILE), BF16),
            pltpu.VMEM((2, 2 * TILE, rows_tap * TILE), BF16),
            pltpu.VMEM((2, 2 * TILE, rows_tap * TILE), BF16),
            pltpu.VMEM((seq + 16, rows_tap * TILE), F32),
            pltpu.VMEM((seq, seq), F32),
        ],
        compiler_params=pltpu.CompilerParams(vmem_limit_bytes=56 << 20),
        cost_estimate=pl.CostEstimate(flops=20 * 10**9, transcendentals=10**6, bytes_accessed=8 << 20),
    )(blk_table, ker, mix, gain, q, k, v)


def pair_backward(blk_table, ker, mix, gain, q, k, v, zg, y, p, seq, blk, scale):
    width = q.shape[1]
    micro = y.shape[0]
    rows_tap, keys_tap = ker.shape[1:]
    tiles = seq // TILE
    smem = pl.BlockSpec(memory_space=pltpu.SMEM)
    per = lambda shape: pl.BlockSpec((1,) + shape, lambda m: (m,) + (0,) * len(shape))
    low = jax.ShapeDtypeStruct(q.shape, BF16)
    taps = -(-rows_tap * keys_tap // 8) * 8
    return pl.pallas_call(
        functools.partial(backward_kernel, seq, blk, rows_tap, keys_tap, scale),
        name="pair_backward",
        grid=(micro,),
        out_shape=(
            low, low, low,
            jax.ShapeDtypeStruct((1, width), F32),
            jax.ShapeDtypeStruct((2, width), F32),
            jax.ShapeDtypeStruct((2, taps, TILE), F32),
        ),
        in_specs=[smem, smem, whole(mix.shape), whole(gain.shape)]
        + [whole(q.shape)] * 4
        + [per((2, seq, width)), per((2, seq, seq))],
        out_specs=(whole(q.shape),) * 3 + (whole((1, width)), whole((2, width)), whole((2, taps, TILE))),
        scratch_shapes=[
            pltpu.VMEM((2, seq, width), BF16),
            pltpu.VMEM((seq + TILE + 8, width), F32),
            pltpu.VMEM((seq + TILE, width), BF16),
            pltpu.VMEM((seq, width), BF16),
            pltpu.VMEM((seq, seq + TILE), BF16),
            pltpu.VMEM((2, rows_tap * 3 * TILE, 2 * TILE), BF16),
            pltpu.VMEM((seq, width), F32),
            pltpu.VMEM((2, seq, width), BF16),
            pltpu.VMEM((seq + 8, seq), F32),
            pltpu.VMEM((seq, tiles * rows_tap * TILE), BF16),
            pltpu.VMEM((seq, seq + TILE), BF16),
            pltpu.VMEM((seq, width), F32),
            pltpu.VMEM((seq + TILE, width), F32),
            pltpu.VMEM((2, 2 * TILE, rows_tap * TILE), F32),
        ],
        compiler_params=pltpu.CompilerParams(vmem_limit_bytes=56 << 20),
        cost_estimate=pl.CostEstimate(flops=30 * 10**9, transcendentals=10**5, bytes_accessed=12 << 20),
    )(blk_table, ker, mix, gain, q, k, v, zg, y, p)


PRECISE = lax.Precision.HIGHEST


def normalize(values):
    factor = lax.rsqrt(jnp.mean(values * values, axis=-1, keepdims=True) + EPSILON)
    return (values * factor, factor)


def normalize_back(normed, factor, gain, upstream):
    gain_grad = jnp.sum(upstream * normed, axis=0)
    scaled = upstream * gain
    return (
        factor * (scaled - normed * jnp.mean(scaled * normed, axis=-1, keepdims=True)),
        gain_grad,
    )


def add_rows(target, update, offset):
    current = lax.dynamic_slice_in_dim(target, offset, update.shape[0], 0)
    return lax.dynamic_update_slice_in_dim(target, current + update, offset, 0)


def masked_scores(query_ext, key_pad, offset, row_pos, layout):
    block_rows, halo_rows, key_reach, key_block, groups, score_scale = layout
    extent = key_block + 4 * key_reach
    key_slab = lax.dynamic_slice_in_dim(key_pad, offset, extent, 0)
    raw_scores = (
        jnp.einsum("nrhd,khd->nhrk", query_ext, key_slab, preferred_element_type=jnp.float32)
        * score_scale
    )
    key_pos = offset - 2 * key_reach + jnp.arange(extent, dtype=jnp.int32)
    keep_mask = (key_pos[None, None, :] <= row_pos[:, :, None]) & (key_pos >= 0)[None, None, :]
    return jnp.where(keep_mask[:, None], raw_scores, 0.0)


def convolve(zeroed, kernel, shift, extent, layout):
    block_rows, halo_rows, key_reach = (layout[0], layout[1], layout[2])
    result = jnp.zeros(zeroed.shape[:2] + (block_rows, extent), jnp.float32)
    for row_tap in range(halo_rows + 1):
        for key_tap in range(2 * key_reach + 1):
            column = shift + 3 * key_reach - key_tap
            result = (
                result
                + kernel[:, row_tap, key_tap][None, :, None, None]
                * zeroed[
                    :,
                    :,
                    halo_rows - row_tap : halo_rows - row_tap + block_rows,
                    column : column + extent,
                ]
            )
    return result


def attend_forward(query_ext, row_pos, key_pad, value_pad, kernel, layout):
    block_rows, halo_rows, key_reach, key_block, groups, score_scale = layout
    members = query_ext.shape[0]
    head_count = query_ext.shape[2]
    pair_width = value_pad.shape[1] // groups
    block_count = jnp.max(row_pos) // key_block + 1

    def advance(position, carried):
        running_max, running_sum, gathered = carried
        offset = position * key_block
        zeroed = masked_scores(query_ext, key_pad, offset, row_pos, layout)
        logits = convolve(zeroed, kernel, 0, key_block, layout)
        key_pos = offset + jnp.arange(key_block, dtype=jnp.int32)
        valid_mask = key_pos[None, None, :] <= row_pos[:, halo_rows:, None]
        logits = jnp.where(valid_mask[:, None], logits, NEGATIVE)
        new_max = jnp.maximum(running_max, jnp.max(logits, axis=-1))
        shrink = jnp.exp(running_max - new_max)
        weights = jnp.exp(logits - new_max[..., None])
        running_sum = running_sum * shrink + jnp.sum(weights, axis=-1)
        value_slab = lax.dynamic_slice_in_dim(
            value_pad, offset + 2 * key_reach, key_block, 0
        ).reshape(key_block, groups, pair_width)
        low_weights = weights.astype(jnp.bfloat16).reshape(
            members, groups, 2, block_rows, key_block
        )
        gathered = gathered * shrink.reshape(members, groups, 2, block_rows, 1) + jnp.einsum(
            "ngpik,kgc->ngpic", low_weights, value_slab, preferred_element_type=jnp.float32
        )
        return (new_max, running_sum, gathered)

    initial = (
        jnp.full((members, head_count, block_rows), NEGATIVE, jnp.float32),
        jnp.zeros((members, head_count, block_rows), jnp.float32),
        jnp.zeros((members, groups, 2, block_rows, pair_width), jnp.float32),
    )
    running_max, running_sum, gathered = lax.fori_loop(0, block_count, advance, initial)
    mixed_in = gathered / running_sum.reshape(members, groups, 2, block_rows, 1)
    return (mixed_in, running_max + jnp.log(running_sum))


def attend_backward(
    query_ext,
    row_pos,
    key_pad,
    value_pad,
    kernel,
    log_total,
    mixed_low,
    delta_rows,
    key_acc,
    value_acc,
    layout,
):
    block_rows, halo_rows, key_reach, key_block, groups, score_scale = layout
    members = query_ext.shape[0]
    ext_rows = query_ext.shape[1]
    head_count = query_ext.shape[2]
    model_width = value_pad.shape[1]
    pair_width = model_width // groups
    extent = key_block + 2 * key_reach
    block_count = jnp.max(row_pos) // key_block + 1

    def advance(position, carried):
        query_grad, key_acc, value_acc, kernel_grad = carried
        offset = position * key_block
        zeroed = masked_scores(query_ext, key_pad, offset, row_pos, layout)
        logits = convolve(zeroed, kernel, -key_reach, extent, layout)
        key_pos = offset - key_reach + jnp.arange(extent, dtype=jnp.int32)
        valid_mask = (key_pos[None, None, :] <= row_pos[:, halo_rows:, None]) & (key_pos >= 0)[
            None, None, :
        ]
        probability = jnp.where(valid_mask[:, None], jnp.exp(logits - log_total[..., None]), 0.0)
        value_slab = lax.dynamic_slice_in_dim(value_pad, offset + key_reach, extent, 0).reshape(
            extent, groups, pair_width
        )
        prob_grad = jnp.einsum(
            "ngpic,kgc->ngpik", mixed_low, value_slab, preferred_element_type=jnp.float32
        ).reshape(members, head_count, block_rows, extent)
        logit_grad = probability * (prob_grad - delta_rows[..., None])
        central = (
            probability[..., key_reach : key_reach + key_block]
            .astype(jnp.bfloat16)
            .reshape(members, groups, 2, block_rows, key_block)
        )
        value_part = jnp.einsum(
            "ngpik,ngpic->kgc", central, mixed_low, preferred_element_type=jnp.float32
        ).reshape(key_block, model_width)
        value_acc = add_rows(value_acc, value_part, offset)
        middle = logit_grad[..., key_reach : key_reach + key_block]
        tap_sums = []
        for row_tap in range(halo_rows + 1):
            for key_tap in range(2 * key_reach + 1):
                column = 3 * key_reach - key_tap
                tap_sums.append(
                    jnp.sum(
                        middle
                        * zeroed[
                            :,
                            :,
                            halo_rows - row_tap : halo_rows - row_tap + block_rows,
                            column : column + key_block,
                        ],
                        axis=(0, 2, 3),
                    )
                )
        kernel_grad = kernel_grad + jnp.stack(tap_sums, axis=1).reshape(
            head_count, halo_rows + 1, 2 * key_reach + 1
        )
        padded = jnp.pad(logit_grad, ((0, 0), (0, 0), (halo_rows, halo_rows), (0, 0)))
        score_grad = jnp.zeros((members, head_count, ext_rows, key_block), jnp.float32)
        for row_tap in range(halo_rows + 1):
            for key_tap in range(2 * key_reach + 1):
                score_grad = (
                    score_grad
                    + kernel[:, row_tap, key_tap][None, :, None, None]
                    * padded[:, :, row_tap : row_tap + ext_rows, key_tap : key_tap + key_block]
                )
        key_central = offset + jnp.arange(key_block, dtype=jnp.int32)
        keep_mask = (key_central[None, None, :] <= row_pos[:, :, None]) & (key_central >= 0)[
            None, None, :
        ]
        score_low = jnp.where(keep_mask[:, None], score_grad, 0.0).astype(jnp.bfloat16)
        key_slab = lax.dynamic_slice_in_dim(key_pad, offset + 2 * key_reach, key_block, 0)
        query_grad = (
            query_grad
            + jnp.einsum("nhrk,khd->nrhd", score_low, key_slab, preferred_element_type=jnp.float32)
            * score_scale
        )
        key_part = (
            jnp.einsum(
                "nhrk,nrhd->khd", score_low, query_ext, preferred_element_type=jnp.float32
            ).reshape(key_block, model_width)
            * score_scale
        )
        key_acc = add_rows(key_acc, key_part, offset)
        return (query_grad, key_acc, value_acc, kernel_grad)

    initial = (
        jnp.zeros(query_ext.shape, jnp.float32),
        key_acc,
        value_acc,
        jnp.zeros(kernel.shape, jnp.float32),
    )
    return lax.fori_loop(0, block_count, advance, initial)


def reorder(selection, rows):
    return jnp.dot(
        selection.astype(rows.dtype), rows, precision=PRECISE, preferred_element_type=jnp.float32
    ).astype(rows.dtype)


def pick(table, places):
    return jnp.stack(
        [lax.dynamic_index_in_dim(table, places[i], 0, keepdims=False) for i in range(2)]
    )


def accumulate(previous, update):
    return (
        update
        if previous is None
        else tuple((left + right for left, right in zip(previous, update)))
    )


def general_device(
    inputs,
    out_grad,
    pair_index,
    norm_gain,
    query_weight,
    key_weight,
    value_weight,
    score_kernel,
    head_mixing,
    group_gain,
    output_weight,
    second_gain,
    gate_weight,
    up_weight,
    down_weight,
):
    micro_count = inputs.shape[0]
    local_rows = inputs.shape[2]
    block_rows = local_rows // 2
    model_width = inputs.shape[3]
    head_count = score_kernel.shape[0]
    head_dim = model_width // head_count
    groups = head_count // 2
    halo_rows = score_kernel.shape[1] - 1
    key_reach = (score_kernel.shape[2] - 1) // 2
    block_count = 2 * lax.axis_size("ctx")
    seq_length = block_count * block_rows
    key_block = min(512, seq_length)
    layout = (block_rows, halo_rows, key_reach, key_block, groups, head_dim ** (-0.5))
    extended = block_rows + halo_rows
    my_index = lax.axis_index("ctx")
    slot_ids = jnp.arange(block_count, dtype=jnp.int32)
    mix_table = head_mixing.reshape(groups, 2, 2)
    pad_width = ((2 * key_reach, 2 * key_reach), (0, 0))
    layer_rows = []
    input_rows = []
    feed_sums = None
    attention_sums = None
    kernel_total = jnp.zeros(score_kernel.shape, jnp.float32)
    mixing_total = jnp.zeros(head_mixing.shape, jnp.float32)
    for batch_index in range(micro_count):
        gain_first, query_full, key_full, value_full, gain_group, out_full = (
            lax.all_gather(norm_gain, ("seq", "ctx"), axis=0, tiled=True),
            lax.all_gather(query_weight, ("seq", "ctx"), axis=0, tiled=True),
            lax.all_gather(key_weight, ("seq", "ctx"), axis=0, tiled=True),
            lax.all_gather(value_weight, ("seq", "ctx"), axis=0, tiled=True),
            lax.all_gather(group_gain, ("seq", "ctx"), axis=0, tiled=True),
            lax.all_gather(output_weight, ("seq", "ctx"), axis=0, tiled=True),
        )
        tokens = inputs[batch_index, 0].astype(jnp.float32)
        normed_first, factor_first = normalize(tokens)
        hidden = (normed_first * gain_first.astype(jnp.float32)).astype(jnp.bfloat16)
        query_proj = jnp.dot(hidden, query_full, preferred_element_type=jnp.float32).astype(
            jnp.bfloat16
        )
        key_proj = jnp.dot(hidden, key_full, preferred_element_type=jnp.float32).astype(
            jnp.bfloat16
        )
        value_proj = jnp.dot(hidden, value_full, preferred_element_type=jnp.float32).astype(
            jnp.bfloat16
        )
        tail_rows = jnp.concatenate(
            [query_proj[block_rows - halo_rows : block_rows], query_proj[local_rows - halo_rows :]],
            axis=0,
        )
        key_dealt, value_dealt, tail_dealt = (
            lax.all_gather(key_proj, "ctx", axis=0, tiled=True),
            lax.all_gather(value_proj, "ctx", axis=0, tiled=True),
            lax.all_gather(tail_rows, "ctx", axis=0, tiled=True),
        )
        pairs_row = pair_index[batch_index]
        owner_pair = jnp.repeat(pairs_row, 2)
        block_of_slot = jnp.where(slot_ids % 2 == 0, owner_pair, block_count - 1 - owner_pair)
        to_natural = (block_of_slot[None, :] == slot_ids[:, None]).astype(jnp.float32)
        slot_of_block = jnp.sum(
            jnp.where(block_of_slot[None, :] == slot_ids[:, None], slot_ids[None, :], 0), axis=1
        )
        my_pair = lax.dynamic_index_in_dim(pairs_row, my_index, 0, keepdims=False)
        my_blocks = jnp.stack([my_pair, block_count - 1 - my_pair])
        key_pad = jnp.pad(
            reorder(to_natural, key_dealt.reshape(block_count, -1)).reshape(
                seq_length, model_width
            ),
            pad_width,
        ).reshape(-1, head_count, head_dim)
        value_pad = jnp.pad(
            reorder(to_natural, value_dealt.reshape(block_count, -1)).reshape(
                seq_length, model_width
            ),
            pad_width,
        )
        tail_blocks = reorder(to_natural, tail_dealt.reshape(block_count, -1)).reshape(
            block_count, halo_rows, model_width
        )
        previous = jnp.concatenate(
            [jnp.zeros((1, halo_rows, model_width), jnp.bfloat16), tail_blocks[:-1]], axis=0
        )
        query_ext = jnp.concatenate(
            [pick(previous, my_blocks), query_proj.reshape(2, block_rows, model_width)], axis=1
        ).reshape(2, extended, head_count, head_dim)
        row_pos = (
            my_blocks[:, None] * block_rows
            - halo_rows
            + jnp.arange(extended, dtype=jnp.int32)[None, :]
        )
        mixed_in, log_total = attend_forward(
            query_ext, row_pos, key_pad, value_pad, score_kernel, layout
        )
        mixed_six = mixed_in.reshape(2, groups, 2, block_rows, 2, head_dim)
        heads_out = jnp.einsum(
            "gqp,ngpiqd->nigqd", mix_table, mixed_six, precision=PRECISE
        ).reshape(local_rows, head_count, head_dim)
        group_normed, group_factor = normalize(heads_out)
        normed_low = (
            group_normed.reshape(local_rows, model_width) * gain_group.astype(jnp.float32)
        ).astype(jnp.bfloat16)
        residual = tokens + jnp.dot(normed_low, out_full, preferred_element_type=jnp.float32)
        gain_second, gate_full, up_full, down_full = (
            lax.all_gather(second_gain, ("seq", "ctx"), axis=0, tiled=True),
            lax.all_gather(gate_weight, ("seq", "ctx"), axis=0, tiled=True),
            lax.all_gather(up_weight, ("seq", "ctx"), axis=0, tiled=True),
            lax.all_gather(down_weight, ("seq", "ctx"), axis=0, tiled=True),
        )
        normed_second, factor_second = normalize(residual)
        second_hidden = (normed_second * gain_second.astype(jnp.float32)).astype(jnp.bfloat16)
        gate_proj = jnp.dot(second_hidden, gate_full, preferred_element_type=jnp.float32)
        up_proj = jnp.dot(second_hidden, up_full, preferred_element_type=jnp.float32)
        activated = (jax.nn.silu(gate_proj) * up_proj).astype(jnp.bfloat16)
        layer_rows.append(
            (residual + jnp.dot(activated, down_full, preferred_element_type=jnp.float32)).astype(
                jnp.bfloat16
            )
        )
        gain_second, gate_full, up_full, down_full = (
            lax.all_gather(second_gain, ("seq", "ctx"), axis=0, tiled=True),
            lax.all_gather(gate_weight, ("seq", "ctx"), axis=0, tiled=True),
            lax.all_gather(up_weight, ("seq", "ctx"), axis=0, tiled=True),
            lax.all_gather(down_weight, ("seq", "ctx"), axis=0, tiled=True),
        )
        grad_rows = out_grad[batch_index, 0]
        hid_grad = jnp.dot(grad_rows, down_full.T, preferred_element_type=jnp.float32)
        down_grad = jnp.dot(activated.T, grad_rows, preferred_element_type=jnp.float32)
        sigmoid_gate = jax.nn.sigmoid(gate_proj)
        up_low = (hid_grad * gate_proj * sigmoid_gate).astype(jnp.bfloat16)
        gate_low = (
            hid_grad * up_proj * sigmoid_gate * (1.0 + gate_proj * (1.0 - sigmoid_gate))
        ).astype(jnp.bfloat16)
        second_grad = jnp.dot(gate_low, gate_full.T, preferred_element_type=jnp.float32) + jnp.dot(
            up_low, up_full.T, preferred_element_type=jnp.float32
        )
        gate_grad = jnp.dot(second_hidden.T, gate_low, preferred_element_type=jnp.float32)
        up_grad = jnp.dot(second_hidden.T, up_low, preferred_element_type=jnp.float32)
        residual_part, gain_second_grad = normalize_back(
            normed_second, factor_second, gain_second.astype(jnp.float32), second_grad
        )
        residual_grad = grad_rows.astype(jnp.float32) + residual_part
        feed_shards = (
            lax.psum_scatter(gain_second_grad, ("seq", "ctx"), scatter_dimension=0, tiled=True),
            lax.psum_scatter(gate_grad, ("seq", "ctx"), scatter_dimension=0, tiled=True),
            lax.psum_scatter(up_grad, ("seq", "ctx"), scatter_dimension=0, tiled=True),
            lax.psum_scatter(down_grad, ("seq", "ctx"), scatter_dimension=0, tiled=True),
        )
        feed_sums = accumulate(feed_sums, feed_shards)
        gain_first, query_full, key_full, value_full, gain_group, out_full = (
            lax.all_gather(norm_gain, ("seq", "ctx"), axis=0, tiled=True),
            lax.all_gather(query_weight, ("seq", "ctx"), axis=0, tiled=True),
            lax.all_gather(key_weight, ("seq", "ctx"), axis=0, tiled=True),
            lax.all_gather(value_weight, ("seq", "ctx"), axis=0, tiled=True),
            lax.all_gather(group_gain, ("seq", "ctx"), axis=0, tiled=True),
            lax.all_gather(output_weight, ("seq", "ctx"), axis=0, tiled=True),
        )
        attended_low = residual_grad.astype(jnp.bfloat16)
        out_weight_grad = jnp.dot(normed_low.T, attended_low, preferred_element_type=jnp.float32)
        normed_grad = jnp.dot(attended_low, out_full.T, preferred_element_type=jnp.float32)
        heads_grad, gain_group_grad = normalize_back(
            group_normed,
            group_factor,
            gain_group.astype(jnp.float32).reshape(head_count, head_dim),
            normed_grad.reshape(local_rows, head_count, head_dim),
        )
        heads_five = heads_grad.reshape(2, block_rows, groups, 2, head_dim)
        mixing_total = mixing_total + jnp.einsum(
            "nigqd,ngpiqd->gqp", heads_five, mixed_six, precision=PRECISE
        ).reshape(head_count, 2)
        mixed_grad = jnp.einsum(
            "gqp,nigqd->ngpiqd", mix_table, heads_five, precision=PRECISE
        ).reshape(2, groups, 2, block_rows, 2 * head_dim)
        mixed_low = mixed_grad.astype(jnp.bfloat16)
        delta_rows = jnp.sum(mixed_low.astype(jnp.float32) * mixed_in, axis=-1).reshape(
            2, head_count, block_rows
        )
        key_acc = jnp.zeros((seq_length, model_width), jnp.float32)
        value_acc = jnp.zeros((seq_length, model_width), jnp.float32)
        query_grad, key_acc, value_acc, kernel_part = attend_backward(
            query_ext,
            row_pos,
            key_pad,
            value_pad,
            score_kernel,
            log_total,
            mixed_low,
            delta_rows,
            key_acc,
            value_acc,
            layout,
        )
        kernel_total = kernel_total + kernel_part
        halo_grad = query_grad[:, :halo_rows].reshape(2, halo_rows, model_width)
        own_grad = query_grad[:, halo_rows:].reshape(2, block_rows, model_width)
        target_slot = pick(slot_of_block, jnp.maximum(my_blocks - 1, 0))
        routing = ((slot_ids[None, :] == target_slot[:, None]) & (my_blocks > 0)[:, None]).astype(
            jnp.float32
        )
        tail_grad = jnp.einsum("ws,wrc->src", routing, halo_grad, precision=PRECISE).reshape(
            block_count * halo_rows, model_width
        )
        key_back = reorder(to_natural.T, key_acc.reshape(block_count, -1)).reshape(
            seq_length, model_width
        )
        value_back = reorder(to_natural.T, value_acc.reshape(block_count, -1)).reshape(
            seq_length, model_width
        )
        key_mine, value_mine, tail_mine = (
            lax.psum_scatter(
                key_back.astype(jnp.bfloat16), "ctx", scatter_dimension=0, tiled=True
            ).astype(jnp.float32),
            lax.psum_scatter(
                value_back.astype(jnp.bfloat16), "ctx", scatter_dimension=0, tiled=True
            ).astype(jnp.float32),
            lax.psum_scatter(
                tail_grad.astype(jnp.bfloat16), "ctx", scatter_dimension=0, tiled=True
            ).astype(jnp.float32),
        )
        tail_mine = tail_mine.reshape(2, halo_rows, model_width)
        query_total = jnp.concatenate(
            [
                own_grad[:, : block_rows - halo_rows],
                own_grad[:, block_rows - halo_rows :] + tail_mine,
            ],
            axis=1,
        ).reshape(local_rows, model_width)
        query_low = query_total.astype(jnp.bfloat16)
        key_low = key_mine.astype(jnp.bfloat16)
        value_low = value_mine.astype(jnp.bfloat16)
        query_w_grad = jnp.dot(hidden.T, query_low, preferred_element_type=jnp.float32)
        key_w_grad = jnp.dot(hidden.T, key_low, preferred_element_type=jnp.float32)
        value_w_grad = jnp.dot(hidden.T, value_low, preferred_element_type=jnp.float32)
        hidden_grad = (
            jnp.dot(query_low, query_full.T, preferred_element_type=jnp.float32)
            + jnp.dot(key_low, key_full.T, preferred_element_type=jnp.float32)
            + jnp.dot(value_low, value_full.T, preferred_element_type=jnp.float32)
        )
        token_part, gain_first_grad = normalize_back(
            normed_first, factor_first, gain_first.astype(jnp.float32), hidden_grad
        )
        input_rows.append((residual_grad + token_part).astype(jnp.bfloat16))
        attention_shards = (
            lax.psum_scatter(gain_first_grad, ("seq", "ctx"), scatter_dimension=0, tiled=True),
            lax.psum_scatter(query_w_grad, ("seq", "ctx"), scatter_dimension=0, tiled=True),
            lax.psum_scatter(key_w_grad, ("seq", "ctx"), scatter_dimension=0, tiled=True),
            lax.psum_scatter(value_w_grad, ("seq", "ctx"), scatter_dimension=0, tiled=True),
            lax.psum_scatter(
                gain_group_grad.reshape(model_width),
                ("seq", "ctx"),
                scatter_dimension=0,
                tiled=True,
            ),
            lax.psum_scatter(out_weight_grad, ("seq", "ctx"), scatter_dimension=0, tiled=True),
        )
        attention_sums = accumulate(attention_sums, attention_shards)
    kernel_sum, mixing_sum = lax.psum((kernel_total, mixing_total), ("seq", "ctx"))
    layer_out = jnp.stack(layer_rows)[:, None]
    input_grad = jnp.stack(input_rows)[:, None]
    return (
        layer_out,
        input_grad,
        attention_sums[0],
        attention_sums[1],
        attention_sums[2],
        attention_sums[3],
        kernel_sum,
        mixing_sum,
        attention_sums[4],
        attention_sums[5],
        feed_sums[0],
        feed_sums[1],
        feed_sums[2],
        feed_sums[3],
    )


def shared_sum(values, groups):
    moved = lax.all_to_all(values.astype(BF16), "ctx", 0, 0, tiled=True)
    parts = moved.reshape(groups, -1, values.shape[1]).astype(F32)
    return jnp.sum(parts, axis=0)


def on_device(
    inputs,
    out_grad,
    pair_index,
    norm_gain,
    query_weight,
    key_weight,
    value_weight,
    score_kernel,
    head_mixing,
    group_gain,
    output_weight,
    second_gain,
    gate_weight,
    up_weight,
    down_weight,
):
    groups, planes = lax.axis_size("ctx"), lax.axis_size("seq")
    heads, width = score_kernel.shape[0], inputs.shape[3]
    if heads != 2 * groups or (groups * inputs.shape[2]) % TILE:
        return general_device(
            inputs, out_grad, pair_index, norm_gain, query_weight, key_weight, value_weight,
            score_kernel, head_mixing, group_gain, output_weight, second_gain, gate_weight,
            up_weight, down_weight,
        )
    micro, local = inputs.shape[0], inputs.shape[2]
    blk, seq = local // 2, local * groups
    blocks = seq // blk
    pair = width // groups
    owned = width // (groups * planes)
    hidden = gate_weight.shape[1]
    chunk = hidden // (groups * planes)
    me = lax.axis_index("ctx")
    tokens_low = inputs.reshape(micro * local, width)
    grads_low = out_grad.reshape(micro * local, width)

    gains = lax.all_gather(
        jnp.stack([norm_gain, group_gain, second_gain]), ("seq", "ctx"), axis=1, tiled=True
    ).astype(F32)
    gain_first, gain_group, gain_second = gains[0], gains[1], gains[2]

    def split_columns(weight):
        return jnp.transpose(weight.reshape(owned, groups, pair), (1, 0, 2))

    def split_hidden(weight):
        return jnp.transpose(weight.reshape(owned, planes, groups, chunk), (2, 0, 1, 3)).reshape(
            groups, owned, planes * chunk
        )

    all_tokens = lax.all_gather(tokens_low, "ctx", axis=0, tiled=True)
    qkv_mine = lax.all_to_all(
        jnp.concatenate(
            [split_columns(query_weight), split_columns(key_weight), split_columns(value_weight)],
            axis=2,
        ),
        "ctx", 0, 0, tiled=True,
    ).reshape(groups * owned, 3 * pair)
    qkv = lax.all_gather(qkv_mine, "seq", axis=0, tiled=True)
    feed_mine = lax.all_to_all(
        jnp.concatenate([split_hidden(gate_weight), split_hidden(up_weight)], axis=2),
        "ctx", 0, 0, tiled=True,
    ).reshape(groups * owned, 2 * planes * chunk)
    out_full = lax.all_gather(output_weight, ("seq", "ctx"), axis=0, tiled=True)
    feed = lax.all_gather(feed_mine, "seq", axis=0, tiled=True)
    down = lax.all_gather(down_weight, "seq", axis=0, tiled=True)
    all_grads = lax.all_gather(grads_low, "ctx", axis=0, tiled=True)

    slots = jnp.arange(blocks, dtype=jnp.int32)
    owner = jnp.repeat(pair_index, 2, axis=1)
    block_of_slot = jnp.where(slots % 2 == 0, owner, blocks - 1 - owner)
    place = (
        (slots // 2)[None] * (2 * micro)
        + 2 * jnp.arange(micro, dtype=jnp.int32)[:, None]
        + (slots % 2)[None]
    )
    blk_table = jnp.sum(
        jnp.where(block_of_slot[:, None, :] == slots[None, :, None], place[:, None, :], 0), axis=2
    ).astype(jnp.int32)
    ker = lax.dynamic_slice_in_dim(score_kernel, 2 * me, 2, 0)
    mix = jnp.repeat(lax.dynamic_slice_in_dim(head_mixing, 2 * me, 2, 0), pair // 2, axis=0).T
    gain_pair = lax.dynamic_slice_in_dim(gain_group, pair * me, pair, 0)[None]
    scale = (width // heads) ** (-0.5)

    normed_all, _ = normalize(all_tokens.astype(F32))
    hidden_all = (normed_all * gain_first).astype(BF16)
    q, k, v = (
        jnp.dot(hidden_all, qkv[:, pair * i : pair * (i + 1)], preferred_element_type=F32).astype(BF16)
        for i in range(3)
    )
    mixed, y, prob = pair_forward(blk_table, ker, mix, gain_pair, q, k, v, micro, seq, blk, scale)
    mixed_tok = jnp.transpose(
        lax.all_to_all(mixed, "ctx", 0, 0, tiled=True).reshape(groups, -1, pair), (1, 0, 2)
    ).reshape(-1, width)
    tokens = tokens_low.astype(F32)
    residual = tokens + jnp.dot(mixed_tok, out_full, preferred_element_type=F32)
    normed_second, factor_second = normalize(residual)
    second_low = (normed_second * gain_second).astype(BF16)
    second_all = lax.all_gather(second_low, "ctx", axis=0, tiled=True)

    half = planes * chunk
    both = jnp.dot(second_all, feed, preferred_element_type=F32)
    gate, up = both[:, :half], both[:, half:]
    hid_grad = lax.dot_general(all_grads, down, (((1,), (1,)), ((), ())), preferred_element_type=F32)
    sigmoid = jax.nn.sigmoid(gate)
    active = (gate * sigmoid * up).astype(BF16)
    up_low = (hid_grad * gate * sigmoid).astype(BF16)
    gate_low = (hid_grad * up * sigmoid * (1.0 + gate * (1.0 - sigmoid))).astype(BF16)
    lows = jnp.concatenate([gate_low, up_low], axis=1)
    second_part = lax.dot_general(lows, feed, (((1,), (1,)), ((), ())), preferred_element_type=F32)
    second_grad = shared_sum(second_part, groups)
    feed_grad = lax.dot_general(second_all, lows, (((0,), (0,)), ((), ())), preferred_element_type=F32)
    down_grad = lax.dot_general(active, all_grads, (((0,), (0,)), ((), ())), preferred_element_type=F32)
    layer_part = jnp.dot(active, down, preferred_element_type=F32)
    layer_out = (residual + shared_sum(layer_part, groups)).astype(BF16)

    residual_part, gain_second_grad = normalize_back(
        normed_second, factor_second, gain_second, second_grad
    )
    residual_grad = grads_low.astype(F32) + residual_part
    attended_low = residual_grad.astype(BF16)
    mixed_grad = lax.dot_general(
        attended_low, out_full, (((1,), (1,)), ((), ())), preferred_element_type=F32
    ).astype(BF16)
    mixed_grad = lax.all_to_all(
        jnp.transpose(mixed_grad.reshape(-1, groups, pair), (1, 0, 2)), "ctx", 0, 0, tiled=True
    ).reshape(-1, pair)
    all_attended = lax.all_gather(attended_low, "ctx", axis=0, tiled=True)
    mixed_rows = lax.all_to_all(
        jnp.transpose(
            mixed_tok.reshape(-1, planes, groups, owned), (2, 0, 1, 3)
        ).reshape(groups, -1, planes * owned),
        "ctx", 0, 0, tiled=True,
    ).reshape(-1, planes * owned)
    out_w_grad = lax.dot_general(
        mixed_rows, all_attended, (((0,), (0,)), ((), ())), preferred_element_type=F32
    )
    q_low, k_low, v_low, group_part, mix_part, ker_part = pair_backward(
        blk_table, ker, mix, gain_pair, q, k, v, mixed_grad, y, prob, seq, blk, scale
    )
    qkv_low = jnp.concatenate([q_low, k_low, v_low], axis=1)
    hidden_part = lax.dot_general(qkv_low, qkv, (((1,), (1,)), ((), ())), preferred_element_type=F32)
    hidden_grad = shared_sum(hidden_part, groups)
    qkv_grad = lax.dot_general(hidden_all, qkv_low, (((0,), (0,)), ((), ())), preferred_element_type=F32)
    normed_first, factor_first = normalize(tokens)
    token_part, gain_first_grad = normalize_back(normed_first, factor_first, gain_first, hidden_grad)
    input_grad = (residual_grad + token_part).astype(BF16)

    def over_planes(value):
        return lax.psum_scatter(value.astype(BF16), "seq", scatter_dimension=0, tiled=True)

    down_out = over_planes(down_grad).astype(F32)
    out_w_out = over_planes(out_w_grad).astype(F32)
    feed_back = lax.all_to_all(over_planes(feed_grad), "ctx", 0, 0, tiled=True)
    feed_back = jnp.transpose(
        feed_back.reshape(groups, owned, 2, planes, chunk), (2, 1, 3, 0, 4)
    ).reshape(2, owned, hidden).astype(F32)
    qkv_back = lax.all_to_all(over_planes(qkv_grad), "ctx", 0, 0, tiled=True)
    qkv_back = jnp.transpose(qkv_back.reshape(groups, owned, 3, pair), (2, 1, 0, 3)).reshape(
        3, owned, width
    ).astype(F32)

    taps = score_kernel.shape[1] * score_kernel.shape[2]
    ker_mine = jnp.sum(ker_part, axis=2)[:, :taps]
    mix_mine = jnp.sum(mix_part.reshape(2, 2, pair // 2), axis=2).T
    group_all = lax.dynamic_update_slice(jnp.zeros((width,), F32), group_part[0], (pair * me,))
    ker_all = lax.dynamic_update_slice(jnp.zeros((heads, taps), F32), ker_mine, (2 * me, 0))
    mix_all = lax.dynamic_update_slice(jnp.zeros((heads, 2), F32), mix_mine, (2 * me, 0))
    sums = lax.psum(
        jnp.concatenate(
            [gain_first_grad, gain_second_grad, group_all, ker_all.reshape(-1), mix_all.reshape(-1)]
        ),
        ("seq", "ctx"),
    )
    at = (lax.axis_index("seq") * groups + me) * owned
    gain_outs = [
        lax.dynamic_slice_in_dim(sums[width * i : width * (i + 1)], at, owned, 0) for i in range(3)
    ]
    ker_out = sums[3 * width : 3 * width + heads * taps].reshape(score_kernel.shape)
    mix_out = sums[3 * width + heads * taps :].reshape(heads, 2)
    shape = inputs.shape
    return (
        layer_out.reshape(shape),
        input_grad.reshape(shape),
        gain_outs[0],
        qkv_back[0],
        qkv_back[1],
        qkv_back[2],
        ker_out,
        mix_out,
        gain_outs[2],
        out_w_out,
        gain_outs[1],
        feed_back[0],
        feed_back[1],
        down_out,
    )


def solution(mesh):
    placed = (
        P(None, "seq", "ctx", None),
        P(None, "seq", "ctx", None),
        P(),
        P(("seq", "ctx")),
        P(("seq", "ctx"), None),
        P(("seq", "ctx"), None),
        P(("seq", "ctx"), None),
        P(),
        P(),
        P(("seq", "ctx")),
        P(("seq", "ctx"), None),
        P(("seq", "ctx")),
        P(("seq", "ctx"), None),
        P(("seq", "ctx"), None),
        P(("seq", "ctx"), None),
    )
    return jax.shard_map(
        on_device,
        mesh=mesh,
        in_specs=placed,
        out_specs=(
            P(None, "seq", "ctx", None),
            P(None, "seq", "ctx", None),
            P(("seq", "ctx")),
            P(("seq", "ctx"), None),
            P(("seq", "ctx"), None),
            P(("seq", "ctx"), None),
            P(),
            P(),
            P(("seq", "ctx")),
            P(("seq", "ctx"), None),
            P(("seq", "ctx")),
            P(("seq", "ctx"), None),
            P(("seq", "ctx"), None),
            P(("seq", "ctx"), None),
        ),
        check_vma=False,
    )
```

```python
import functools

import jax
import jax.numpy as jnp
from jax import lax
from jax.experimental import pallas as pl
from jax.experimental.pallas import tpu as pltpu
from jax.sharding import PartitionSpec as P

EPSILON = 1e-05
NEGATIVE = -1e30
F32 = jnp.float32
BF16 = jnp.bfloat16
TILE = 128


def nt(left, right):
    return lax.dot_general(left, right, (((1,), (1,)), ((), ())), preferred_element_type=F32)


def tn(left, right):
    return lax.dot_general(left, right, (((0,), (0,)), ((), ())), preferred_element_type=F32)


def nn(left, right):
    return lax.dot_general(left, right, (((1,), (0,)), ((), ())), preferred_element_type=F32)


def natural_rows(blk_ref, m, blk, seq):
    return [pl.multiple_of(blk_ref[m, b] * blk, blk) for b in range(seq // blk)]


def head_lanes(width):
    return lax.broadcasted_iota(jnp.int32, (1, width), 1) < width // 2


def load_heads(blk_ref, m, blk, seq, qkv_ref, qm, kf, ks, vn):
    width = vn.shape[1]
    first = head_lanes(width)
    kf[0:8, :] = jnp.zeros((8, width), F32)
    kf[seq : seq + TILE + 8, :] = jnp.zeros((TILE + 8, width), F32)
    for b, row in enumerate(natural_rows(blk_ref, m, blk, seq)):
        here = pl.ds(blk * b, blk)
        q = qkv_ref[pl.ds(row, blk), 0:width].astype(F32)
        qm[0, here, :] = jnp.where(first, q, 0.0).astype(BF16)
        qm[1, here, :] = jnp.where(first, 0.0, q).astype(BF16)
        kf[pl.ds(blk * b + 5, blk), :] = qkv_ref[pl.ds(row, blk), width : 2 * width].astype(F32)
        vn[here, :] = qkv_ref[pl.ds(row, blk), 2 * width : 3 * width]
    ks[...] = kf[0 : seq + TILE, :].astype(BF16)


def scores(qm, ks, h, rb, upto, scale):
    rows = pl.ds(TILE * rb, TILE)
    raw = nt(qm[h, rows, :], ks[0 : TILE * upto, :]) * scale
    key = lax.broadcasted_iota(jnp.int32, raw.shape, 1) - 5
    row = lax.broadcasted_iota(jnp.int32, raw.shape, 0) + TILE * rb
    return jnp.where((key >= 0) & (key <= row), raw, 0.0)


def head_factor(values, first, dim):
    squares = values * values
    own = jnp.sum(jnp.where(first, squares, 0.0), axis=1, keepdims=True)
    other = jnp.sum(jnp.where(first, 0.0, squares), axis=1, keepdims=True)
    return jnp.where(
        first, lax.rsqrt(own / dim + EPSILON), lax.rsqrt(other / dim + EPSILON)
    )


def forward_kernel(
    seq, blk, rows_tap, keys_tap, scale,
    blk_ref, ker_ref, mix_ref, gain_ref, qkv_ref,
    z_ref, y_ref, p_ref,
    qm, kf, ks, vn, shi, slo, thi, tlo, run, logit,
):
    m = pl.program_id(0)
    width = vn.shape[1]
    first = head_lanes(width)
    tiles = seq // TILE

    @pl.when(m == 0)
    def _():
        shi[...] = jnp.zeros(shi.shape, BF16)
        slo[...] = jnp.zeros(slo.shape, BF16)
        away = lax.broadcasted_iota(jnp.int32, (2 * TILE, TILE), 0) - lax.broadcasted_iota(
            jnp.int32, (2 * TILE, TILE), 1
        )
        for h in range(2):
            for a in range(rows_tap):
                band = jnp.zeros((2 * TILE, TILE), F32)
                for t in range(keys_tap):
                    band = jnp.where(away == keys_tap - 1 - t, ker_ref[h, a, t], band)
                high = band.astype(BF16)
                thi[h, :, TILE * a : TILE * (a + 1)] = high
                tlo[h, :, TILE * a : TILE * (a + 1)] = (band - high.astype(F32)).astype(BF16)

    load_heads(blk_ref, m, blk, seq, qkv_ref, qm, kf, ks, vn)
    for h in range(2):
        for rb in range(tiles):
            upto = min(rb + 2, tiles + 1)
            zeroed = scores(qm, ks, h, rb, upto, scale)
            high = zeroed.astype(BF16)
            shi[pl.ds(16 + TILE * rb, TILE), 0 : TILE * upto] = high
            slo[pl.ds(16 + TILE * rb, TILE), 0 : TILE * upto] = (zeroed - high.astype(F32)).astype(BF16)
        for b in range(tiles):
            count = seq - TILE * b
            rows = pl.ds(TILE * b, count + 16)
            lanes = pl.ds(TILE * b, 2 * TILE)
            high, low = shi[rows, lanes], slo[rows, lanes]
            run[0 : count + 16, :] = nn(high, thi[h]) + nn(low, thi[h]) + nn(high, tlo[h])
            total = run[16 : 16 + count, 0:TILE]
            for a in range(1, rows_tap):
                total = total + run[pl.ds(16 - a, count), TILE * a : TILE * (a + 1)]
            logit[pl.ds(TILE * b, count), TILE * b : TILE * (b + 1)] = total
        for rb in range(tiles):
            rows = pl.ds(TILE * rb, TILE)
            wide = TILE * (rb + 1)
            value = logit[rows, 0:wide]
            key = lax.broadcasted_iota(jnp.int32, value.shape, 1)
            row = lax.broadcasted_iota(jnp.int32, value.shape, 0) + TILE * rb
            value = jnp.where(key <= row, value, NEGATIVE)
            weight = jnp.exp(value - jnp.max(value, axis=1, keepdims=True))
            weight = weight / jnp.sum(weight, axis=1, keepdims=True)
            lowered = weight.astype(BF16)
            p_ref[0, h, rows, 0:wide] = lowered
            y_ref[0, h, rows, :] = nn(lowered, vn[0:wide, :])
    out = mix_ref[0:1, :] * y_ref[0, 0] + mix_ref[1:2, :] * y_ref[0, 1]
    normed = out * head_factor(out, first, width // 2)
    final = (normed * gain_ref[...]).astype(BF16)
    for b, row in enumerate(natural_rows(blk_ref, m, blk, seq)):
        z_ref[pl.ds(row, blk), :] = final[blk * b : blk * (b + 1), :]


def backward_kernel(
    seq, blk, rows_tap, keys_tap, scale,
    blk_ref, ker_ref, mix_ref, gain_ref, qkv_ref, zg_ref, y_ref, p_ref,
    low_ref, gg_ref, hm_ref, kg_ref,
    qm, kf, ks, vn, sb, up, zn, yl, cg, cs, eb, qa, ka, acc,
):
    m = pl.program_id(0)
    width = vn.shape[1]
    first = head_lanes(width)
    tiles = seq // TILE
    wide_u = 3 * TILE
    span = keys_tap - 1
    lanes_all = rows_tap * TILE

    @pl.when(m == 0)
    def _():
        gg_ref[...] = jnp.zeros(gg_ref.shape, F32)
        hm_ref[...] = jnp.zeros(hm_ref.shape, F32)
        acc[...] = jnp.zeros(acc.shape, F32)
        cg[...] = jnp.zeros(cg.shape, F32)
        cs[...] = jnp.zeros(cs.shape, BF16)
        eb[...] = jnp.zeros(eb.shape, BF16)
        sb[...] = jnp.zeros(sb.shape, BF16)
        away = lax.broadcasted_iota(jnp.int32, (wide_u, 2 * TILE), 0) - lax.broadcasted_iota(
            jnp.int32, (wide_u, 2 * TILE), 1
        )
        for h in range(2):
            for a in range(rows_tap):
                band = jnp.zeros((wide_u, 2 * TILE), F32)
                for t in range(keys_tap):
                    band = jnp.where(away == TILE - span + t, ker_ref[h, a, t], band)
                up[h, wide_u * a : wide_u * (a + 1), :] = band.astype(BF16)

    load_heads(blk_ref, m, blk, seq, qkv_ref, qm, kf, ks, vn)
    places = natural_rows(blk_ref, m, blk, seq)
    for b, row in enumerate(places):
        zn[pl.ds(blk * b, blk), :] = zg_ref[pl.ds(row, blk), :].astype(F32)
    dim = width // 2
    y0, y1 = y_ref[0, 0], y_ref[0, 1]
    out = mix_ref[0:1, :] * y0 + mix_ref[1:2, :] * y1
    factor = head_factor(out, first, dim)
    normed = out * factor
    upstream = zn[...]
    gg_ref[...] += jnp.sum(upstream * normed, axis=0, keepdims=True)
    scaled = upstream * gain_ref[...]
    both = scaled * normed
    own = jnp.sum(jnp.where(first, both, 0.0), axis=1, keepdims=True) / dim
    other = jnp.sum(jnp.where(first, 0.0, both), axis=1, keepdims=True) / dim
    out_grad = factor * (scaled - normed * jnp.where(first, own, other))
    hm_ref[0:1, :] += jnp.sum(out_grad * y0, axis=0, keepdims=True)
    hm_ref[1:2, :] += jnp.sum(out_grad * y1, axis=0, keepdims=True)
    yl[0] = (mix_ref[0:1, :] * out_grad).astype(BF16)
    yl[1] = (mix_ref[1:2, :] * out_grad).astype(BF16)

    for b in range(tiles):
        rows = pl.ds(TILE * b, seq - TILE * b)
        lanes = pl.ds(TILE * b, TILE)
        part = tn(p_ref[0, 0, rows, lanes], yl[0, rows, :]) + tn(p_ref[0, 1, rows, lanes], yl[1, rows, :])
        part = part.astype(BF16)
        for i in range(TILE // blk):
            low_ref[pl.ds(places[b * (TILE // blk) + i], blk), 2 * width : 3 * width] = part[blk * i : blk * (i + 1), :]

    ka[...] = jnp.zeros(ka.shape, F32)
    for h in range(2):
        for rb in range(tiles):
            rows = pl.ds(TILE * rb, TILE)
            upto = min(rb + 2, tiles + 1)
            sb[rows, 0 : TILE * upto] = scores(qm, ks, h, rb, upto, scale).astype(BF16)
            wide = TILE * (rb + 1)
            prob = p_ref[0, h, rows, 0:wide].astype(F32)
            grad = nt(yl[h, rows, :], vn[0:wide, :])
            both = prob * grad
            cg[rows, 0:wide] = both - prob * jnp.sum(both, axis=1, keepdims=True)
        for b in range(tiles):
            start = max(0, TILE * b - 16)
            count = seq - start
            for a in range(rows_tap):
                cs[pl.ds(start, count), pl.ds(lanes_all * b + TILE * a, TILE)] = cg[
                    pl.ds(start + a, count), TILE * b : TILE * (b + 1)
                ].astype(BF16)
            acc[h] += tn(
                sb[pl.ds(start, count), pl.ds(TILE * b, 2 * TILE)],
                cs[pl.ds(start, count), pl.ds(lanes_all * b, lanes_all)],
            )
        for b in range(0, tiles + 1, 2):
            start = max(0, TILE * b - 16)
            count = seq - start
            columns = min(2, tiles + 1 - b)
            left, right = [], []
            for a in range(rows_tap):
                for piece in range(columns + 1):
                    block = b - 1 + piece
                    if 0 <= block < tiles:
                        left.append(cs[pl.ds(start, count), pl.ds(lanes_all * block + TILE * a, TILE)])
                        right.append(
                            up[h, pl.ds(wide_u * a + TILE * piece, TILE), 0 : TILE * columns]
                        )
            grad = nn(jnp.concatenate(left, axis=1), jnp.concatenate(right, axis=0))
            key = lax.broadcasted_iota(jnp.int32, grad.shape, 1) + TILE * b - 5
            row = lax.broadcasted_iota(jnp.int32, grad.shape, 0) + start
            low = jnp.where((key >= 0) & (key <= row), grad, 0.0).astype(BF16)
            eb[pl.ds(start, count), pl.ds(TILE * b, TILE * columns)] = low
            ka[pl.ds(TILE * b, TILE * columns), :] += tn(low, qm[h, pl.ds(start, count), :])
        for rb in range(tiles):
            rows = pl.ds(TILE * rb, TILE)
            upto = min(rb + 2, tiles + 1)
            part = nn(eb[rows, 0 : TILE * upto], ks[0 : TILE * upto, :]) * scale
            if h == 0:
                qa[rows, :] = part
            else:
                qa[rows, :] = jnp.where(first, qa[rows, :], part)
    for b, row in enumerate(places):
        low_ref[pl.ds(row, blk), 0:width] = qa[pl.ds(blk * b, blk), :].astype(BF16)
        low_ref[pl.ds(row, blk), width : 2 * width] = (ka[pl.ds(blk * b + 5, blk), :] * scale).astype(BF16)

    @pl.when(m == pl.num_programs(0) - 1)
    def _():
        away = lax.broadcasted_iota(jnp.int32, (2 * TILE, TILE), 0) - lax.broadcasted_iota(
            jnp.int32, (2 * TILE, TILE), 1
        )
        for h in range(2):
            for a in range(rows_tap):
                table = acc[h, :, TILE * a : TILE * (a + 1)]
                for t in range(keys_tap):
                    at = a * keys_tap + t
                    kg_ref[h, at : at + 1, :] = jnp.sum(
                        jnp.where(away == span - t, table, 0.0), axis=0, keepdims=True
                    )


def whole(shape):
    return pl.BlockSpec(shape, lambda m: (0,) * len(shape))


def pair_forward(blk_table, ker, mix, gain, qkv, micro, seq, blk, scale):
    width = qkv.shape[1] // 3
    mixed = (qkv.shape[0], width)
    rows_tap, keys_tap = ker.shape[1:]
    smem = pl.BlockSpec(memory_space=pltpu.SMEM)
    per = lambda shape: pl.BlockSpec((1,) + shape, lambda m: (m,) + (0,) * len(shape))
    return pl.pallas_call(
        functools.partial(forward_kernel, seq, blk, rows_tap, keys_tap, scale),
        name="pair_forward",
        grid=(micro,),
        out_shape=(
            jax.ShapeDtypeStruct(mixed, BF16),
            jax.ShapeDtypeStruct((micro, 2, seq, width), F32),
            jax.ShapeDtypeStruct((micro, 2, seq, seq), BF16),
        ),
        in_specs=[smem, smem, whole(mix.shape), whole(gain.shape), whole(qkv.shape)],
        out_specs=(whole(mixed), per((2, seq, width)), per((2, seq, seq))),
        scratch_shapes=[
            pltpu.VMEM((2, seq, width), BF16),
            pltpu.VMEM((seq + TILE + 8, width), F32),
            pltpu.VMEM((seq + TILE, width), BF16),
            pltpu.VMEM((seq, width), BF16),
            pltpu.VMEM((seq + 16, seq + TILE), BF16),
            pltpu.VMEM((seq + 16, seq + TILE), BF16),
            pltpu.VMEM((2, 2 * TILE, rows_tap * TILE), BF16),
            pltpu.VMEM((2, 2 * TILE, rows_tap * TILE), BF16),
            pltpu.VMEM((seq + 16, rows_tap * TILE), F32),
            pltpu.VMEM((seq, seq), F32),
        ],
        compiler_params=pltpu.CompilerParams(vmem_limit_bytes=56 << 20),
        cost_estimate=pl.CostEstimate(flops=20 * 10**9, transcendentals=10**6, bytes_accessed=8 << 20),
    )(blk_table, ker, mix, gain, qkv)


def pair_backward(blk_table, ker, mix, gain, qkv, zg, y, p, seq, blk, scale):
    width = qkv.shape[1] // 3
    micro = y.shape[0]
    rows_tap, keys_tap = ker.shape[1:]
    tiles = seq // TILE
    smem = pl.BlockSpec(memory_space=pltpu.SMEM)
    per = lambda shape: pl.BlockSpec((1,) + shape, lambda m: (m,) + (0,) * len(shape))
    taps = -(-rows_tap * keys_tap // 8) * 8
    return pl.pallas_call(
        functools.partial(backward_kernel, seq, blk, rows_tap, keys_tap, scale),
        name="pair_backward",
        grid=(micro,),
        out_shape=(
            jax.ShapeDtypeStruct(qkv.shape, BF16),
            jax.ShapeDtypeStruct((1, width), F32),
            jax.ShapeDtypeStruct((2, width), F32),
            jax.ShapeDtypeStruct((2, taps, TILE), F32),
        ),
        in_specs=[smem, smem, whole(mix.shape), whole(gain.shape), whole(qkv.shape), whole(zg.shape)]
        + [per((2, seq, width)), per((2, seq, seq))],
        out_specs=(whole(qkv.shape), whole((1, width)), whole((2, width)), whole((2, taps, TILE))),
        scratch_shapes=[
            pltpu.VMEM((2, seq, width), BF16),
            pltpu.VMEM((seq + TILE + 8, width), F32),
            pltpu.VMEM((seq + TILE, width), BF16),
            pltpu.VMEM((seq, width), BF16),
            pltpu.VMEM((seq, seq + TILE), BF16),
            pltpu.VMEM((2, rows_tap * 3 * TILE, 2 * TILE), BF16),
            pltpu.VMEM((seq, width), F32),
            pltpu.VMEM((2, seq, width), BF16),
            pltpu.VMEM((seq + 8, seq), F32),
            pltpu.VMEM((seq, tiles * rows_tap * TILE), BF16),
            pltpu.VMEM((seq, seq + TILE), BF16),
            pltpu.VMEM((seq, width), F32),
            pltpu.VMEM((seq + TILE, width), F32),
            pltpu.VMEM((2, 2 * TILE, rows_tap * TILE), F32),
        ],
        compiler_params=pltpu.CompilerParams(vmem_limit_bytes=56 << 20),
        cost_estimate=pl.CostEstimate(flops=30 * 10**9, transcendentals=10**5, bytes_accessed=12 << 20),
    )(blk_table, ker, mix, gain, qkv, zg, y, p)


MESH = pl.DeviceIdType.MESH
CHIPS = (6, 2, 4)


def peer(offset):
    mine = lax.axis_index("ctx")
    y = (mine // 4 + offset // 4) % 2
    x = ((mine // 2) % 2 + (offset // 2) % 2) % 2
    core = (mine % 2 + offset % 2) % 2
    return y * 4 + x * 2 + core


def greet(places):
    barrier = pltpu.get_barrier_semaphore()
    for place in places:
        pl.semaphore_signal(barrier, inc=1, device_id=place, device_id_type=MESH)
    pl.semaphore_wait(barrier, len(places))


def remote(source, target, send, receive, place):
    return pltpu.make_async_remote_copy(
        src_ref=source, dst_ref=target, send_sem=send, recv_sem=receive,
        device_id=place, device_id_type=MESH,
    )


def exchange_start(plane, mine, source, target, sends, receives):
    copies = [
        remote(source.at[peer(d)], target.at[mine], sends.at[d], receives.at[d], (plane, peer(d)))
        for d in (6, 7, 2, 3, 4, 5, 1)
    ]
    for copy in copies:
        copy.start()
    return copies


def spread_start(plane, mine, source, target, sends, receives):
    copies = {
        d: remote(source, target.at[mine], sends.at[d], receives.at[d], (plane, peer(d)))
        for d in CHIPS + (1,)
    }
    for copy in copies.values():
        copy.start()
    return copies


def spread_pass(plane, copies, d, target, sends, receives):
    copies[d].wait_recv()
    block = peer(d)
    copy = remote(target.at[block], target.at[block], sends.at[d + 1], receives.at[d + 1], (plane, peer(1)))
    copy.start()
    copies[d + 1] = copy


def spread_finish(copies):
    for d in (1, 3, 5, 7):
        copies[d].wait_recv()
    for copy in copies.values():
        copy.wait_send()


def spread(plane, mine, target, sends, receives):
    copies = spread_start(plane, mine, target.at[mine], target, sends, receives)
    for d in (2, 4, 6):
        spread_pass(plane, copies, d, target, sends, receives)
    spread_finish(copies)


def gather_sum_start(plane, part, near, sends, receives):
    copies = {}
    for d in CHIPS + (0,):
        copies[d] = remote(
            part.at[peer(d + 1)], near.at[d // 2], sends.at[d], receives.at[d], (plane, peer(1))
        )
        copies[d].start()
    return copies


def gather_sum_pass(plane, copies, part, near, stage, far, sends, receives):
    for d in CHIPS:
        copies[d].wait_recv()
        stage[d // 2] = (part[peer(d)].astype(F32) + near[d // 2].astype(F32)).astype(BF16)
        copy = remote(
            stage.at[d // 2], far.at[d // 2], sends.at[d + 1], receives.at[d + 1], (plane, peer(d))
        )
        copy.start()
        copies[d + 1] = copy
    copies[0].wait_recv()


def gather_sum_finish(copies):
    for d in (3, 5, 7):
        copies[d].wait_recv()
    for copy in copies.values():
        copy.wait_send()


def gather_sum_total(mine, part, near, far):
    total = part[mine].astype(F32) + near[0].astype(F32)
    for i in (1, 2, 3):
        total = total + far[i].astype(F32)
    return total


class Line:
    def __init__(self, sources, targets, planes, sends, receives):
        self.sources, self.targets, self.planes = sources, targets, planes
        self.sends, self.receives = sends, receives
        self.plane, self.mine = lax.axis_index("seq"), lax.axis_index("ctx")

    def copy(self, i, up, step):
        block = jnp.clip(self.plane - step if up else self.plane + step, 0, self.planes - 1)
        next_plane = jnp.clip(self.plane + 1 if up else self.plane - 1, 0, self.planes - 1)
        at = (i, int(up), step)
        target = self.targets[i].at[block]
        source = target if step else self.sources[i]
        return remote(source, target, self.sends.at[at], self.receives.at[at], (next_plane, self.mine))

    def arrived(self, i, up, step):
        block = jnp.clip(self.plane - 1 - step if up else self.plane + 1 + step, 0, self.planes - 1)
        at = (i, int(up), step)
        target = self.targets[i].at[block]
        from_plane = jnp.clip(self.plane - 1 if up else self.plane + 1, 0, self.planes - 1)
        return remote(target, target, self.sends.at[at], self.receives.at[at], (from_plane, self.mine))

    def step(self, step):
        for up in (True, False):
            have = self.plane >= step if up else self.plane + step < self.planes
            more = self.plane + 1 < self.planes if up else self.plane > 0
            for i in range(len(self.targets)):
                if step:
                    @pl.when(have)
                    def _(i=i, up=up):
                        self.arrived(i, up, step - 1).wait_recv()

                if step < self.planes - 1:
                    @pl.when(have & more)
                    def _(i=i, up=up):
                        self.copy(i, up, step).start()

    def finish(self):
        for step in range(self.planes - 1):
            for up in (True, False):
                have = self.plane >= step if up else self.plane + step < self.planes
                more = self.plane + 1 < self.planes if up else self.plane > 0
                for i in range(len(self.targets)):
                    @pl.when(have & more)
                    def _(i=i, up=up, step=step):
                        self.copy(i, up, step).wait_send()


def plane_peers(plane, offsets):
    return [(plane, peer(d)) for d in offsets]


def other_planes(plane, mine, planes):
    return [((plane + d) % planes, mine) for d in range(1, planes)]


class Relay:
    def __init__(self, target, planes, sends, receives):
        self.target, self.planes, self.sends, self.receives = target, planes, sends, receives
        self.plane, self.mine = lax.axis_index("seq"), lax.axis_index("ctx")
        origin = self.mine // 2
        self.source = self.plane == origin
        self.above, self.below = self.plane > origin, self.plane < origin
        self.up = (self.source | self.above) & (self.plane + 1 < planes)
        self.down = (self.source | self.below) & (self.plane > 0)

    def copy(self, i, up):
        place = jnp.clip(self.plane + 1 if up else self.plane - 1, 0, self.planes - 1)
        at = (int(up), i)
        block = self.target.at[i]
        return remote(block, block, self.sends.at[at], self.receives.at[at], (place, self.mine))

    def start(self, i):
        for up, go in ((True, self.up), (False, self.down)):
            @pl.when(self.source & go)
            def _():
                self.copy(i, up).start()

    def hand_on(self, i):
        for up, got, go in ((True, self.above, self.up), (False, self.below, self.down)):
            @pl.when(got)
            def _():
                self.copy(i, up).wait_recv()

            @pl.when(got & go)
            def _():
                self.copy(i, up).start()

    def finish(self, i):
        for up, go in ((True, self.up), (False, self.down)):
            @pl.when(go)
            def _():
                self.copy(i, up).wait_send()


def enter_kernel(
    planes, feed, qkv, out_w, gains, tokens, grads,
    feed_out, qkv_out, out_w_out, gains_out, tokens_out, grads_out,
    deal_sends, deal_receives, row_sends, row_receives, sends, receives,
    line_sends, line_receives, relay_sends, relay_receives, local,
):
    plane, mine = lax.axis_index("seq"), lax.axis_index("ctx")
    keep = [
        pltpu.make_async_copy(qkv.at[mine], qkv_out.at[plane, mine], local.at[0]),
        pltpu.make_async_copy(gains, gains_out.at[plane, mine], local.at[1]),
        pltpu.make_async_copy(feed.at[mine], feed_out.at[mine], local.at[2]),
        pltpu.make_async_copy(tokens, tokens_out.at[mine], local.at[3]),
        pltpu.make_async_copy(grads, grads_out.at[mine], local.at[4]),
    ]
    for copy in keep:
        copy.start()
    greet(plane_peers(plane, range(1, 8)) + other_planes(plane, mine, planes))
    qkv_copies = exchange_start(plane, mine, qkv, qkv_out.at[plane], deal_sends.at[0], deal_receives.at[0])
    gain_copies = [
        remote(gains, gains_out.at[plane, mine], deal_sends.at[1, d], deal_receives.at[1, d], (plane, peer(d)))
        for d in (6, 7, 2, 3, 4, 5, 1)
    ]
    for copy in gain_copies:
        copy.start()
    owner = 2 * plane + mine // 4
    here = owner == mine
    slot = mine % 4
    send_rows = remote(out_w, out_w_out.at[slot], row_sends, row_receives.at[slot], (plane, owner))
    keep_rows = pltpu.make_async_copy(out_w, out_w_out.at[slot], local.at[5])

    @pl.when(here)
    def _():
        keep_rows.start()

    @pl.when(jnp.logical_not(here))
    def _():
        send_rows.start()

    copies = spread_start(plane, mine, tokens, tokens_out, sends.at[0], receives.at[0])
    keep[0].wait()
    for copy in qkv_copies:
        copy.wait_recv()
    keep[1].wait()
    for copy in gain_copies:
        copy.wait_recv()
    line = Line(
        [qkv_out.at[plane], gains_out.at[plane]], [qkv_out, gains_out], planes, line_sends, line_receives
    )
    line.step(0)
    relay = Relay(out_w_out, planes, relay_sends, relay_receives)

    @pl.when(here)
    def _():
        keep_rows.wait()

    for r in range(4):
        @pl.when(relay.source & (4 * (mine % 2) + r != mine))
        def _():
            remote(out_w, out_w_out.at[r], row_sends, row_receives.at[r], (plane, owner)).wait_recv()

        relay.start(r)
    for d in (2, 4, 6):
        spread_pass(plane, copies, d, tokens_out, sends.at[0], receives.at[0])
    more = spread_start(plane, mine, grads, grads_out, sends.at[1], receives.at[1])
    line.step(1)
    deals = exchange_start(plane, mine, feed, feed_out, deal_sends.at[2], deal_receives.at[2])
    spread_pass(plane, more, 2, grads_out, sends.at[1], receives.at[1])
    spread_pass(plane, more, 4, grads_out, sends.at[1], receives.at[1])
    for step in range(2, planes):
        line.step(step)
        if step == 2:
            relay.hand_on(0)
            spread_pass(plane, more, 6, grads_out, sends.at[1], receives.at[1])
    for i in range(1, 4):
        relay.hand_on(i)
    for i in range(4):
        relay.finish(i)
    spread_finish(copies)
    spread_finish(more)
    for copy in qkv_copies + gain_copies:
        copy.wait_send()
    for copy in deals:
        copy.wait()

    @pl.when(jnp.logical_not(here))
    def _():
        send_rows.wait_send()

    for copy in keep[2:]:
        copy.wait()
    line.finish()


def inverse_root(values):
    return lax.rsqrt(jnp.mean(values * values, axis=1, keepdims=True) + EPSILON)


def second_kernel(
    planes, part, tokens, gain, feed, residual, spread_out, feed_out,
    near, stage, far, rs_sends, rs_receives, sends, receives, line_sends, line_receives, local,
):
    plane, mine = lax.axis_index("seq"), lax.axis_index("ctx")
    keep = pltpu.make_async_copy(feed, feed_out.at[plane], local)
    keep.start()
    greet(plane_peers(plane, (1, 2, 4, 6)) + other_planes(plane, mine, planes))
    copies = gather_sum_start(plane, part, near, rs_sends, rs_receives)
    line = Line([feed], [feed_out], planes, line_sends, line_receives)
    line.step(0)
    gather_sum_pass(plane, copies, part, near, stage, far, rs_sends, rs_receives)
    gather_sum_finish(copies)
    line.step(1)
    value = tokens[...].astype(F32) + gather_sum_total(mine, part, near, far)
    residual[...] = value
    spread_out[mine] = (value * inverse_root(value) * gain[...]).astype(BF16)
    spread(plane, mine, spread_out, sends, receives)
    for step in range(2, planes):
        line.step(step)
    keep.wait()
    line.finish()


def back_through_norm(upstream, values, gain):
    factor = inverse_root(values)
    normed = values * factor
    scaled = upstream * gain
    grad = factor * (scaled - normed * jnp.mean(scaled * normed, axis=1, keepdims=True))
    return grad, jnp.sum(upstream * normed, axis=0, keepdims=True)


def back_kernel(part, residual, grads, gain, residual_grad, gain_grad, spread_out, near, stage, far, rs_sends, rs_receives, sends, receives):
    plane, mine = lax.axis_index("seq"), lax.axis_index("ctx")
    greet(plane_peers(plane, (1, 2, 4, 6)))
    copies = gather_sum_start(plane, part, near, rs_sends, rs_receives)
    gather_sum_pass(plane, copies, part, near, stage, far, rs_sends, rs_receives)
    gather_sum_finish(copies)
    grad, gain_part = back_through_norm(gather_sum_total(mine, part, near, far), residual[...], gain[...])
    grad = grad + grads[...].astype(F32)
    gain_grad[...] = gain_part
    residual_grad[...] = grad
    spread_out[mine] = grad.astype(BF16)
    spread(plane, mine, spread_out, sends, receives)


class Fold:
    def __init__(self, own, stage, landed, planes, sends, receives):
        self.own, self.stage, self.landed, self.planes = own, stage, landed, planes
        self.sends, self.receives = sends, receives
        self.plane, self.mine = lax.axis_index("seq"), lax.axis_index("ctx")

    def copy(self, j, up):
        place = jnp.clip(self.plane + 1 if up else self.plane - 1, 0, self.planes - 1)
        at = (int(up), j)
        return remote(self.stage.at[at], self.landed.at[at], self.sends.at[at], self.receives.at[at], (place, self.mine))

    def advance(self, j, up):
        active = self.plane < j if up else self.plane > j
        inner = self.plane > 0 if up else self.plane < self.planes - 1

        @pl.when(active & inner)
        def _():
            self.copy(j, up).wait_recv()
            self.stage[int(up), j] = (
                self.own[j].astype(F32) + self.landed[int(up), j].astype(F32)
            ).astype(BF16)

        @pl.when(active & jnp.logical_not(inner))
        def _():
            self.stage[int(up), j] = self.own[j]

        @pl.when(active)
        def _():
            self.copy(j, up).start()

    def round(self, i):
        self.advance(self.planes - 1 - i, True)
        self.advance(i, False)

    def total(self, out):
        for j in range(self.planes):
            @pl.when(self.plane == j)
            def _():
                value = self.own[j].astype(F32)
                if j > 0:
                    self.copy(j, True).wait_recv()
                    value = value + self.landed[1, j].astype(F32)
                if j < self.planes - 1:
                    self.copy(j, False).wait_recv()
                    value = value + self.landed[0, j].astype(F32)
                rows = out.shape[1]
                for p in range(out.shape[0]):
                    out[p] = value[rows * p : rows * (p + 1), :].astype(BF16)

    def finish(self):
        for j in range(self.planes):
            for up in (True, False):
                @pl.when(self.plane < j if up else self.plane > j)
                def _():
                    self.copy(j, up).wait_send()


def leave_kernel(
    planes, part, layer_part, residual, residual_grad, tokens, gain, small, qkv_grad, feed_grad, out_w_grad,
    input_grad, layer_out, small_out, qkv_out, feed_out, out_w_out,
    near, stage, far, layer_near, layer_stage, layer_far, small_plane, small_all,
    fold_stage, fold_landed, qkv_sum, row_stage, row_landed, row_sum,
    rs_sends, rs_receives, small_sends, small_receives, fold_sends, fold_receives, row_fold_sends, row_fold_receives,
    deal_sends, deal_receives, row_sends, row_receives, local,
):
    plane, mine = lax.axis_index("seq"), lax.axis_index("ctx")
    keep_feed = pltpu.make_async_copy(feed_grad.at[mine], feed_out.at[mine], local.at[0])
    keep_feed.start()
    greet([((plane + dz) % planes, peer(d)) for dz in range(planes) for d in range(8) if dz or d])
    fold = Fold(qkv_grad, fold_stage, fold_landed, planes, fold_sends, fold_receives)
    row_fold = Fold(out_w_grad, row_stage, row_landed, planes, row_fold_sends, row_fold_receives)
    copies = gather_sum_start(plane, part, near, rs_sends.at[0], rs_receives.at[0])

    ends = (plane == 0) | (plane == planes - 1)

    @pl.when(ends)
    def _():
        for i in range(planes - 1):
            fold.round(i)
            row_fold.round(i)

    layer_copies = gather_sum_start(plane, layer_part, layer_near, rs_sends.at[1], rs_receives.at[1])
    gather_sum_pass(plane, copies, part, near, stage, far, rs_sends.at[0], rs_receives.at[0])

    @pl.when(jnp.logical_not(ends))
    def _():
        for i in range(2):
            fold.round(i)
            row_fold.round(i)

    rows = exchange_start(plane, mine, feed_grad, feed_out, deal_sends.at[0], deal_receives.at[0])
    gather_sum_pass(plane, layer_copies, layer_part, layer_near, layer_stage, layer_far, rs_sends.at[1], rs_receives.at[1])

    @pl.when(jnp.logical_not(ends))
    def _():
        for i in range(2, planes - 1):
            fold.round(i)
            row_fold.round(i)

    gather_sum_finish(copies)
    grad, gain_part = back_through_norm(
        gather_sum_total(mine, part, near, far), tokens[...].astype(F32), gain[...]
    )
    small_plane[mine] = small[...]
    small_plane[mine, 0:1, :] = gain_part
    near_copies = [
        remote(small_plane.at[mine], small_plane.at[mine], small_sends.at[0, d], small_receives.at[0, d], (plane, peer(d)))
        for d in range(1, 8)
    ]
    for copy in near_copies:
        copy.start()
    input_grad[...] = (residual_grad[...] + grad).astype(BF16)
    for copy in near_copies:
        copy.wait()
    total = small_plane[0]
    for i in range(1, 8):
        total = total + small_plane[i]
    small_all[plane] = total
    far_copies = [
        remote(small_all.at[plane], small_all.at[plane], small_sends.at[1, d], small_receives.at[1, d], ((plane + d) % planes, mine))
        for d in range(1, planes)
    ]
    for copy in far_copies:
        copy.start()
    row_fold.total(row_sum)
    owner_plane, owner = mine // 2, 4 * (mine % 2) + plane
    here = (owner_plane == plane) & (owner == mine)
    send_rows = remote(row_sum.at[0], out_w_out, row_sends, row_receives, (owner_plane, owner))
    keep_rows = pltpu.make_async_copy(row_sum.at[0], out_w_out, local.at[1])

    @pl.when(here)
    def _():
        keep_rows.start()

    @pl.when(jnp.logical_not(here))
    def _():
        send_rows.start()

    fold.total(qkv_sum)
    keep_qkv = pltpu.make_async_copy(qkv_sum.at[mine], qkv_out.at[mine], local.at[2])
    keep_qkv.start()
    rows += exchange_start(plane, mine, qkv_sum, qkv_out, deal_sends.at[1], deal_receives.at[1])
    gather_sum_finish(layer_copies)
    layer_out[...] = (residual[...] + gather_sum_total(mine, layer_part, layer_near, layer_far)).astype(BF16)
    for copy in far_copies:
        copy.wait()
    total = small_all[0]
    for i in range(1, planes):
        total = total + small_all[i]
    small_out[...] = total
    for copy in rows:
        copy.wait()

    @pl.when(here)
    def _():
        keep_rows.wait()

    @pl.when(jnp.logical_not(here))
    def _():
        send_rows.wait()

    row_fold.finish()
    keep_feed.wait()
    keep_qkv.wait()
    fold.finish()


def finish_kernel(qkv, feed, out_w, down, q_out, k_out, v_out, gate_out, up_out, out_w_out, down_out):
    groups, _, three = qkv.shape
    pair = three // 3
    half = feed.shape[2] // 2
    planes = half // TILE
    for c in range(groups):
        for i, out in enumerate((q_out, k_out, v_out)):
            out[:, pair * c : pair * (c + 1)] = qkv[c, :, pair * i : pair * (i + 1)].astype(F32)
        for i, out in enumerate((gate_out, up_out)):
            for s in range(planes):
                at = TILE * (groups * s + c)
                out[:, at : at + TILE] = feed[c, :, half * i + TILE * s : half * i + TILE * (s + 1)].astype(F32)
    out_w_out[...] = out_w[...].astype(F32)
    down_out[...] = down[...].astype(F32)


DMA = pltpu.SemaphoreType.DMA
ANYWHERE = pl.BlockSpec(memory_space=pl.ANY)
ON_CHIP = pl.BlockSpec(memory_space=pltpu.VMEM)


def communicate(kernel, name, number, micros, outs, scratch, args, spec, specs=None, out_specs=None):
    return pl.pallas_call(
        kernel,
        name=name,
        out_shape=tuple(jax.ShapeDtypeStruct(shape, kind) for shape, kind in outs),
        in_specs=specs or [spec] * len(args),
        out_specs=out_specs or (spec,) * len(outs),
        scratch_shapes=scratch,
        compiler_params=pltpu.CompilerParams(
            collective_id=number, has_side_effects=True, vmem_limit_bytes=48 << 20
        ),
        cost_estimate=pl.CostEstimate(flops=0, transcendentals=0, bytes_accessed=micros * 3500000),
    )(*args)


def sum_scratch(rows, width, count=1):
    return [pltpu.VMEM((4, rows, width), BF16)] * (3 * count)


PRECISE = lax.Precision.HIGHEST


def normalize(values):
    factor = lax.rsqrt(jnp.mean(values * values, axis=-1, keepdims=True) + EPSILON)
    return (values * factor, factor)


def normalize_back(normed, factor, gain, upstream):
    gain_grad = jnp.sum(upstream * normed, axis=0)
    scaled = upstream * gain
    return (
        factor * (scaled - normed * jnp.mean(scaled * normed, axis=-1, keepdims=True)),
        gain_grad,
    )


def add_rows(target, update, offset):
    current = lax.dynamic_slice_in_dim(target, offset, update.shape[0], 0)
    return lax.dynamic_update_slice_in_dim(target, current + update, offset, 0)


def masked_scores(query_ext, key_pad, offset, row_pos, layout):
    block_rows, halo_rows, key_reach, key_block, groups, score_scale = layout
    extent = key_block + 4 * key_reach
    key_slab = lax.dynamic_slice_in_dim(key_pad, offset, extent, 0)
    raw_scores = (
        jnp.einsum("nrhd,khd->nhrk", query_ext, key_slab, preferred_element_type=jnp.float32)
        * score_scale
    )
    key_pos = offset - 2 * key_reach + jnp.arange(extent, dtype=jnp.int32)
    keep_mask = (key_pos[None, None, :] <= row_pos[:, :, None]) & (key_pos >= 0)[None, None, :]
    return jnp.where(keep_mask[:, None], raw_scores, 0.0)


def convolve(zeroed, kernel, shift, extent, layout):
    block_rows, halo_rows, key_reach = (layout[0], layout[1], layout[2])
    result = jnp.zeros(zeroed.shape[:2] + (block_rows, extent), jnp.float32)
    for row_tap in range(halo_rows + 1):
        for key_tap in range(2 * key_reach + 1):
            column = shift + 3 * key_reach - key_tap
            result = (
                result
                + kernel[:, row_tap, key_tap][None, :, None, None]
                * zeroed[
                    :,
                    :,
                    halo_rows - row_tap : halo_rows - row_tap + block_rows,
                    column : column + extent,
                ]
            )
    return result


def attend_forward(query_ext, row_pos, key_pad, value_pad, kernel, layout):
    block_rows, halo_rows, key_reach, key_block, groups, score_scale = layout
    members = query_ext.shape[0]
    head_count = query_ext.shape[2]
    pair_width = value_pad.shape[1] // groups
    block_count = jnp.max(row_pos) // key_block + 1

    def advance(position, carried):
        running_max, running_sum, gathered = carried
        offset = position * key_block
        zeroed = masked_scores(query_ext, key_pad, offset, row_pos, layout)
        logits = convolve(zeroed, kernel, 0, key_block, layout)
        key_pos = offset + jnp.arange(key_block, dtype=jnp.int32)
        valid_mask = key_pos[None, None, :] <= row_pos[:, halo_rows:, None]
        logits = jnp.where(valid_mask[:, None], logits, NEGATIVE)
        new_max = jnp.maximum(running_max, jnp.max(logits, axis=-1))
        shrink = jnp.exp(running_max - new_max)
        weights = jnp.exp(logits - new_max[..., None])
        running_sum = running_sum * shrink + jnp.sum(weights, axis=-1)
        value_slab = lax.dynamic_slice_in_dim(
            value_pad, offset + 2 * key_reach, key_block, 0
        ).reshape(key_block, groups, pair_width)
        low_weights = weights.astype(jnp.bfloat16).reshape(
            members, groups, 2, block_rows, key_block
        )
        gathered = gathered * shrink.reshape(members, groups, 2, block_rows, 1) + jnp.einsum(
            "ngpik,kgc->ngpic", low_weights, value_slab, preferred_element_type=jnp.float32
        )
        return (new_max, running_sum, gathered)

    initial = (
        jnp.full((members, head_count, block_rows), NEGATIVE, jnp.float32),
        jnp.zeros((members, head_count, block_rows), jnp.float32),
        jnp.zeros((members, groups, 2, block_rows, pair_width), jnp.float32),
    )
    running_max, running_sum, gathered = lax.fori_loop(0, block_count, advance, initial)
    mixed_in = gathered / running_sum.reshape(members, groups, 2, block_rows, 1)
    return (mixed_in, running_max + jnp.log(running_sum))


def attend_backward(
    query_ext,
    row_pos,
    key_pad,
    value_pad,
    kernel,
    log_total,
    mixed_low,
    delta_rows,
    key_acc,
    value_acc,
    layout,
):
    block_rows, halo_rows, key_reach, key_block, groups, score_scale = layout
    members = query_ext.shape[0]
    ext_rows = query_ext.shape[1]
    head_count = query_ext.shape[2]
    model_width = value_pad.shape[1]
    pair_width = model_width // groups
    extent = key_block + 2 * key_reach
    block_count = jnp.max(row_pos) // key_block + 1

    def advance(position, carried):
        query_grad, key_acc, value_acc, kernel_grad = carried
        offset = position * key_block
        zeroed = masked_scores(query_ext, key_pad, offset, row_pos, layout)
        logits = convolve(zeroed, kernel, -key_reach, extent, layout)
        key_pos = offset - key_reach + jnp.arange(extent, dtype=jnp.int32)
        valid_mask = (key_pos[None, None, :] <= row_pos[:, halo_rows:, None]) & (key_pos >= 0)[
            None, None, :
        ]
        probability = jnp.where(valid_mask[:, None], jnp.exp(logits - log_total[..., None]), 0.0)
        value_slab = lax.dynamic_slice_in_dim(value_pad, offset + key_reach, extent, 0).reshape(
            extent, groups, pair_width
        )
        prob_grad = jnp.einsum(
            "ngpic,kgc->ngpik", mixed_low, value_slab, preferred_element_type=jnp.float32
        ).reshape(members, head_count, block_rows, extent)
        logit_grad = probability * (prob_grad - delta_rows[..., None])
        central = (
            probability[..., key_reach : key_reach + key_block]
            .astype(jnp.bfloat16)
            .reshape(members, groups, 2, block_rows, key_block)
        )
        value_part = jnp.einsum(
            "ngpik,ngpic->kgc", central, mixed_low, preferred_element_type=jnp.float32
        ).reshape(key_block, model_width)
        value_acc = add_rows(value_acc, value_part, offset)
        middle = logit_grad[..., key_reach : key_reach + key_block]
        tap_sums = []
        for row_tap in range(halo_rows + 1):
            for key_tap in range(2 * key_reach + 1):
                column = 3 * key_reach - key_tap
                tap_sums.append(
                    jnp.sum(
                        middle
                        * zeroed[
                            :,
                            :,
                            halo_rows - row_tap : halo_rows - row_tap + block_rows,
                            column : column + key_block,
                        ],
                        axis=(0, 2, 3),
                    )
                )
        kernel_grad = kernel_grad + jnp.stack(tap_sums, axis=1).reshape(
            head_count, halo_rows + 1, 2 * key_reach + 1
        )
        padded = jnp.pad(logit_grad, ((0, 0), (0, 0), (halo_rows, halo_rows), (0, 0)))
        score_grad = jnp.zeros((members, head_count, ext_rows, key_block), jnp.float32)
        for row_tap in range(halo_rows + 1):
            for key_tap in range(2 * key_reach + 1):
                score_grad = (
                    score_grad
                    + kernel[:, row_tap, key_tap][None, :, None, None]
                    * padded[:, :, row_tap : row_tap + ext_rows, key_tap : key_tap + key_block]
                )
        key_central = offset + jnp.arange(key_block, dtype=jnp.int32)
        keep_mask = (key_central[None, None, :] <= row_pos[:, :, None]) & (key_central >= 0)[
            None, None, :
        ]
        score_low = jnp.where(keep_mask[:, None], score_grad, 0.0).astype(jnp.bfloat16)
        key_slab = lax.dynamic_slice_in_dim(key_pad, offset + 2 * key_reach, key_block, 0)
        query_grad = (
            query_grad
            + jnp.einsum("nhrk,khd->nrhd", score_low, key_slab, preferred_element_type=jnp.float32)
            * score_scale
        )
        key_part = (
            jnp.einsum(
                "nhrk,nrhd->khd", score_low, query_ext, preferred_element_type=jnp.float32
            ).reshape(key_block, model_width)
            * score_scale
        )
        key_acc = add_rows(key_acc, key_part, offset)
        return (query_grad, key_acc, value_acc, kernel_grad)

    initial = (
        jnp.zeros(query_ext.shape, jnp.float32),
        key_acc,
        value_acc,
        jnp.zeros(kernel.shape, jnp.float32),
    )
    return lax.fori_loop(0, block_count, advance, initial)


def reorder(selection, rows):
    return jnp.dot(
        selection.astype(rows.dtype), rows, precision=PRECISE, preferred_element_type=jnp.float32
    ).astype(rows.dtype)


def pick(table, places):
    return jnp.stack(
        [lax.dynamic_index_in_dim(table, places[i], 0, keepdims=False) for i in range(2)]
    )


def accumulate(previous, update):
    return (
        update
        if previous is None
        else tuple((left + right for left, right in zip(previous, update)))
    )


def general_device(
    inputs,
    out_grad,
    pair_index,
    norm_gain,
    query_weight,
    key_weight,
    value_weight,
    score_kernel,
    head_mixing,
    group_gain,
    output_weight,
    second_gain,
    gate_weight,
    up_weight,
    down_weight,
):
    micro_count = inputs.shape[0]
    local_rows = inputs.shape[2]
    block_rows = local_rows // 2
    model_width = inputs.shape[3]
    head_count = score_kernel.shape[0]
    head_dim = model_width // head_count
    groups = head_count // 2
    halo_rows = score_kernel.shape[1] - 1
    key_reach = (score_kernel.shape[2] - 1) // 2
    block_count = 2 * lax.axis_size("ctx")
    seq_length = block_count * block_rows
    key_block = min(512, seq_length)
    layout = (block_rows, halo_rows, key_reach, key_block, groups, head_dim ** (-0.5))
    extended = block_rows + halo_rows
    my_index = lax.axis_index("ctx")
    slot_ids = jnp.arange(block_count, dtype=jnp.int32)
    mix_table = head_mixing.reshape(groups, 2, 2)
    pad_width = ((2 * key_reach, 2 * key_reach), (0, 0))
    layer_rows = []
    input_rows = []
    feed_sums = None
    attention_sums = None
    kernel_total = jnp.zeros(score_kernel.shape, jnp.float32)
    mixing_total = jnp.zeros(head_mixing.shape, jnp.float32)
    for batch_index in range(micro_count):
        gain_first, query_full, key_full, value_full, gain_group, out_full = (
            lax.all_gather(norm_gain, ("seq", "ctx"), axis=0, tiled=True),
            lax.all_gather(query_weight, ("seq", "ctx"), axis=0, tiled=True),
            lax.all_gather(key_weight, ("seq", "ctx"), axis=0, tiled=True),
            lax.all_gather(value_weight, ("seq", "ctx"), axis=0, tiled=True),
            lax.all_gather(group_gain, ("seq", "ctx"), axis=0, tiled=True),
            lax.all_gather(output_weight, ("seq", "ctx"), axis=0, tiled=True),
        )
        tokens = inputs[batch_index, 0].astype(jnp.float32)
        normed_first, factor_first = normalize(tokens)
        hidden = (normed_first * gain_first.astype(jnp.float32)).astype(jnp.bfloat16)
        query_proj = jnp.dot(hidden, query_full, preferred_element_type=jnp.float32).astype(
            jnp.bfloat16
        )
        key_proj = jnp.dot(hidden, key_full, preferred_element_type=jnp.float32).astype(
            jnp.bfloat16
        )
        value_proj = jnp.dot(hidden, value_full, preferred_element_type=jnp.float32).astype(
            jnp.bfloat16
        )
        tail_rows = jnp.concatenate(
            [query_proj[block_rows - halo_rows : block_rows], query_proj[local_rows - halo_rows :]],
            axis=0,
        )
        key_dealt, value_dealt, tail_dealt = (
            lax.all_gather(key_proj, "ctx", axis=0, tiled=True),
            lax.all_gather(value_proj, "ctx", axis=0, tiled=True),
            lax.all_gather(tail_rows, "ctx", axis=0, tiled=True),
        )
        pairs_row = pair_index[batch_index]
        owner_pair = jnp.repeat(pairs_row, 2)
        block_of_slot = jnp.where(slot_ids % 2 == 0, owner_pair, block_count - 1 - owner_pair)
        to_natural = (block_of_slot[None, :] == slot_ids[:, None]).astype(jnp.float32)
        slot_of_block = jnp.sum(
            jnp.where(block_of_slot[None, :] == slot_ids[:, None], slot_ids[None, :], 0), axis=1
        )
        my_pair = lax.dynamic_index_in_dim(pairs_row, my_index, 0, keepdims=False)
        my_blocks = jnp.stack([my_pair, block_count - 1 - my_pair])
        key_pad = jnp.pad(
            reorder(to_natural, key_dealt.reshape(block_count, -1)).reshape(
                seq_length, model_width
            ),
            pad_width,
        ).reshape(-1, head_count, head_dim)
        value_pad = jnp.pad(
            reorder(to_natural, value_dealt.reshape(block_count, -1)).reshape(
                seq_length, model_width
            ),
            pad_width,
        )
        tail_blocks = reorder(to_natural, tail_dealt.reshape(block_count, -1)).reshape(
            block_count, halo_rows, model_width
        )
        previous = jnp.concatenate(
            [jnp.zeros((1, halo_rows, model_width), jnp.bfloat16), tail_blocks[:-1]], axis=0
        )
        query_ext = jnp.concatenate(
            [pick(previous, my_blocks), query_proj.reshape(2, block_rows, model_width)], axis=1
        ).reshape(2, extended, head_count, head_dim)
        row_pos = (
            my_blocks[:, None] * block_rows
            - halo_rows
            + jnp.arange(extended, dtype=jnp.int32)[None, :]
        )
        mixed_in, log_total = attend_forward(
            query_ext, row_pos, key_pad, value_pad, score_kernel, layout
        )
        mixed_six = mixed_in.reshape(2, groups, 2, block_rows, 2, head_dim)
        heads_out = jnp.einsum(
            "gqp,ngpiqd->nigqd", mix_table, mixed_six, precision=PRECISE
        ).reshape(local_rows, head_count, head_dim)
        group_normed, group_factor = normalize(heads_out)
        normed_low = (
            group_normed.reshape(local_rows, model_width) * gain_group.astype(jnp.float32)
        ).astype(jnp.bfloat16)
        residual = tokens + jnp.dot(normed_low, out_full, preferred_element_type=jnp.float32)
        gain_second, gate_full, up_full, down_full = (
            lax.all_gather(second_gain, ("seq", "ctx"), axis=0, tiled=True),
            lax.all_gather(gate_weight, ("seq", "ctx"), axis=0, tiled=True),
            lax.all_gather(up_weight, ("seq", "ctx"), axis=0, tiled=True),
            lax.all_gather(down_weight, ("seq", "ctx"), axis=0, tiled=True),
        )
        normed_second, factor_second = normalize(residual)
        second_hidden = (normed_second * gain_second.astype(jnp.float32)).astype(jnp.bfloat16)
        gate_proj = jnp.dot(second_hidden, gate_full, preferred_element_type=jnp.float32)
        up_proj = jnp.dot(second_hidden, up_full, preferred_element_type=jnp.float32)
        activated = (jax.nn.silu(gate_proj) * up_proj).astype(jnp.bfloat16)
        layer_rows.append(
            (residual + jnp.dot(activated, down_full, preferred_element_type=jnp.float32)).astype(
                jnp.bfloat16
            )
        )
        gain_second, gate_full, up_full, down_full = (
            lax.all_gather(second_gain, ("seq", "ctx"), axis=0, tiled=True),
            lax.all_gather(gate_weight, ("seq", "ctx"), axis=0, tiled=True),
            lax.all_gather(up_weight, ("seq", "ctx"), axis=0, tiled=True),
            lax.all_gather(down_weight, ("seq", "ctx"), axis=0, tiled=True),
        )
        grad_rows = out_grad[batch_index, 0]
        hid_grad = jnp.dot(grad_rows, down_full.T, preferred_element_type=jnp.float32)
        down_grad = jnp.dot(activated.T, grad_rows, preferred_element_type=jnp.float32)
        sigmoid_gate = jax.nn.sigmoid(gate_proj)
        up_low = (hid_grad * gate_proj * sigmoid_gate).astype(jnp.bfloat16)
        gate_low = (
            hid_grad * up_proj * sigmoid_gate * (1.0 + gate_proj * (1.0 - sigmoid_gate))
        ).astype(jnp.bfloat16)
        second_grad = jnp.dot(gate_low, gate_full.T, preferred_element_type=jnp.float32) + jnp.dot(
            up_low, up_full.T, preferred_element_type=jnp.float32
        )
        gate_grad = jnp.dot(second_hidden.T, gate_low, preferred_element_type=jnp.float32)
        up_grad = jnp.dot(second_hidden.T, up_low, preferred_element_type=jnp.float32)
        residual_part, gain_second_grad = normalize_back(
            normed_second, factor_second, gain_second.astype(jnp.float32), second_grad
        )
        residual_grad = grad_rows.astype(jnp.float32) + residual_part
        feed_shards = (
            lax.psum_scatter(gain_second_grad, ("seq", "ctx"), scatter_dimension=0, tiled=True),
            lax.psum_scatter(gate_grad, ("seq", "ctx"), scatter_dimension=0, tiled=True),
            lax.psum_scatter(up_grad, ("seq", "ctx"), scatter_dimension=0, tiled=True),
            lax.psum_scatter(down_grad, ("seq", "ctx"), scatter_dimension=0, tiled=True),
        )
        feed_sums = accumulate(feed_sums, feed_shards)
        gain_first, query_full, key_full, value_full, gain_group, out_full = (
            lax.all_gather(norm_gain, ("seq", "ctx"), axis=0, tiled=True),
            lax.all_gather(query_weight, ("seq", "ctx"), axis=0, tiled=True),
            lax.all_gather(key_weight, ("seq", "ctx"), axis=0, tiled=True),
            lax.all_gather(value_weight, ("seq", "ctx"), axis=0, tiled=True),
            lax.all_gather(group_gain, ("seq", "ctx"), axis=0, tiled=True),
            lax.all_gather(output_weight, ("seq", "ctx"), axis=0, tiled=True),
        )
        attended_low = residual_grad.astype(jnp.bfloat16)
        out_weight_grad = jnp.dot(normed_low.T, attended_low, preferred_element_type=jnp.float32)
        normed_grad = jnp.dot(attended_low, out_full.T, preferred_element_type=jnp.float32)
        heads_grad, gain_group_grad = normalize_back(
            group_normed,
            group_factor,
            gain_group.astype(jnp.float32).reshape(head_count, head_dim),
            normed_grad.reshape(local_rows, head_count, head_dim),
        )
        heads_five = heads_grad.reshape(2, block_rows, groups, 2, head_dim)
        mixing_total = mixing_total + jnp.einsum(
            "nigqd,ngpiqd->gqp", heads_five, mixed_six, precision=PRECISE
        ).reshape(head_count, 2)
        mixed_grad = jnp.einsum(
            "gqp,nigqd->ngpiqd", mix_table, heads_five, precision=PRECISE
        ).reshape(2, groups, 2, block_rows, 2 * head_dim)
        mixed_low = mixed_grad.astype(jnp.bfloat16)
        delta_rows = jnp.sum(mixed_low.astype(jnp.float32) * mixed_in, axis=-1).reshape(
            2, head_count, block_rows
        )
        key_acc = jnp.zeros((seq_length, model_width), jnp.float32)
        value_acc = jnp.zeros((seq_length, model_width), jnp.float32)
        query_grad, key_acc, value_acc, kernel_part = attend_backward(
            query_ext,
            row_pos,
            key_pad,
            value_pad,
            score_kernel,
            log_total,
            mixed_low,
            delta_rows,
            key_acc,
            value_acc,
            layout,
        )
        kernel_total = kernel_total + kernel_part
        halo_grad = query_grad[:, :halo_rows].reshape(2, halo_rows, model_width)
        own_grad = query_grad[:, halo_rows:].reshape(2, block_rows, model_width)
        target_slot = pick(slot_of_block, jnp.maximum(my_blocks - 1, 0))
        routing = ((slot_ids[None, :] == target_slot[:, None]) & (my_blocks > 0)[:, None]).astype(
            jnp.float32
        )
        tail_grad = jnp.einsum("ws,wrc->src", routing, halo_grad, precision=PRECISE).reshape(
            block_count * halo_rows, model_width
        )
        key_back = reorder(to_natural.T, key_acc.reshape(block_count, -1)).reshape(
            seq_length, model_width
        )
        value_back = reorder(to_natural.T, value_acc.reshape(block_count, -1)).reshape(
            seq_length, model_width
        )
        key_mine, value_mine, tail_mine = (
            lax.psum_scatter(
                key_back.astype(jnp.bfloat16), "ctx", scatter_dimension=0, tiled=True
            ).astype(jnp.float32),
            lax.psum_scatter(
                value_back.astype(jnp.bfloat16), "ctx", scatter_dimension=0, tiled=True
            ).astype(jnp.float32),
            lax.psum_scatter(
                tail_grad.astype(jnp.bfloat16), "ctx", scatter_dimension=0, tiled=True
            ).astype(jnp.float32),
        )
        tail_mine = tail_mine.reshape(2, halo_rows, model_width)
        query_total = jnp.concatenate(
            [
                own_grad[:, : block_rows - halo_rows],
                own_grad[:, block_rows - halo_rows :] + tail_mine,
            ],
            axis=1,
        ).reshape(local_rows, model_width)
        query_low = query_total.astype(jnp.bfloat16)
        key_low = key_mine.astype(jnp.bfloat16)
        value_low = value_mine.astype(jnp.bfloat16)
        query_w_grad = jnp.dot(hidden.T, query_low, preferred_element_type=jnp.float32)
        key_w_grad = jnp.dot(hidden.T, key_low, preferred_element_type=jnp.float32)
        value_w_grad = jnp.dot(hidden.T, value_low, preferred_element_type=jnp.float32)
        hidden_grad = (
            jnp.dot(query_low, query_full.T, preferred_element_type=jnp.float32)
            + jnp.dot(key_low, key_full.T, preferred_element_type=jnp.float32)
            + jnp.dot(value_low, value_full.T, preferred_element_type=jnp.float32)
        )
        token_part, gain_first_grad = normalize_back(
            normed_first, factor_first, gain_first.astype(jnp.float32), hidden_grad
        )
        input_rows.append((residual_grad + token_part).astype(jnp.bfloat16))
        attention_shards = (
            lax.psum_scatter(gain_first_grad, ("seq", "ctx"), scatter_dimension=0, tiled=True),
            lax.psum_scatter(query_w_grad, ("seq", "ctx"), scatter_dimension=0, tiled=True),
            lax.psum_scatter(key_w_grad, ("seq", "ctx"), scatter_dimension=0, tiled=True),
            lax.psum_scatter(value_w_grad, ("seq", "ctx"), scatter_dimension=0, tiled=True),
            lax.psum_scatter(
                gain_group_grad.reshape(model_width),
                ("seq", "ctx"),
                scatter_dimension=0,
                tiled=True,
            ),
            lax.psum_scatter(out_weight_grad, ("seq", "ctx"), scatter_dimension=0, tiled=True),
        )
        attention_sums = accumulate(attention_sums, attention_shards)
    kernel_sum, mixing_sum = lax.psum((kernel_total, mixing_total), ("seq", "ctx"))
    layer_out = jnp.stack(layer_rows)[:, None]
    input_grad = jnp.stack(input_rows)[:, None]
    return (
        layer_out,
        input_grad,
        attention_sums[0],
        attention_sums[1],
        attention_sums[2],
        attention_sums[3],
        kernel_sum,
        mixing_sum,
        attention_sums[4],
        attention_sums[5],
        feed_sums[0],
        feed_sums[1],
        feed_sums[2],
        feed_sums[3],
    )


def on_device(
    inputs,
    out_grad,
    pair_index,
    norm_gain,
    query_weight,
    key_weight,
    value_weight,
    score_kernel,
    head_mixing,
    group_gain,
    output_weight,
    second_gain,
    gate_weight,
    up_weight,
    down_weight,
):
    groups, planes = lax.axis_size("ctx"), lax.axis_size("seq")
    heads, width = score_kernel.shape[0], inputs.shape[3]
    if groups != 8 or heads != 2 * groups or (groups * inputs.shape[2]) % TILE:
        return general_device(
            inputs, out_grad, pair_index, norm_gain, query_weight, key_weight, value_weight,
            score_kernel, head_mixing, group_gain, output_weight, second_gain, gate_weight,
            up_weight, down_weight,
        )
    micro, local = inputs.shape[0], inputs.shape[2]
    blk, seq = local // 2, local * groups
    blocks = seq // blk
    pair = width // groups
    owned = width // (groups * planes)
    hidden = gate_weight.shape[1]
    chunk = hidden // (groups * planes)
    me = lax.axis_index("ctx")
    tokens_low = inputs.reshape(micro * local, width)
    grads_low = out_grad.reshape(micro * local, width)

    packed = jnp.pad(
        jnp.stack([norm_gain, group_gain, second_gain]).astype(F32), ((0, 5), (0, TILE - owned))
    )

    def split_columns(weight):
        return jnp.transpose(weight.reshape(owned, groups, pair), (1, 0, 2))

    def split_hidden(weight):
        return jnp.transpose(weight.reshape(owned, planes, groups, chunk), (2, 0, 1, 3)).reshape(
            groups, owned, planes * chunk
        )

    qkv_send = jnp.concatenate(
        [split_columns(query_weight), split_columns(key_weight), split_columns(value_weight)], axis=2
    )
    feed_send = jnp.concatenate([split_hidden(gate_weight), split_hidden(up_weight)], axis=2)
    rows_all = micro * local
    feed_mine, qkv, out_rows, gains, all_tokens, all_grads = communicate(
        functools.partial(enter_kernel, planes), "enter", 1, 60,
        [
            (feed_send.shape, BF16),
            ((planes,) + qkv_send.shape, BF16),
            ((4, owned, width), BF16),
            ((planes, groups) + packed.shape, F32),
            ((groups, rows_all, width), BF16),
            ((groups, rows_all, width), BF16),
        ],
        [DMA((3, groups))] * 2 + [DMA, DMA((4,))] + [DMA((2, groups))] * 2
        + [DMA((2, 2, planes))] * 2 + [DMA((2, 4))] * 2 + [DMA((6,))],
        (feed_send, qkv_send, output_weight, packed, tokens_low, grads_low), ANYWHERE,
    )
    all_tokens, down_mine = lax.optimization_barrier((all_tokens.reshape(-1, width), down_weight))
    all_grads = all_grads.reshape(-1, width)
    down = lax.all_gather(down_mine, "seq", axis=0, tiled=True)
    gains = jnp.transpose(gains.reshape((groups * planes,) + packed.shape)[:, :3, :owned], (1, 0, 2))
    gains = gains.reshape(3, width)
    gain_first, gain_group, gain_second = gains[0:1], gains[1:2], gains[2:3]
    qkv = qkv.reshape(width, 3 * pair)
    out_rows = out_rows.reshape(pair, width)

    slots = jnp.arange(blocks, dtype=jnp.int32)
    owner = jnp.repeat(pair_index, 2, axis=1)
    block_of_slot = jnp.where(slots % 2 == 0, owner, blocks - 1 - owner)
    place = (
        (slots // 2)[None] * (2 * micro)
        + 2 * jnp.arange(micro, dtype=jnp.int32)[:, None]
        + (slots % 2)[None]
    )
    blk_table = jnp.sum(
        jnp.where(block_of_slot[:, None, :] == slots[None, :, None], place[:, None, :], 0), axis=2
    ).astype(jnp.int32)
    ker = lax.dynamic_slice_in_dim(score_kernel, 2 * me, 2, 0)
    mix = jnp.repeat(lax.dynamic_slice_in_dim(head_mixing, 2 * me, 2, 0), pair // 2, axis=0).T
    gain_pair = lax.dynamic_slice_in_dim(gain_group, pair * me, pair, 1)
    scale = (width // heads) ** (-0.5)

    normed_all, _ = normalize(all_tokens.astype(F32))
    hidden_all = (normed_all * gain_first).astype(BF16)
    heads_in = jnp.dot(hidden_all, qkv, preferred_element_type=F32).astype(BF16)
    mixed, y, prob = pair_forward(blk_table, ker, mix, gain_pair, heads_in, micro, seq, blk, scale)
    attended = jnp.dot(mixed, out_rows, preferred_element_type=F32).astype(BF16)
    sum_spec = sum_scratch(rows_all, width) + [DMA((groups,))] * 4
    residual, second_all, feed = communicate(
        functools.partial(second_kernel, planes), "second", 2, 50,
        [
            ((rows_all, width), F32),
            ((groups, rows_all, width), BF16),
            ((planes,) + feed_send.shape, BF16),
        ],
        sum_spec + [DMA((1, 2, planes))] * 2 + [DMA],
        (attended.reshape(groups, rows_all, width), tokens_low, gain_second, feed_mine),
        None, [ON_CHIP] * 3 + [ANYWHERE], (ON_CHIP, ON_CHIP, ANYWHERE),
    )
    feed = feed.reshape(width, -1)
    second_all = second_all.reshape(-1, width)

    half = planes * chunk
    both = jnp.dot(second_all, feed, preferred_element_type=F32)
    gate, up = both[:, :half], both[:, half:]
    hid_grad = lax.dot_general(all_grads, down, (((1,), (1,)), ((), ())), preferred_element_type=F32)
    sigmoid = jax.nn.sigmoid(gate)
    active = (gate * sigmoid * up).astype(BF16)
    up_low = (hid_grad * gate * sigmoid).astype(BF16)
    gate_low = (hid_grad * up * sigmoid * (1.0 + gate * (1.0 - sigmoid))).astype(BF16)
    lows = jnp.concatenate([gate_low, up_low], axis=1)
    second_part = lax.dot_general(lows, feed, (((1,), (1,)), ((), ())), preferred_element_type=F32)
    feed_grad = lax.dot_general(second_all, lows, (((0,), (0,)), ((), ())), preferred_element_type=F32)
    down_grad = lax.dot_general(active, all_grads, (((0,), (0,)), ((), ())), preferred_element_type=F32)
    second_part, feed_grad, down_grad = lax.optimization_barrier(
        (second_part.astype(BF16), feed_grad.astype(BF16), down_grad.astype(BF16))
    )
    layer_part = jnp.dot(active, down, preferred_element_type=F32)
    residual_grad, gain_second_grad, all_attended = communicate(
        back_kernel, "back", 3, 45,
        [((rows_all, width), F32), ((1, width), F32), ((groups, rows_all, width), BF16)],
        sum_spec,
        (second_part.reshape(groups, rows_all, width), residual, grads_low, gain_second),
        ON_CHIP,
    )
    all_attended = all_attended.reshape(-1, width)
    mixed_grad = lax.dot_general(
        all_attended, out_rows, (((1,), (1,)), ((), ())), preferred_element_type=F32
    ).astype(BF16)
    out_w_grad = lax.dot_general(
        mixed, all_attended, (((0,), (0,)), ((), ())), preferred_element_type=F32
    )
    qkv_low, group_part, mix_part, ker_part = pair_backward(
        blk_table, ker, mix, gain_pair, heads_in, mixed_grad, y, prob, seq, blk, scale
    )
    hidden_part = lax.dot_general(qkv_low, qkv, (((1,), (1,)), ((), ())), preferred_element_type=F32)
    qkv_grad = lax.dot_general(hidden_all, qkv_low, (((0,), (0,)), ((), ())), preferred_element_type=F32)
    taps = score_kernel.shape[1] * score_kernel.shape[2]
    ker_mine = jnp.sum(ker_part, axis=2)[:, :taps]
    mix_mine = jnp.sum(mix_part.reshape(2, 2, pair // 2), axis=2).T
    row = lax.dynamic_update_slice
    group_all = row(jnp.zeros((1, width), F32), group_part, (0, pair * me))
    ker_all = row(jnp.zeros((heads, taps), F32), ker_mine, (2 * me, 0)).reshape(1, -1)
    mix_all = row(jnp.zeros((heads, 2), F32), mix_mine, (2 * me, 0)).reshape(1, -1)
    tap_rows = -(-heads * taps // width)
    taps_all = jnp.pad(ker_all, ((0, 0), (0, tap_rows * width - heads * taps))).reshape(-1, width)
    mix_all = jnp.pad(mix_all, ((0, 0), (0, width - 2 * heads)))
    small = jnp.concatenate(
        [jnp.zeros((1, width), F32), gain_second_grad, group_all, mix_all, taps_all]
    )
    small = jnp.pad(small, ((0, -small.shape[0] % 8), (0, 0)))
    down_sum = lax.psum_scatter(down_grad, "seq", scatter_dimension=0, tiled=True)
    feed_sum = lax.psum_scatter(feed_grad, "seq", scatter_dimension=0, tiled=True)
    input_grad, layer_out, sums, qkv_back, feed_back, out_w_back = communicate(
        functools.partial(leave_kernel, planes), "leave", 4, 60,
        [
            ((rows_all, width), BF16),
            ((rows_all, width), BF16),
            (small.shape, F32),
            (qkv_send.shape, BF16),
            (feed_send.shape, BF16),
            (output_weight.shape, BF16),
        ],
        sum_scratch(rows_all, width, 2)
        + [pltpu.VMEM((groups,) + small.shape, F32), pltpu.VMEM((planes,) + small.shape, F32)]
        + [pltpu.VMEM((2, planes, groups * owned, 3 * pair), BF16)] * 2
        + [pltpu.VMEM(qkv_send.shape, BF16)]
        + [pltpu.VMEM((2, planes, owned, width), BF16)] * 2
        + [pltpu.VMEM((1, owned, width), BF16)]
        + [DMA((2, groups))] * 4
        + [DMA((2, planes))] * 4
        + [DMA((2, groups))] * 2
        + [DMA, DMA, DMA((3,))],
        (
            hidden_part.astype(BF16).reshape(groups, rows_all, width),
            layer_part.astype(BF16).reshape(groups, rows_all, width),
            residual, residual_grad, tokens_low, gain_first, small,
            qkv_grad.astype(BF16).reshape(planes, groups * owned, 3 * pair),
            feed_sum.reshape(feed_send.shape), out_w_grad.astype(BF16).reshape(planes, owned, width),
        ),
        None, [ON_CHIP] * 8 + [ANYWHERE, ON_CHIP], (ON_CHIP,) * 3 + (ANYWHERE,) * 3,
    )
    plain = [(owned, width)] * 3 + [(owned, hidden)] * 2 + [(owned, width), (chunk, width)]
    q_back, k_back, v_back, gate_back, up_back, out_w_out, down_out = pl.pallas_call(
        finish_kernel,
        name="finish",
        out_shape=tuple(jax.ShapeDtypeStruct(shape, F32) for shape in plain),
        compiler_params=pltpu.CompilerParams(vmem_limit_bytes=32 << 20),
    )(qkv_back, feed_back, out_w_back, down_sum)

    at = (lax.axis_index("seq") * groups + me) * owned
    gain_outs = [lax.dynamic_slice_in_dim(sums[i], at, owned, 0) for i in range(3)]
    ker_out = sums[4 : 4 + tap_rows].reshape(-1)[: heads * taps].reshape(score_kernel.shape)
    mix_out = sums[3, : 2 * heads].reshape(heads, 2)
    shape = inputs.shape
    return (
        layer_out.reshape(shape),
        input_grad.reshape(shape),
        gain_outs[0],
        q_back,
        k_back,
        v_back,
        ker_out,
        mix_out,
        gain_outs[2],
        out_w_out,
        gain_outs[1],
        gate_back,
        up_back,
        down_out,
    )


def solution(mesh):
    placed = (
        P(None, "seq", "ctx", None),
        P(None, "seq", "ctx", None),
        P(),
        P(("seq", "ctx")),
        P(("seq", "ctx"), None),
        P(("seq", "ctx"), None),
        P(("seq", "ctx"), None),
        P(),
        P(),
        P(("seq", "ctx")),
        P(("seq", "ctx"), None),
        P(("seq", "ctx")),
        P(("seq", "ctx"), None),
        P(("seq", "ctx"), None),
        P(("seq", "ctx"), None),
    )
    return jax.shard_map(
        on_device,
        mesh=mesh,
        in_specs=placed,
        out_specs=(
            P(None, "seq", "ctx", None),
            P(None, "seq", "ctx", None),
            P(("seq", "ctx")),
            P(("seq", "ctx"), None),
            P(("seq", "ctx"), None),
            P(("seq", "ctx"), None),
            P(),
            P(),
            P(("seq", "ctx")),
            P(("seq", "ctx"), None),
            P(("seq", "ctx")),
            P(("seq", "ctx"), None),
            P(("seq", "ctx"), None),
            P(("seq", "ctx"), None),
        ),
        check_vma=False,
    )
```

```python
import functools

import jax
import jax.numpy as jnp
from jax import lax
from jax.experimental import pallas as pl
from jax.experimental.pallas import tpu as pltpu
from jax.sharding import PartitionSpec as P

EPSILON = 1e-05
NEGATIVE = -1e30
F32 = jnp.float32
BF16 = jnp.bfloat16
TILE = 128


def nt(left, right):
    return lax.dot_general(left, right, (((1,), (1,)), ((), ())), preferred_element_type=F32)


def tn(left, right):
    return lax.dot_general(left, right, (((0,), (0,)), ((), ())), preferred_element_type=F32)


def nn(left, right):
    return lax.dot_general(left, right, (((1,), (0,)), ((), ())), preferred_element_type=F32)


def natural_rows(blk_ref, m, blk, seq):
    return [pl.multiple_of(blk_ref[m, b] * blk, blk) for b in range(seq // blk)]


def head_lanes(width):
    return lax.broadcasted_iota(jnp.int32, (1, width), 1) < width // 2


def load_heads(blk_ref, m, blk, seq, qkv_ref, qm, kf, ks, vn):
    width = vn.shape[1]
    first = head_lanes(width)
    kf[0:8, :] = jnp.zeros((8, width), F32)
    kf[seq : seq + TILE + 8, :] = jnp.zeros((TILE + 8, width), F32)
    for b, row in enumerate(natural_rows(blk_ref, m, blk, seq)):
        here = pl.ds(blk * b, blk)
        q = qkv_ref[pl.ds(row, blk), 0:width].astype(F32)
        qm[0, here, :] = jnp.where(first, q, 0.0).astype(BF16)
        qm[1, here, :] = jnp.where(first, 0.0, q).astype(BF16)
        kf[pl.ds(blk * b + 5, blk), :] = qkv_ref[pl.ds(row, blk), width : 2 * width].astype(F32)
        vn[here, :] = qkv_ref[pl.ds(row, blk), 2 * width : 3 * width]
    ks[...] = kf[0 : seq + TILE, :].astype(BF16)


def scores(qm, ks, h, rb, upto, scale):
    rows = pl.ds(TILE * rb, TILE)
    raw = nt(qm[h, rows, :], ks[0 : TILE * upto, :]) * scale
    key = lax.broadcasted_iota(jnp.int32, raw.shape, 1) - 5
    row = lax.broadcasted_iota(jnp.int32, raw.shape, 0) + TILE * rb
    return jnp.where((key >= 0) & (key <= row), raw, 0.0)


def head_factor(values, first, dim):
    squares = values * values
    own = jnp.sum(jnp.where(first, squares, 0.0), axis=1, keepdims=True)
    other = jnp.sum(jnp.where(first, 0.0, squares), axis=1, keepdims=True)
    return jnp.where(
        first, lax.rsqrt(own / dim + EPSILON), lax.rsqrt(other / dim + EPSILON)
    )


def forward_kernel(
    seq, blk, rows_tap, keys_tap, scale,
    blk_ref, ker_ref, mix_ref, gain_ref, qkv_ref,
    z_ref, y_ref, p_ref,
    qm, kf, ks, vn, shi, slo, thi, tlo, run, logit,
):
    m = pl.program_id(0)
    width = vn.shape[1]
    first = head_lanes(width)
    tiles = seq // TILE

    @pl.when(m == 0)
    def _():
        shi[...] = jnp.zeros(shi.shape, BF16)
        slo[...] = jnp.zeros(slo.shape, BF16)
        away = lax.broadcasted_iota(jnp.int32, (2 * TILE, TILE), 0) - lax.broadcasted_iota(
            jnp.int32, (2 * TILE, TILE), 1
        )
        for h in range(2):
            for a in range(rows_tap):
                band = jnp.zeros((2 * TILE, TILE), F32)
                for t in range(keys_tap):
                    band = jnp.where(away == keys_tap - 1 - t, ker_ref[h, a, t], band)
                high = band.astype(BF16)
                thi[h, :, TILE * a : TILE * (a + 1)] = high
                tlo[h, :, TILE * a : TILE * (a + 1)] = (band - high.astype(F32)).astype(BF16)

    load_heads(blk_ref, m, blk, seq, qkv_ref, qm, kf, ks, vn)
    for h in range(2):
        for rb in range(tiles):
            upto = min(rb + 2, tiles + 1)
            zeroed = scores(qm, ks, h, rb, upto, scale)
            high = zeroed.astype(BF16)
            shi[pl.ds(16 + TILE * rb, TILE), 0 : TILE * upto] = high
            slo[pl.ds(16 + TILE * rb, TILE), 0 : TILE * upto] = (zeroed - high.astype(F32)).astype(BF16)
        for b in range(tiles):
            count = seq - TILE * b
            rows = pl.ds(TILE * b, count + 16)
            lanes = pl.ds(TILE * b, 2 * TILE)
            high, low = shi[rows, lanes], slo[rows, lanes]
            run[0 : count + 16, :] = nn(high, thi[h]) + nn(low, thi[h]) + nn(high, tlo[h])
            total = run[16 : 16 + count, 0:TILE]
            for a in range(1, rows_tap):
                total = total + run[pl.ds(16 - a, count), TILE * a : TILE * (a + 1)]
            logit[pl.ds(TILE * b, count), TILE * b : TILE * (b + 1)] = total
        for rb in range(tiles):
            rows = pl.ds(TILE * rb, TILE)
            wide = TILE * (rb + 1)
            value = logit[rows, 0:wide]
            key = lax.broadcasted_iota(jnp.int32, value.shape, 1)
            row = lax.broadcasted_iota(jnp.int32, value.shape, 0) + TILE * rb
            value = jnp.where(key <= row, value, NEGATIVE)
            weight = jnp.exp(value - jnp.max(value, axis=1, keepdims=True))
            weight = weight / jnp.sum(weight, axis=1, keepdims=True)
            lowered = weight.astype(BF16)
            p_ref[0, h, rows, 0:wide] = lowered
            y_ref[0, h, rows, :] = nn(lowered, vn[0:wide, :])
    out = mix_ref[0:1, :] * y_ref[0, 0] + mix_ref[1:2, :] * y_ref[0, 1]
    normed = out * head_factor(out, first, width // 2)
    final = (normed * gain_ref[1:2, :]).astype(BF16)
    for b, row in enumerate(natural_rows(blk_ref, m, blk, seq)):
        z_ref[pl.ds(row, blk), :] = final[blk * b : blk * (b + 1), :]


def backward_kernel(
    seq, blk, rows_tap, keys_tap, scale,
    blk_ref, ker_ref, mix_ref, gain_ref, qkv_ref, zg_ref, y_ref, p_ref,
    low_ref, gg_ref, hm_ref, kg_ref,
    qm, kf, ks, vn, sb, up, zn, yl, cg, cs, eb, qa, ka, acc,
):
    m = pl.program_id(0)
    width = vn.shape[1]
    first = head_lanes(width)
    tiles = seq // TILE
    wide_u = 3 * TILE
    span = keys_tap - 1
    lanes_all = rows_tap * TILE

    @pl.when(m == 0)
    def _():
        gg_ref[...] = jnp.zeros(gg_ref.shape, F32)
        hm_ref[...] = jnp.zeros(hm_ref.shape, F32)
        acc[...] = jnp.zeros(acc.shape, F32)
        cg[...] = jnp.zeros(cg.shape, F32)
        cs[...] = jnp.zeros(cs.shape, BF16)
        eb[...] = jnp.zeros(eb.shape, BF16)
        sb[...] = jnp.zeros(sb.shape, BF16)
        away = lax.broadcasted_iota(jnp.int32, (wide_u, 2 * TILE), 0) - lax.broadcasted_iota(
            jnp.int32, (wide_u, 2 * TILE), 1
        )
        for h in range(2):
            for a in range(rows_tap):
                band = jnp.zeros((wide_u, 2 * TILE), F32)
                for t in range(keys_tap):
                    band = jnp.where(away == TILE - span + t, ker_ref[h, a, t], band)
                up[h, wide_u * a : wide_u * (a + 1), :] = band.astype(BF16)

    load_heads(blk_ref, m, blk, seq, qkv_ref, qm, kf, ks, vn)
    places = natural_rows(blk_ref, m, blk, seq)
    for b, row in enumerate(places):
        zn[pl.ds(blk * b, blk), :] = zg_ref[pl.ds(row, blk), :].astype(F32)
    dim = width // 2
    y0, y1 = y_ref[0, 0], y_ref[0, 1]
    out = mix_ref[0:1, :] * y0 + mix_ref[1:2, :] * y1
    factor = head_factor(out, first, dim)
    normed = out * factor
    upstream = zn[...]
    gg_ref[...] += jnp.sum(upstream * normed, axis=0, keepdims=True)
    scaled = upstream * gain_ref[1:2, :]
    both = scaled * normed
    own = jnp.sum(jnp.where(first, both, 0.0), axis=1, keepdims=True) / dim
    other = jnp.sum(jnp.where(first, 0.0, both), axis=1, keepdims=True) / dim
    out_grad = factor * (scaled - normed * jnp.where(first, own, other))
    hm_ref[0:1, :] += jnp.sum(out_grad * y0, axis=0, keepdims=True)
    hm_ref[1:2, :] += jnp.sum(out_grad * y1, axis=0, keepdims=True)
    yl[0] = (mix_ref[0:1, :] * out_grad).astype(BF16)
    yl[1] = (mix_ref[1:2, :] * out_grad).astype(BF16)

    for b in range(tiles):
        rows = pl.ds(TILE * b, seq - TILE * b)
        lanes = pl.ds(TILE * b, TILE)
        part = tn(p_ref[0, 0, rows, lanes], yl[0, rows, :]) + tn(p_ref[0, 1, rows, lanes], yl[1, rows, :])
        part = part.astype(BF16)
        for i in range(TILE // blk):
            low_ref[pl.ds(places[b * (TILE // blk) + i], blk), 2 * width : 3 * width] = part[blk * i : blk * (i + 1), :]

    ka[...] = jnp.zeros(ka.shape, F32)
    for h in range(2):
        for rb in range(tiles):
            rows = pl.ds(TILE * rb, TILE)
            upto = min(rb + 2, tiles + 1)
            sb[rows, 0 : TILE * upto] = scores(qm, ks, h, rb, upto, scale).astype(BF16)
            wide = TILE * (rb + 1)
            prob = p_ref[0, h, rows, 0:wide].astype(F32)
            grad = nt(yl[h, rows, :], vn[0:wide, :])
            both = prob * grad
            cg[rows, 0:wide] = both - prob * jnp.sum(both, axis=1, keepdims=True)
        for b in range(tiles):
            start = max(0, TILE * b - 16)
            count = seq - start
            for a in range(rows_tap):
                cs[pl.ds(start, count), pl.ds(lanes_all * b + TILE * a, TILE)] = cg[
                    pl.ds(start + a, count), TILE * b : TILE * (b + 1)
                ].astype(BF16)
            acc[h] += tn(
                sb[pl.ds(start, count), pl.ds(TILE * b, 2 * TILE)],
                cs[pl.ds(start, count), pl.ds(lanes_all * b, lanes_all)],
            )
        for b in range(0, tiles + 1, 2):
            start = max(0, TILE * b - 16)
            count = seq - start
            columns = min(2, tiles + 1 - b)
            left, right = [], []
            for a in range(rows_tap):
                for piece in range(columns + 1):
                    block = b - 1 + piece
                    if 0 <= block < tiles:
                        left.append(cs[pl.ds(start, count), pl.ds(lanes_all * block + TILE * a, TILE)])
                        right.append(
                            up[h, pl.ds(wide_u * a + TILE * piece, TILE), 0 : TILE * columns]
                        )
            grad = nn(jnp.concatenate(left, axis=1), jnp.concatenate(right, axis=0))
            key = lax.broadcasted_iota(jnp.int32, grad.shape, 1) + TILE * b - 5
            row = lax.broadcasted_iota(jnp.int32, grad.shape, 0) + start
            low = jnp.where((key >= 0) & (key <= row), grad, 0.0).astype(BF16)
            eb[pl.ds(start, count), pl.ds(TILE * b, TILE * columns)] = low
            ka[pl.ds(TILE * b, TILE * columns), :] += tn(low, qm[h, pl.ds(start, count), :])
        for rb in range(tiles):
            rows = pl.ds(TILE * rb, TILE)
            upto = min(rb + 2, tiles + 1)
            part = nn(eb[rows, 0 : TILE * upto], ks[0 : TILE * upto, :]) * scale
            if h == 0:
                qa[rows, :] = part
            else:
                qa[rows, :] = jnp.where(first, qa[rows, :], part)
    for b, row in enumerate(places):
        low_ref[pl.ds(row, blk), 0:width] = qa[pl.ds(blk * b, blk), :].astype(BF16)
        low_ref[pl.ds(row, blk), width : 2 * width] = (ka[pl.ds(blk * b + 5, blk), :] * scale).astype(BF16)

    @pl.when(m == pl.num_programs(0) - 1)
    def _():
        away = lax.broadcasted_iota(jnp.int32, (2 * TILE, TILE), 0) - lax.broadcasted_iota(
            jnp.int32, (2 * TILE, TILE), 1
        )
        for h in range(2):
            for a in range(rows_tap):
                table = acc[h, :, TILE * a : TILE * (a + 1)]
                for t in range(keys_tap):
                    at = a * keys_tap + t
                    kg_ref[h, at : at + 1, :] = jnp.sum(
                        jnp.where(away == span - t, table, 0.0), axis=0, keepdims=True
                    )


def whole(shape):
    return pl.BlockSpec(shape, lambda m: (0,) * len(shape))


def pair_forward(blk_table, ker, mix, gain, qkv, micro, seq, blk, scale):
    width = qkv.shape[1] // 3
    mixed = (qkv.shape[0], width)
    rows_tap, keys_tap = ker.shape[1:]
    smem = pl.BlockSpec(memory_space=pltpu.SMEM)
    per = lambda shape: pl.BlockSpec((1,) + shape, lambda m: (m,) + (0,) * len(shape))
    return pl.pallas_call(
        functools.partial(forward_kernel, seq, blk, rows_tap, keys_tap, scale),
        name="pair_forward",
        grid=(micro,),
        out_shape=(
            jax.ShapeDtypeStruct(mixed, BF16),
            jax.ShapeDtypeStruct((micro, 2, seq, width), F32),
            jax.ShapeDtypeStruct((micro, 2, seq, seq), BF16),
        ),
        in_specs=[smem, smem, whole(mix.shape), whole(gain.shape), whole(qkv.shape)],
        out_specs=(whole(mixed), per((2, seq, width)), per((2, seq, seq))),
        scratch_shapes=[
            pltpu.VMEM((2, seq, width), BF16),
            pltpu.VMEM((seq + TILE + 8, width), F32),
            pltpu.VMEM((seq + TILE, width), BF16),
            pltpu.VMEM((seq, width), BF16),
            pltpu.VMEM((seq + 16, seq + TILE), BF16),
            pltpu.VMEM((seq + 16, seq + TILE), BF16),
            pltpu.VMEM((2, 2 * TILE, rows_tap * TILE), BF16),
            pltpu.VMEM((2, 2 * TILE, rows_tap * TILE), BF16),
            pltpu.VMEM((seq + 16, rows_tap * TILE), F32),
            pltpu.VMEM((seq, seq), F32),
        ],
        compiler_params=pltpu.CompilerParams(vmem_limit_bytes=56 << 20),
        cost_estimate=pl.CostEstimate(flops=20 * 10**9, transcendentals=10**6, bytes_accessed=8 << 20),
    )(blk_table, ker, mix, gain, qkv)


def pair_backward(blk_table, ker, mix, gain, qkv, zg, y, p, seq, blk, scale):
    width = qkv.shape[1] // 3
    micro = y.shape[0]
    rows_tap, keys_tap = ker.shape[1:]
    tiles = seq // TILE
    smem = pl.BlockSpec(memory_space=pltpu.SMEM)
    per = lambda shape: pl.BlockSpec((1,) + shape, lambda m: (m,) + (0,) * len(shape))
    taps = -(-rows_tap * keys_tap // 8) * 8
    return pl.pallas_call(
        functools.partial(backward_kernel, seq, blk, rows_tap, keys_tap, scale),
        name="pair_backward",
        grid=(micro,),
        out_shape=(
            jax.ShapeDtypeStruct(qkv.shape, BF16),
            jax.ShapeDtypeStruct((1, width), F32),
            jax.ShapeDtypeStruct((2, width), F32),
            jax.ShapeDtypeStruct((2, taps, TILE), F32),
        ),
        in_specs=[smem, smem, whole(mix.shape), whole(gain.shape), whole(qkv.shape), whole(zg.shape)]
        + [per((2, seq, width)), per((2, seq, seq))],
        out_specs=(whole(qkv.shape), whole((1, width)), whole((2, width)), whole((2, taps, TILE))),
        scratch_shapes=[
            pltpu.VMEM((2, seq, width), BF16),
            pltpu.VMEM((seq + TILE + 8, width), F32),
            pltpu.VMEM((seq + TILE, width), BF16),
            pltpu.VMEM((seq, width), BF16),
            pltpu.VMEM((seq, seq + TILE), BF16),
            pltpu.VMEM((2, rows_tap * 3 * TILE, 2 * TILE), BF16),
            pltpu.VMEM((seq, width), F32),
            pltpu.VMEM((2, seq, width), BF16),
            pltpu.VMEM((seq + 8, seq), F32),
            pltpu.VMEM((seq, tiles * rows_tap * TILE), BF16),
            pltpu.VMEM((seq, seq + TILE), BF16),
            pltpu.VMEM((seq, width), F32),
            pltpu.VMEM((seq + TILE, width), F32),
            pltpu.VMEM((2, 2 * TILE, rows_tap * TILE), F32),
        ],
        compiler_params=pltpu.CompilerParams(vmem_limit_bytes=56 << 20),
        cost_estimate=pl.CostEstimate(flops=30 * 10**9, transcendentals=10**5, bytes_accessed=12 << 20),
    )(blk_table, ker, mix, gain, qkv, zg, y, p)


MESH = pl.DeviceIdType.MESH


def peer(offset):
    mine = lax.axis_index("ctx")
    y = (mine // 4 + offset // 4) % 2
    x = ((mine // 2) % 2 + (offset // 2) % 2) % 2
    core = (mine % 2 + offset % 2) % 2
    return y * 4 + x * 2 + core


def greet(places):
    barrier = pltpu.get_barrier_semaphore()
    for place in places:
        pl.semaphore_signal(barrier, inc=1, device_id=place, device_id_type=MESH)
    pl.semaphore_wait(barrier, len(places))


def remote(source, target, send, receive, place):
    return pltpu.make_async_remote_copy(
        src_ref=source, dst_ref=target, send_sem=send, recv_sem=receive,
        device_id=place, device_id_type=MESH,
    )


def exchange_start(plane, mine, source, target, sends, receives):
    copies = [
        remote(source.at[peer(d)], target.at[mine], sends.at[d], receives.at[d], (plane, peer(d)))
        for d in (6, 7, 2, 3, 4, 5, 1)
    ]
    for copy in copies:
        copy.start()
    return copies


class Spread:
    def __init__(self, source, target, sends, receives):
        self.plane, self.mine = lax.axis_index("seq"), lax.axis_index("ctx")
        self.source, self.target, self.sends, self.receives = source, target, sends, receives
        self.copies = {}
        half = target.shape[1] // 2
        self.first, self.second = pl.ds(0, half), pl.ds(half, half)

    def send(self, key, source, target, offset):
        copy = remote(source, target, self.sends.at[key], self.receives.at[key], (self.plane, peer(offset)))
        copy.start()
        self.copies[key] = copy

    def hand_on(self, key, block, offset, rows=None):
        piece = self.target.at[block] if rows is None else self.target.at[block, rows]
        self.send(key, piece, piece, offset)

    def start(self):
        for d in (2, 4, 1):
            self.send(d, self.source, self.target.at[self.mine], d)

    def near(self):
        self.copies[2].wait_recv()
        self.hand_on(6, peer(2), 4, self.first)
        self.hand_on(3, peer(2), 1)
        self.copies[4].wait_recv()
        self.hand_on(0, peer(4), 2, self.second)
        self.hand_on(5, peer(4), 1)

    def across(self):
        self.copies[6].wait_recv()
        self.hand_on(7, peer(6), 1, self.first)
        self.copies[0].wait_recv()
        self.hand_on(8, peer(6), 1, self.second)

    def finish(self):
        for key in (1, 3, 5, 7, 8):
            self.copies[key].wait_recv()
        for copy in self.copies.values():
            copy.wait_send()


class PlaneSum:
    def __init__(self, terms, part, own, near, stage, far, hop, sends, receives):
        self.plane, self.mine = lax.axis_index("seq"), lax.axis_index("ctx")
        self.terms, self.part, self.own = terms, part, own
        self.near, self.stage, self.far, self.hop = near, stage, far, hop
        self.sends, self.receives = sends, receives
        self.copies = {}
        half = part.shape[1] // 2
        self.first, self.second = pl.ds(0, half), pl.ds(half, half)

    def send(self, key, source, target, offset):
        copy = remote(source, target, self.sends.at[key], self.receives.at[key], (self.plane, peer(offset)))
        copy.start()
        self.copies[key] = copy

    def start(self):
        self.part[...] = self.terms(1 - self.mine % 2).astype(BF16)
        for d in (6, 2, 4, 0):
            self.send(d, self.part.at[peer(d) // 2], self.near.at[d // 2], 1)

    def prepare(self):
        self.own[...] = self.terms(self.mine % 2)

    def chip_sum(self, d):
        self.copies[d].wait_recv()
        self.stage[d // 2] = (self.own[peer(d) // 2] + self.near[d // 2].astype(F32)).astype(BF16)

    def add_hop(self, slot, rows, hop):
        self.stage[slot, rows, :] = (
            self.stage[slot, rows, :].astype(F32) + self.hop[hop].astype(F32)
        ).astype(BF16)

    def run(self):
        first, second = self.first, self.second
        self.chip_sum(6)
        self.send(1, self.stage.at[3, first], self.hop.at[0], 2)
        self.send(3, self.stage.at[3, second], self.hop.at[1], 4)
        self.chip_sum(2)
        self.send(5, self.stage.at[1, first], self.far.at[0, first], 2)
        self.chip_sum(4)
        self.send(7, self.stage.at[2, second], self.far.at[1, second], 4)
        self.copies[1].wait_recv()
        self.add_hop(2, first, 0)
        self.send(8, self.stage.at[2, first], self.far.at[1, first], 4)
        self.copies[3].wait_recv()
        self.add_hop(1, second, 1)
        self.send(9, self.stage.at[1, second], self.far.at[0, second], 2)

    def total(self):
        self.copies[0].wait_recv()
        value = self.own[self.mine // 2] + self.near[0].astype(F32)
        for key in (5, 7, 8, 9):
            self.copies[key].wait_recv()
        return value + self.far[0].astype(F32) + self.far[1].astype(F32)

    def finish(self):
        for copy in self.copies.values():
            copy.wait_send()


def terms_of(values, product):
    chips, _, rows, width = values.shape

    def terms(core):
        left = values[:, core].reshape(chips * rows, width)
        return product(left).reshape(chips, rows, -1)

    return terms


class Line:
    def __init__(self, sources, targets, planes, sends, receives):
        self.sources, self.targets, self.planes = sources, targets, planes
        self.sends, self.receives = sends, receives
        self.plane, self.mine = lax.axis_index("seq"), lax.axis_index("ctx")

    def copy(self, i, up, step):
        block = jnp.clip(self.plane - step if up else self.plane + step, 0, self.planes - 1)
        next_plane = jnp.clip(self.plane + 1 if up else self.plane - 1, 0, self.planes - 1)
        at = (i, int(up), step)
        target = self.targets[i].at[block]
        source = target if step else self.sources[i]
        return remote(source, target, self.sends.at[at], self.receives.at[at], (next_plane, self.mine))

    def arrived(self, i, up, step):
        block = jnp.clip(self.plane - 1 - step if up else self.plane + 1 + step, 0, self.planes - 1)
        at = (i, int(up), step)
        target = self.targets[i].at[block]
        from_plane = jnp.clip(self.plane - 1 if up else self.plane + 1, 0, self.planes - 1)
        return remote(target, target, self.sends.at[at], self.receives.at[at], (from_plane, self.mine))

    def step(self, step):
        for up in (True, False):
            have = self.plane >= step if up else self.plane + step < self.planes
            more = self.plane + 1 < self.planes if up else self.plane > 0
            for i in range(len(self.targets)):
                if step:
                    @pl.when(have)
                    def _(i=i, up=up):
                        self.arrived(i, up, step - 1).wait_recv()

                if step < self.planes - 1:
                    @pl.when(have & more)
                    def _(i=i, up=up):
                        self.copy(i, up, step).start()

    def finish(self):
        for step in range(self.planes - 1):
            for up in (True, False):
                have = self.plane >= step if up else self.plane + step < self.planes
                more = self.plane + 1 < self.planes if up else self.plane > 0
                for i in range(len(self.targets)):
                    @pl.when(have & more)
                    def _(i=i, up=up, step=step):
                        self.copy(i, up, step).wait_send()


def plane_peers(plane, offsets):
    return [(plane, peer(d)) for d in offsets]


def other_planes(plane, mine, planes):
    return [((plane + d) % planes, mine) for d in range(1, planes)]


class RowDeal:
    def __init__(self, gathered, dealt, sends, receives, local):
        self.plane, self.mine = lax.axis_index("seq"), lax.axis_index("ctx")
        self.gathered, self.dealt, self.sends, self.receives, self.local = gathered, dealt, sends, receives, local

    def out(self, s, back):
        if back:
            target = 4 * (self.mine % 2) + s
            source, place = self.dealt.at[s], self.gathered.at[self.mine // 2]
        else:
            target = 2 * s + self.mine // 4
            source, place = self.gathered.at[s], self.dealt.at[self.mine % 4]
        slot = self.mine // 2 if back else self.mine % 4
        copy = remote(source, place, self.sends.at[s], self.receives.at[slot], (self.plane, target))
        keep = pltpu.make_async_copy(source, place, self.local)
        return target == self.mine, copy, keep

    def into(self, r, back):
        if back:
            origin = 2 * r + self.mine // 4
            place = self.gathered.at[r]
        else:
            origin = 4 * (self.mine % 2) + r
            place = self.dealt.at[r]
        return origin == self.mine, remote(place, place, self.sends.at[r], self.receives.at[r], (self.plane, origin))

    def start(self, back):
        for s in range(4):
            here, copy, keep = self.out(s, back)

            @pl.when(here)
            def _():
                keep.start()

            @pl.when(jnp.logical_not(here))
            def _():
                copy.start()

    def wait(self, back):
        for s in range(4):
            here, copy, keep = self.out(s, back)

            @pl.when(here)
            def _():
                keep.wait()

            @pl.when(jnp.logical_not(here))
            def _():
                copy.wait_send()

        for r in range(4):
            here, copy = self.into(r, back)

            @pl.when(jnp.logical_not(here))
            def _():
                copy.wait_recv()


def enter_kernel(
    planes, q, k, v, gate, up, gains, tokens, out_w,
    feed_out, qkv_out, gains_out, tokens_out, out_w_out,
    q_near, k_near, v_near, gate_near, up_near, gains_near, packed, qkv, feed,
    deal_sends, deal_receives, sends, receives, row_sends, row_receives, line_sends, line_receives, local,
):
    plane, mine = lax.axis_index("seq"), lax.axis_index("ctx")
    loads = [
        pltpu.make_async_copy(source, place, local.at[5 + i])
        for i, (source, place) in enumerate(
            ((gains, gains_near), (q, q_near), (k, k_near), (v, v_near), (gate, gate_near), (up, up_near))
        )
    ]
    keep = [
        pltpu.make_async_copy(qkv.at[mine], qkv_out.at[plane, mine], local.at[0]),
        pltpu.make_async_copy(packed, gains_out.at[plane, mine], local.at[1]),
        pltpu.make_async_copy(feed.at[mine], feed_out.at[mine], local.at[2]),
        pltpu.make_async_copy(tokens, tokens_out.at[mine], local.at[3]),
        pltpu.make_async_copy(out_w, out_w_out.at[plane], local.at[4]),
    ]
    for copy in loads + keep[3:]:
        copy.start()
    groups, _, three = qkv.shape
    pair = three // 3
    half = feed.shape[2] // 2
    for copy in loads[:4]:
        copy.wait()
    packed[...] = jnp.zeros(packed.shape, F32)
    packed[0:3, 0 : gains.shape[1]] = gains_near[...].astype(F32)
    for c in range(groups):
        for i, weight in enumerate((q_near, k_near, v_near)):
            qkv[c, :, pair * i : pair * (i + 1)] = weight[:, pair * c : pair * (c + 1)]
    for copy in keep[:2]:
        copy.start()
    greet(plane_peers(plane, range(1, 8)) + other_planes(plane, mine, planes))
    first = exchange_start(plane, mine, qkv, qkv_out.at[plane], deal_sends.at[0], deal_receives.at[0])
    for d in (6, 7, 2, 3, 4, 5, 1):
        copy = remote(packed, gains_out.at[plane, mine], deal_sends.at[1, d], deal_receives.at[1, d], (plane, peer(d)))
        copy.start()
        first.append(copy)
    rows = Line([out_w], [out_w_out], planes, row_sends, row_receives)
    rows.step(0)
    for copy in loads[4:]:
        copy.wait()
    for c in range(groups):
        for i, weight in enumerate((gate_near, up_near)):
            for s in range(half // TILE):
                at = TILE * (groups * s + c)
                feed[c, :, half * i + TILE * s : half * i + TILE * (s + 1)] = weight[:, at : at + TILE]
    keep[2].start()
    keep[0].wait()
    keep[1].wait()
    for copy in first:
        copy.wait_recv()
    line = Line(
        [qkv_out.at[plane], gains_out.at[plane]], [qkv_out, gains_out], planes, line_sends, line_receives
    )
    line.step(0)
    spread = Spread(tokens, tokens_out, sends, receives)
    spread.start()
    rows.step(1)
    line.step(1)
    spread.near()
    deals = exchange_start(plane, mine, feed, feed_out, deal_sends.at[2], deal_receives.at[2])
    rows.step(2)
    line.step(2)
    spread.across()
    for step in range(3, planes):
        rows.step(step)
        line.step(step)
    spread.finish()
    for copy in first:
        copy.wait_send()
    for copy in deals:
        copy.wait()
    for copy in keep[2:]:
        copy.wait()
    line.finish()
    rows.finish()


def heads_kernel(
    planes, tokens, qkv, gains, out_w, grads, hidden, heads, gains_out, pair_gain, out_w_out, grads_out,
    row_sends, row_receives, sends, receives, local,
):
    plane, mine = lax.axis_index("seq"), lax.axis_index("ctx")
    keep = pltpu.make_async_copy(grads, grads_out.at[mine], local.at[1])
    keep.start()
    greet(plane_peers(plane, range(1, 8)))
    spread = Spread(grads, grads_out, sends, receives)
    spread.start()
    deal = RowDeal(out_w, out_w_out, row_sends, row_receives, local.at[0])
    deal.start(False)
    groups = tokens.shape[0]
    owned = out_w.shape[1]
    for s in range(planes):
        for c in range(groups):
            at = owned * (groups * s + c)
            gains_out[:, at : at + owned] = gains[s, c, :, 0:owned]
    for r in range(4):
        pair_gain[:, owned * r : owned * (r + 1)] = gains[mine // 2, 4 * (mine % 2) + r, :, 0:owned]
    gain = gains_out[0:1, :]
    for i in range(groups):
        value = tokens[i].astype(F32)
        low = (value * inverse_root(value) * gain).astype(BF16)
        rows = pl.ds(value.shape[0] * i, value.shape[0])
        hidden[:, rows] = low.T
        heads[rows, :] = nn(low, qkv[...]).astype(BF16)
        if i == groups // 2:
            spread.near()
    deal.wait(False)
    spread.across()
    spread.finish()
    keep.wait()


def inverse_root(values):
    return lax.rsqrt(jnp.mean(values * values, axis=1, keepdims=True) + EPSILON)


def second_kernel(
    mixed, out_w, tokens, gains, residual, spread_out,
    part, own, near, stage, far, hop, sum_sends, sum_receives, sends, receives,
):
    plane, mine = lax.axis_index("seq"), lax.axis_index("ctx")
    greet(plane_peers(plane, (1, 2, 4)))
    rows = PlaneSum(
        terms_of(mixed, lambda left: nn(left, out_w[...])), part, own, near, stage, far, hop,
        sum_sends, sum_receives,
    )
    rows.start()
    rows.prepare()
    rows.run()
    value = tokens[...].astype(F32) + rows.total()
    spread_out[mine] = (value * inverse_root(value) * gains[2:3, :]).astype(BF16)
    spread = Spread(spread_out.at[mine], spread_out, sends, receives)
    spread.start()
    residual[...] = value
    rows.finish()
    spread.near()
    spread.across()
    spread.finish()


def back_through_norm(upstream, values, gain):
    factor = inverse_root(values)
    normed = values * factor
    scaled = upstream * gain
    grad = factor * (scaled - normed * jnp.mean(scaled * normed, axis=1, keepdims=True))
    return grad, jnp.sum(upstream * normed, axis=0, keepdims=True)


def back_kernel(
    lows, feed, residual, grads, gains, residual_grad, gain_grad, spread_out,
    part, own, near, stage, far, hop, sum_sends, sum_receives, sends, receives,
):
    plane, mine = lax.axis_index("seq"), lax.axis_index("ctx")
    greet(plane_peers(plane, (1, 2, 4)))
    rows = PlaneSum(
        terms_of(lows, lambda left: nt(left, feed[...])), part, own, near, stage, far, hop,
        sum_sends, sum_receives,
    )
    rows.start()
    rows.prepare()
    rows.run()
    grad, gain_part = back_through_norm(rows.total(), residual[...], gains[2:3, :])
    grad = grad + grads[...].astype(F32)
    spread_out[mine] = grad.astype(BF16)
    spread = Spread(spread_out.at[mine], spread_out, sends, receives)
    spread.start()
    gain_grad[...] = gain_part
    residual_grad[...] = grad
    rows.finish()
    spread.near()
    spread.across()
    spread.finish()


class Fold:
    def __init__(self, own, stage, landed, planes, sends, receives):
        self.own, self.stage, self.landed, self.planes = own, stage, landed, planes
        self.sends, self.receives = sends, receives
        self.plane, self.mine = lax.axis_index("seq"), lax.axis_index("ctx")

    def copy(self, j, up):
        place = jnp.clip(self.plane + 1 if up else self.plane - 1, 0, self.planes - 1)
        at = (int(up), j)
        return remote(self.stage.at[at], self.landed.at[at], self.sends.at[at], self.receives.at[at], (place, self.mine))

    def advance(self, j, up):
        active = self.plane < j if up else self.plane > j
        inner = self.plane > 0 if up else self.plane < self.planes - 1

        @pl.when(active & inner)
        def _():
            self.copy(j, up).wait_recv()
            self.stage[int(up), j] = (
                self.own[j].astype(F32) + self.landed[int(up), j].astype(F32)
            ).astype(BF16)

        @pl.when(active & jnp.logical_not(inner))
        def _():
            self.stage[int(up), j] = self.own[j]

        @pl.when(active)
        def _():
            self.copy(j, up).start()

    def round(self, i):
        self.advance(self.planes - 1 - i, True)
        self.advance(i, False)

    def total(self, out):
        for j in range(self.planes):
            @pl.when(self.plane == j)
            def _():
                value = self.own[j].astype(F32)
                if j > 0:
                    self.copy(j, True).wait_recv()
                    value = value + self.landed[1, j].astype(F32)
                if j < self.planes - 1:
                    self.copy(j, False).wait_recv()
                    value = value + self.landed[0, j].astype(F32)
                rows = out.shape[1]
                for p in range(out.shape[0]):
                    out[p] = value[rows * p : rows * (p + 1), :].astype(BF16)

    def finish(self):
        for j in range(self.planes):
            for up in (True, False):
                @pl.when(self.plane < j if up else self.plane > j)
                def _():
                    self.copy(j, up).wait_send()


def leave_kernel(
    planes, qkv_low, qkv, hidden, active, down, residual, residual_grad, tokens, gains, small, feed_grad, out_w_grad,
    input_grad, layer_out, small_out, qkv_out, feed_out, out_w_out,
    part, own, near, stage, far, hop, layer_part, layer_own, layer_near, layer_stage, layer_far, layer_hop, small_plane, small_all,
    qkv_grad, fold_stage, fold_landed, qkv_sum, row_grad, row_stage, row_landed,
    sum_sends, sum_receives, layer_sends, layer_receives, small_sends, small_receives,
    fold_sends, fold_receives, row_fold_sends, row_fold_receives, deal_sends, deal_receives,
    row_sends, row_receives, local,
):
    plane, mine = lax.axis_index("seq"), lax.axis_index("ctx")
    keep_feed = pltpu.make_async_copy(feed_grad.at[mine], feed_out.at[mine], local.at[0])
    keep_feed.start()
    greet(plane_peers(plane, range(1, 8)) + other_planes(plane, mine, planes))
    row_deal = RowDeal(row_grad, out_w_grad, row_sends, row_receives, local.at[1])
    row_deal.start(True)
    rows = PlaneSum(
        terms_of(qkv_low, lambda left: nt(left, qkv[...])), part, own, near, stage, far, hop,
        sum_sends, sum_receives,
    )
    layer = PlaneSum(
        terms_of(active, lambda left: nn(left, down[...])), layer_part, layer_own, layer_near, layer_stage, layer_far, layer_hop,
        layer_sends, layer_receives,
    )
    fold = Fold(qkv_grad, fold_stage, fold_landed, planes, fold_sends, fold_receives)
    row_fold = Fold(row_grad, row_stage, row_landed, planes, row_fold_sends, row_fold_receives)
    ends = (plane == 0) | (plane == planes - 1)
    lows = qkv_low[...].reshape(hidden.shape[1], qkv_low.shape[3])
    block = qkv_grad.shape[1]

    def project(i):
        j = jnp.where(plane < planes // 2, planes - 1 - i, i)
        columns = hidden[pl.ds(pl.multiple_of(block * j, block), block), :]
        qkv_grad[j] = nn(columns, lows).astype(BF16)

    def rounds(which, outer, inner):
        for here, i in ((ends, outer), (jnp.logical_not(ends), inner)):
            if 0 <= i < planes - 1:
                @pl.when(here)
                def _():
                    which.round(i)

    rows.start()
    project(0)
    rounds(fold, 0, -1)
    rows.prepare()
    for i in range(1, planes):
        project(i)
    rounds(fold, 1, -1)
    row_deal.wait(True)
    rows.run()
    deals = exchange_start(plane, mine, feed_grad, feed_out, deal_sends.at[0], deal_receives.at[0])
    rounds(fold, 2, 0)
    layer.start()
    layer.prepare()
    rounds(row_fold, 0, -1)
    grad, gain_part = back_through_norm(rows.total(), tokens[...].astype(F32), gains[0:1, :])
    small_plane[mine] = small[...]
    small_plane[mine, 0:1, :] = gain_part
    near_copies = [
        remote(small_plane.at[mine], small_plane.at[mine], small_sends.at[0, d], small_receives.at[0, d], (plane, peer(d)))
        for d in range(1, 8)
    ]
    for copy in near_copies:
        copy.start()
    input_grad[...] = (residual_grad[...] + grad).astype(BF16)
    rounds(fold, -1, 1)
    rounds(row_fold, 1, 0)
    layer.run()
    rounds(row_fold, 2, -1)
    for copy in near_copies:
        copy.wait()
    total = small_plane[0]
    for i in range(1, 8):
        total = total + small_plane[i]
    small_all[plane] = total
    far_copies = [
        remote(small_all.at[plane], small_all.at[plane], small_sends.at[1, d], small_receives.at[1, d], ((plane + d) % planes, mine))
        for d in range(1, planes)
    ]
    for copy in far_copies:
        copy.start()
    rounds(fold, -1, 2)
    rounds(row_fold, -1, 1)
    fold.total(qkv_sum)
    keep_qkv = pltpu.make_async_copy(qkv_sum.at[mine], qkv_out.at[mine], local.at[2])
    keep_qkv.start()
    deals += exchange_start(plane, mine, qkv_sum, qkv_out, deal_sends.at[1], deal_receives.at[1])
    rounds(row_fold, -1, 2)
    row_fold.total(out_w_out)
    layer_out[...] = (residual[...] + layer.total()).astype(BF16)
    rows.finish()
    layer.finish()
    for copy in far_copies:
        copy.wait()
    total = small_all[0]
    for i in range(1, planes):
        total = total + small_all[i]
    small_out[...] = total
    for copy in deals:
        copy.wait()
    row_fold.finish()
    keep_feed.wait()
    keep_qkv.wait()
    fold.finish()


def finish_kernel(count, *refs):
    ins, outs = refs[:6], refs[6 : 6 + count]
    near, made = refs[6 + count : 12 + count], refs[12 + count : 12 + 2 * count - 2]
    loads, stores = refs[-2:]
    moves = [pltpu.make_async_copy(ins[i], near[i], loads.at[i]) for i in range(6)]
    for move in moves:
        move.start()
    qkv, feed, out_w, down, grad, layer = near
    groups, _, three = qkv.shape
    pair = three // 3
    half = feed.shape[2] // 2
    results = list(made) + [grad, layer]
    out = [pltpu.make_async_copy(results[i], outs[i], stores.at[i]) for i in range(count)]
    moves[3].wait()
    made[6][...] = down[...].astype(F32)
    out[6].start()
    moves[2].wait()
    made[5][...] = out_w[0].astype(F32)
    out[5].start()
    for i in (4, 5):
        moves[i].wait()
        out[i + 3].start()
    moves[1].wait()
    for i in range(2):
        for c in range(groups):
            for s in range(half // TILE):
                at = TILE * (groups * s + c)
                made[3 + i][:, at : at + TILE] = feed[
                    c, :, half * i + TILE * s : half * i + TILE * (s + 1)
                ].astype(F32)
        out[3 + i].start()
    moves[0].wait()
    for i in range(3):
        for c in range(groups):
            made[i][:, pair * c : pair * (c + 1)] = qkv[c, :, pair * i : pair * (i + 1)].astype(F32)
        out[i].start()
    for copy in out:
        copy.wait()


DMA = pltpu.SemaphoreType.DMA
ANYWHERE = pl.BlockSpec(memory_space=pl.ANY)
ON_CHIP = pl.BlockSpec(memory_space=pltpu.VMEM)


def communicate(kernel, name, number, micros, outs, scratch, args, spec, specs=None, out_specs=None):
    return pl.pallas_call(
        kernel,
        name=name,
        out_shape=tuple(jax.ShapeDtypeStruct(shape, kind) for shape, kind in outs),
        in_specs=specs or [spec] * len(args),
        out_specs=out_specs or (spec,) * len(outs),
        scratch_shapes=scratch,
        compiler_params=pltpu.CompilerParams(
            collective_id=number, has_side_effects=True, vmem_limit_bytes=56 << 20
        ),
        cost_estimate=pl.CostEstimate(flops=0, transcendentals=0, bytes_accessed=micros * 3500000),
    )(*args)


def sum_scratch(rows, width):
    return [
        pltpu.VMEM((4, rows, width), BF16),
        pltpu.VMEM((4, rows, width), F32),
        pltpu.VMEM((4, rows, width), BF16),
        pltpu.VMEM((4, rows, width), BF16),
        pltpu.VMEM((2, rows, width), BF16),
        pltpu.VMEM((2, rows // 2, width), BF16),
        DMA((10,)),
        DMA((10,)),
    ]


PRECISE = lax.Precision.HIGHEST


def normalize(values):
    factor = lax.rsqrt(jnp.mean(values * values, axis=-1, keepdims=True) + EPSILON)
    return (values * factor, factor)


def normalize_back(normed, factor, gain, upstream):
    gain_grad = jnp.sum(upstream * normed, axis=0)
    scaled = upstream * gain
    return (
        factor * (scaled - normed * jnp.mean(scaled * normed, axis=-1, keepdims=True)),
        gain_grad,
    )


def add_rows(target, update, offset):
    current = lax.dynamic_slice_in_dim(target, offset, update.shape[0], 0)
    return lax.dynamic_update_slice_in_dim(target, current + update, offset, 0)


def masked_scores(query_ext, key_pad, offset, row_pos, layout):
    block_rows, halo_rows, key_reach, key_block, groups, score_scale = layout
    extent = key_block + 4 * key_reach
    key_slab = lax.dynamic_slice_in_dim(key_pad, offset, extent, 0)
    raw_scores = (
        jnp.einsum("nrhd,khd->nhrk", query_ext, key_slab, preferred_element_type=jnp.float32)
        * score_scale
    )
    key_pos = offset - 2 * key_reach + jnp.arange(extent, dtype=jnp.int32)
    keep_mask = (key_pos[None, None, :] <= row_pos[:, :, None]) & (key_pos >= 0)[None, None, :]
    return jnp.where(keep_mask[:, None], raw_scores, 0.0)


def convolve(zeroed, kernel, shift, extent, layout):
    block_rows, halo_rows, key_reach = (layout[0], layout[1], layout[2])
    result = jnp.zeros(zeroed.shape[:2] + (block_rows, extent), jnp.float32)
    for row_tap in range(halo_rows + 1):
        for key_tap in range(2 * key_reach + 1):
            column = shift + 3 * key_reach - key_tap
            result = (
                result
                + kernel[:, row_tap, key_tap][None, :, None, None]
                * zeroed[
                    :,
                    :,
                    halo_rows - row_tap : halo_rows - row_tap + block_rows,
                    column : column + extent,
                ]
            )
    return result


def attend_forward(query_ext, row_pos, key_pad, value_pad, kernel, layout):
    block_rows, halo_rows, key_reach, key_block, groups, score_scale = layout
    members = query_ext.shape[0]
    head_count = query_ext.shape[2]
    pair_width = value_pad.shape[1] // groups
    block_count = jnp.max(row_pos) // key_block + 1

    def advance(position, carried):
        running_max, running_sum, gathered = carried
        offset = position * key_block
        zeroed = masked_scores(query_ext, key_pad, offset, row_pos, layout)
        logits = convolve(zeroed, kernel, 0, key_block, layout)
        key_pos = offset + jnp.arange(key_block, dtype=jnp.int32)
        valid_mask = key_pos[None, None, :] <= row_pos[:, halo_rows:, None]
        logits = jnp.where(valid_mask[:, None], logits, NEGATIVE)
        new_max = jnp.maximum(running_max, jnp.max(logits, axis=-1))
        shrink = jnp.exp(running_max - new_max)
        weights = jnp.exp(logits - new_max[..., None])
        running_sum = running_sum * shrink + jnp.sum(weights, axis=-1)
        value_slab = lax.dynamic_slice_in_dim(
            value_pad, offset + 2 * key_reach, key_block, 0
        ).reshape(key_block, groups, pair_width)
        low_weights = weights.astype(jnp.bfloat16).reshape(
            members, groups, 2, block_rows, key_block
        )
        gathered = gathered * shrink.reshape(members, groups, 2, block_rows, 1) + jnp.einsum(
            "ngpik,kgc->ngpic", low_weights, value_slab, preferred_element_type=jnp.float32
        )
        return (new_max, running_sum, gathered)

    initial = (
        jnp.full((members, head_count, block_rows), NEGATIVE, jnp.float32),
        jnp.zeros((members, head_count, block_rows), jnp.float32),
        jnp.zeros((members, groups, 2, block_rows, pair_width), jnp.float32),
    )
    running_max, running_sum, gathered = lax.fori_loop(0, block_count, advance, initial)
    mixed_in = gathered / running_sum.reshape(members, groups, 2, block_rows, 1)
    return (mixed_in, running_max + jnp.log(running_sum))


def attend_backward(
    query_ext,
    row_pos,
    key_pad,
    value_pad,
    kernel,
    log_total,
    mixed_low,
    delta_rows,
    key_acc,
    value_acc,
    layout,
):
    block_rows, halo_rows, key_reach, key_block, groups, score_scale = layout
    members = query_ext.shape[0]
    ext_rows = query_ext.shape[1]
    head_count = query_ext.shape[2]
    model_width = value_pad.shape[1]
    pair_width = model_width // groups
    extent = key_block + 2 * key_reach
    block_count = jnp.max(row_pos) // key_block + 1

    def advance(position, carried):
        query_grad, key_acc, value_acc, kernel_grad = carried
        offset = position * key_block
        zeroed = masked_scores(query_ext, key_pad, offset, row_pos, layout)
        logits = convolve(zeroed, kernel, -key_reach, extent, layout)
        key_pos = offset - key_reach + jnp.arange(extent, dtype=jnp.int32)
        valid_mask = (key_pos[None, None, :] <= row_pos[:, halo_rows:, None]) & (key_pos >= 0)[
            None, None, :
        ]
        probability = jnp.where(valid_mask[:, None], jnp.exp(logits - log_total[..., None]), 0.0)
        value_slab = lax.dynamic_slice_in_dim(value_pad, offset + key_reach, extent, 0).reshape(
            extent, groups, pair_width
        )
        prob_grad = jnp.einsum(
            "ngpic,kgc->ngpik", mixed_low, value_slab, preferred_element_type=jnp.float32
        ).reshape(members, head_count, block_rows, extent)
        logit_grad = probability * (prob_grad - delta_rows[..., None])
        central = (
            probability[..., key_reach : key_reach + key_block]
            .astype(jnp.bfloat16)
            .reshape(members, groups, 2, block_rows, key_block)
        )
        value_part = jnp.einsum(
            "ngpik,ngpic->kgc", central, mixed_low, preferred_element_type=jnp.float32
        ).reshape(key_block, model_width)
        value_acc = add_rows(value_acc, value_part, offset)
        middle = logit_grad[..., key_reach : key_reach + key_block]
        tap_sums = []
        for row_tap in range(halo_rows + 1):
            for key_tap in range(2 * key_reach + 1):
                column = 3 * key_reach - key_tap
                tap_sums.append(
                    jnp.sum(
                        middle
                        * zeroed[
                            :,
                            :,
                            halo_rows - row_tap : halo_rows - row_tap + block_rows,
                            column : column + key_block,
                        ],
                        axis=(0, 2, 3),
                    )
                )
        kernel_grad = kernel_grad + jnp.stack(tap_sums, axis=1).reshape(
            head_count, halo_rows + 1, 2 * key_reach + 1
        )
        padded = jnp.pad(logit_grad, ((0, 0), (0, 0), (halo_rows, halo_rows), (0, 0)))
        score_grad = jnp.zeros((members, head_count, ext_rows, key_block), jnp.float32)
        for row_tap in range(halo_rows + 1):
            for key_tap in range(2 * key_reach + 1):
                score_grad = (
                    score_grad
                    + kernel[:, row_tap, key_tap][None, :, None, None]
                    * padded[:, :, row_tap : row_tap + ext_rows, key_tap : key_tap + key_block]
                )
        key_central = offset + jnp.arange(key_block, dtype=jnp.int32)
        keep_mask = (key_central[None, None, :] <= row_pos[:, :, None]) & (key_central >= 0)[
            None, None, :
        ]
        score_low = jnp.where(keep_mask[:, None], score_grad, 0.0).astype(jnp.bfloat16)
        key_slab = lax.dynamic_slice_in_dim(key_pad, offset + 2 * key_reach, key_block, 0)
        query_grad = (
            query_grad
            + jnp.einsum("nhrk,khd->nrhd", score_low, key_slab, preferred_element_type=jnp.float32)
            * score_scale
        )
        key_part = (
            jnp.einsum(
                "nhrk,nrhd->khd", score_low, query_ext, preferred_element_type=jnp.float32
            ).reshape(key_block, model_width)
            * score_scale
        )
        key_acc = add_rows(key_acc, key_part, offset)
        return (query_grad, key_acc, value_acc, kernel_grad)

    initial = (
        jnp.zeros(query_ext.shape, jnp.float32),
        key_acc,
        value_acc,
        jnp.zeros(kernel.shape, jnp.float32),
    )
    return lax.fori_loop(0, block_count, advance, initial)


def reorder(selection, rows):
    return jnp.dot(
        selection.astype(rows.dtype), rows, precision=PRECISE, preferred_element_type=jnp.float32
    ).astype(rows.dtype)


def pick(table, places):
    return jnp.stack(
        [lax.dynamic_index_in_dim(table, places[i], 0, keepdims=False) for i in range(2)]
    )


def accumulate(previous, update):
    return (
        update
        if previous is None
        else tuple((left + right for left, right in zip(previous, update)))
    )


def general_device(
    inputs,
    out_grad,
    pair_index,
    norm_gain,
    query_weight,
    key_weight,
    value_weight,
    score_kernel,
    head_mixing,
    group_gain,
    output_weight,
    second_gain,
    gate_weight,
    up_weight,
    down_weight,
):
    micro_count = inputs.shape[0]
    local_rows = inputs.shape[2]
    block_rows = local_rows // 2
    model_width = inputs.shape[3]
    head_count = score_kernel.shape[0]
    head_dim = model_width // head_count
    groups = head_count // 2
    halo_rows = score_kernel.shape[1] - 1
    key_reach = (score_kernel.shape[2] - 1) // 2
    block_count = 2 * lax.axis_size("ctx")
    seq_length = block_count * block_rows
    key_block = min(512, seq_length)
    layout = (block_rows, halo_rows, key_reach, key_block, groups, head_dim ** (-0.5))
    extended = block_rows + halo_rows
    my_index = lax.axis_index("ctx")
    slot_ids = jnp.arange(block_count, dtype=jnp.int32)
    mix_table = head_mixing.reshape(groups, 2, 2)
    pad_width = ((2 * key_reach, 2 * key_reach), (0, 0))
    layer_rows = []
    input_rows = []
    feed_sums = None
    attention_sums = None
    kernel_total = jnp.zeros(score_kernel.shape, jnp.float32)
    mixing_total = jnp.zeros(head_mixing.shape, jnp.float32)
    for batch_index in range(micro_count):
        gain_first, query_full, key_full, value_full, gain_group, out_full = (
            lax.all_gather(norm_gain, ("seq", "ctx"), axis=0, tiled=True),
            lax.all_gather(query_weight, ("seq", "ctx"), axis=0, tiled=True),
            lax.all_gather(key_weight, ("seq", "ctx"), axis=0, tiled=True),
            lax.all_gather(value_weight, ("seq", "ctx"), axis=0, tiled=True),
            lax.all_gather(group_gain, ("seq", "ctx"), axis=0, tiled=True),
            lax.all_gather(output_weight, ("seq", "ctx"), axis=0, tiled=True),
        )
        tokens = inputs[batch_index, 0].astype(jnp.float32)
        normed_first, factor_first = normalize(tokens)
        hidden = (normed_first * gain_first.astype(jnp.float32)).astype(jnp.bfloat16)
        query_proj = jnp.dot(hidden, query_full, preferred_element_type=jnp.float32).astype(
            jnp.bfloat16
        )
        key_proj = jnp.dot(hidden, key_full, preferred_element_type=jnp.float32).astype(
            jnp.bfloat16
        )
        value_proj = jnp.dot(hidden, value_full, preferred_element_type=jnp.float32).astype(
            jnp.bfloat16
        )
        tail_rows = jnp.concatenate(
            [query_proj[block_rows - halo_rows : block_rows], query_proj[local_rows - halo_rows :]],
            axis=0,
        )
        key_dealt, value_dealt, tail_dealt = (
            lax.all_gather(key_proj, "ctx", axis=0, tiled=True),
            lax.all_gather(value_proj, "ctx", axis=0, tiled=True),
            lax.all_gather(tail_rows, "ctx", axis=0, tiled=True),
        )
        pairs_row = pair_index[batch_index]
        owner_pair = jnp.repeat(pairs_row, 2)
        block_of_slot = jnp.where(slot_ids % 2 == 0, owner_pair, block_count - 1 - owner_pair)
        to_natural = (block_of_slot[None, :] == slot_ids[:, None]).astype(jnp.float32)
        slot_of_block = jnp.sum(
            jnp.where(block_of_slot[None, :] == slot_ids[:, None], slot_ids[None, :], 0), axis=1
        )
        my_pair = lax.dynamic_index_in_dim(pairs_row, my_index, 0, keepdims=False)
        my_blocks = jnp.stack([my_pair, block_count - 1 - my_pair])
        key_pad = jnp.pad(
            reorder(to_natural, key_dealt.reshape(block_count, -1)).reshape(
                seq_length, model_width
            ),
            pad_width,
        ).reshape(-1, head_count, head_dim)
        value_pad = jnp.pad(
            reorder(to_natural, value_dealt.reshape(block_count, -1)).reshape(
                seq_length, model_width
            ),
            pad_width,
        )
        tail_blocks = reorder(to_natural, tail_dealt.reshape(block_count, -1)).reshape(
            block_count, halo_rows, model_width
        )
        previous = jnp.concatenate(
            [jnp.zeros((1, halo_rows, model_width), jnp.bfloat16), tail_blocks[:-1]], axis=0
        )
        query_ext = jnp.concatenate(
            [pick(previous, my_blocks), query_proj.reshape(2, block_rows, model_width)], axis=1
        ).reshape(2, extended, head_count, head_dim)
        row_pos = (
            my_blocks[:, None] * block_rows
            - halo_rows
            + jnp.arange(extended, dtype=jnp.int32)[None, :]
        )
        mixed_in, log_total = attend_forward(
            query_ext, row_pos, key_pad, value_pad, score_kernel, layout
        )
        mixed_six = mixed_in.reshape(2, groups, 2, block_rows, 2, head_dim)
        heads_out = jnp.einsum(
            "gqp,ngpiqd->nigqd", mix_table, mixed_six, precision=PRECISE
        ).reshape(local_rows, head_count, head_dim)
        group_normed, group_factor = normalize(heads_out)
        normed_low = (
            group_normed.reshape(local_rows, model_width) * gain_group.astype(jnp.float32)
        ).astype(jnp.bfloat16)
        residual = tokens + jnp.dot(normed_low, out_full, preferred_element_type=jnp.float32)
        gain_second, gate_full, up_full, down_full = (
            lax.all_gather(second_gain, ("seq", "ctx"), axis=0, tiled=True),
            lax.all_gather(gate_weight, ("seq", "ctx"), axis=0, tiled=True),
            lax.all_gather(up_weight, ("seq", "ctx"), axis=0, tiled=True),
            lax.all_gather(down_weight, ("seq", "ctx"), axis=0, tiled=True),
        )
        normed_second, factor_second = normalize(residual)
        second_hidden = (normed_second * gain_second.astype(jnp.float32)).astype(jnp.bfloat16)
        gate_proj = jnp.dot(second_hidden, gate_full, preferred_element_type=jnp.float32)
        up_proj = jnp.dot(second_hidden, up_full, preferred_element_type=jnp.float32)
        activated = (jax.nn.silu(gate_proj) * up_proj).astype(jnp.bfloat16)
        layer_rows.append(
            (residual + jnp.dot(activated, down_full, preferred_element_type=jnp.float32)).astype(
                jnp.bfloat16
            )
        )
        gain_second, gate_full, up_full, down_full = (
            lax.all_gather(second_gain, ("seq", "ctx"), axis=0, tiled=True),
            lax.all_gather(gate_weight, ("seq", "ctx"), axis=0, tiled=True),
            lax.all_gather(up_weight, ("seq", "ctx"), axis=0, tiled=True),
            lax.all_gather(down_weight, ("seq", "ctx"), axis=0, tiled=True),
        )
        grad_rows = out_grad[batch_index, 0]
        hid_grad = jnp.dot(grad_rows, down_full.T, preferred_element_type=jnp.float32)
        down_grad = jnp.dot(activated.T, grad_rows, preferred_element_type=jnp.float32)
        sigmoid_gate = jax.nn.sigmoid(gate_proj)
        up_low = (hid_grad * gate_proj * sigmoid_gate).astype(jnp.bfloat16)
        gate_low = (
            hid_grad * up_proj * sigmoid_gate * (1.0 + gate_proj * (1.0 - sigmoid_gate))
        ).astype(jnp.bfloat16)
        second_grad = jnp.dot(gate_low, gate_full.T, preferred_element_type=jnp.float32) + jnp.dot(
            up_low, up_full.T, preferred_element_type=jnp.float32
        )
        gate_grad = jnp.dot(second_hidden.T, gate_low, preferred_element_type=jnp.float32)
        up_grad = jnp.dot(second_hidden.T, up_low, preferred_element_type=jnp.float32)
        residual_part, gain_second_grad = normalize_back(
            normed_second, factor_second, gain_second.astype(jnp.float32), second_grad
        )
        residual_grad = grad_rows.astype(jnp.float32) + residual_part
        feed_shards = (
            lax.psum_scatter(gain_second_grad, ("seq", "ctx"), scatter_dimension=0, tiled=True),
            lax.psum_scatter(gate_grad, ("seq", "ctx"), scatter_dimension=0, tiled=True),
            lax.psum_scatter(up_grad, ("seq", "ctx"), scatter_dimension=0, tiled=True),
            lax.psum_scatter(down_grad, ("seq", "ctx"), scatter_dimension=0, tiled=True),
        )
        feed_sums = accumulate(feed_sums, feed_shards)
        gain_first, query_full, key_full, value_full, gain_group, out_full = (
            lax.all_gather(norm_gain, ("seq", "ctx"), axis=0, tiled=True),
            lax.all_gather(query_weight, ("seq", "ctx"), axis=0, tiled=True),
            lax.all_gather(key_weight, ("seq", "ctx"), axis=0, tiled=True),
            lax.all_gather(value_weight, ("seq", "ctx"), axis=0, tiled=True),
            lax.all_gather(group_gain, ("seq", "ctx"), axis=0, tiled=True),
            lax.all_gather(output_weight, ("seq", "ctx"), axis=0, tiled=True),
        )
        attended_low = residual_grad.astype(jnp.bfloat16)
        out_weight_grad = jnp.dot(normed_low.T, attended_low, preferred_element_type=jnp.float32)
        normed_grad = jnp.dot(attended_low, out_full.T, preferred_element_type=jnp.float32)
        heads_grad, gain_group_grad = normalize_back(
            group_normed,
            group_factor,
            gain_group.astype(jnp.float32).reshape(head_count, head_dim),
            normed_grad.reshape(local_rows, head_count, head_dim),
        )
        heads_five = heads_grad.reshape(2, block_rows, groups, 2, head_dim)
        mixing_total = mixing_total + jnp.einsum(
            "nigqd,ngpiqd->gqp", heads_five, mixed_six, precision=PRECISE
        ).reshape(head_count, 2)
        mixed_grad = jnp.einsum(
            "gqp,nigqd->ngpiqd", mix_table, heads_five, precision=PRECISE
        ).reshape(2, groups, 2, block_rows, 2 * head_dim)
        mixed_low = mixed_grad.astype(jnp.bfloat16)
        delta_rows = jnp.sum(mixed_low.astype(jnp.float32) * mixed_in, axis=-1).reshape(
            2, head_count, block_rows
        )
        key_acc = jnp.zeros((seq_length, model_width), jnp.float32)
        value_acc = jnp.zeros((seq_length, model_width), jnp.float32)
        query_grad, key_acc, value_acc, kernel_part = attend_backward(
            query_ext,
            row_pos,
            key_pad,
            value_pad,
            score_kernel,
            log_total,
            mixed_low,
            delta_rows,
            key_acc,
            value_acc,
            layout,
        )
        kernel_total = kernel_total + kernel_part
        halo_grad = query_grad[:, :halo_rows].reshape(2, halo_rows, model_width)
        own_grad = query_grad[:, halo_rows:].reshape(2, block_rows, model_width)
        target_slot = pick(slot_of_block, jnp.maximum(my_blocks - 1, 0))
        routing = ((slot_ids[None, :] == target_slot[:, None]) & (my_blocks > 0)[:, None]).astype(
            jnp.float32
        )
        tail_grad = jnp.einsum("ws,wrc->src", routing, halo_grad, precision=PRECISE).reshape(
            block_count * halo_rows, model_width
        )
        key_back = reorder(to_natural.T, key_acc.reshape(block_count, -1)).reshape(
            seq_length, model_width
        )
        value_back = reorder(to_natural.T, value_acc.reshape(block_count, -1)).reshape(
            seq_length, model_width
        )
        key_mine, value_mine, tail_mine = (
            lax.psum_scatter(
                key_back.astype(jnp.bfloat16), "ctx", scatter_dimension=0, tiled=True
            ).astype(jnp.float32),
            lax.psum_scatter(
                value_back.astype(jnp.bfloat16), "ctx", scatter_dimension=0, tiled=True
            ).astype(jnp.float32),
            lax.psum_scatter(
                tail_grad.astype(jnp.bfloat16), "ctx", scatter_dimension=0, tiled=True
            ).astype(jnp.float32),
        )
        tail_mine = tail_mine.reshape(2, halo_rows, model_width)
        query_total = jnp.concatenate(
            [
                own_grad[:, : block_rows - halo_rows],
                own_grad[:, block_rows - halo_rows :] + tail_mine,
            ],
            axis=1,
        ).reshape(local_rows, model_width)
        query_low = query_total.astype(jnp.bfloat16)
        key_low = key_mine.astype(jnp.bfloat16)
        value_low = value_mine.astype(jnp.bfloat16)
        query_w_grad = jnp.dot(hidden.T, query_low, preferred_element_type=jnp.float32)
        key_w_grad = jnp.dot(hidden.T, key_low, preferred_element_type=jnp.float32)
        value_w_grad = jnp.dot(hidden.T, value_low, preferred_element_type=jnp.float32)
        hidden_grad = (
            jnp.dot(query_low, query_full.T, preferred_element_type=jnp.float32)
            + jnp.dot(key_low, key_full.T, preferred_element_type=jnp.float32)
            + jnp.dot(value_low, value_full.T, preferred_element_type=jnp.float32)
        )
        token_part, gain_first_grad = normalize_back(
            normed_first, factor_first, gain_first.astype(jnp.float32), hidden_grad
        )
        input_rows.append((residual_grad + token_part).astype(jnp.bfloat16))
        attention_shards = (
            lax.psum_scatter(gain_first_grad, ("seq", "ctx"), scatter_dimension=0, tiled=True),
            lax.psum_scatter(query_w_grad, ("seq", "ctx"), scatter_dimension=0, tiled=True),
            lax.psum_scatter(key_w_grad, ("seq", "ctx"), scatter_dimension=0, tiled=True),
            lax.psum_scatter(value_w_grad, ("seq", "ctx"), scatter_dimension=0, tiled=True),
            lax.psum_scatter(
                gain_group_grad.reshape(model_width),
                ("seq", "ctx"),
                scatter_dimension=0,
                tiled=True,
            ),
            lax.psum_scatter(out_weight_grad, ("seq", "ctx"), scatter_dimension=0, tiled=True),
        )
        attention_sums = accumulate(attention_sums, attention_shards)
    kernel_sum, mixing_sum = lax.psum((kernel_total, mixing_total), ("seq", "ctx"))
    layer_out = jnp.stack(layer_rows)[:, None]
    input_grad = jnp.stack(input_rows)[:, None]
    return (
        layer_out,
        input_grad,
        attention_sums[0],
        attention_sums[1],
        attention_sums[2],
        attention_sums[3],
        kernel_sum,
        mixing_sum,
        attention_sums[4],
        attention_sums[5],
        feed_sums[0],
        feed_sums[1],
        feed_sums[2],
        feed_sums[3],
    )


def on_device(
    inputs,
    out_grad,
    pair_index,
    norm_gain,
    query_weight,
    key_weight,
    value_weight,
    score_kernel,
    head_mixing,
    group_gain,
    output_weight,
    second_gain,
    gate_weight,
    up_weight,
    down_weight,
):
    groups, planes = lax.axis_size("ctx"), lax.axis_size("seq")
    heads, width = score_kernel.shape[0], inputs.shape[3]
    if groups != 8 or heads != 2 * groups or (groups * inputs.shape[2]) % TILE:
        return general_device(
            inputs, out_grad, pair_index, norm_gain, query_weight, key_weight, value_weight,
            score_kernel, head_mixing, group_gain, output_weight, second_gain, gate_weight,
            up_weight, down_weight,
        )
    micro, local = inputs.shape[0], inputs.shape[2]
    blk, seq = local // 2, local * groups
    blocks = seq // blk
    pair = width // groups
    owned = width // (groups * planes)
    hidden = gate_weight.shape[1]
    chunk = hidden // (groups * planes)
    me = lax.axis_index("ctx")
    tokens_low = inputs.reshape(micro * local, width)
    grads_low = out_grad.reshape(micro * local, width)

    rows_all = micro * local
    qkv_shape = (groups, owned, 3 * pair)
    feed_shape = (groups, owned, 2 * planes * chunk)
    gain_rows = jnp.stack([norm_gain, group_gain, second_gain])
    spread_sems = [DMA((9,))] * 2
    feed_mine, qkv, gains, all_tokens, out_rows = communicate(
        functools.partial(enter_kernel, planes), "enter", 1, 50,
        [
            (feed_shape, BF16),
            ((planes,) + qkv_shape, BF16),
            ((planes, groups, 8, TILE), F32),
            ((groups, rows_all, width), BF16),
            ((planes, owned, width), BF16),
        ],
        [pltpu.VMEM((owned, width), BF16)] * 3 + [pltpu.VMEM((owned, hidden), BF16)] * 2
        + [pltpu.VMEM((3, owned), BF16), pltpu.VMEM((8, TILE), F32)]
        + [pltpu.VMEM(qkv_shape, BF16), pltpu.VMEM(feed_shape, BF16)]
        + [DMA((3, groups))] * 2 + spread_sems + [DMA((1, 2, planes))] * 2
        + [DMA((2, 2, planes))] * 2 + [DMA((11,))],
        (
            query_weight, key_weight, value_weight, gate_weight, up_weight, gain_rows, tokens_low,
            output_weight,
        ),
        ANYWHERE,
    )
    all_tokens, down_mine = lax.optimization_barrier((all_tokens, down_weight))
    feed = lax.all_gather(feed_mine.reshape(groups * owned, -1), "seq", axis=0, tiled=True)
    down = lax.all_gather(down_mine, "seq", axis=0, tiled=True)
    qkv = qkv.reshape(width, 3 * pair)
    hidden_all, heads_in, gains, gain_pair, out_rows, all_grads = communicate(
        functools.partial(heads_kernel, planes), "heads", 2, 20,
        [
            ((width, groups * rows_all), BF16),
            ((groups * rows_all, 3 * pair), BF16),
            ((8, width), F32),
            ((8, pair), F32),
            ((4, owned, width), BF16),
            ((groups, rows_all, width), BF16),
        ],
        [DMA((4,))] * 2 + spread_sems + [DMA((2,))],
        (all_tokens, qkv, gains, out_rows, grads_low),
        None, [ON_CHIP] * 3 + [ANYWHERE] * 2, (ON_CHIP,) * 4 + (ANYWHERE,) * 2,
    )
    all_grads = all_grads.reshape(-1, width)
    out_rows = out_rows.reshape(pair, width)

    slots = jnp.arange(blocks, dtype=jnp.int32)
    owner = jnp.repeat(pair_index, 2, axis=1)
    block_of_slot = jnp.where(slots % 2 == 0, owner, blocks - 1 - owner)
    place = (
        (slots // 2)[None] * (2 * micro)
        + 2 * jnp.arange(micro, dtype=jnp.int32)[:, None]
        + (slots % 2)[None]
    )
    blk_table = jnp.sum(
        jnp.where(block_of_slot[:, None, :] == slots[None, :, None], place[:, None, :], 0), axis=2
    ).astype(jnp.int32)
    ker = lax.dynamic_slice_in_dim(score_kernel, 2 * me, 2, 0)
    mix = jnp.repeat(lax.dynamic_slice_in_dim(head_mixing, 2 * me, 2, 0), pair // 2, axis=0).T
    scale = (width // heads) ** (-0.5)

    mixed, y, prob = pair_forward(blk_table, ker, mix, gain_pair, heads_in, micro, seq, blk, scale)
    by_core = (groups // 2, 2, rows_all)
    sum_spec = sum_scratch(rows_all, width)
    residual, second_all = communicate(
        second_kernel, "second", 3, 40,
        [((rows_all, width), F32), ((groups, rows_all, width), BF16)],
        sum_spec + spread_sems,
        (mixed.reshape(by_core + (pair,)), out_rows, tokens_low, gains), ON_CHIP,
    )
    second_all = second_all.reshape(-1, width)

    half = planes * chunk
    both = jnp.dot(second_all, feed, preferred_element_type=F32)
    gate, up = both[:, :half], both[:, half:]
    sigmoid = jax.nn.sigmoid(gate)
    active = (gate * sigmoid * up).astype(BF16)
    down_grad = lax.dot_general(active, all_grads, (((0,), (0,)), ((), ())), preferred_element_type=F32)
    all_grads, down_grad = lax.optimization_barrier((all_grads, down_grad.astype(BF16)))
    hid_grad = lax.dot_general(all_grads, down, (((1,), (1,)), ((), ())), preferred_element_type=F32)
    up_low = (hid_grad * gate * sigmoid).astype(BF16)
    gate_low = (hid_grad * up * sigmoid * (1.0 + gate * (1.0 - sigmoid))).astype(BF16)
    lows = jnp.concatenate([gate_low, up_low], axis=1)
    feed_grad = lax.dot_general(second_all, lows, (((0,), (0,)), ((), ())), preferred_element_type=F32)
    lows, feed_grad = lax.optimization_barrier((lows, feed_grad.astype(BF16)))
    feed_sum = lax.psum_scatter(feed_grad, "seq", scatter_dimension=0, tiled=True)
    down_sum = lax.psum_scatter(down_grad, "seq", scatter_dimension=0, tiled=True)
    residual_grad, gain_second_grad, all_attended = communicate(
        back_kernel, "back", 4, 40,
        [((rows_all, width), F32), ((1, width), F32), ((groups, rows_all, width), BF16)],
        sum_spec + spread_sems,
        (lows.reshape(by_core + (2 * half,)), feed, residual, grads_low, gains),
        ON_CHIP,
    )
    all_attended = all_attended.reshape(-1, width)
    mixed_grad = lax.dot_general(
        all_attended, out_rows, (((1,), (1,)), ((), ())), preferred_element_type=F32
    ).astype(BF16)
    out_w_grad = lax.dot_general(
        mixed, all_attended, (((0,), (0,)), ((), ())), preferred_element_type=F32
    )
    mixed_grad, down_sum = lax.optimization_barrier((mixed_grad, down_sum))
    qkv_low, group_part, mix_part, ker_part = pair_backward(
        blk_table, ker, mix, gain_pair, heads_in, mixed_grad, y, prob, seq, blk, scale
    )
    taps = score_kernel.shape[1] * score_kernel.shape[2]
    ker_mine = jnp.sum(ker_part, axis=2)[:, :taps]
    mix_mine = jnp.sum(mix_part.reshape(2, 2, pair // 2), axis=2).T
    row = lax.dynamic_update_slice
    group_all = row(jnp.zeros((1, width), F32), group_part, (0, pair * me))
    ker_all = row(jnp.zeros((heads, taps), F32), ker_mine, (2 * me, 0)).reshape(1, -1)
    mix_all = row(jnp.zeros((heads, 2), F32), mix_mine, (2 * me, 0)).reshape(1, -1)
    tap_rows = -(-heads * taps // width)
    taps_all = jnp.pad(ker_all, ((0, 0), (0, tap_rows * width - heads * taps))).reshape(-1, width)
    mix_all = jnp.pad(mix_all, ((0, 0), (0, width - 2 * heads)))
    small = jnp.concatenate(
        [jnp.zeros((1, width), F32), gain_second_grad, group_all, mix_all, taps_all]
    )
    small = jnp.pad(small, ((0, -small.shape[0] % 8), (0, 0)))
    input_grad, layer_out, sums, qkv_back, feed_back, out_w_back = communicate(
        functools.partial(leave_kernel, planes), "leave", 5, 55,
        [
            ((rows_all, width), BF16),
            ((rows_all, width), BF16),
            (small.shape, F32),
            (qkv_shape, BF16),
            (feed_shape, BF16),
            ((1, owned, width), BF16),
        ],
        sum_spec[:6] * 2
        + [pltpu.VMEM((groups,) + small.shape, F32), pltpu.VMEM((planes,) + small.shape, F32)]
        + [pltpu.VMEM((planes, groups * owned, 3 * pair), BF16)]
        + [pltpu.VMEM((2, planes, groups * owned, 3 * pair), BF16)] * 2
        + [pltpu.VMEM(qkv_shape, BF16)]
        + [pltpu.VMEM((planes, owned, width), BF16)]
        + [pltpu.VMEM((2, planes, owned, width), BF16)] * 2
        + sum_spec[6:] * 2
        + [DMA((2, groups))] * 2
        + [DMA((2, planes))] * 4
        + [DMA((2, groups))] * 2
        + [DMA((4,))] * 2 + [DMA((3,))],
        (
            qkv_low.reshape(by_core + (3 * pair,)), qkv, hidden_all,
            active.reshape(by_core + (half,)), down,
            residual, residual_grad, tokens_low, gains, small,
            feed_sum.reshape(feed_shape),
            out_w_grad.astype(BF16).reshape(4, owned, width),
        ),
        None, [ON_CHIP] * 10 + [ANYWHERE] * 2, (ON_CHIP,) * 3 + (ANYWHERE,) * 2 + (ON_CHIP,),
    )
    plain = [(owned, width)] * 3 + [(owned, hidden)] * 2 + [(owned, width), (chunk, width)]
    landed = (qkv_back, feed_back, out_w_back, down_sum, input_grad, layer_out)
    out_shapes = [jax.ShapeDtypeStruct(shape, F32) for shape in plain]
    out_shapes += [jax.ShapeDtypeStruct((rows_all, width), BF16)] * 2
    q_back, k_back, v_back, gate_back, up_back, out_w_out, down_out, input_grad, layer_out = pl.pallas_call(
        functools.partial(finish_kernel, len(out_shapes)),
        name="finish",
        out_shape=tuple(out_shapes),
        in_specs=[ANYWHERE] * 6,
        out_specs=(ANYWHERE,) * len(out_shapes),
        scratch_shapes=[pltpu.VMEM(value.shape, BF16) for value in landed]
        + [pltpu.VMEM(shape, F32) for shape in plain]
        + [DMA((6,)), DMA((len(out_shapes),))],
        compiler_params=pltpu.CompilerParams(vmem_limit_bytes=32 << 20),
    )(*landed)

    at = (lax.axis_index("seq") * groups + me) * owned
    gain_outs = [lax.dynamic_slice_in_dim(sums[i], at, owned, 0) for i in range(3)]
    ker_out = sums[4 : 4 + tap_rows].reshape(-1)[: heads * taps].reshape(score_kernel.shape)
    mix_out = sums[3, : 2 * heads].reshape(heads, 2)
    shape = inputs.shape
    return (
        layer_out.reshape(shape),
        input_grad.reshape(shape),
        gain_outs[0],
        q_back,
        k_back,
        v_back,
        ker_out,
        mix_out,
        gain_outs[2],
        out_w_out,
        gain_outs[1],
        gate_back,
        up_back,
        down_out,
    )


def solution(mesh):
    placed = (
        P(None, "seq", "ctx", None),
        P(None, "seq", "ctx", None),
        P(),
        P(("seq", "ctx")),
        P(("seq", "ctx"), None),
        P(("seq", "ctx"), None),
        P(("seq", "ctx"), None),
        P(),
        P(),
        P(("seq", "ctx")),
        P(("seq", "ctx"), None),
        P(("seq", "ctx")),
        P(("seq", "ctx"), None),
        P(("seq", "ctx"), None),
        P(("seq", "ctx"), None),
    )
    return jax.shard_map(
        on_device,
        mesh=mesh,
        in_specs=placed,
        out_specs=(
            P(None, "seq", "ctx", None),
            P(None, "seq", "ctx", None),
            P(("seq", "ctx")),
            P(("seq", "ctx"), None),
            P(("seq", "ctx"), None),
            P(("seq", "ctx"), None),
            P(),
            P(),
            P(("seq", "ctx")),
            P(("seq", "ctx"), None),
            P(("seq", "ctx")),
            P(("seq", "ctx"), None),
            P(("seq", "ctx"), None),
            P(("seq", "ctx"), None),
        ),
        check_vma=False,
    )
```

```python
import functools

import jax
import jax.numpy as jnp
from jax import lax
from jax.experimental import pallas as pl
from jax.experimental.pallas import tpu as pltpu
from jax.sharding import PartitionSpec as P

EPSILON = 1e-05
NEGATIVE = -1e30
F32 = jnp.float32
BF16 = jnp.bfloat16
TILE = 128


def nt(left, right):
    return lax.dot_general(left, right, (((1,), (1,)), ((), ())), preferred_element_type=F32)


def tn(left, right):
    return lax.dot_general(left, right, (((0,), (0,)), ((), ())), preferred_element_type=F32)


def nn(left, right):
    return lax.dot_general(left, right, (((1,), (0,)), ((), ())), preferred_element_type=F32)


def natural_rows(blk_ref, m, blk, seq):
    return [pl.multiple_of(blk_ref[m, b] * blk, blk) for b in range(seq // blk)]


def head_lanes(width):
    return lax.broadcasted_iota(jnp.int32, (1, width), 1) < width // 2


def load_heads(blk_ref, m, blk, seq, qkv_ref, qm, kf, ks, vn):
    width = vn.shape[1]
    first = head_lanes(width)
    kf[0:8, :] = jnp.zeros((8, width), F32)
    kf[seq : seq + TILE + 8, :] = jnp.zeros((TILE + 8, width), F32)
    for b, row in enumerate(natural_rows(blk_ref, m, blk, seq)):
        here = pl.ds(blk * b, blk)
        q = qkv_ref[pl.ds(row, blk), 0:width].astype(F32)
        qm[0, here, :] = jnp.where(first, q, 0.0).astype(BF16)
        qm[1, here, :] = jnp.where(first, 0.0, q).astype(BF16)
        kf[pl.ds(blk * b + 5, blk), :] = qkv_ref[pl.ds(row, blk), width : 2 * width].astype(F32)
        vn[here, :] = qkv_ref[pl.ds(row, blk), 2 * width : 3 * width]
    ks[...] = kf[0 : seq + TILE, :].astype(BF16)


def scores(qm, ks, h, rb, upto, scale):
    rows = pl.ds(TILE * rb, TILE)
    raw = nt(qm[h, rows, :], ks[0 : TILE * upto, :]) * scale
    key = lax.broadcasted_iota(jnp.int32, raw.shape, 1) - 5
    row = lax.broadcasted_iota(jnp.int32, raw.shape, 0) + TILE * rb
    return jnp.where((key >= 0) & (key <= row), raw, 0.0)


def head_factor(values, first, dim):
    squares = values * values
    own = jnp.sum(jnp.where(first, squares, 0.0), axis=1, keepdims=True)
    other = jnp.sum(jnp.where(first, 0.0, squares), axis=1, keepdims=True)
    return jnp.where(
        first, lax.rsqrt(own / dim + EPSILON), lax.rsqrt(other / dim + EPSILON)
    )


def forward_kernel(
    seq, blk, rows_tap, keys_tap, scale,
    blk_ref, ker_ref, mix_ref, gain_ref, qkv_ref,
    z_ref, y_ref, p_ref,
    qm, kf, ks, vn, shi, slo, thi, tlo, run, logit,
):
    m = pl.program_id(0)
    width = vn.shape[1]
    first = head_lanes(width)
    tiles = seq // TILE

    @pl.when(m == 0)
    def _():
        shi[...] = jnp.zeros(shi.shape, BF16)
        slo[...] = jnp.zeros(slo.shape, BF16)
        away = lax.broadcasted_iota(jnp.int32, (2 * TILE, TILE), 0) - lax.broadcasted_iota(
            jnp.int32, (2 * TILE, TILE), 1
        )
        for h in range(2):
            for a in range(rows_tap):
                band = jnp.zeros((2 * TILE, TILE), F32)
                for t in range(keys_tap):
                    band = jnp.where(away == keys_tap - 1 - t, ker_ref[h, a, t], band)
                high = band.astype(BF16)
                thi[h, :, TILE * a : TILE * (a + 1)] = high
                tlo[h, :, TILE * a : TILE * (a + 1)] = (band - high.astype(F32)).astype(BF16)

    load_heads(blk_ref, m, blk, seq, qkv_ref, qm, kf, ks, vn)
    for h in range(2):
        for rb in range(tiles):
            upto = min(rb + 2, tiles + 1)
            zeroed = scores(qm, ks, h, rb, upto, scale)
            high = zeroed.astype(BF16)
            shi[pl.ds(16 + TILE * rb, TILE), 0 : TILE * upto] = high
            slo[pl.ds(16 + TILE * rb, TILE), 0 : TILE * upto] = (zeroed - high.astype(F32)).astype(BF16)
        for b in range(tiles):
            count = seq - TILE * b
            rows = pl.ds(TILE * b, count + 16)
            lanes = pl.ds(TILE * b, 2 * TILE)
            high, low = shi[rows, lanes], slo[rows, lanes]
            run[0 : count + 16, :] = nn(high, thi[h]) + nn(low, thi[h]) + nn(high, tlo[h])
            total = run[16 : 16 + count, 0:TILE]
            for a in range(1, rows_tap):
                total = total + run[pl.ds(16 - a, count), TILE * a : TILE * (a + 1)]
            logit[pl.ds(TILE * b, count), TILE * b : TILE * (b + 1)] = total
        for rb in range(tiles):
            rows = pl.ds(TILE * rb, TILE)
            wide = TILE * (rb + 1)
            value = logit[rows, 0:wide]
            key = lax.broadcasted_iota(jnp.int32, value.shape, 1)
            row = lax.broadcasted_iota(jnp.int32, value.shape, 0) + TILE * rb
            value = jnp.where(key <= row, value, NEGATIVE)
            weight = jnp.exp(value - jnp.max(value, axis=1, keepdims=True))
            weight = weight / jnp.sum(weight, axis=1, keepdims=True)
            lowered = weight.astype(BF16)
            p_ref[0, h, rows, 0:wide] = lowered
            y_ref[0, h, rows, :] = nn(lowered, vn[0:wide, :])
    out = mix_ref[0:1, :] * y_ref[0, 0] + mix_ref[1:2, :] * y_ref[0, 1]
    normed = out * head_factor(out, first, width // 2)
    final = (normed * gain_ref[1:2, :]).astype(BF16)
    for b, row in enumerate(natural_rows(blk_ref, m, blk, seq)):
        z_ref[pl.ds(row, blk), :] = final[blk * b : blk * (b + 1), :]


def backward_kernel(
    seq, blk, rows_tap, keys_tap, scale,
    blk_ref, ker_ref, mix_ref, gain_ref, qkv_ref, zg_ref, y_ref, p_ref,
    low_ref, misc_ref,
    qm, kf, ks, vn, sb, up, zn, yl, cg, cs, eb, qa, ka, acc, taps,
):
    m = pl.program_id(0)
    width = vn.shape[1]
    first = head_lanes(width)
    tiles = seq // TILE
    wide_u = 3 * TILE
    span = keys_tap - 1
    lanes_all = rows_tap * TILE

    @pl.when(m == 0)
    def _():
        misc_ref[...] = jnp.zeros(misc_ref.shape, F32)
        taps[...] = jnp.zeros(taps.shape, F32)
        acc[...] = jnp.zeros(acc.shape, F32)
        cg[...] = jnp.zeros(cg.shape, F32)
        cs[...] = jnp.zeros(cs.shape, BF16)
        eb[...] = jnp.zeros(eb.shape, BF16)
        sb[...] = jnp.zeros(sb.shape, BF16)
        away = lax.broadcasted_iota(jnp.int32, (wide_u, 2 * TILE), 0) - lax.broadcasted_iota(
            jnp.int32, (wide_u, 2 * TILE), 1
        )
        for h in range(2):
            for a in range(rows_tap):
                band = jnp.zeros((wide_u, 2 * TILE), F32)
                for t in range(keys_tap):
                    band = jnp.where(away == TILE - span + t, ker_ref[h, a, t], band)
                up[h, wide_u * a : wide_u * (a + 1), :] = band.astype(BF16)

    load_heads(blk_ref, m, blk, seq, qkv_ref, qm, kf, ks, vn)
    places = natural_rows(blk_ref, m, blk, seq)
    for b, row in enumerate(places):
        zn[pl.ds(blk * b, blk), :] = zg_ref[pl.ds(row, blk), :].astype(F32)
    dim = width // 2
    y0, y1 = y_ref[0, 0], y_ref[0, 1]
    out = mix_ref[0:1, :] * y0 + mix_ref[1:2, :] * y1
    factor = head_factor(out, first, dim)
    normed = out * factor
    upstream = zn[...]
    misc_ref[16:17, 0:width] += jnp.sum(upstream * normed, axis=0, keepdims=True)
    scaled = upstream * gain_ref[1:2, :]
    both = scaled * normed
    own = jnp.sum(jnp.where(first, both, 0.0), axis=1, keepdims=True) / dim
    other = jnp.sum(jnp.where(first, 0.0, both), axis=1, keepdims=True) / dim
    out_grad = factor * (scaled - normed * jnp.where(first, own, other))
    misc_ref[17:18, 0:width] += jnp.sum(out_grad * y0, axis=0, keepdims=True)
    misc_ref[18:19, 0:width] += jnp.sum(out_grad * y1, axis=0, keepdims=True)
    yl[0] = (mix_ref[0:1, :] * out_grad).astype(BF16)
    yl[1] = (mix_ref[1:2, :] * out_grad).astype(BF16)

    for b in range(tiles):
        rows = pl.ds(TILE * b, seq - TILE * b)
        lanes = pl.ds(TILE * b, TILE)
        part = tn(p_ref[0, 0, rows, lanes], yl[0, rows, :]) + tn(p_ref[0, 1, rows, lanes], yl[1, rows, :])
        part = part.astype(BF16)
        for i in range(TILE // blk):
            low_ref[pl.ds(places[b * (TILE // blk) + i], blk), 2 * width : 3 * width] = part[blk * i : blk * (i + 1), :]

    ka[...] = jnp.zeros(ka.shape, F32)
    for h in range(2):
        for rb in range(tiles):
            rows = pl.ds(TILE * rb, TILE)
            upto = min(rb + 2, tiles + 1)
            sb[rows, 0 : TILE * upto] = scores(qm, ks, h, rb, upto, scale).astype(BF16)
            wide = TILE * (rb + 1)
            prob = p_ref[0, h, rows, 0:wide].astype(F32)
            grad = nt(yl[h, rows, :], vn[0:wide, :])
            both = prob * grad
            cg[rows, 0:wide] = both - prob * jnp.sum(both, axis=1, keepdims=True)
        for b in range(tiles):
            start = max(0, TILE * b - 16)
            count = seq - start
            for a in range(rows_tap):
                cs[pl.ds(start, count), pl.ds(lanes_all * b + TILE * a, TILE)] = cg[
                    pl.ds(start + a, count), TILE * b : TILE * (b + 1)
                ].astype(BF16)
            acc[h] += tn(
                sb[pl.ds(start, count), pl.ds(TILE * b, 2 * TILE)],
                cs[pl.ds(start, count), pl.ds(lanes_all * b, lanes_all)],
            )
        for b in range(0, tiles + 1, 2):
            start = max(0, TILE * b - 16)
            count = seq - start
            columns = min(2, tiles + 1 - b)
            left, right = [], []
            for a in range(rows_tap):
                for piece in range(columns + 1):
                    block = b - 1 + piece
                    if 0 <= block < tiles:
                        left.append(cs[pl.ds(start, count), pl.ds(lanes_all * block + TILE * a, TILE)])
                        right.append(
                            up[h, pl.ds(wide_u * a + TILE * piece, TILE), 0 : TILE * columns]
                        )
            grad = nn(jnp.concatenate(left, axis=1), jnp.concatenate(right, axis=0))
            key = lax.broadcasted_iota(jnp.int32, grad.shape, 1) + TILE * b - 5
            row = lax.broadcasted_iota(jnp.int32, grad.shape, 0) + start
            low = jnp.where((key >= 0) & (key <= row), grad, 0.0).astype(BF16)
            eb[pl.ds(start, count), pl.ds(TILE * b, TILE * columns)] = low
            ka[pl.ds(TILE * b, TILE * columns), :] += tn(low, qm[h, pl.ds(start, count), :])
        for rb in range(tiles):
            rows = pl.ds(TILE * rb, TILE)
            upto = min(rb + 2, tiles + 1)
            part = nn(eb[rows, 0 : TILE * upto], ks[0 : TILE * upto, :]) * scale
            if h == 0:
                qa[rows, :] = part
            else:
                qa[rows, :] = jnp.where(first, qa[rows, :], part)
    for b, row in enumerate(places):
        low_ref[pl.ds(row, blk), 0:width] = qa[pl.ds(blk * b, blk), :].astype(BF16)
        low_ref[pl.ds(row, blk), width : 2 * width] = (ka[pl.ds(blk * b + 5, blk), :] * scale).astype(BF16)

    @pl.when(m == pl.num_programs(0) - 1)
    def _():
        away = lax.broadcasted_iota(jnp.int32, (2 * TILE, TILE), 0) - lax.broadcasted_iota(
            jnp.int32, (2 * TILE, TILE), 1
        )
        for h in range(2):
            for a in range(rows_tap):
                table = acc[h, :, TILE * a : TILE * (a + 1)]
                for t in range(keys_tap):
                    at = a * keys_tap + t
                    taps[at : at + 1, :] = jnp.sum(
                        jnp.where(away == span - t, table, 0.0), axis=0, keepdims=True
                    )
            count = taps.shape[0]
            tap = lax.broadcasted_iota(jnp.int32, (8, count), 1) - keys_tap * lax.broadcasted_iota(
                jnp.int32, (8, count), 0
            )
            rows = ((tap >= 0) & (tap < keys_tap)).astype(F32)
            at = lax.broadcasted_iota(jnp.int32, (count, TILE), 0)
            lane = lax.broadcasted_iota(jnp.int32, (count, TILE), 1)
            value = jnp.sum(taps[...], axis=1, keepdims=True)
            lanes = jnp.zeros((count, TILE), F32)
            for a in range(rows_tap):
                lanes = jnp.where((at == keys_tap * a + lane) & (lane < keys_tap), value, lanes)
            misc_ref[8 * h : 8 * h + 8, 0:TILE] = lax.dot_general(
                rows, lanes, (((1,), (0,)), ((), ())),
                precision=lax.Precision.HIGHEST, preferred_element_type=F32,
            )


def whole(shape):
    return pl.BlockSpec(shape, lambda m: (0,) * len(shape))


def pair_forward(blk_table, ker, mix, gain, qkv, micro, seq, blk, scale):
    width = qkv.shape[1] // 3
    mixed = (qkv.shape[0], width)
    rows_tap, keys_tap = ker.shape[1:]
    smem = pl.BlockSpec(memory_space=pltpu.SMEM)
    per = lambda shape: pl.BlockSpec((1,) + shape, lambda m: (m,) + (0,) * len(shape))
    return pl.pallas_call(
        functools.partial(forward_kernel, seq, blk, rows_tap, keys_tap, scale),
        name="pair_forward",
        grid=(micro,),
        out_shape=(
            jax.ShapeDtypeStruct(mixed, BF16),
            jax.ShapeDtypeStruct((micro, 2, seq, width), F32),
            jax.ShapeDtypeStruct((micro, 2, seq, seq), BF16),
        ),
        in_specs=[smem, smem, whole(mix.shape), whole(gain.shape), whole(qkv.shape)],
        out_specs=(whole(mixed), per((2, seq, width)), per((2, seq, seq))),
        scratch_shapes=[
            pltpu.VMEM((2, seq, width), BF16),
            pltpu.VMEM((seq + TILE + 8, width), F32),
            pltpu.VMEM((seq + TILE, width), BF16),
            pltpu.VMEM((seq, width), BF16),
            pltpu.VMEM((seq + 16, seq + TILE), BF16),
            pltpu.VMEM((seq + 16, seq + TILE), BF16),
            pltpu.VMEM((2, 2 * TILE, rows_tap * TILE), BF16),
            pltpu.VMEM((2, 2 * TILE, rows_tap * TILE), BF16),
            pltpu.VMEM((seq + 16, rows_tap * TILE), F32),
            pltpu.VMEM((seq, seq), F32),
        ],
        compiler_params=pltpu.CompilerParams(vmem_limit_bytes=56 << 20),
        cost_estimate=pl.CostEstimate(flops=20 * 10**9, transcendentals=10**6, bytes_accessed=8 << 20),
    )(blk_table, ker, mix, gain, qkv)


def pair_backward(blk_table, ker, mix, gain, qkv, zg, y, p, seq, blk, scale):
    width = qkv.shape[1] // 3
    micro = y.shape[0]
    rows_tap, keys_tap = ker.shape[1:]
    tiles = seq // TILE
    smem = pl.BlockSpec(memory_space=pltpu.SMEM)
    per = lambda shape: pl.BlockSpec((1,) + shape, lambda m: (m,) + (0,) * len(shape))
    taps = -(-rows_tap * keys_tap // 8) * 8
    return pl.pallas_call(
        functools.partial(backward_kernel, seq, blk, rows_tap, keys_tap, scale),
        name="pair_backward",
        grid=(micro,),
        out_shape=(
            jax.ShapeDtypeStruct(qkv.shape, BF16),
            jax.ShapeDtypeStruct((24, 2 * TILE), F32),
        ),
        in_specs=[smem, smem, whole(mix.shape), whole(gain.shape), whole(qkv.shape), whole(zg.shape)]
        + [per((2, seq, width)), per((2, seq, seq))],
        out_specs=(whole(qkv.shape), whole((24, 2 * TILE))),
        scratch_shapes=[
            pltpu.VMEM((2, seq, width), BF16),
            pltpu.VMEM((seq + TILE + 8, width), F32),
            pltpu.VMEM((seq + TILE, width), BF16),
            pltpu.VMEM((seq, width), BF16),
            pltpu.VMEM((seq, seq + TILE), BF16),
            pltpu.VMEM((2, rows_tap * 3 * TILE, 2 * TILE), BF16),
            pltpu.VMEM((seq, width), F32),
            pltpu.VMEM((2, seq, width), BF16),
            pltpu.VMEM((seq + 8, seq), F32),
            pltpu.VMEM((seq, tiles * rows_tap * TILE), BF16),
            pltpu.VMEM((seq, seq + TILE), BF16),
            pltpu.VMEM((seq, width), F32),
            pltpu.VMEM((seq + TILE, width), F32),
            pltpu.VMEM((2, 2 * TILE, rows_tap * TILE), F32),
            pltpu.VMEM((taps, TILE), F32),
        ],
        compiler_params=pltpu.CompilerParams(vmem_limit_bytes=56 << 20),
        cost_estimate=pl.CostEstimate(flops=30 * 10**9, transcendentals=10**5, bytes_accessed=12 << 20),
    )(blk_table, ker, mix, gain, qkv, zg, y, p)


MESH = pl.DeviceIdType.MESH


def peer(offset):
    mine = lax.axis_index("ctx")
    y = (mine // 4 + offset // 4) % 2
    x = ((mine // 2) % 2 + (offset // 2) % 2) % 2
    core = (mine % 2 + offset % 2) % 2
    return y * 4 + x * 2 + core


def greet(places):
    barrier = pltpu.get_barrier_semaphore()
    for place in places:
        pl.semaphore_signal(barrier, inc=1, device_id=place, device_id_type=MESH)
    return lambda: pl.semaphore_wait(barrier, len(places))


def remote(source, target, send, receive, place):
    return pltpu.make_async_remote_copy(
        src_ref=source, dst_ref=target, send_sem=send, recv_sem=receive,
        device_id=place, device_id_type=MESH,
    )


def exchange_start(plane, mine, source, target, sends, receives):
    copies = [
        remote(source.at[peer(d)], target.at[mine], sends.at[d], receives.at[d], (plane, peer(d)))
        for d in (6, 7, 2, 3, 4, 5, 1)
    ]
    for copy in copies:
        copy.start()
    return copies


class Spread:
    def __init__(self, source, target, sends, receives):
        self.plane, self.mine = lax.axis_index("seq"), lax.axis_index("ctx")
        self.source, self.target, self.sends, self.receives = source, target, sends, receives
        self.copies = {}
        half = target.shape[1] // 2
        self.first, self.second = pl.ds(0, half), pl.ds(half, half)

    def send(self, key, source, target, offset):
        copy = remote(source, target, self.sends.at[key], self.receives.at[key], (self.plane, peer(offset)))
        copy.start()
        self.copies[key] = copy

    def hand_on(self, key, block, offset, rows=None):
        piece = self.target.at[block] if rows is None else self.target.at[block, rows]
        self.send(key, piece, piece, offset)

    def start(self):
        for d in (2, 4, 1):
            self.send(d, self.source, self.target.at[self.mine], d)

    def near(self):
        self.copies[2].wait_recv()
        self.hand_on(6, peer(2), 4, self.first)
        self.hand_on(3, peer(2), 1)
        self.copies[4].wait_recv()
        self.hand_on(0, peer(4), 2, self.second)
        self.hand_on(5, peer(4), 1)

    def across(self):
        self.copies[6].wait_recv()
        self.hand_on(7, peer(6), 1, self.first)
        self.copies[0].wait_recv()
        self.hand_on(8, peer(6), 1, self.second)

    def finish(self):
        for key in (1, 3, 5, 7, 8):
            self.copies[key].wait_recv()
        for copy in self.copies.values():
            copy.wait_send()


class PlaneSum:
    def __init__(self, terms, part, own, near, stage, far, hop, sends, receives):
        self.plane, self.mine = lax.axis_index("seq"), lax.axis_index("ctx")
        self.terms, self.part, self.own = terms, part, own
        self.near, self.stage, self.far, self.hop = near, stage, far, hop
        self.sends, self.receives = sends, receives
        self.copies = {}
        half = part.shape[1] // 2
        self.first, self.second = pl.ds(0, half), pl.ds(half, half)

    def send(self, key, source, target, offset):
        copy = remote(source, target, self.sends.at[key], self.receives.at[key], (self.plane, peer(offset)))
        copy.start()
        self.copies[key] = copy

    def start(self, met):
        self.part[...] = self.terms(1 - self.mine % 2).astype(BF16)
        met()
        for d in (6, 2, 4, 0):
            self.send(d, self.part.at[peer(d) // 2], self.near.at[d // 2], 1)

    def prepare(self):
        self.own[...] = self.terms(self.mine % 2)

    def chip_sum(self, d):
        self.copies[d].wait_recv()
        self.stage[d // 2] = (self.own[peer(d) // 2] + self.near[d // 2].astype(F32)).astype(BF16)

    def add_hop(self, slot, rows, hop):
        self.stage[slot, rows, :] = (
            self.stage[slot, rows, :].astype(F32) + self.hop[hop].astype(F32)
        ).astype(BF16)

    def run(self):
        first, second = self.first, self.second
        self.chip_sum(6)
        self.send(1, self.stage.at[3, first], self.hop.at[0], 2)
        self.send(3, self.stage.at[3, second], self.hop.at[1], 4)
        self.chip_sum(2)
        self.send(5, self.stage.at[1, first], self.far.at[0, first], 2)
        self.chip_sum(4)
        self.send(7, self.stage.at[2, second], self.far.at[1, second], 4)
        self.copies[1].wait_recv()
        self.add_hop(2, first, 0)
        self.send(8, self.stage.at[2, first], self.far.at[1, first], 4)
        self.copies[3].wait_recv()
        self.add_hop(1, second, 1)
        self.send(9, self.stage.at[1, second], self.far.at[0, second], 2)

    def total(self):
        self.copies[0].wait_recv()
        value = self.own[self.mine // 2] + self.near[0].astype(F32)
        for key in (5, 7, 8, 9):
            self.copies[key].wait_recv()
        return value + self.far[0].astype(F32) + self.far[1].astype(F32)

    def finish(self):
        for copy in self.copies.values():
            copy.wait_send()


class Fetch:
    def __init__(self, source, buffer, sem):
        self.copy, self.buffer, self.ready = pltpu.make_async_copy(source, buffer, sem), buffer, False
        self.copy.start()

    def get(self):
        if not self.ready:
            self.copy.wait()
            self.ready = True
        return self.buffer


def fetch(sources, buffers, sems):
    return [Fetch(source, buffer, sems.at[i]) for i, (source, buffer) in enumerate(zip(sources, buffers))]


def put(buffer, out, sem):
    copy = pltpu.make_async_copy(buffer, out, sem)
    copy.start()
    return copy


def terms_of(values, product):
    chips, _, rows, width = values.buffer.shape

    def terms(core):
        left = values.get()[:, core].reshape(chips * rows, width)
        return product(left).reshape(chips, rows, -1)

    return terms


class Line:
    def __init__(self, sources, targets, planes, sends, receives):
        self.sources, self.targets, self.planes = sources, targets, planes
        self.sends, self.receives = sends, receives
        self.plane, self.mine = lax.axis_index("seq"), lax.axis_index("ctx")

    def copy(self, i, up, step):
        block = jnp.clip(self.plane - step if up else self.plane + step, 0, self.planes - 1)
        next_plane = jnp.clip(self.plane + 1 if up else self.plane - 1, 0, self.planes - 1)
        at = (i, int(up), step)
        target = self.targets[i].at[block]
        source = target if step else self.sources[i]
        return remote(source, target, self.sends.at[at], self.receives.at[at], (next_plane, self.mine))

    def arrived(self, i, up, step):
        block = jnp.clip(self.plane - 1 - step if up else self.plane + 1 + step, 0, self.planes - 1)
        at = (i, int(up), step)
        target = self.targets[i].at[block]
        from_plane = jnp.clip(self.plane - 1 if up else self.plane + 1, 0, self.planes - 1)
        return remote(target, target, self.sends.at[at], self.receives.at[at], (from_plane, self.mine))

    def step(self, step):
        for up in (True, False):
            have = self.plane >= step if up else self.plane + step < self.planes
            more = self.plane + 1 < self.planes if up else self.plane > 0
            for i in range(len(self.targets)):
                if step:
                    @pl.when(have)
                    def _(i=i, up=up):
                        self.arrived(i, up, step - 1).wait_recv()

                if step < self.planes - 1:
                    @pl.when(have & more)
                    def _(i=i, up=up):
                        self.copy(i, up, step).start()

    def finish(self):
        for step in range(self.planes - 1):
            for up in (True, False):
                have = self.plane >= step if up else self.plane + step < self.planes
                more = self.plane + 1 < self.planes if up else self.plane > 0
                for i in range(len(self.targets)):
                    @pl.when(have & more)
                    def _(i=i, up=up, step=step):
                        self.copy(i, up, step).wait_send()


def plane_peers(plane, offsets):
    return [(plane, peer(d)) for d in offsets]


def other_planes(plane, mine, planes):
    return [((plane + d) % planes, mine) for d in range(1, planes)]


class RowDeal:
    def __init__(self, gathered, dealt, sends, receives, local):
        self.plane, self.mine = lax.axis_index("seq"), lax.axis_index("ctx")
        self.gathered, self.dealt, self.sends, self.receives, self.local = gathered, dealt, sends, receives, local

    def out(self, s, back):
        if back:
            target = 4 * (self.mine % 2) + s
            source, place = self.dealt.at[s], self.gathered.at[self.mine // 2]
        else:
            target = 2 * s + self.mine // 4
            source, place = self.gathered.at[s], self.dealt.at[self.mine % 4]
        slot = self.mine // 2 if back else self.mine % 4
        copy = remote(source, place, self.sends.at[s], self.receives.at[slot], (self.plane, target))
        keep = pltpu.make_async_copy(source, place, self.local)
        return target == self.mine, copy, keep

    def into(self, r, back):
        if back:
            origin = 2 * r + self.mine // 4
            place = self.gathered.at[r]
        else:
            origin = 4 * (self.mine % 2) + r
            place = self.dealt.at[r]
        return origin == self.mine, remote(place, place, self.sends.at[r], self.receives.at[r], (self.plane, origin))

    def start(self, back):
        for s in range(4):
            here, copy, keep = self.out(s, back)

            @pl.when(here)
            def _():
                keep.start()

            @pl.when(jnp.logical_not(here))
            def _():
                copy.start()

    def wait(self, back):
        for s in range(4):
            here, copy, keep = self.out(s, back)

            @pl.when(here)
            def _():
                keep.wait()

            @pl.when(jnp.logical_not(here))
            def _():
                copy.wait_send()

        for r in range(4):
            here, copy = self.into(r, back)

            @pl.when(jnp.logical_not(here))
            def _():
                copy.wait_recv()


def enter_kernel(
    planes, q, k, v, gate, up, gains, tokens, out_w,
    feed_out, qkv_out, gains_out, tokens_out, out_w_out,
    q_near, k_near, v_near, gate_near, up_near, gains_near, packed, qkv, feed,
    deal_sends, deal_receives, sends, receives, row_sends, row_receives, line_sends, line_receives, local,
):
    plane, mine = lax.axis_index("seq"), lax.axis_index("ctx")
    loads = [
        pltpu.make_async_copy(source, place, local.at[5 + i])
        for i, (source, place) in enumerate(
            ((gains, gains_near), (q, q_near), (k, k_near), (v, v_near), (gate, gate_near), (up, up_near))
        )
    ]
    keep = [
        pltpu.make_async_copy(qkv.at[mine], qkv_out.at[plane, mine], local.at[0]),
        pltpu.make_async_copy(packed, gains_out.at[plane, mine], local.at[1]),
        pltpu.make_async_copy(feed.at[mine], feed_out.at[mine], local.at[2]),
        pltpu.make_async_copy(tokens, tokens_out.at[mine], local.at[3]),
        pltpu.make_async_copy(out_w, out_w_out.at[plane], local.at[4]),
    ]
    for copy in loads + keep[3:]:
        copy.start()
    met = greet(plane_peers(plane, range(1, 8)) + other_planes(plane, mine, planes))
    groups, _, three = qkv.shape
    pair = three // 3
    half = feed.shape[2] // 2
    for copy in loads[:4]:
        copy.wait()
    packed[...] = jnp.zeros(packed.shape, F32)
    packed[0:3, 0 : gains.shape[1]] = gains_near[...].astype(F32)
    for c in range(groups):
        for i, weight in enumerate((q_near, k_near, v_near)):
            qkv[c, :, pair * i : pair * (i + 1)] = weight[:, pair * c : pair * (c + 1)]
    for copy in keep[:2]:
        copy.start()
    met()
    first = exchange_start(plane, mine, qkv, qkv_out.at[plane], deal_sends.at[0], deal_receives.at[0])
    for d in (6, 7, 2, 3, 4, 5, 1):
        copy = remote(packed, gains_out.at[plane, mine], deal_sends.at[1, d], deal_receives.at[1, d], (plane, peer(d)))
        copy.start()
        first.append(copy)
    rows = Line([out_w], [out_w_out], planes, row_sends, row_receives)
    rows.step(0)
    for copy in loads[4:]:
        copy.wait()
    for c in range(groups):
        for i, weight in enumerate((gate_near, up_near)):
            for s in range(half // TILE):
                at = TILE * (groups * s + c)
                feed[c, :, half * i + TILE * s : half * i + TILE * (s + 1)] = weight[:, at : at + TILE]
    keep[2].start()
    keep[0].wait()
    keep[1].wait()
    for copy in first:
        copy.wait_recv()
    line = Line(
        [qkv_out.at[plane], gains_out.at[plane]], [qkv_out, gains_out], planes, line_sends, line_receives
    )
    line.step(0)
    spread = Spread(tokens, tokens_out, sends, receives)
    spread.start()
    rows.step(1)
    line.step(1)
    spread.near()
    deals = exchange_start(plane, mine, feed, feed_out, deal_sends.at[2], deal_receives.at[2])
    rows.step(2)
    line.step(2)
    spread.across()
    for step in range(3, planes):
        rows.step(step)
        line.step(step)
    spread.finish()
    for copy in first:
        copy.wait_send()
    for copy in deals:
        copy.wait()
    for copy in keep[2:]:
        copy.wait()
    line.finish()
    rows.finish()


def heads_kernel(
    planes, tokens, qkv, gains, out_w, grads, hidden, heads, gains_out, pair_gain, out_w_out, grads_out,
    tokens_near, qkv_near, hidden_near, heads_near,
    row_sends, row_receives, sends, receives, loads, stores, local,
):
    plane, mine = lax.axis_index("seq"), lax.axis_index("ctx")
    groups = tokens.shape[0]
    weight = Fetch(qkv, qkv_near, loads.at[groups])
    blocks = [Fetch(tokens.at[i], tokens_near.at[i], loads.at[i]) for i in range(groups)]
    keep = pltpu.make_async_copy(grads, grads_out.at[mine], local.at[1])
    keep.start()
    greet(plane_peers(plane, range(1, 8)))()
    spread = Spread(grads, grads_out, sends, receives)
    spread.start()
    deal = RowDeal(out_w, out_w_out, row_sends, row_receives, local.at[0])
    deal.start(False)
    owned = out_w.shape[1]
    for s in range(planes):
        for c in range(groups):
            at = owned * (groups * s + c)
            gains_out[:, at : at + owned] = gains[s, c, :, 0:owned]
    for r in range(4):
        pair_gain[:, owned * r : owned * (r + 1)] = gains[mine // 2, 4 * (mine % 2) + r, :, 0:owned]
    gain = gains_out[0:1, :]
    out = []
    for i in range(groups):
        value = blocks[i].get()[...].astype(F32)
        low = (value * inverse_root(value) * gain).astype(BF16)
        rows = pl.ds(value.shape[0] * i, value.shape[0])
        hidden_near[:, rows] = low.T
        out.append(put(hidden_near.at[:, rows], hidden.at[:, rows], stores.at[0, i]))
        heads_near[rows, :] = nn(low, weight.get()[...]).astype(BF16)
        out.append(put(heads_near.at[rows], heads.at[rows], stores.at[1, i]))
        if i == groups - 3:
            spread.near()
    deal.wait(False)
    spread.across()
    for copy in out:
        copy.wait()
    spread.finish()
    keep.wait()


def inverse_root(values):
    return lax.rsqrt(jnp.mean(values * values, axis=1, keepdims=True) + EPSILON)


def second_kernel(
    mixed, out_w, tokens, gains, residual, spread_out,
    mixed_near, out_w_near, tokens_near, residual_near, own_near, loads,
    part, own, near, stage, far, hop, sum_sends, sum_receives, sends, receives,
):
    plane, mine = lax.axis_index("seq"), lax.axis_index("ctx")
    left, weight, rows_in = fetch(
        (mixed, out_w, tokens), (mixed_near, out_w_near, tokens_near), loads
    )
    met = greet(plane_peers(plane, (1, 2, 4)))
    rows = PlaneSum(
        terms_of(left, lambda value: nn(value, weight.get()[...])), part, own, near, stage, far, hop,
        sum_sends, sum_receives,
    )
    rows.start(met)
    rows.prepare()
    rows.run()
    value = rows_in.get()[...].astype(F32) + rows.total()
    own_near[...] = (value * inverse_root(value) * gains[2:3, :]).astype(BF16)
    spread = Spread(own_near, spread_out, sends, receives)
    spread.start()
    keep = put(own_near, spread_out.at[mine], loads.at[3])
    residual_near[...] = value
    out = put(residual_near, residual, loads.at[4])
    rows.finish()
    spread.near()
    spread.across()
    keep.wait()
    out.wait()
    spread.finish()


def back_through_norm(upstream, values, gain):
    factor = inverse_root(values)
    normed = values * factor
    scaled = upstream * gain
    grad = factor * (scaled - normed * jnp.mean(scaled * normed, axis=1, keepdims=True))
    return grad, jnp.sum(upstream * normed, axis=0, keepdims=True)


def back_kernel(
    lows, feed, residual, grads, out_w, mixed, gains, residual_grad, gain_grad, mixed_grad, out_w_grad,
    lows_near, feed_near, residual_near, grads_near, out_w_near, mixed_near, residual_grad_near, gathered, total, loads,
    part, own, near, stage, far, hop, sum_sends, sum_receives, sends, receives,
):
    plane, mine = lax.axis_index("seq"), lax.axis_index("ctx")
    weight, left, before, upstream, out_rows, taken = fetch(
        (feed, lows, residual, grads, out_w, mixed),
        (feed_near, lows_near, residual_near, grads_near, out_w_near, mixed_near),
        loads,
    )
    met = greet(plane_peers(plane, (1, 2, 4)))
    rows = PlaneSum(
        terms_of(left, lambda value: nt(value, weight.get()[...])), part, own, near, stage, far, hop,
        sum_sends, sum_receives,
    )
    rows.start(met)
    rows.prepare()
    rows.run()
    grad, gain_part = back_through_norm(rows.total(), before.get()[...], gains[2:3, :])
    grad = grad + upstream.get()[...].astype(F32)
    gathered[mine] = grad.astype(BF16)
    spread = Spread(gathered.at[mine], gathered, sends, receives)
    spread.start()
    gain_grad[...] = gain_part
    residual_grad_near[...] = grad
    out = put(residual_grad_near, residual_grad, loads.at[6])
    taken.get()

    def use(d):
        block = peer(d) if d else mine
        value = gathered[block]
        mixed_grad[block] = nt(value, out_rows.get()[...]).astype(BF16)
        term = tn(mixed_near[block], value)
        total[...] = total[...] + term if d else term

    use(0)
    rows.finish()
    spread.near()
    use(2)
    use(4)
    spread.copies[1].wait_recv()
    use(1)
    spread.across()
    use(6)
    for keys, d in (((3,), 3), ((5,), 5), ((7, 8), 7)):
        for key in keys:
            spread.copies[key].wait_recv()
        use(d)
    out_w_grad[...] = total[...].astype(BF16)
    for copy in spread.copies.values():
        copy.wait_send()
    out.wait()


class Fold:
    def __init__(self, own, stage, landed, planes, sends, receives):
        self.own, self.stage, self.landed, self.planes = own, stage, landed, planes
        self.sends, self.receives = sends, receives
        self.plane, self.mine = lax.axis_index("seq"), lax.axis_index("ctx")

    def copy(self, j, up):
        place = jnp.clip(self.plane + 1 if up else self.plane - 1, 0, self.planes - 1)
        at = (int(up), j)
        return remote(self.stage.at[at], self.landed.at[at], self.sends.at[at], self.receives.at[at], (place, self.mine))

    def advance(self, j, up):
        active = self.plane < j if up else self.plane > j
        inner = self.plane > 0 if up else self.plane < self.planes - 1

        @pl.when(active & inner)
        def _():
            self.copy(j, up).wait_recv()
            self.stage[int(up), j] = (
                self.own[j].astype(F32) + self.landed[int(up), j].astype(F32)
            ).astype(BF16)

        @pl.when(active & jnp.logical_not(inner))
        def _():
            self.stage[int(up), j] = self.own[j]

        @pl.when(active)
        def _():
            self.copy(j, up).start()

    def round(self, i):
        self.advance(self.planes - 1 - i, True)
        self.advance(i, False)

    def total(self, store):
        for j in range(self.planes):
            @pl.when(self.plane == j)
            def _():
                value = self.own[j].astype(F32)
                if j > 0:
                    self.copy(j, True).wait_recv()
                    value = value + self.landed[1, j].astype(F32)
                if j < self.planes - 1:
                    self.copy(j, False).wait_recv()
                    value = value + self.landed[0, j].astype(F32)
                store(value.astype(BF16))

    def finish(self):
        for j in range(self.planes):
            for up in (True, False):
                @pl.when(self.plane < j if up else self.plane > j)
                def _():
                    self.copy(j, up).wait_send()


def layer_kernel(
    active, down, residual, out_w_grad, layer_out, row_grad,
    active_near, down_near, residual_near, loads,
    part, own, near, stage, far, hop, sum_sends, sum_receives, row_sends, row_receives, local,
):
    plane, mine = lax.axis_index("seq"), lax.axis_index("ctx")
    left, weight, before = fetch(
        (active, down, residual), (active_near, down_near, residual_near), loads
    )
    met = greet(plane_peers(plane, range(1, 8)))
    rows = PlaneSum(
        terms_of(left, lambda value: nn(value, weight.get()[...])), part, own, near, stage, far, hop,
        sum_sends, sum_receives,
    )
    rows.start(met)
    deal = RowDeal(row_grad, out_w_grad, row_sends, row_receives, local)
    deal.start(True)
    rows.prepare()
    rows.run()
    layer_out[...] = (before.get()[...] + rows.total()).astype(BF16)
    deal.wait(True)
    rows.finish()


def leave_kernel(
    planes, qkv_low_in, qkv_in, hidden_in, residual_grad_in, tokens_in,
    gains, second_grad, misc, feed_grad, row_grad,
    input_grad, small_out, misc_out, qkv_out, feed_out, out_w_out,
    qkv_low_near, qkv_near, hidden_near, residual_grad_near, tokens_near, loads,
    misc_all, misc_sends, misc_receives,
    part, own, near, stage, far, hop, small_plane, small_all,
    grads, fold_stage, fold_landed, qkv_sum,
    sum_sends, sum_receives, small_sends, small_receives,
    fold_sends, fold_receives, deal_sends, deal_receives, local,
):
    plane, mine = lax.axis_index("seq"), lax.axis_index("ctx")
    qkv_low, qkv, hidden, residual_grad, tokens = fetch(
        (qkv_low_in, qkv_in, hidden_in, residual_grad_in, tokens_in),
        (qkv_low_near, qkv_near, hidden_near, residual_grad_near, tokens_near),
        loads,
    )
    keep_feed = pltpu.make_async_copy(feed_grad.at[mine], feed_out.at[mine], local.at[0])
    keep_feed.start()
    misc_all[plane] = misc[...]
    met = greet(plane_peers(plane, range(1, 8)) + other_planes(plane, mine, planes))
    misc_copies = [
        remote(misc_all.at[plane], misc_all.at[plane], misc_sends.at[0, d], misc_receives.at[0, d], ((plane + d) % planes, mine))
        for d in range(1, planes)
    ]
    rows = PlaneSum(
        terms_of(qkv_low, lambda left: nt(left, qkv.get()[...])), part, own, near, stage, far, hop,
        sum_sends, sum_receives,
    )
    halves = [pl.ds(grads.shape[1] // 2 * k, grads.shape[1] // 2) for k in range(2)]
    folds = [
        Fold(
            grads.at[:, rows], fold_stage.at[:, :, rows], fold_landed.at[:, :, rows], planes,
            fold_sends.at[k], fold_receives.at[k],
        )
        for k, rows in enumerate(halves)
    ]
    ends = (plane == 0) | (plane == planes - 1)
    block, owned = grads.shape[1], row_grad.shape[1]
    three = qkv_low_in.shape[3]
    pair = three // 3

    def project(i):
        j = jnp.where(plane < planes // 2, planes - 1 - i, i)
        lows = qkv_low.get()[...].reshape(hidden_near.shape[1], three)
        columns = hidden.get()[pl.ds(pl.multiple_of(block * j, block), block), :]
        grads[j, :, 0:three] = nn(columns, lows).astype(BF16)
        for p in range(block // owned):
            grads[j, owned * p : owned * (p + 1), three : three + pair] = row_grad[
                j, :, pair * p : pair * (p + 1)
            ]

    def rounds(outer, inner):
        for here, i in ((ends, outer), (jnp.logical_not(ends), inner)):
            if 0 <= i < planes - 1:
                @pl.when(here)
                def _():
                    for fold in folds:
                        fold.round(i)

    rows.start(met)
    for copy in misc_copies:
        copy.start()
    project(0)
    rounds(0, -1)
    rows.prepare()
    for i in range(1, planes):
        project(i)
    rounds(1, -1)
    rows.run()
    rounds(2, 0)
    deals = exchange_start(plane, mine, feed_grad, feed_out, deal_sends.at[0], deal_receives.at[0])
    for copy in misc_copies:
        copy.wait()
    total = misc_all[0]
    for i in range(1, planes):
        total = total + misc_all[i]
    misc_out[mine] = total
    misc_copies = [
        remote(misc_out.at[mine], misc_out.at[mine], misc_sends.at[1, d], misc_receives.at[1, d], (plane, peer(d)))
        for d in range(1, 8)
    ]
    for copy in misc_copies:
        copy.start()
    grad, gain_part = back_through_norm(rows.total(), tokens.get()[...].astype(F32), gains[0:1, :])
    small_plane[mine] = jnp.zeros(small_plane.shape[1:], F32)
    small_plane[mine, 0:1, :] = gain_part
    small_plane[mine, 1:2, :] = second_grad[...]
    near_copies = [
        remote(small_plane.at[mine], small_plane.at[mine], small_sends.at[0, d], small_receives.at[0, d], (plane, peer(d)))
        for d in range(1, 8)
    ]
    for copy in near_copies:
        copy.start()
    input_grad[...] = (residual_grad.get()[...] + grad).astype(BF16)
    rounds(-1, 1)
    for copy in near_copies:
        copy.wait()
    total = small_plane[0]
    for i in range(1, 8):
        total = total + small_plane[i]
    small_all[plane] = total
    far_copies = [
        remote(small_all.at[plane], small_all.at[plane], small_sends.at[1, d], small_receives.at[1, d], ((plane + d) % planes, mine))
        for d in range(1, planes)
    ]
    for copy in far_copies:
        copy.start()
    rounds(-1, 2)
    for k, fold in enumerate(folds):
        def store(value, k=k):
            count = value.shape[0] // owned
            for p in range(count):
                piece = value[owned * p : owned * (p + 1), :]
                qkv_sum[count * k + p] = piece[:, 0:three]
                at = pair * (count * k + p)
                out_w_out[0, :, at : at + pair] = piece[:, three : three + pair]

        fold.total(store)
    keep_qkv = pltpu.make_async_copy(qkv_sum.at[mine], qkv_out.at[mine], local.at[2])
    keep_qkv.start()
    deals += exchange_start(plane, mine, qkv_sum, qkv_out, deal_sends.at[1], deal_receives.at[1])
    rows.finish()
    for copy in far_copies:
        copy.wait()
    total = small_all[0]
    for i in range(1, planes):
        total = total + small_all[i]
    small_out[...] = total
    for copy in deals + misc_copies:
        copy.wait()
    keep_feed.wait()
    keep_qkv.wait()
    for fold in folds:
        fold.finish()


def finish_kernel(count, place, small, misc, *refs):
    ins, outs = refs[:6], refs[6 : 6 + count]
    norm_out, group_out, second_out, ker_out, mix_out = refs[6 + count : 11 + count]
    near, made = refs[11 + count : 17 + count], refs[17 + count : 17 + 2 * count - 2]
    loads, stores = refs[-2:]
    moves = [pltpu.make_async_copy(ins[i], near[i], loads.at[i]) for i in range(6)]
    for move in moves:
        move.start()
    qkv, feed, out_w, down, grad, layer = near
    groups, owned, three = qkv.shape
    pair = three // 3
    half = feed.shape[2] // 2
    results = list(made) + [grad, layer]
    out = [pltpu.make_async_copy(results[i], outs[i], stores.at[i]) for i in range(count)]
    moves[3].wait()
    made[6][...] = down[...].astype(F32)
    out[6].start()
    moves[2].wait()
    made[5][...] = out_w[0].astype(F32)
    out[5].start()
    for i in (4, 5):
        moves[i].wait()
        out[i + 3].start()
    moves[1].wait()
    for i in range(2):
        for c in range(groups):
            for s in range(half // TILE):
                at = TILE * (groups * s + c)
                made[3 + i][:, at : at + TILE] = feed[
                    c, :, half * i + TILE * s : half * i + TILE * (s + 1)
                ].astype(F32)
        out[3 + i].start()
    moves[0].wait()
    for i in range(3):
        for c in range(groups):
            made[i][:, pair * c : pair * (c + 1)] = qkv[c, :, pair * i : pair * (i + 1)].astype(F32)
        out[i].start()
    flat = place[0]
    width = small.shape[1]
    turned = pltpu.roll(small[...], (width - owned * flat) % width, 1)
    norm_out[...] = turned[0:1, 0:owned]
    second_out[...] = turned[1:2, 0:owned]
    rows = misc[flat // 4]
    wide = rows.shape[1]
    turned = pltpu.roll(rows, (wide - owned * (flat % 4)) % wide, 1)
    group_out[...] = turned[16:17, 0:owned]
    heads = [(c, h) for c in range(groups) for h in range(2)]
    for a in range(ker_out.shape[1]):
        rows = jnp.concatenate([misc[c, 8 * h + a : 8 * h + a + 1, 0:TILE] for c, h in heads], axis=0)
        ker_out[:, a, :] = rows.T[0 : ker_out.shape[0], :]
    for p in range(2):
        sums = [
            jnp.sum(misc[c, 17 + p : 18 + p, pair // 2 * h : pair // 2 * (h + 1)], axis=1, keepdims=True)
            for c, h in heads
        ]
        mix_out[p : p + 1, :] = jnp.broadcast_to(jnp.concatenate(sums, axis=0), (len(heads), TILE)).T[0:1, :]
    for copy in out:
        copy.wait()


DMA = pltpu.SemaphoreType.DMA
ANYWHERE = pl.BlockSpec(memory_space=pl.ANY)
ON_CHIP = pl.BlockSpec(memory_space=pltpu.VMEM)


def communicate(kernel, name, number, micros, outs, scratch, args, spec, specs=None, out_specs=None):
    return pl.pallas_call(
        kernel,
        name=name,
        out_shape=tuple(jax.ShapeDtypeStruct(shape, kind) for shape, kind in outs),
        in_specs=specs or [spec] * len(args),
        out_specs=out_specs or (spec,) * len(outs),
        scratch_shapes=scratch,
        compiler_params=pltpu.CompilerParams(
            collective_id=number, has_side_effects=True, vmem_limit_bytes=56 << 20
        ),
        cost_estimate=pl.CostEstimate(flops=0, transcendentals=0, bytes_accessed=micros * 3500000),
    )(*args)


def sum_scratch(rows, width):
    return [
        pltpu.VMEM((4, rows, width), BF16),
        pltpu.VMEM((4, rows, width), F32),
        pltpu.VMEM((4, rows, width), BF16),
        pltpu.VMEM((4, rows, width), BF16),
        pltpu.VMEM((2, rows, width), BF16),
        pltpu.VMEM((2, rows // 2, width), BF16),
        DMA((10,)),
        DMA((10,)),
    ]


PRECISE = lax.Precision.HIGHEST


def normalize(values):
    factor = lax.rsqrt(jnp.mean(values * values, axis=-1, keepdims=True) + EPSILON)
    return (values * factor, factor)


def normalize_back(normed, factor, gain, upstream):
    gain_grad = jnp.sum(upstream * normed, axis=0)
    scaled = upstream * gain
    return (
        factor * (scaled - normed * jnp.mean(scaled * normed, axis=-1, keepdims=True)),
        gain_grad,
    )


def add_rows(target, update, offset):
    current = lax.dynamic_slice_in_dim(target, offset, update.shape[0], 0)
    return lax.dynamic_update_slice_in_dim(target, current + update, offset, 0)


def masked_scores(query_ext, key_pad, offset, row_pos, layout):
    block_rows, halo_rows, key_reach, key_block, groups, score_scale = layout
    extent = key_block + 4 * key_reach
    key_slab = lax.dynamic_slice_in_dim(key_pad, offset, extent, 0)
    raw_scores = (
        jnp.einsum("nrhd,khd->nhrk", query_ext, key_slab, preferred_element_type=jnp.float32)
        * score_scale
    )
    key_pos = offset - 2 * key_reach + jnp.arange(extent, dtype=jnp.int32)
    keep_mask = (key_pos[None, None, :] <= row_pos[:, :, None]) & (key_pos >= 0)[None, None, :]
    return jnp.where(keep_mask[:, None], raw_scores, 0.0)


def convolve(zeroed, kernel, shift, extent, layout):
    block_rows, halo_rows, key_reach = (layout[0], layout[1], layout[2])
    result = jnp.zeros(zeroed.shape[:2] + (block_rows, extent), jnp.float32)
    for row_tap in range(halo_rows + 1):
        for key_tap in range(2 * key_reach + 1):
            column = shift + 3 * key_reach - key_tap
            result = (
                result
                + kernel[:, row_tap, key_tap][None, :, None, None]
                * zeroed[
                    :,
                    :,
                    halo_rows - row_tap : halo_rows - row_tap + block_rows,
                    column : column + extent,
                ]
            )
    return result


def attend_forward(query_ext, row_pos, key_pad, value_pad, kernel, layout):
    block_rows, halo_rows, key_reach, key_block, groups, score_scale = layout
    members = query_ext.shape[0]
    head_count = query_ext.shape[2]
    pair_width = value_pad.shape[1] // groups
    block_count = jnp.max(row_pos) // key_block + 1

    def advance(position, carried):
        running_max, running_sum, gathered = carried
        offset = position * key_block
        zeroed = masked_scores(query_ext, key_pad, offset, row_pos, layout)
        logits = convolve(zeroed, kernel, 0, key_block, layout)
        key_pos = offset + jnp.arange(key_block, dtype=jnp.int32)
        valid_mask = key_pos[None, None, :] <= row_pos[:, halo_rows:, None]
        logits = jnp.where(valid_mask[:, None], logits, NEGATIVE)
        new_max = jnp.maximum(running_max, jnp.max(logits, axis=-1))
        shrink = jnp.exp(running_max - new_max)
        weights = jnp.exp(logits - new_max[..., None])
        running_sum = running_sum * shrink + jnp.sum(weights, axis=-1)
        value_slab = lax.dynamic_slice_in_dim(
            value_pad, offset + 2 * key_reach, key_block, 0
        ).reshape(key_block, groups, pair_width)
        low_weights = weights.astype(jnp.bfloat16).reshape(
            members, groups, 2, block_rows, key_block
        )
        gathered = gathered * shrink.reshape(members, groups, 2, block_rows, 1) + jnp.einsum(
            "ngpik,kgc->ngpic", low_weights, value_slab, preferred_element_type=jnp.float32
        )
        return (new_max, running_sum, gathered)

    initial = (
        jnp.full((members, head_count, block_rows), NEGATIVE, jnp.float32),
        jnp.zeros((members, head_count, block_rows), jnp.float32),
        jnp.zeros((members, groups, 2, block_rows, pair_width), jnp.float32),
    )
    running_max, running_sum, gathered = lax.fori_loop(0, block_count, advance, initial)
    mixed_in = gathered / running_sum.reshape(members, groups, 2, block_rows, 1)
    return (mixed_in, running_max + jnp.log(running_sum))


def attend_backward(
    query_ext,
    row_pos,
    key_pad,
    value_pad,
    kernel,
    log_total,
    mixed_low,
    delta_rows,
    key_acc,
    value_acc,
    layout,
):
    block_rows, halo_rows, key_reach, key_block, groups, score_scale = layout
    members = query_ext.shape[0]
    ext_rows = query_ext.shape[1]
    head_count = query_ext.shape[2]
    model_width = value_pad.shape[1]
    pair_width = model_width // groups
    extent = key_block + 2 * key_reach
    block_count = jnp.max(row_pos) // key_block + 1

    def advance(position, carried):
        query_grad, key_acc, value_acc, kernel_grad = carried
        offset = position * key_block
        zeroed = masked_scores(query_ext, key_pad, offset, row_pos, layout)
        logits = convolve(zeroed, kernel, -key_reach, extent, layout)
        key_pos = offset - key_reach + jnp.arange(extent, dtype=jnp.int32)
        valid_mask = (key_pos[None, None, :] <= row_pos[:, halo_rows:, None]) & (key_pos >= 0)[
            None, None, :
        ]
        probability = jnp.where(valid_mask[:, None], jnp.exp(logits - log_total[..., None]), 0.0)
        value_slab = lax.dynamic_slice_in_dim(value_pad, offset + key_reach, extent, 0).reshape(
            extent, groups, pair_width
        )
        prob_grad = jnp.einsum(
            "ngpic,kgc->ngpik", mixed_low, value_slab, preferred_element_type=jnp.float32
        ).reshape(members, head_count, block_rows, extent)
        logit_grad = probability * (prob_grad - delta_rows[..., None])
        central = (
            probability[..., key_reach : key_reach + key_block]
            .astype(jnp.bfloat16)
            .reshape(members, groups, 2, block_rows, key_block)
        )
        value_part = jnp.einsum(
            "ngpik,ngpic->kgc", central, mixed_low, preferred_element_type=jnp.float32
        ).reshape(key_block, model_width)
        value_acc = add_rows(value_acc, value_part, offset)
        middle = logit_grad[..., key_reach : key_reach + key_block]
        tap_sums = []
        for row_tap in range(halo_rows + 1):
            for key_tap in range(2 * key_reach + 1):
                column = 3 * key_reach - key_tap
                tap_sums.append(
                    jnp.sum(
                        middle
                        * zeroed[
                            :,
                            :,
                            halo_rows - row_tap : halo_rows - row_tap + block_rows,
                            column : column + key_block,
                        ],
                        axis=(0, 2, 3),
                    )
                )
        kernel_grad = kernel_grad + jnp.stack(tap_sums, axis=1).reshape(
            head_count, halo_rows + 1, 2 * key_reach + 1
        )
        padded = jnp.pad(logit_grad, ((0, 0), (0, 0), (halo_rows, halo_rows), (0, 0)))
        score_grad = jnp.zeros((members, head_count, ext_rows, key_block), jnp.float32)
        for row_tap in range(halo_rows + 1):
            for key_tap in range(2 * key_reach + 1):
                score_grad = (
                    score_grad
                    + kernel[:, row_tap, key_tap][None, :, None, None]
                    * padded[:, :, row_tap : row_tap + ext_rows, key_tap : key_tap + key_block]
                )
        key_central = offset + jnp.arange(key_block, dtype=jnp.int32)
        keep_mask = (key_central[None, None, :] <= row_pos[:, :, None]) & (key_central >= 0)[
            None, None, :
        ]
        score_low = jnp.where(keep_mask[:, None], score_grad, 0.0).astype(jnp.bfloat16)
        key_slab = lax.dynamic_slice_in_dim(key_pad, offset + 2 * key_reach, key_block, 0)
        query_grad = (
            query_grad
            + jnp.einsum("nhrk,khd->nrhd", score_low, key_slab, preferred_element_type=jnp.float32)
            * score_scale
        )
        key_part = (
            jnp.einsum(
                "nhrk,nrhd->khd", score_low, query_ext, preferred_element_type=jnp.float32
            ).reshape(key_block, model_width)
            * score_scale
        )
        key_acc = add_rows(key_acc, key_part, offset)
        return (query_grad, key_acc, value_acc, kernel_grad)

    initial = (
        jnp.zeros(query_ext.shape, jnp.float32),
        key_acc,
        value_acc,
        jnp.zeros(kernel.shape, jnp.float32),
    )
    return lax.fori_loop(0, block_count, advance, initial)


def reorder(selection, rows):
    return jnp.dot(
        selection.astype(rows.dtype), rows, precision=PRECISE, preferred_element_type=jnp.float32
    ).astype(rows.dtype)


def pick(table, places):
    return jnp.stack(
        [lax.dynamic_index_in_dim(table, places[i], 0, keepdims=False) for i in range(2)]
    )


def accumulate(previous, update):
    return (
        update
        if previous is None
        else tuple((left + right for left, right in zip(previous, update)))
    )


def general_device(
    inputs,
    out_grad,
    pair_index,
    norm_gain,
    query_weight,
    key_weight,
    value_weight,
    score_kernel,
    head_mixing,
    group_gain,
    output_weight,
    second_gain,
    gate_weight,
    up_weight,
    down_weight,
):
    micro_count = inputs.shape[0]
    local_rows = inputs.shape[2]
    block_rows = local_rows // 2
    model_width = inputs.shape[3]
    head_count = score_kernel.shape[0]
    head_dim = model_width // head_count
    groups = head_count // 2
    halo_rows = score_kernel.shape[1] - 1
    key_reach = (score_kernel.shape[2] - 1) // 2
    block_count = 2 * lax.axis_size("ctx")
    seq_length = block_count * block_rows
    key_block = min(512, seq_length)
    layout = (block_rows, halo_rows, key_reach, key_block, groups, head_dim ** (-0.5))
    extended = block_rows + halo_rows
    my_index = lax.axis_index("ctx")
    slot_ids = jnp.arange(block_count, dtype=jnp.int32)
    mix_table = head_mixing.reshape(groups, 2, 2)
    pad_width = ((2 * key_reach, 2 * key_reach), (0, 0))
    layer_rows = []
    input_rows = []
    feed_sums = None
    attention_sums = None
    kernel_total = jnp.zeros(score_kernel.shape, jnp.float32)
    mixing_total = jnp.zeros(head_mixing.shape, jnp.float32)
    for batch_index in range(micro_count):
        gain_first, query_full, key_full, value_full, gain_group, out_full = (
            lax.all_gather(norm_gain, ("seq", "ctx"), axis=0, tiled=True),
            lax.all_gather(query_weight, ("seq", "ctx"), axis=0, tiled=True),
            lax.all_gather(key_weight, ("seq", "ctx"), axis=0, tiled=True),
            lax.all_gather(value_weight, ("seq", "ctx"), axis=0, tiled=True),
            lax.all_gather(group_gain, ("seq", "ctx"), axis=0, tiled=True),
            lax.all_gather(output_weight, ("seq", "ctx"), axis=0, tiled=True),
        )
        tokens = inputs[batch_index, 0].astype(jnp.float32)
        normed_first, factor_first = normalize(tokens)
        hidden = (normed_first * gain_first.astype(jnp.float32)).astype(jnp.bfloat16)
        query_proj = jnp.dot(hidden, query_full, preferred_element_type=jnp.float32).astype(
            jnp.bfloat16
        )
        key_proj = jnp.dot(hidden, key_full, preferred_element_type=jnp.float32).astype(
            jnp.bfloat16
        )
        value_proj = jnp.dot(hidden, value_full, preferred_element_type=jnp.float32).astype(
            jnp.bfloat16
        )
        tail_rows = jnp.concatenate(
            [query_proj[block_rows - halo_rows : block_rows], query_proj[local_rows - halo_rows :]],
            axis=0,
        )
        key_dealt, value_dealt, tail_dealt = (
            lax.all_gather(key_proj, "ctx", axis=0, tiled=True),
            lax.all_gather(value_proj, "ctx", axis=0, tiled=True),
            lax.all_gather(tail_rows, "ctx", axis=0, tiled=True),
        )
        pairs_row = pair_index[batch_index]
        owner_pair = jnp.repeat(pairs_row, 2)
        block_of_slot = jnp.where(slot_ids % 2 == 0, owner_pair, block_count - 1 - owner_pair)
        to_natural = (block_of_slot[None, :] == slot_ids[:, None]).astype(jnp.float32)
        slot_of_block = jnp.sum(
            jnp.where(block_of_slot[None, :] == slot_ids[:, None], slot_ids[None, :], 0), axis=1
        )
        my_pair = lax.dynamic_index_in_dim(pairs_row, my_index, 0, keepdims=False)
        my_blocks = jnp.stack([my_pair, block_count - 1 - my_pair])
        key_pad = jnp.pad(
            reorder(to_natural, key_dealt.reshape(block_count, -1)).reshape(
                seq_length, model_width
            ),
            pad_width,
        ).reshape(-1, head_count, head_dim)
        value_pad = jnp.pad(
            reorder(to_natural, value_dealt.reshape(block_count, -1)).reshape(
                seq_length, model_width
            ),
            pad_width,
        )
        tail_blocks = reorder(to_natural, tail_dealt.reshape(block_count, -1)).reshape(
            block_count, halo_rows, model_width
        )
        previous = jnp.concatenate(
            [jnp.zeros((1, halo_rows, model_width), jnp.bfloat16), tail_blocks[:-1]], axis=0
        )
        query_ext = jnp.concatenate(
            [pick(previous, my_blocks), query_proj.reshape(2, block_rows, model_width)], axis=1
        ).reshape(2, extended, head_count, head_dim)
        row_pos = (
            my_blocks[:, None] * block_rows
            - halo_rows
            + jnp.arange(extended, dtype=jnp.int32)[None, :]
        )
        mixed_in, log_total = attend_forward(
            query_ext, row_pos, key_pad, value_pad, score_kernel, layout
        )
        mixed_six = mixed_in.reshape(2, groups, 2, block_rows, 2, head_dim)
        heads_out = jnp.einsum(
            "gqp,ngpiqd->nigqd", mix_table, mixed_six, precision=PRECISE
        ).reshape(local_rows, head_count, head_dim)
        group_normed, group_factor = normalize(heads_out)
        normed_low = (
            group_normed.reshape(local_rows, model_width) * gain_group.astype(jnp.float32)
        ).astype(jnp.bfloat16)
        residual = tokens + jnp.dot(normed_low, out_full, preferred_element_type=jnp.float32)
        gain_second, gate_full, up_full, down_full = (
            lax.all_gather(second_gain, ("seq", "ctx"), axis=0, tiled=True),
            lax.all_gather(gate_weight, ("seq", "ctx"), axis=0, tiled=True),
            lax.all_gather(up_weight, ("seq", "ctx"), axis=0, tiled=True),
            lax.all_gather(down_weight, ("seq", "ctx"), axis=0, tiled=True),
        )
        normed_second, factor_second = normalize(residual)
        second_hidden = (normed_second * gain_second.astype(jnp.float32)).astype(jnp.bfloat16)
        gate_proj = jnp.dot(second_hidden, gate_full, preferred_element_type=jnp.float32)
        up_proj = jnp.dot(second_hidden, up_full, preferred_element_type=jnp.float32)
        activated = (jax.nn.silu(gate_proj) * up_proj).astype(jnp.bfloat16)
        layer_rows.append(
            (residual + jnp.dot(activated, down_full, preferred_element_type=jnp.float32)).astype(
                jnp.bfloat16
            )
        )
        gain_second, gate_full, up_full, down_full = (
            lax.all_gather(second_gain, ("seq", "ctx"), axis=0, tiled=True),
            lax.all_gather(gate_weight, ("seq", "ctx"), axis=0, tiled=True),
            lax.all_gather(up_weight, ("seq", "ctx"), axis=0, tiled=True),
            lax.all_gather(down_weight, ("seq", "ctx"), axis=0, tiled=True),
        )
        grad_rows = out_grad[batch_index, 0]
        hid_grad = jnp.dot(grad_rows, down_full.T, preferred_element_type=jnp.float32)
        down_grad = jnp.dot(activated.T, grad_rows, preferred_element_type=jnp.float32)
        sigmoid_gate = jax.nn.sigmoid(gate_proj)
        up_low = (hid_grad * gate_proj * sigmoid_gate).astype(jnp.bfloat16)
        gate_low = (
            hid_grad * up_proj * sigmoid_gate * (1.0 + gate_proj * (1.0 - sigmoid_gate))
        ).astype(jnp.bfloat16)
        second_grad = jnp.dot(gate_low, gate_full.T, preferred_element_type=jnp.float32) + jnp.dot(
            up_low, up_full.T, preferred_element_type=jnp.float32
        )
        gate_grad = jnp.dot(second_hidden.T, gate_low, preferred_element_type=jnp.float32)
        up_grad = jnp.dot(second_hidden.T, up_low, preferred_element_type=jnp.float32)
        residual_part, gain_second_grad = normalize_back(
            normed_second, factor_second, gain_second.astype(jnp.float32), second_grad
        )
        residual_grad = grad_rows.astype(jnp.float32) + residual_part
        feed_shards = (
            lax.psum_scatter(gain_second_grad, ("seq", "ctx"), scatter_dimension=0, tiled=True),
            lax.psum_scatter(gate_grad, ("seq", "ctx"), scatter_dimension=0, tiled=True),
            lax.psum_scatter(up_grad, ("seq", "ctx"), scatter_dimension=0, tiled=True),
            lax.psum_scatter(down_grad, ("seq", "ctx"), scatter_dimension=0, tiled=True),
        )
        feed_sums = accumulate(feed_sums, feed_shards)
        gain_first, query_full, key_full, value_full, gain_group, out_full = (
            lax.all_gather(norm_gain, ("seq", "ctx"), axis=0, tiled=True),
            lax.all_gather(query_weight, ("seq", "ctx"), axis=0, tiled=True),
            lax.all_gather(key_weight, ("seq", "ctx"), axis=0, tiled=True),
            lax.all_gather(value_weight, ("seq", "ctx"), axis=0, tiled=True),
            lax.all_gather(group_gain, ("seq", "ctx"), axis=0, tiled=True),
            lax.all_gather(output_weight, ("seq", "ctx"), axis=0, tiled=True),
        )
        attended_low = residual_grad.astype(jnp.bfloat16)
        out_weight_grad = jnp.dot(normed_low.T, attended_low, preferred_element_type=jnp.float32)
        normed_grad = jnp.dot(attended_low, out_full.T, preferred_element_type=jnp.float32)
        heads_grad, gain_group_grad = normalize_back(
            group_normed,
            group_factor,
            gain_group.astype(jnp.float32).reshape(head_count, head_dim),
            normed_grad.reshape(local_rows, head_count, head_dim),
        )
        heads_five = heads_grad.reshape(2, block_rows, groups, 2, head_dim)
        mixing_total = mixing_total + jnp.einsum(
            "nigqd,ngpiqd->gqp", heads_five, mixed_six, precision=PRECISE
        ).reshape(head_count, 2)
        mixed_grad = jnp.einsum(
            "gqp,nigqd->ngpiqd", mix_table, heads_five, precision=PRECISE
        ).reshape(2, groups, 2, block_rows, 2 * head_dim)
        mixed_low = mixed_grad.astype(jnp.bfloat16)
        delta_rows = jnp.sum(mixed_low.astype(jnp.float32) * mixed_in, axis=-1).reshape(
            2, head_count, block_rows
        )
        key_acc = jnp.zeros((seq_length, model_width), jnp.float32)
        value_acc = jnp.zeros((seq_length, model_width), jnp.float32)
        query_grad, key_acc, value_acc, kernel_part = attend_backward(
            query_ext,
            row_pos,
            key_pad,
            value_pad,
            score_kernel,
            log_total,
            mixed_low,
            delta_rows,
            key_acc,
            value_acc,
            layout,
        )
        kernel_total = kernel_total + kernel_part
        halo_grad = query_grad[:, :halo_rows].reshape(2, halo_rows, model_width)
        own_grad = query_grad[:, halo_rows:].reshape(2, block_rows, model_width)
        target_slot = pick(slot_of_block, jnp.maximum(my_blocks - 1, 0))
        routing = ((slot_ids[None, :] == target_slot[:, None]) & (my_blocks > 0)[:, None]).astype(
            jnp.float32
        )
        tail_grad = jnp.einsum("ws,wrc->src", routing, halo_grad, precision=PRECISE).reshape(
            block_count * halo_rows, model_width
        )
        key_back = reorder(to_natural.T, key_acc.reshape(block_count, -1)).reshape(
            seq_length, model_width
        )
        value_back = reorder(to_natural.T, value_acc.reshape(block_count, -1)).reshape(
            seq_length, model_width
        )
        key_mine, value_mine, tail_mine = (
            lax.psum_scatter(
                key_back.astype(jnp.bfloat16), "ctx", scatter_dimension=0, tiled=True
            ).astype(jnp.float32),
            lax.psum_scatter(
                value_back.astype(jnp.bfloat16), "ctx", scatter_dimension=0, tiled=True
            ).astype(jnp.float32),
            lax.psum_scatter(
                tail_grad.astype(jnp.bfloat16), "ctx", scatter_dimension=0, tiled=True
            ).astype(jnp.float32),
        )
        tail_mine = tail_mine.reshape(2, halo_rows, model_width)
        query_total = jnp.concatenate(
            [
                own_grad[:, : block_rows - halo_rows],
                own_grad[:, block_rows - halo_rows :] + tail_mine,
            ],
            axis=1,
        ).reshape(local_rows, model_width)
        query_low = query_total.astype(jnp.bfloat16)
        key_low = key_mine.astype(jnp.bfloat16)
        value_low = value_mine.astype(jnp.bfloat16)
        query_w_grad = jnp.dot(hidden.T, query_low, preferred_element_type=jnp.float32)
        key_w_grad = jnp.dot(hidden.T, key_low, preferred_element_type=jnp.float32)
        value_w_grad = jnp.dot(hidden.T, value_low, preferred_element_type=jnp.float32)
        hidden_grad = (
            jnp.dot(query_low, query_full.T, preferred_element_type=jnp.float32)
            + jnp.dot(key_low, key_full.T, preferred_element_type=jnp.float32)
            + jnp.dot(value_low, value_full.T, preferred_element_type=jnp.float32)
        )
        token_part, gain_first_grad = normalize_back(
            normed_first, factor_first, gain_first.astype(jnp.float32), hidden_grad
        )
        input_rows.append((residual_grad + token_part).astype(jnp.bfloat16))
        attention_shards = (
            lax.psum_scatter(gain_first_grad, ("seq", "ctx"), scatter_dimension=0, tiled=True),
            lax.psum_scatter(query_w_grad, ("seq", "ctx"), scatter_dimension=0, tiled=True),
            lax.psum_scatter(key_w_grad, ("seq", "ctx"), scatter_dimension=0, tiled=True),
            lax.psum_scatter(value_w_grad, ("seq", "ctx"), scatter_dimension=0, tiled=True),
            lax.psum_scatter(
                gain_group_grad.reshape(model_width),
                ("seq", "ctx"),
                scatter_dimension=0,
                tiled=True,
            ),
            lax.psum_scatter(out_weight_grad, ("seq", "ctx"), scatter_dimension=0, tiled=True),
        )
        attention_sums = accumulate(attention_sums, attention_shards)
    kernel_sum, mixing_sum = lax.psum((kernel_total, mixing_total), ("seq", "ctx"))
    layer_out = jnp.stack(layer_rows)[:, None]
    input_grad = jnp.stack(input_rows)[:, None]
    return (
        layer_out,
        input_grad,
        attention_sums[0],
        attention_sums[1],
        attention_sums[2],
        attention_sums[3],
        kernel_sum,
        mixing_sum,
        attention_sums[4],
        attention_sums[5],
        feed_sums[0],
        feed_sums[1],
        feed_sums[2],
        feed_sums[3],
    )


def on_device(
    inputs,
    out_grad,
    pair_index,
    norm_gain,
    query_weight,
    key_weight,
    value_weight,
    score_kernel,
    head_mixing,
    group_gain,
    output_weight,
    second_gain,
    gate_weight,
    up_weight,
    down_weight,
):
    groups, planes = lax.axis_size("ctx"), lax.axis_size("seq")
    heads, width = score_kernel.shape[0], inputs.shape[3]
    if groups != 8 or heads != 2 * groups or (groups * inputs.shape[2]) % TILE:
        return general_device(
            inputs, out_grad, pair_index, norm_gain, query_weight, key_weight, value_weight,
            score_kernel, head_mixing, group_gain, output_weight, second_gain, gate_weight,
            up_weight, down_weight,
        )
    micro, local = inputs.shape[0], inputs.shape[2]
    blk, seq = local // 2, local * groups
    blocks = seq // blk
    pair = width // groups
    owned = width // (groups * planes)
    hidden = gate_weight.shape[1]
    chunk = hidden // (groups * planes)
    me = lax.axis_index("ctx")
    tokens_low = inputs.reshape(micro * local, width)
    grads_low = out_grad.reshape(micro * local, width)

    rows_all = micro * local
    qkv_shape = (groups, owned, 3 * pair)
    feed_shape = (groups, owned, 2 * planes * chunk)
    gain_rows = jnp.stack([norm_gain, group_gain, second_gain])
    spread_sems = [DMA((9,))] * 2
    feed_mine, qkv, gains, all_tokens, out_rows = communicate(
        functools.partial(enter_kernel, planes), "enter", 1, 50,
        [
            (feed_shape, BF16),
            ((planes,) + qkv_shape, BF16),
            ((planes, groups, 8, TILE), F32),
            ((groups, rows_all, width), BF16),
            ((planes, owned, width), BF16),
        ],
        [pltpu.VMEM((owned, width), BF16)] * 3 + [pltpu.VMEM((owned, hidden), BF16)] * 2
        + [pltpu.VMEM((3, owned), BF16), pltpu.VMEM((8, TILE), F32)]
        + [pltpu.VMEM(qkv_shape, BF16), pltpu.VMEM(feed_shape, BF16)]
        + [DMA((3, groups))] * 2 + spread_sems + [DMA((1, 2, planes))] * 2
        + [DMA((2, 2, planes))] * 2 + [DMA((11,))],
        (
            query_weight, key_weight, value_weight, gate_weight, up_weight, gain_rows, tokens_low,
            output_weight,
        ),
        ANYWHERE,
    )
    all_tokens, down_mine = lax.optimization_barrier((all_tokens, down_weight))
    feed = lax.all_gather(feed_mine.reshape(groups * owned, -1), "seq", axis=0, tiled=True)
    down = lax.all_gather(down_mine, "seq", axis=0, tiled=True)
    qkv = qkv.reshape(width, 3 * pair)
    hidden_all, heads_in, gains, gain_pair, out_rows, all_grads = communicate(
        functools.partial(heads_kernel, planes), "heads", 2, 20,
        [
            ((width, groups * rows_all), BF16),
            ((groups * rows_all, 3 * pair), BF16),
            ((8, width), F32),
            ((8, pair), F32),
            ((4, owned, width), BF16),
            ((groups, rows_all, width), BF16),
        ],
        [
            pltpu.VMEM((groups, rows_all, width), BF16),
            pltpu.VMEM((width, 3 * pair), BF16),
            pltpu.VMEM((width, groups * rows_all), BF16),
            pltpu.VMEM((groups * rows_all, 3 * pair), BF16),
        ]
        + [DMA((4,))] * 2 + spread_sems + [DMA((groups + 1,)), DMA((2, groups)), DMA((2,))],
        (all_tokens, qkv, gains, out_rows, grads_low),
        None, [ANYWHERE] * 2 + [ON_CHIP] + [ANYWHERE] * 2, (ANYWHERE,) * 2 + (ON_CHIP,) * 2 + (ANYWHERE,) * 2,
    )
    all_grads = all_grads.reshape(-1, width)
    out_rows = out_rows.reshape(pair, width)

    slots = jnp.arange(blocks, dtype=jnp.int32)
    owner = jnp.repeat(pair_index, 2, axis=1)
    block_of_slot = jnp.where(slots % 2 == 0, owner, blocks - 1 - owner)
    place = (
        (slots // 2)[None] * (2 * micro)
        + 2 * jnp.arange(micro, dtype=jnp.int32)[:, None]
        + (slots % 2)[None]
    )
    blk_table = jnp.sum(
        jnp.where(block_of_slot[:, None, :] == slots[None, :, None], place[:, None, :], 0), axis=2
    ).astype(jnp.int32)
    ker = lax.dynamic_slice_in_dim(score_kernel, 2 * me, 2, 0)
    mix = jnp.repeat(lax.dynamic_slice_in_dim(head_mixing, 2 * me, 2, 0), pair // 2, axis=0).T
    scale = (width // heads) ** (-0.5)

    mixed, y, prob = pair_forward(blk_table, ker, mix, gain_pair, heads_in, micro, seq, blk, scale)
    by_core = (groups // 2, 2, rows_all)
    sum_spec = sum_scratch(rows_all, width)
    residual, second_all = communicate(
        second_kernel, "second", 3, 40,
        [((rows_all, width), F32), ((groups, rows_all, width), BF16)],
        [
            pltpu.VMEM(by_core + (pair,), BF16),
            pltpu.VMEM((pair, width), BF16),
            pltpu.VMEM((rows_all, width), BF16),
            pltpu.VMEM((rows_all, width), F32),
            pltpu.VMEM((rows_all, width), BF16),
            DMA((5,)),
        ]
        + sum_spec + spread_sems,
        (mixed.reshape(by_core + (pair,)), out_rows, tokens_low, gains),
        None, [ANYWHERE] * 3 + [ON_CHIP], (ANYWHERE,) * 2,
    )
    second_all = second_all.reshape(-1, width)

    half = planes * chunk
    both = jnp.dot(second_all, feed, preferred_element_type=F32)
    gate, up = both[:, :half], both[:, half:]
    sigmoid = jax.nn.sigmoid(gate)
    active = (gate * sigmoid * up).astype(BF16)
    slopes = jnp.concatenate(
        [up * sigmoid * (1.0 + gate * (1.0 - sigmoid)), gate * sigmoid], axis=1
    )
    down_grad = lax.dot_general(active, all_grads, (((0,), (0,)), ((), ())), preferred_element_type=F32)
    all_grads, down_grad, slopes = lax.optimization_barrier((all_grads, down_grad.astype(BF16), slopes))
    hid_grad = lax.dot_general(all_grads, down, (((1,), (1,)), ((), ())), preferred_element_type=F32)
    lows = (jnp.concatenate([hid_grad, hid_grad], axis=1) * slopes).astype(BF16)
    feed_grad = lax.dot_general(second_all, lows, (((0,), (0,)), ((), ())), preferred_element_type=F32)
    lows, feed_grad = lax.optimization_barrier((lows, feed_grad.astype(BF16)))
    feed_sum = lax.psum_scatter(feed_grad, "seq", scatter_dimension=0, tiled=True)
    down_sum = lax.psum_scatter(down_grad, "seq", scatter_dimension=0, tiled=True)
    residual_grad, gain_second_grad, mixed_grad, out_w_grad = communicate(
        back_kernel, "back", 4, 42,
        [
            ((rows_all, width), F32),
            ((1, width), F32),
            ((groups, rows_all, pair), BF16),
            ((pair, width), BF16),
        ],
        [
            pltpu.VMEM(by_core + (2 * half,), BF16),
            pltpu.VMEM((width, 2 * half), BF16),
            pltpu.VMEM((rows_all, width), F32),
            pltpu.VMEM((rows_all, width), BF16),
            pltpu.VMEM((pair, width), BF16),
            pltpu.VMEM((groups, rows_all, pair), BF16),
            pltpu.VMEM((rows_all, width), F32),
            pltpu.VMEM((groups, rows_all, width), BF16),
            pltpu.VMEM((pair, width), F32),
            DMA((7,)),
        ]
        + sum_spec + spread_sems,
        (
            lows.reshape(by_core + (2 * half,)), feed, residual, grads_low, out_rows,
            mixed.reshape(groups, rows_all, pair), gains,
        ),
        None, [ANYWHERE] * 6 + [ON_CHIP], (ANYWHERE, ON_CHIP, ON_CHIP, ON_CHIP),
    )
    mixed_grad = mixed_grad.reshape(-1, pair)
    mixed_grad, down_sum = lax.optimization_barrier((mixed_grad, down_sum))
    qkv_low, misc = pair_backward(
        blk_table, ker, mix, gain_pair, heads_in, mixed_grad, y, prob, seq, blk, scale
    )
    small = (8, width)
    layer_out, row_grad = communicate(
        layer_kernel, "layer", 6, 18, [((rows_all, width), BF16), ((planes, owned, width), BF16)],
        [
            pltpu.VMEM(by_core + (half,), BF16),
            pltpu.VMEM((half, width), BF16),
            pltpu.VMEM((rows_all, width), F32),
            DMA((3,)),
        ]
        + sum_spec + [DMA((4,))] * 2 + [DMA],
        (
            active.reshape(by_core + (half,)), down, residual,
            out_w_grad.reshape(4, owned, width),
        ),
        None, [ANYWHERE] * 4, (ON_CHIP, ANYWHERE),
    )
    input_grad, sums, misc, qkv_back, feed_back, out_w_back = communicate(
        functools.partial(leave_kernel, planes), "leave", 5, 55,
        [
            ((rows_all, width), BF16),
            (small, F32),
            ((groups,) + misc.shape, F32),
            (qkv_shape, BF16),
            (feed_shape, BF16),
            ((1, owned, width), BF16),
        ],
        [
            pltpu.VMEM(by_core + (3 * pair,), BF16),
            pltpu.VMEM((width, 3 * pair), BF16),
            pltpu.VMEM(hidden_all.shape, BF16),
            pltpu.VMEM((rows_all, width), F32),
            pltpu.VMEM((rows_all, width), BF16),
            DMA((5,)),
            pltpu.VMEM((planes,) + misc.shape, F32),
            DMA((2, groups)),
            DMA((2, groups)),
        ]
        + sum_spec[:6]
        + [pltpu.VMEM((groups,) + small, F32), pltpu.VMEM((planes,) + small, F32)]
        + [pltpu.VMEM((planes, groups * owned, 4 * pair), BF16)]
        + [pltpu.VMEM((2, planes, groups * owned, 4 * pair), BF16)] * 2
        + [pltpu.VMEM(qkv_shape, BF16)]
        + sum_spec[6:]
        + [DMA((2, groups))] * 2
        + [DMA((2, 2, planes))] * 2
        + [DMA((2, groups))] * 2
        + [DMA((3,))],
        (
            qkv_low.reshape(by_core + (3 * pair,)), qkv, hidden_all,
            residual_grad, tokens_low, gains, gain_second_grad, misc,
            feed_sum.reshape(feed_shape), row_grad,
        ),
        None, [ANYWHERE] * 5 + [ON_CHIP] * 3 + [ANYWHERE, ON_CHIP],
        (ON_CHIP,) * 3 + (ANYWHERE,) * 2 + (ON_CHIP,),
    )
    plain = [(owned, width)] * 3 + [(owned, hidden)] * 2 + [(owned, width), (chunk, width)]
    landed = (qkv_back, feed_back, out_w_back, down_sum, input_grad, layer_out)
    out_shapes = [jax.ShapeDtypeStruct(shape, F32) for shape in plain]
    out_shapes += [jax.ShapeDtypeStruct((rows_all, width), BF16)] * 2
    row = jax.ShapeDtypeStruct((1, owned), F32)
    flat_index = (lax.axis_index("seq") * groups + me).astype(jnp.int32).reshape(1)
    results = pl.pallas_call(
        functools.partial(finish_kernel, len(out_shapes)),
        name="finish",
        out_shape=tuple(out_shapes)
        + (row, row, row)
        + (jax.ShapeDtypeStruct(score_kernel.shape[::-1], F32), jax.ShapeDtypeStruct((2, heads), F32)),
        in_specs=[pl.BlockSpec(memory_space=pltpu.SMEM)] + [ON_CHIP] * 2 + [ANYWHERE] * 6,
        out_specs=(ANYWHERE,) * len(out_shapes) + (ON_CHIP,) * 5,
        scratch_shapes=[pltpu.VMEM(value.shape, BF16) for value in landed]
        + [pltpu.VMEM(shape, F32) for shape in plain]
        + [DMA((6,)), DMA((len(out_shapes),))],
        compiler_params=pltpu.CompilerParams(vmem_limit_bytes=60 << 20),
    )(flat_index, sums, misc, *landed)
    q_back, k_back, v_back, gate_back, up_back, out_w_out, down_out, input_grad, layer_out = results[:9]
    gain_outs = [value.reshape(owned) for value in results[9:12]]
    ker_out, mix_out = jnp.transpose(results[12], (2, 1, 0)), results[13].T

    shape = inputs.shape
    return (
        layer_out.reshape(shape),
        input_grad.reshape(shape),
        gain_outs[0],
        q_back,
        k_back,
        v_back,
        ker_out,
        mix_out,
        gain_outs[1],
        out_w_out,
        gain_outs[2],
        gate_back,
        up_back,
        down_out,
    )


def solution(mesh):
    placed = (
        P(None, "seq", "ctx", None),
        P(None, "seq", "ctx", None),
        P(),
        P(("seq", "ctx")),
        P(("seq", "ctx"), None),
        P(("seq", "ctx"), None),
        P(("seq", "ctx"), None),
        P(),
        P(),
        P(("seq", "ctx")),
        P(("seq", "ctx"), None),
        P(("seq", "ctx")),
        P(("seq", "ctx"), None),
        P(("seq", "ctx"), None),
        P(("seq", "ctx"), None),
    )
    return jax.shard_map(
        on_device,
        mesh=mesh,
        in_specs=placed,
        out_specs=(
            P(None, "seq", "ctx", None),
            P(None, "seq", "ctx", None),
            P(("seq", "ctx")),
            P(("seq", "ctx"), None),
            P(("seq", "ctx"), None),
            P(("seq", "ctx"), None),
            P(),
            P(),
            P(("seq", "ctx")),
            P(("seq", "ctx"), None),
            P(("seq", "ctx")),
            P(("seq", "ctx"), None),
            P(("seq", "ctx"), None),
            P(("seq", "ctx"), None),
        ),
        check_vma=False,
    )
```

```python
import functools

import jax
import jax.numpy as jnp
from jax import lax
from jax.experimental import pallas as pl
from jax.experimental.pallas import tpu as pltpu
from jax.sharding import PartitionSpec as P

EPSILON = 1e-05
NEGATIVE = -1e30
F32 = jnp.float32
BF16 = jnp.bfloat16
TILE = 128


def nt(left, right):
    return lax.dot_general(left, right, (((1,), (1,)), ((), ())), preferred_element_type=F32)


def tn(left, right):
    return lax.dot_general(left, right, (((0,), (0,)), ((), ())), preferred_element_type=F32)


def nn(left, right):
    return lax.dot_general(left, right, (((1,), (0,)), ((), ())), preferred_element_type=F32)


def natural_rows(blk_ref, m, blk, seq):
    return [pl.multiple_of(blk_ref[m, b] * blk, blk) for b in range(seq // blk)]


def head_lanes(width):
    return lax.broadcasted_iota(jnp.int32, (1, width), 1) < width // 2


def load_heads(blk_ref, m, blk, seq, qkv_ref, qm, kf, ks, vn):
    width = vn.shape[1]
    first = head_lanes(width)
    kf[0:8, :] = jnp.zeros((8, width), F32)
    kf[seq : seq + TILE + 8, :] = jnp.zeros((TILE + 8, width), F32)
    for b, row in enumerate(natural_rows(blk_ref, m, blk, seq)):
        here = pl.ds(blk * b, blk)
        q = qkv_ref[pl.ds(row, blk), 0:width].astype(F32)
        qm[0, here, :] = jnp.where(first, q, 0.0).astype(BF16)
        qm[1, here, :] = jnp.where(first, 0.0, q).astype(BF16)
        kf[pl.ds(blk * b + 5, blk), :] = qkv_ref[pl.ds(row, blk), width : 2 * width].astype(F32)
        vn[here, :] = qkv_ref[pl.ds(row, blk), 2 * width : 3 * width]
    ks[...] = kf[0 : seq + TILE, :].astype(BF16)


def scores(qm, ks, h, rb, upto, scale):
    rows = pl.ds(TILE * rb, TILE)
    raw = nt(qm[h, rows, :], ks[0 : TILE * upto, :]) * scale
    key = lax.broadcasted_iota(jnp.int32, raw.shape, 1) - 5
    row = lax.broadcasted_iota(jnp.int32, raw.shape, 0) + TILE * rb
    return jnp.where((key >= 0) & (key <= row), raw, 0.0)


def head_factor(values, first, dim):
    squares = values * values
    own = jnp.sum(jnp.where(first, squares, 0.0), axis=1, keepdims=True)
    other = jnp.sum(jnp.where(first, 0.0, squares), axis=1, keepdims=True)
    return jnp.where(
        first, lax.rsqrt(own / dim + EPSILON), lax.rsqrt(other / dim + EPSILON)
    )


def forward_kernel(
    seq, blk, rows_tap, keys_tap, scale,
    blk_ref, ker_ref, mix_ref, gain_ref, qkv_ref,
    z_ref, y_ref, p_ref,
    qm, kf, ks, vn, shi, slo, thi, tlo, run, logit,
):
    m = pl.program_id(0)
    width = vn.shape[1]
    first = head_lanes(width)
    tiles = seq // TILE

    @pl.when(m == 0)
    def _():
        shi[...] = jnp.zeros(shi.shape, BF16)
        slo[...] = jnp.zeros(slo.shape, BF16)
        away = lax.broadcasted_iota(jnp.int32, (2 * TILE, TILE), 0) - lax.broadcasted_iota(
            jnp.int32, (2 * TILE, TILE), 1
        )
        for h in range(2):
            for a in range(rows_tap):
                band = jnp.zeros((2 * TILE, TILE), F32)
                for t in range(keys_tap):
                    band = jnp.where(away == keys_tap - 1 - t, ker_ref[h, a, t], band)
                high = band.astype(BF16)
                thi[h, :, TILE * a : TILE * (a + 1)] = high
                tlo[h, :, TILE * a : TILE * (a + 1)] = (band - high.astype(F32)).astype(BF16)

    load_heads(blk_ref, m, blk, seq, qkv_ref, qm, kf, ks, vn)
    for h in range(2):
        for rb in range(tiles):
            upto = min(rb + 2, tiles + 1)
            zeroed = scores(qm, ks, h, rb, upto, scale)
            high = zeroed.astype(BF16)
            shi[pl.ds(16 + TILE * rb, TILE), 0 : TILE * upto] = high
            slo[pl.ds(16 + TILE * rb, TILE), 0 : TILE * upto] = (zeroed - high.astype(F32)).astype(BF16)
        for b in range(tiles):
            count = seq - TILE * b
            rows = pl.ds(TILE * b, count + 16)
            lanes = pl.ds(TILE * b, 2 * TILE)
            high, low = shi[rows, lanes], slo[rows, lanes]
            run[0 : count + 16, :] = nn(high, thi[h]) + nn(low, thi[h]) + nn(high, tlo[h])
            total = run[16 : 16 + count, 0:TILE]
            for a in range(1, rows_tap):
                total = total + run[pl.ds(16 - a, count), TILE * a : TILE * (a + 1)]
            logit[pl.ds(TILE * b, count), TILE * b : TILE * (b + 1)] = total
        for rb in range(tiles):
            rows = pl.ds(TILE * rb, TILE)
            wide = TILE * (rb + 1)
            value = logit[rows, 0:wide]
            key = lax.broadcasted_iota(jnp.int32, value.shape, 1)
            row = lax.broadcasted_iota(jnp.int32, value.shape, 0) + TILE * rb
            value = jnp.where(key <= row, value, NEGATIVE)
            weight = jnp.exp(value - jnp.max(value, axis=1, keepdims=True))
            weight = weight / jnp.sum(weight, axis=1, keepdims=True)
            lowered = weight.astype(BF16)
            p_ref[0, h, rows, 0:wide] = lowered
            y_ref[0, h, rows, :] = nn(lowered, vn[0:wide, :])
    out = mix_ref[0:1, :] * y_ref[0, 0] + mix_ref[1:2, :] * y_ref[0, 1]
    normed = out * head_factor(out, first, width // 2)
    final = (normed * gain_ref[1:2, :]).astype(BF16)
    for b, row in enumerate(natural_rows(blk_ref, m, blk, seq)):
        z_ref[pl.ds(row, blk), :] = final[blk * b : blk * (b + 1), :]


def backward_kernel(
    seq, blk, rows_tap, keys_tap, scale,
    blk_ref, ker_ref, mix_ref, gain_ref, qkv_ref, zg_ref, y_ref, p_ref,
    low_ref, misc_ref,
    qm, kf, ks, vn, sb, up, zn, yl, cg, cs, eb, qa, ka, acc, taps,
):
    m = pl.program_id(0)
    width = vn.shape[1]
    first = head_lanes(width)
    tiles = seq // TILE
    wide_u = 3 * TILE
    span = keys_tap - 1
    lanes_all = rows_tap * TILE

    @pl.when(m == 0)
    def _():
        misc_ref[...] = jnp.zeros(misc_ref.shape, F32)
        taps[...] = jnp.zeros(taps.shape, F32)
        acc[...] = jnp.zeros(acc.shape, F32)
        cg[seq : seq + 8, :] = jnp.zeros((8, seq), F32)
        for b in range(1, tiles):
            start = TILE * b - 16
            cg[start : TILE * b, TILE * b : TILE * (b + 1)] = jnp.zeros((16, TILE), F32)
            cs[0:start, lanes_all * b : lanes_all * (b + 1)] = jnp.zeros((start, lanes_all), BF16)
        eb[...] = jnp.zeros(eb.shape, BF16)
        sb[...] = jnp.zeros(sb.shape, BF16)
        away = lax.broadcasted_iota(jnp.int32, (2 * TILE, TILE), 0) - lax.broadcasted_iota(
            jnp.int32, (2 * TILE, TILE), 1
        )
        none = jnp.zeros((TILE, TILE), BF16)
        for h in range(2):
            for a in range(rows_tap):
                band = jnp.zeros((2 * TILE, TILE), F32)
                for t in range(keys_tap):
                    band = jnp.where(away == TILE - span + t, ker_ref[h, a, t], band)
                band = band.astype(BF16)
                at = wide_u * a
                up[h, at : at + 2 * TILE, 0:TILE] = band
                up[h, at + 2 * TILE : at + wide_u, 0:TILE] = none
                up[h, at : at + TILE, TILE : 2 * TILE] = none
                up[h, at + TILE : at + wide_u, TILE : 2 * TILE] = band

    load_heads(blk_ref, m, blk, seq, qkv_ref, qm, kf, ks, vn)
    places = natural_rows(blk_ref, m, blk, seq)
    for b, row in enumerate(places):
        zn[pl.ds(blk * b, blk), :] = zg_ref[pl.ds(row, blk), :].astype(F32)
    dim = width // 2
    y0, y1 = y_ref[0, 0], y_ref[0, 1]
    out = mix_ref[0:1, :] * y0 + mix_ref[1:2, :] * y1
    factor = head_factor(out, first, dim)
    normed = out * factor
    upstream = zn[...]
    misc_ref[16:17, 0:width] += jnp.sum(upstream * normed, axis=0, keepdims=True)
    scaled = upstream * gain_ref[1:2, :]
    both = scaled * normed
    own = jnp.sum(jnp.where(first, both, 0.0), axis=1, keepdims=True) / dim
    other = jnp.sum(jnp.where(first, 0.0, both), axis=1, keepdims=True) / dim
    out_grad = factor * (scaled - normed * jnp.where(first, own, other))
    misc_ref[17:18, 0:width] += jnp.sum(out_grad * y0, axis=0, keepdims=True)
    misc_ref[18:19, 0:width] += jnp.sum(out_grad * y1, axis=0, keepdims=True)
    yl[0] = (mix_ref[0:1, :] * out_grad).astype(BF16)
    yl[1] = (mix_ref[1:2, :] * out_grad).astype(BF16)

    for b in range(tiles):
        rows = pl.ds(TILE * b, seq - TILE * b)
        lanes = pl.ds(TILE * b, TILE)
        part = tn(p_ref[0, 0, rows, lanes], yl[0, rows, :]) + tn(p_ref[0, 1, rows, lanes], yl[1, rows, :])
        part = part.astype(BF16)
        for i in range(TILE // blk):
            low_ref[pl.ds(places[b * (TILE // blk) + i], blk), 2 * width : 3 * width] = part[blk * i : blk * (i + 1), :]

    ka[...] = jnp.zeros(ka.shape, F32)
    for h in range(2):
        for rb in range(tiles):
            rows = pl.ds(TILE * rb, TILE)
            upto = min(rb + 2, tiles + 1)
            sb[rows, 0 : TILE * upto] = scores(qm, ks, h, rb, upto, scale).astype(BF16)
            wide = TILE * (rb + 1)
            prob = p_ref[0, h, rows, 0:wide].astype(F32)
            grad = nt(yl[h, rows, :], vn[0:wide, :])
            both = prob * grad
            cg[rows, 0:wide] = both - prob * jnp.sum(both, axis=1, keepdims=True)
        for b in range(tiles):
            start = max(0, TILE * b - 16)
            count = seq - start
            for a in range(rows_tap):
                cs[pl.ds(start, count), pl.ds(lanes_all * b + TILE * a, TILE)] = cg[
                    pl.ds(start + a, count), TILE * b : TILE * (b + 1)
                ].astype(BF16)
            acc[h] += tn(
                sb[pl.ds(start, count), pl.ds(TILE * b, TILE + 16)],
                cs[pl.ds(start, count), pl.ds(lanes_all * b, lanes_all)],
            )
        for b in range(0, tiles + 1, 2):
            start = max(0, TILE * b - 16)
            count = seq - start
            columns = min(2, tiles + 1 - b)
            left, right = [], []
            for a in range(rows_tap):
                for piece in range(columns + 1):
                    block = b - 1 + piece
                    if 0 <= block < tiles:
                        left.append(cs[pl.ds(start, count), pl.ds(lanes_all * block + TILE * a, TILE)])
                        right.append(
                            up[h, pl.ds(wide_u * a + TILE * piece, TILE), 0 : TILE * columns]
                        )
            grad = nn(jnp.concatenate(left, axis=1), jnp.concatenate(right, axis=0))
            key = lax.broadcasted_iota(jnp.int32, grad.shape, 1) + TILE * b - 5
            row = lax.broadcasted_iota(jnp.int32, grad.shape, 0) + start
            low = jnp.where((key >= 0) & (key <= row), grad, 0.0).astype(BF16)
            eb[pl.ds(start, count), pl.ds(TILE * b, TILE * columns)] = low
            ka[pl.ds(TILE * b, TILE * columns), :] += tn(low, qm[h, pl.ds(start, count), :])
        for rb in range(tiles):
            rows = pl.ds(TILE * rb, TILE)
            upto = min(rb + 2, tiles + 1)
            part = nn(eb[rows, 0 : TILE * upto], ks[0 : TILE * upto, :]) * scale
            if h == 0:
                qa[rows, :] = part
            else:
                qa[rows, :] = jnp.where(first, qa[rows, :], part)
    for b, row in enumerate(places):
        low_ref[pl.ds(row, blk), 0:width] = qa[pl.ds(blk * b, blk), :].astype(BF16)
        low_ref[pl.ds(row, blk), width : 2 * width] = (ka[pl.ds(blk * b + 5, blk), :] * scale).astype(BF16)

    @pl.when(m == pl.num_programs(0) - 1)
    def _():
        away = lax.broadcasted_iota(jnp.int32, (TILE + 16, TILE), 0) - lax.broadcasted_iota(
            jnp.int32, (TILE + 16, TILE), 1
        )
        for h in range(2):
            for a in range(rows_tap):
                table = acc[h, :, TILE * a : TILE * (a + 1)]
                for t in range(keys_tap):
                    at = a * keys_tap + t
                    taps[at : at + 1, :] = jnp.sum(
                        jnp.where(away == span - t, table, 0.0), axis=0, keepdims=True
                    )
            count = taps.shape[0]
            tap = lax.broadcasted_iota(jnp.int32, (8, count), 1) - keys_tap * lax.broadcasted_iota(
                jnp.int32, (8, count), 0
            )
            rows = ((tap >= 0) & (tap < keys_tap)).astype(F32)
            at = lax.broadcasted_iota(jnp.int32, (count, TILE), 0)
            lane = lax.broadcasted_iota(jnp.int32, (count, TILE), 1)
            value = jnp.sum(taps[...], axis=1, keepdims=True)
            lanes = jnp.zeros((count, TILE), F32)
            for a in range(rows_tap):
                lanes = jnp.where((at == keys_tap * a + lane) & (lane < keys_tap), value, lanes)
            misc_ref[8 * h : 8 * h + 8, 0:TILE] = lax.dot_general(
                rows, lanes, (((1,), (0,)), ((), ())),
                precision=lax.Precision.HIGHEST, preferred_element_type=F32,
            )


def whole(shape):
    return pl.BlockSpec(shape, lambda m: (0,) * len(shape))


def pair_forward(blk_table, ker, mix, gain, qkv, micro, seq, blk, scale):
    width = qkv.shape[1] // 3
    mixed = (qkv.shape[0], width)
    rows_tap, keys_tap = ker.shape[1:]
    smem = pl.BlockSpec(memory_space=pltpu.SMEM)
    per = lambda shape: pl.BlockSpec((1,) + shape, lambda m: (m,) + (0,) * len(shape))
    return pl.pallas_call(
        functools.partial(forward_kernel, seq, blk, rows_tap, keys_tap, scale),
        name="pair_forward",
        grid=(micro,),
        out_shape=(
            jax.ShapeDtypeStruct(mixed, BF16),
            jax.ShapeDtypeStruct((micro, 2, seq, width), F32),
            jax.ShapeDtypeStruct((micro, 2, seq, seq), BF16),
        ),
        in_specs=[smem, smem, whole(mix.shape), whole(gain.shape), whole(qkv.shape)],
        out_specs=(whole(mixed), per((2, seq, width)), per((2, seq, seq))),
        scratch_shapes=[
            pltpu.VMEM((2, seq, width), BF16),
            pltpu.VMEM((seq + TILE + 8, width), F32),
            pltpu.VMEM((seq + TILE, width), BF16),
            pltpu.VMEM((seq, width), BF16),
            pltpu.VMEM((seq + 16, seq + TILE), BF16),
            pltpu.VMEM((seq + 16, seq + TILE), BF16),
            pltpu.VMEM((2, 2 * TILE, rows_tap * TILE), BF16),
            pltpu.VMEM((2, 2 * TILE, rows_tap * TILE), BF16),
            pltpu.VMEM((seq + 16, rows_tap * TILE), F32),
            pltpu.VMEM((seq, seq), F32),
        ],
        compiler_params=pltpu.CompilerParams(vmem_limit_bytes=56 << 20),
        cost_estimate=pl.CostEstimate(flops=20 * 10**9, transcendentals=10**6, bytes_accessed=8 << 20),
    )(blk_table, ker, mix, gain, qkv)


def pair_backward(blk_table, ker, mix, gain, qkv, zg, y, p, seq, blk, scale):
    width = qkv.shape[1] // 3
    micro = y.shape[0]
    rows_tap, keys_tap = ker.shape[1:]
    tiles = seq // TILE
    smem = pl.BlockSpec(memory_space=pltpu.SMEM)
    per = lambda shape: pl.BlockSpec((1,) + shape, lambda m: (m,) + (0,) * len(shape))
    taps = -(-rows_tap * keys_tap // 8) * 8
    return pl.pallas_call(
        functools.partial(backward_kernel, seq, blk, rows_tap, keys_tap, scale),
        name="pair_backward",
        grid=(micro,),
        out_shape=(
            jax.ShapeDtypeStruct(qkv.shape, BF16),
            jax.ShapeDtypeStruct((24, 2 * TILE), F32),
        ),
        in_specs=[smem, smem, whole(mix.shape), whole(gain.shape), whole(qkv.shape), whole(zg.shape)]
        + [per((2, seq, width)), per((2, seq, seq))],
        out_specs=(whole(qkv.shape), whole((24, 2 * TILE))),
        scratch_shapes=[
            pltpu.VMEM((2, seq, width), BF16),
            pltpu.VMEM((seq + TILE + 8, width), F32),
            pltpu.VMEM((seq + TILE, width), BF16),
            pltpu.VMEM((seq, width), BF16),
            pltpu.VMEM((seq, seq + TILE), BF16),
            pltpu.VMEM((2, rows_tap * 3 * TILE, 2 * TILE), BF16),
            pltpu.VMEM((seq, width), F32),
            pltpu.VMEM((2, seq, width), BF16),
            pltpu.VMEM((seq + 8, seq), F32),
            pltpu.VMEM((seq, tiles * rows_tap * TILE), BF16),
            pltpu.VMEM((seq, seq + TILE), BF16),
            pltpu.VMEM((seq, width), F32),
            pltpu.VMEM((seq + TILE, width), F32),
            pltpu.VMEM((2, TILE + 16, rows_tap * TILE), F32),
            pltpu.VMEM((taps, TILE), F32),
        ],
        compiler_params=pltpu.CompilerParams(vmem_limit_bytes=56 << 20),
        cost_estimate=pl.CostEstimate(flops=30 * 10**9, transcendentals=10**5, bytes_accessed=12 << 20),
    )(blk_table, ker, mix, gain, qkv, zg, y, p)


MESH = pl.DeviceIdType.MESH


def peer(offset):
    mine = lax.axis_index("ctx")
    y = (mine // 4 + offset // 4) % 2
    x = ((mine // 2) % 2 + (offset // 2) % 2) % 2
    core = (mine % 2 + offset % 2) % 2
    return y * 4 + x * 2 + core


def greet(places):
    barrier = pltpu.get_barrier_semaphore()
    for place in places:
        pl.semaphore_signal(barrier, inc=1, device_id=place, device_id_type=MESH)
    return lambda: pl.semaphore_wait(barrier, len(places))


def remote(source, target, send, receive, place):
    return pltpu.make_async_remote_copy(
        src_ref=source, dst_ref=target, send_sem=send, recv_sem=receive,
        device_id=place, device_id_type=MESH,
    )


def exchange_start(plane, mine, source, target, sends, receives):
    copies = [
        remote(source.at[peer(d)], target.at[mine], sends.at[d], receives.at[d], (plane, peer(d)))
        for d in (6, 7, 2, 3, 4, 5, 1)
    ]
    for copy in copies:
        copy.start()
    return copies


class Spread:
    def __init__(self, source, target, sends, receives):
        self.plane, self.mine = lax.axis_index("seq"), lax.axis_index("ctx")
        self.source, self.target, self.sends, self.receives = source, target, sends, receives
        self.copies = {}
        half = target.shape[1] // 2
        self.first, self.second = pl.ds(0, half), pl.ds(half, half)

    def send(self, key, source, target, offset):
        copy = remote(source, target, self.sends.at[key], self.receives.at[key], (self.plane, peer(offset)))
        copy.start()
        self.copies[key] = copy

    def hand_on(self, key, block, offset, rows=None):
        piece = self.target.at[block] if rows is None else self.target.at[block, rows]
        self.send(key, piece, piece, offset)

    def start(self):
        for d in (2, 4, 1):
            self.send(d, self.source, self.target.at[self.mine], d)

    def near(self):
        self.copies[2].wait_recv()
        self.hand_on(6, peer(2), 4, self.first)
        self.hand_on(3, peer(2), 1)
        self.copies[4].wait_recv()
        self.hand_on(0, peer(4), 2, self.second)
        self.hand_on(5, peer(4), 1)

    def across(self):
        self.copies[6].wait_recv()
        self.hand_on(7, peer(6), 1, self.first)
        self.copies[0].wait_recv()
        self.hand_on(8, peer(6), 1, self.second)

    def finish(self):
        for key in (1, 3, 5, 7, 8):
            self.copies[key].wait_recv()
        for copy in self.copies.values():
            copy.wait_send()


class PlaneSum:
    def __init__(self, terms, part, own, near, stage, far, hop, sends, receives):
        self.plane, self.mine = lax.axis_index("seq"), lax.axis_index("ctx")
        self.terms, self.part, self.own = terms, part, own
        self.near, self.stage, self.far, self.hop = near, stage, far, hop
        self.sends, self.receives = sends, receives
        self.copies = {}
        half = part.shape[1] // 2
        self.first, self.second = pl.ds(0, half), pl.ds(half, half)

    def send(self, key, source, target, offset):
        copy = remote(source, target, self.sends.at[key], self.receives.at[key], (self.plane, peer(offset)))
        copy.start()
        self.copies[key] = copy

    def start(self, met):
        self.part[...] = self.terms(1 - self.mine % 2).astype(BF16)
        met()
        for d in (6, 2, 4, 0):
            self.send(d, self.part.at[peer(d) // 2], self.near.at[d // 2], 1)

    def prepare(self):
        self.own[...] = self.terms(self.mine % 2)

    def chip_sum(self, d):
        self.copies[d].wait_recv()
        self.stage[d // 2] = (self.own[peer(d) // 2] + self.near[d // 2].astype(F32)).astype(BF16)

    def add_hop(self, slot, rows, hop):
        self.stage[slot, rows, :] = (
            self.stage[slot, rows, :].astype(F32) + self.hop[hop].astype(F32)
        ).astype(BF16)

    def run(self):
        first, second = self.first, self.second
        self.chip_sum(6)
        self.send(1, self.stage.at[3, first], self.hop.at[0], 2)
        self.send(3, self.stage.at[3, second], self.hop.at[1], 4)
        self.chip_sum(2)
        self.send(5, self.stage.at[1, first], self.far.at[0, first], 2)
        self.chip_sum(4)
        self.send(7, self.stage.at[2, second], self.far.at[1, second], 4)
        self.copies[1].wait_recv()
        self.add_hop(2, first, 0)
        self.send(8, self.stage.at[2, first], self.far.at[1, first], 4)
        self.copies[3].wait_recv()
        self.add_hop(1, second, 1)
        self.send(9, self.stage.at[1, second], self.far.at[0, second], 2)

    def total(self):
        self.copies[0].wait_recv()
        value = self.own[self.mine // 2] + self.near[0].astype(F32)
        for key in (5, 7, 8, 9):
            self.copies[key].wait_recv()
        return value + self.far[0].astype(F32) + self.far[1].astype(F32)

    def finish(self):
        for copy in self.copies.values():
            copy.wait_send()


class Fetch:
    def __init__(self, source, buffer, sem):
        self.copy, self.buffer, self.ready = pltpu.make_async_copy(source, buffer, sem), buffer, False
        self.copy.start()

    def get(self):
        if not self.ready:
            self.copy.wait()
            self.ready = True
        return self.buffer


def fetch(sources, buffers, sems):
    return [Fetch(source, buffer, sems.at[i]) for i, (source, buffer) in enumerate(zip(sources, buffers))]


def put(buffer, out, sem):
    copy = pltpu.make_async_copy(buffer, out, sem)
    copy.start()
    return copy


def terms_of(values, product):
    chips, _, rows, width = values.buffer.shape

    def terms(core):
        left = values.get()[:, core].reshape(chips * rows, width)
        return product(left).reshape(chips, rows, -1)

    return terms


class Line:
    def __init__(self, sources, targets, planes, sends, receives):
        self.sources, self.targets, self.planes = sources, targets, planes
        self.sends, self.receives = sends, receives
        self.plane, self.mine = lax.axis_index("seq"), lax.axis_index("ctx")

    def copy(self, i, up, step):
        block = jnp.clip(self.plane - step if up else self.plane + step, 0, self.planes - 1)
        next_plane = jnp.clip(self.plane + 1 if up else self.plane - 1, 0, self.planes - 1)
        at = (i, int(up), step)
        target = self.targets[i].at[block]
        source = target if step else self.sources[i]
        return remote(source, target, self.sends.at[at], self.receives.at[at], (next_plane, self.mine))

    def arrived(self, i, up, step):
        block = jnp.clip(self.plane - 1 - step if up else self.plane + 1 + step, 0, self.planes - 1)
        at = (i, int(up), step)
        target = self.targets[i].at[block]
        from_plane = jnp.clip(self.plane - 1 if up else self.plane + 1, 0, self.planes - 1)
        return remote(target, target, self.sends.at[at], self.receives.at[at], (from_plane, self.mine))

    def step(self, step):
        for up in (True, False):
            have = self.plane >= step if up else self.plane + step < self.planes
            more = self.plane + 1 < self.planes if up else self.plane > 0
            for i in range(len(self.targets)):
                if step:
                    @pl.when(have)
                    def _(i=i, up=up):
                        self.arrived(i, up, step - 1).wait_recv()

                if step < self.planes - 1:
                    @pl.when(have & more)
                    def _(i=i, up=up):
                        self.copy(i, up, step).start()

    def finish(self):
        for step in range(self.planes - 1):
            for up in (True, False):
                have = self.plane >= step if up else self.plane + step < self.planes
                more = self.plane + 1 < self.planes if up else self.plane > 0
                for i in range(len(self.targets)):
                    @pl.when(have & more)
                    def _(i=i, up=up, step=step):
                        self.copy(i, up, step).wait_send()


def plane_peers(plane, offsets):
    return [(plane, peer(d)) for d in offsets]


def other_planes(plane, mine, planes):
    return [((plane + d) % planes, mine) for d in range(1, planes)]


class RowDeal:
    def __init__(self, gathered, dealt, sends, receives, local):
        self.plane, self.mine = lax.axis_index("seq"), lax.axis_index("ctx")
        self.gathered, self.dealt, self.sends, self.receives, self.local = gathered, dealt, sends, receives, local

    def out(self, s, back):
        if back:
            target = 4 * (self.mine % 2) + s
            source, place = self.dealt.at[s], self.gathered.at[self.mine // 2]
        else:
            target = 2 * s + self.mine // 4
            source, place = self.gathered.at[s], self.dealt.at[self.mine % 4]
        slot = self.mine // 2 if back else self.mine % 4
        copy = remote(source, place, self.sends.at[s], self.receives.at[slot], (self.plane, target))
        keep = pltpu.make_async_copy(source, place, self.local)
        return target == self.mine, copy, keep

    def into(self, r, back):
        if back:
            origin = 2 * r + self.mine // 4
            place = self.gathered.at[r]
        else:
            origin = 4 * (self.mine % 2) + r
            place = self.dealt.at[r]
        return origin == self.mine, remote(place, place, self.sends.at[r], self.receives.at[r], (self.plane, origin))

    def start(self, back):
        for s in range(4):
            here, copy, keep = self.out(s, back)

            @pl.when(here)
            def _():
                keep.start()

            @pl.when(jnp.logical_not(here))
            def _():
                copy.start()

    def wait(self, back):
        for s in range(4):
            here, copy, keep = self.out(s, back)

            @pl.when(here)
            def _():
                keep.wait()

            @pl.when(jnp.logical_not(here))
            def _():
                copy.wait_send()

        for r in range(4):
            here, copy = self.into(r, back)

            @pl.when(jnp.logical_not(here))
            def _():
                copy.wait_recv()


def enter_kernel(
    planes, q, k, v, gate, up, gains, tokens, out_w,
    feed_out, qkv_out, gains_out, tokens_out, out_w_out,
    q_near, k_near, v_near, gate_near, up_near, gains_near, packed, qkv, feed,
    deal_sends, deal_receives, sends, receives, row_sends, row_receives, line_sends, line_receives, local,
):
    plane, mine = lax.axis_index("seq"), lax.axis_index("ctx")
    loads = [
        pltpu.make_async_copy(source, place, local.at[5 + i])
        for i, (source, place) in enumerate(
            ((gains, gains_near), (q, q_near), (k, k_near), (v, v_near), (gate, gate_near), (up, up_near))
        )
    ]
    keep = [
        pltpu.make_async_copy(qkv.at[mine], qkv_out.at[plane, mine], local.at[0]),
        pltpu.make_async_copy(packed, gains_out.at[plane, mine], local.at[1]),
        pltpu.make_async_copy(feed.at[mine], feed_out.at[mine], local.at[2]),
        pltpu.make_async_copy(tokens, tokens_out.at[mine], local.at[3]),
        pltpu.make_async_copy(out_w, out_w_out.at[plane], local.at[4]),
    ]
    for copy in loads + keep[3:]:
        copy.start()
    met = greet(plane_peers(plane, range(1, 8)) + other_planes(plane, mine, planes))
    groups, _, three = qkv.shape
    pair = three // 3
    half = feed.shape[2] // 2
    for copy in loads[:4]:
        copy.wait()
    packed[...] = jnp.zeros(packed.shape, F32)
    packed[0:3, 0 : gains.shape[1]] = gains_near[...].astype(F32)
    for c in range(groups):
        for i, weight in enumerate((q_near, k_near, v_near)):
            qkv[c, :, pair * i : pair * (i + 1)] = weight[:, pair * c : pair * (c + 1)]
    for copy in keep[:2]:
        copy.start()
    met()
    first = exchange_start(plane, mine, qkv, qkv_out.at[plane], deal_sends.at[0], deal_receives.at[0])
    for d in (6, 7, 2, 3, 4, 5, 1):
        copy = remote(packed, gains_out.at[plane, mine], deal_sends.at[1, d], deal_receives.at[1, d], (plane, peer(d)))
        copy.start()
        first.append(copy)
    rows = Line([out_w], [out_w_out], planes, row_sends, row_receives)
    rows.step(0)
    for copy in loads[4:]:
        copy.wait()
    for c in range(groups):
        for i, weight in enumerate((gate_near, up_near)):
            for s in range(half // TILE):
                at = TILE * (groups * s + c)
                feed[c, :, half * i + TILE * s : half * i + TILE * (s + 1)] = weight[:, at : at + TILE]
    keep[2].start()
    keep[0].wait()
    keep[1].wait()
    for copy in first:
        copy.wait_recv()
    line = Line(
        [qkv_out.at[plane], gains_out.at[plane]], [qkv_out, gains_out], planes, line_sends, line_receives
    )
    line.step(0)
    spread = Spread(tokens, tokens_out, sends, receives)
    spread.start()
    rows.step(1)
    line.step(1)
    spread.near()
    deals = exchange_start(plane, mine, feed, feed_out, deal_sends.at[2], deal_receives.at[2])
    rows.step(2)
    line.step(2)
    spread.across()
    for step in range(3, planes):
        rows.step(step)
        line.step(step)
    spread.finish()
    for copy in first:
        copy.wait_send()
    for copy in deals:
        copy.wait()
    for copy in keep[2:]:
        copy.wait()
    line.finish()
    rows.finish()


def heads_kernel(
    planes, tokens, qkv, gains, out_w, grads, hidden, heads, gains_out, pair_gain, out_w_out, grads_out,
    tokens_near, qkv_near, hidden_near, heads_near,
    row_sends, row_receives, sends, receives, loads, stores, local,
):
    plane, mine = lax.axis_index("seq"), lax.axis_index("ctx")
    groups = tokens.shape[0]
    weight = Fetch(qkv, qkv_near, loads.at[groups])
    blocks = [Fetch(tokens.at[i], tokens_near.at[i], loads.at[i]) for i in range(groups)]
    keep = pltpu.make_async_copy(grads, grads_out.at[mine], local.at[1])
    keep.start()
    greet(plane_peers(plane, range(1, 8)))()
    spread = Spread(grads, grads_out, sends, receives)
    spread.start()
    deal = RowDeal(out_w, out_w_out, row_sends, row_receives, local.at[0])
    deal.start(False)
    owned = out_w.shape[1]
    for s in range(planes):
        for c in range(groups):
            at = owned * (groups * s + c)
            gains_out[:, at : at + owned] = gains[s, c, :, 0:owned]
    for r in range(4):
        pair_gain[:, owned * r : owned * (r + 1)] = gains[mine // 2, 4 * (mine % 2) + r, :, 0:owned]
    gain = gains_out[0:1, :]
    out = []
    for i in range(groups):
        value = blocks[i].get()[...].astype(F32)
        low = (value * inverse_root(value) * gain).astype(BF16)
        rows = pl.ds(value.shape[0] * i, value.shape[0])
        hidden_near[:, rows] = low.T
        out.append(put(hidden_near.at[:, rows], hidden.at[:, rows], stores.at[0, i]))
        heads_near[rows, :] = nn(low, weight.get()[...]).astype(BF16)
        out.append(put(heads_near.at[rows], heads.at[rows], stores.at[1, i]))
        if i == groups - 3:
            spread.near()
    deal.wait(False)
    spread.across()
    for copy in out:
        copy.wait()
    spread.finish()
    keep.wait()


def inverse_root(values):
    return lax.rsqrt(jnp.mean(values * values, axis=1, keepdims=True) + EPSILON)


def second_kernel(
    mixed, out_w, tokens, gains, residual, spread_out,
    mixed_near, out_w_near, tokens_near, residual_near, own_near, loads,
    part, own, near, stage, far, hop, sum_sends, sum_receives, sends, receives,
):
    plane, mine = lax.axis_index("seq"), lax.axis_index("ctx")
    left, weight, rows_in = fetch(
        (mixed, out_w, tokens), (mixed_near, out_w_near, tokens_near), loads
    )
    met = greet(plane_peers(plane, (1, 2, 4)))
    rows = PlaneSum(
        terms_of(left, lambda value: nn(value, weight.get()[...])), part, own, near, stage, far, hop,
        sum_sends, sum_receives,
    )
    rows.start(met)
    rows.prepare()
    rows.run()
    value = rows_in.get()[...].astype(F32) + rows.total()
    own_near[...] = (value * inverse_root(value) * gains[2:3, :]).astype(BF16)
    spread = Spread(own_near, spread_out, sends, receives)
    spread.start()
    keep = put(own_near, spread_out.at[mine], loads.at[3])
    residual_near[...] = value
    out = put(residual_near, residual, loads.at[4])
    rows.finish()
    spread.near()
    spread.across()
    keep.wait()
    out.wait()
    spread.finish()


def back_through_norm(upstream, values, gain):
    factor = inverse_root(values)
    normed = values * factor
    scaled = upstream * gain
    grad = factor * (scaled - normed * jnp.mean(scaled * normed, axis=1, keepdims=True))
    return grad, jnp.sum(upstream * normed, axis=0, keepdims=True)


def back_kernel(
    lows, feed, residual, grads, out_w, mixed, gains, residual_grad, gain_grad, mixed_grad, out_w_grad,
    lows_near, feed_near, residual_near, grads_near, out_w_near, mixed_near, residual_grad_near, gathered, total, loads,
    part, own, near, stage, far, hop, sum_sends, sum_receives, sends, receives,
):
    plane, mine = lax.axis_index("seq"), lax.axis_index("ctx")
    weight, left, before, upstream, out_rows, taken = fetch(
        (feed, lows, residual, grads, out_w, mixed),
        (feed_near, lows_near, residual_near, grads_near, out_w_near, mixed_near),
        loads,
    )
    met = greet(plane_peers(plane, (1, 2, 4)))
    rows = PlaneSum(
        terms_of(left, lambda value: nt(value, weight.get()[...])), part, own, near, stage, far, hop,
        sum_sends, sum_receives,
    )
    rows.start(met)
    rows.prepare()
    rows.run()
    grad, gain_part = back_through_norm(rows.total(), before.get()[...], gains[2:3, :])
    grad = grad + upstream.get()[...].astype(F32)
    gathered[mine] = grad.astype(BF16)
    spread = Spread(gathered.at[mine], gathered, sends, receives)
    spread.start()
    gain_grad[...] = gain_part
    residual_grad_near[...] = grad
    out = put(residual_grad_near, residual_grad, loads.at[6])
    taken.get()

    def use(d):
        block = peer(d) if d else mine
        value = gathered[block]
        mixed_grad[block] = nt(value, out_rows.get()[...]).astype(BF16)
        term = tn(mixed_near[block], value)
        total[...] = total[...] + term if d else term

    use(0)
    rows.finish()
    spread.near()
    use(2)
    use(4)
    spread.copies[1].wait_recv()
    use(1)
    spread.across()
    use(6)
    for keys, d in (((3,), 3), ((5,), 5), ((7, 8), 7)):
        for key in keys:
            spread.copies[key].wait_recv()
        use(d)
    out_w_grad[...] = total[...].astype(BF16)
    for copy in spread.copies.values():
        copy.wait_send()
    out.wait()


class Fold:
    def __init__(self, own, stage, landed, planes, sends, receives):
        self.own, self.stage, self.landed, self.planes = own, stage, landed, planes
        self.sends, self.receives = sends, receives
        self.plane, self.mine = lax.axis_index("seq"), lax.axis_index("ctx")

    def copy(self, j, up):
        place = jnp.clip(self.plane + 1 if up else self.plane - 1, 0, self.planes - 1)
        at = (int(up), j)
        return remote(self.stage.at[at], self.landed.at[at], self.sends.at[at], self.receives.at[at], (place, self.mine))

    def advance(self, j, up):
        active = self.plane < j if up else self.plane > j
        inner = self.plane > 0 if up else self.plane < self.planes - 1

        @pl.when(active & inner)
        def _():
            self.copy(j, up).wait_recv()
            self.stage[int(up), j] = (
                self.own[j].astype(F32) + self.landed[int(up), j].astype(F32)
            ).astype(BF16)

        @pl.when(active & jnp.logical_not(inner))
        def _():
            self.stage[int(up), j] = self.own[j]

        @pl.when(active)
        def _():
            self.copy(j, up).start()

    def round(self, i):
        self.advance(self.planes - 1 - i, True)
        self.advance(i, False)

    def total(self, store):
        for j in range(self.planes):
            @pl.when(self.plane == j)
            def _():
                value = self.own[j].astype(F32)
                if j > 0:
                    self.copy(j, True).wait_recv()
                    value = value + self.landed[1, j].astype(F32)
                if j < self.planes - 1:
                    self.copy(j, False).wait_recv()
                    value = value + self.landed[0, j].astype(F32)
                store(value.astype(BF16))

    def finish(self):
        for j in range(self.planes):
            for up in (True, False):
                @pl.when(self.plane < j if up else self.plane > j)
                def _():
                    self.copy(j, up).wait_send()


def layer_kernel(
    active, down, residual, out_w_grad, layer_out, row_grad,
    active_near, down_near, residual_near, loads,
    part, own, near, stage, far, hop, sum_sends, sum_receives, row_sends, row_receives, local,
):
    plane, mine = lax.axis_index("seq"), lax.axis_index("ctx")
    left, weight, before = fetch(
        (active, down, residual), (active_near, down_near, residual_near), loads
    )
    met = greet(plane_peers(plane, range(1, 8)))
    rows = PlaneSum(
        terms_of(left, lambda value: nn(value, weight.get()[...])), part, own, near, stage, far, hop,
        sum_sends, sum_receives,
    )
    rows.start(met)
    deal = RowDeal(row_grad, out_w_grad, row_sends, row_receives, local)
    deal.start(True)
    rows.prepare()
    rows.run()
    layer_out[...] = (before.get()[...] + rows.total()).astype(BF16)
    deal.wait(True)
    rows.finish()


def leave_kernel(
    planes, qkv_low_in, qkv_in, hidden_in, residual_grad_in, tokens_in,
    gains, second_grad, misc, feed_grad, row_grad,
    input_grad, small_out, misc_out, qkv_out, feed_out, out_w_out,
    qkv_low_near, qkv_near, hidden_near, residual_grad_near, tokens_near, loads,
    misc_all, misc_sends, misc_receives,
    part, own, near, stage, far, hop, small_plane, small_all,
    grads, fold_stage, fold_landed, qkv_sum,
    sum_sends, sum_receives, small_sends, small_receives,
    fold_sends, fold_receives, deal_sends, deal_receives, local,
):
    plane, mine = lax.axis_index("seq"), lax.axis_index("ctx")
    qkv_low, qkv, hidden, residual_grad, tokens = fetch(
        (qkv_low_in, qkv_in, hidden_in, residual_grad_in, tokens_in),
        (qkv_low_near, qkv_near, hidden_near, residual_grad_near, tokens_near),
        loads,
    )
    keep_feed = pltpu.make_async_copy(feed_grad.at[mine], feed_out.at[mine], local.at[0])
    keep_feed.start()
    misc_all[plane] = misc[...]
    met = greet(plane_peers(plane, range(1, 8)) + other_planes(plane, mine, planes))
    misc_copies = [
        remote(misc_all.at[plane], misc_all.at[plane], misc_sends.at[0, d], misc_receives.at[0, d], ((plane + d) % planes, mine))
        for d in range(1, planes)
    ]
    rows = PlaneSum(
        terms_of(qkv_low, lambda left: nt(left, qkv.get()[...])), part, own, near, stage, far, hop,
        sum_sends, sum_receives,
    )
    halves = [pl.ds(grads.shape[1] // 2 * k, grads.shape[1] // 2) for k in range(2)]
    folds = [
        Fold(
            grads.at[:, rows], fold_stage.at[:, :, rows], fold_landed.at[:, :, rows], planes,
            fold_sends.at[k], fold_receives.at[k],
        )
        for k, rows in enumerate(halves)
    ]
    ends = (plane == 0) | (plane == planes - 1)
    block, owned = grads.shape[1], row_grad.shape[1]
    three = qkv_low_in.shape[3]
    pair = three // 3

    def project(i):
        j = jnp.where(plane < planes // 2, planes - 1 - i, i)
        lows = qkv_low.get()[...].reshape(hidden_near.shape[1], three)
        columns = hidden.get()[pl.ds(pl.multiple_of(block * j, block), block), :]
        grads[j, :, 0:three] = nn(columns, lows).astype(BF16)
        for p in range(block // owned):
            grads[j, owned * p : owned * (p + 1), three : three + pair] = row_grad[
                j, :, pair * p : pair * (p + 1)
            ]

    def rounds(outer, inner):
        for here, i in ((ends, outer), (jnp.logical_not(ends), inner)):
            if 0 <= i < planes - 1:
                @pl.when(here)
                def _():
                    for fold in folds:
                        fold.round(i)

    rows.start(met)
    for copy in misc_copies:
        copy.start()
    project(0)
    rounds(0, -1)
    rows.prepare()
    for i in range(1, planes):
        project(i)
    rounds(1, -1)
    rows.run()
    rounds(2, 0)
    for copy in misc_copies:
        copy.wait()
    total = misc_all[0]
    for i in range(1, planes):
        total = total + misc_all[i]
    misc_out[mine] = total
    misc_copies = [
        remote(misc_out.at[mine], misc_out.at[mine], misc_sends.at[1, d], misc_receives.at[1, d], (plane, peer(d)))
        for d in range(1, 8)
    ]
    for copy in misc_copies:
        copy.start()
    grad, gain_part = back_through_norm(rows.total(), tokens.get()[...].astype(F32), gains[0:1, :])
    small_plane[mine] = jnp.zeros(small_plane.shape[1:], F32)
    small_plane[mine, 0:1, :] = gain_part
    small_plane[mine, 1:2, :] = second_grad[...]
    near_copies = [
        remote(small_plane.at[mine], small_plane.at[mine], small_sends.at[0, d], small_receives.at[0, d], (plane, peer(d)))
        for d in range(1, 8)
    ]
    for copy in near_copies:
        copy.start()
    input_grad[...] = (residual_grad.get()[...] + grad).astype(BF16)
    deals = exchange_start(plane, mine, feed_grad, feed_out, deal_sends.at[0], deal_receives.at[0])
    rounds(-1, 1)
    for copy in near_copies:
        copy.wait()
    total = small_plane[0]
    for i in range(1, 8):
        total = total + small_plane[i]
    small_all[plane] = total
    far_copies = [
        remote(small_all.at[plane], small_all.at[plane], small_sends.at[1, d], small_receives.at[1, d], ((plane + d) % planes, mine))
        for d in range(1, planes)
    ]
    for copy in far_copies:
        copy.start()
    rounds(-1, 2)
    keep_qkv = pltpu.make_async_copy(qkv_sum.at[mine], qkv_out.at[mine], local.at[2])
    handed = [
        remote(
            qkv_sum.at[peer(d)], qkv_out.at[mine], deal_sends.at[1, d], deal_receives.at[1, d], (plane, peer(d))
        )
        for d in range(1, 8)
    ]
    for k, fold in enumerate(folds):
        def store(value, k=k):
            count = value.shape[0] // owned
            for p in range(count):
                piece = value[owned * p : owned * (p + 1), :]
                qkv_sum[count * k + p] = piece[:, 0:three]
                at = pair * (count * k + p)
                out_w_out[0, :, at : at + pair] = piece[:, three : three + pair]

        fold.total(store)
        same = mine // 4 == k
        for d in range(1, 8):
            @pl.when(same if d < 4 else jnp.logical_not(same))
            def _():
                handed[d - 1].start()

        @pl.when(same)
        def _():
            keep_qkv.start()

    deals += handed
    rows.finish()
    for copy in far_copies:
        copy.wait()
    total = small_all[0]
    for i in range(1, planes):
        total = total + small_all[i]
    small_out[...] = total
    for copy in deals + misc_copies:
        copy.wait()
    keep_feed.wait()
    keep_qkv.wait()
    for fold in folds:
        fold.finish()


def finish_kernel(count, place, small, misc, *refs):
    ins, outs = refs[:6], refs[6 : 6 + count]
    norm_out, group_out, second_out, ker_out, mix_out = refs[6 + count : 11 + count]
    near, made = refs[11 + count : 17 + count], refs[17 + count : 17 + 2 * count - 2]
    loads, stores = refs[-2:]
    moves = [pltpu.make_async_copy(ins[i], near[i], loads.at[i]) for i in range(6)]
    for move in moves:
        move.start()
    qkv, feed, out_w, down, grad, layer = near
    groups, owned, three = qkv.shape
    pair = three // 3
    half = feed.shape[2] // 2
    results = list(made) + [grad, layer]
    out = [pltpu.make_async_copy(results[i], outs[i], stores.at[i]) for i in range(count)]
    moves[3].wait()
    made[6][...] = down[...].astype(F32)
    out[6].start()
    moves[2].wait()
    made[5][...] = out_w[0].astype(F32)
    out[5].start()
    for i in (4, 5):
        moves[i].wait()
        out[i + 3].start()
    moves[1].wait()
    for i in range(2):
        for c in range(groups):
            for s in range(half // TILE):
                at = TILE * (groups * s + c)
                made[3 + i][:, at : at + TILE] = feed[
                    c, :, half * i + TILE * s : half * i + TILE * (s + 1)
                ].astype(F32)
        out[3 + i].start()
    moves[0].wait()
    for i in range(3):
        for c in range(groups):
            made[i][:, pair * c : pair * (c + 1)] = qkv[c, :, pair * i : pair * (i + 1)].astype(F32)
        out[i].start()
    flat = place[0]
    width = small.shape[1]
    turned = pltpu.roll(small[...], (width - owned * flat) % width, 1)
    norm_out[...] = turned[0:1, 0:owned]
    second_out[...] = turned[1:2, 0:owned]
    rows = misc[flat // 4]
    wide = rows.shape[1]
    turned = pltpu.roll(rows, (wide - owned * (flat % 4)) % wide, 1)
    group_out[...] = turned[16:17, 0:owned]
    heads = [(c, h) for c in range(groups) for h in range(2)]
    for a in range(ker_out.shape[1]):
        rows = jnp.concatenate([misc[c, 8 * h + a : 8 * h + a + 1, 0:TILE] for c, h in heads], axis=0)
        ker_out[:, a, :] = rows.T[0 : ker_out.shape[0], :]
    for p in range(2):
        sums = [
            jnp.sum(misc[c, 17 + p : 18 + p, pair // 2 * h : pair // 2 * (h + 1)], axis=1, keepdims=True)
            for c, h in heads
        ]
        mix_out[p : p + 1, :] = jnp.broadcast_to(jnp.concatenate(sums, axis=0), (len(heads), TILE)).T[0:1, :]
    for copy in out:
        copy.wait()


DMA = pltpu.SemaphoreType.DMA
ANYWHERE = pl.BlockSpec(memory_space=pl.ANY)
ON_CHIP = pl.BlockSpec(memory_space=pltpu.VMEM)


def communicate(kernel, name, number, micros, outs, scratch, args, spec, specs=None, out_specs=None):
    return pl.pallas_call(
        kernel,
        name=name,
        out_shape=tuple(jax.ShapeDtypeStruct(shape, kind) for shape, kind in outs),
        in_specs=specs or [spec] * len(args),
        out_specs=out_specs or (spec,) * len(outs),
        scratch_shapes=scratch,
        compiler_params=pltpu.CompilerParams(
            collective_id=number, has_side_effects=True, vmem_limit_bytes=56 << 20
        ),
        cost_estimate=pl.CostEstimate(flops=0, transcendentals=0, bytes_accessed=micros * 3500000),
    )(*args)


def sum_scratch(rows, width):
    return [
        pltpu.VMEM((4, rows, width), BF16),
        pltpu.VMEM((4, rows, width), F32),
        pltpu.VMEM((4, rows, width), BF16),
        pltpu.VMEM((4, rows, width), BF16),
        pltpu.VMEM((2, rows, width), BF16),
        pltpu.VMEM((2, rows // 2, width), BF16),
        DMA((10,)),
        DMA((10,)),
    ]


PRECISE = lax.Precision.HIGHEST


def normalize(values):
    factor = lax.rsqrt(jnp.mean(values * values, axis=-1, keepdims=True) + EPSILON)
    return (values * factor, factor)


def normalize_back(normed, factor, gain, upstream):
    gain_grad = jnp.sum(upstream * normed, axis=0)
    scaled = upstream * gain
    return (
        factor * (scaled - normed * jnp.mean(scaled * normed, axis=-1, keepdims=True)),
        gain_grad,
    )


def add_rows(target, update, offset):
    current = lax.dynamic_slice_in_dim(target, offset, update.shape[0], 0)
    return lax.dynamic_update_slice_in_dim(target, current + update, offset, 0)


def masked_scores(query_ext, key_pad, offset, row_pos, layout):
    block_rows, halo_rows, key_reach, key_block, groups, score_scale = layout
    extent = key_block + 4 * key_reach
    key_slab = lax.dynamic_slice_in_dim(key_pad, offset, extent, 0)
    raw_scores = (
        jnp.einsum("nrhd,khd->nhrk", query_ext, key_slab, preferred_element_type=jnp.float32)
        * score_scale
    )
    key_pos = offset - 2 * key_reach + jnp.arange(extent, dtype=jnp.int32)
    keep_mask = (key_pos[None, None, :] <= row_pos[:, :, None]) & (key_pos >= 0)[None, None, :]
    return jnp.where(keep_mask[:, None], raw_scores, 0.0)


def convolve(zeroed, kernel, shift, extent, layout):
    block_rows, halo_rows, key_reach = (layout[0], layout[1], layout[2])
    result = jnp.zeros(zeroed.shape[:2] + (block_rows, extent), jnp.float32)
    for row_tap in range(halo_rows + 1):
        for key_tap in range(2 * key_reach + 1):
            column = shift + 3 * key_reach - key_tap
            result = (
                result
                + kernel[:, row_tap, key_tap][None, :, None, None]
                * zeroed[
                    :,
                    :,
                    halo_rows - row_tap : halo_rows - row_tap + block_rows,
                    column : column + extent,
                ]
            )
    return result


def attend_forward(query_ext, row_pos, key_pad, value_pad, kernel, layout):
    block_rows, halo_rows, key_reach, key_block, groups, score_scale = layout
    members = query_ext.shape[0]
    head_count = query_ext.shape[2]
    pair_width = value_pad.shape[1] // groups
    block_count = jnp.max(row_pos) // key_block + 1

    def advance(position, carried):
        running_max, running_sum, gathered = carried
        offset = position * key_block
        zeroed = masked_scores(query_ext, key_pad, offset, row_pos, layout)
        logits = convolve(zeroed, kernel, 0, key_block, layout)
        key_pos = offset + jnp.arange(key_block, dtype=jnp.int32)
        valid_mask = key_pos[None, None, :] <= row_pos[:, halo_rows:, None]
        logits = jnp.where(valid_mask[:, None], logits, NEGATIVE)
        new_max = jnp.maximum(running_max, jnp.max(logits, axis=-1))
        shrink = jnp.exp(running_max - new_max)
        weights = jnp.exp(logits - new_max[..., None])
        running_sum = running_sum * shrink + jnp.sum(weights, axis=-1)
        value_slab = lax.dynamic_slice_in_dim(
            value_pad, offset + 2 * key_reach, key_block, 0
        ).reshape(key_block, groups, pair_width)
        low_weights = weights.astype(jnp.bfloat16).reshape(
            members, groups, 2, block_rows, key_block
        )
        gathered = gathered * shrink.reshape(members, groups, 2, block_rows, 1) + jnp.einsum(
            "ngpik,kgc->ngpic", low_weights, value_slab, preferred_element_type=jnp.float32
        )
        return (new_max, running_sum, gathered)

    initial = (
        jnp.full((members, head_count, block_rows), NEGATIVE, jnp.float32),
        jnp.zeros((members, head_count, block_rows), jnp.float32),
        jnp.zeros((members, groups, 2, block_rows, pair_width), jnp.float32),
    )
    running_max, running_sum, gathered = lax.fori_loop(0, block_count, advance, initial)
    mixed_in = gathered / running_sum.reshape(members, groups, 2, block_rows, 1)
    return (mixed_in, running_max + jnp.log(running_sum))


def attend_backward(
    query_ext,
    row_pos,
    key_pad,
    value_pad,
    kernel,
    log_total,
    mixed_low,
    delta_rows,
    key_acc,
    value_acc,
    layout,
):
    block_rows, halo_rows, key_reach, key_block, groups, score_scale = layout
    members = query_ext.shape[0]
    ext_rows = query_ext.shape[1]
    head_count = query_ext.shape[2]
    model_width = value_pad.shape[1]
    pair_width = model_width // groups
    extent = key_block + 2 * key_reach
    block_count = jnp.max(row_pos) // key_block + 1

    def advance(position, carried):
        query_grad, key_acc, value_acc, kernel_grad = carried
        offset = position * key_block
        zeroed = masked_scores(query_ext, key_pad, offset, row_pos, layout)
        logits = convolve(zeroed, kernel, -key_reach, extent, layout)
        key_pos = offset - key_reach + jnp.arange(extent, dtype=jnp.int32)
        valid_mask = (key_pos[None, None, :] <= row_pos[:, halo_rows:, None]) & (key_pos >= 0)[
            None, None, :
        ]
        probability = jnp.where(valid_mask[:, None], jnp.exp(logits - log_total[..., None]), 0.0)
        value_slab = lax.dynamic_slice_in_dim(value_pad, offset + key_reach, extent, 0).reshape(
            extent, groups, pair_width
        )
        prob_grad = jnp.einsum(
            "ngpic,kgc->ngpik", mixed_low, value_slab, preferred_element_type=jnp.float32
        ).reshape(members, head_count, block_rows, extent)
        logit_grad = probability * (prob_grad - delta_rows[..., None])
        central = (
            probability[..., key_reach : key_reach + key_block]
            .astype(jnp.bfloat16)
            .reshape(members, groups, 2, block_rows, key_block)
        )
        value_part = jnp.einsum(
            "ngpik,ngpic->kgc", central, mixed_low, preferred_element_type=jnp.float32
        ).reshape(key_block, model_width)
        value_acc = add_rows(value_acc, value_part, offset)
        middle = logit_grad[..., key_reach : key_reach + key_block]
        tap_sums = []
        for row_tap in range(halo_rows + 1):
            for key_tap in range(2 * key_reach + 1):
                column = 3 * key_reach - key_tap
                tap_sums.append(
                    jnp.sum(
                        middle
                        * zeroed[
                            :,
                            :,
                            halo_rows - row_tap : halo_rows - row_tap + block_rows,
                            column : column + key_block,
                        ],
                        axis=(0, 2, 3),
                    )
                )
        kernel_grad = kernel_grad + jnp.stack(tap_sums, axis=1).reshape(
            head_count, halo_rows + 1, 2 * key_reach + 1
        )
        padded = jnp.pad(logit_grad, ((0, 0), (0, 0), (halo_rows, halo_rows), (0, 0)))
        score_grad = jnp.zeros((members, head_count, ext_rows, key_block), jnp.float32)
        for row_tap in range(halo_rows + 1):
            for key_tap in range(2 * key_reach + 1):
                score_grad = (
                    score_grad
                    + kernel[:, row_tap, key_tap][None, :, None, None]
                    * padded[:, :, row_tap : row_tap + ext_rows, key_tap : key_tap + key_block]
                )
        key_central = offset + jnp.arange(key_block, dtype=jnp.int32)
        keep_mask = (key_central[None, None, :] <= row_pos[:, :, None]) & (key_central >= 0)[
            None, None, :
        ]
        score_low = jnp.where(keep_mask[:, None], score_grad, 0.0).astype(jnp.bfloat16)
        key_slab = lax.dynamic_slice_in_dim(key_pad, offset + 2 * key_reach, key_block, 0)
        query_grad = (
            query_grad
            + jnp.einsum("nhrk,khd->nrhd", score_low, key_slab, preferred_element_type=jnp.float32)
            * score_scale
        )
        key_part = (
            jnp.einsum(
                "nhrk,nrhd->khd", score_low, query_ext, preferred_element_type=jnp.float32
            ).reshape(key_block, model_width)
            * score_scale
        )
        key_acc = add_rows(key_acc, key_part, offset)
        return (query_grad, key_acc, value_acc, kernel_grad)

    initial = (
        jnp.zeros(query_ext.shape, jnp.float32),
        key_acc,
        value_acc,
        jnp.zeros(kernel.shape, jnp.float32),
    )
    return lax.fori_loop(0, block_count, advance, initial)


def reorder(selection, rows):
    return jnp.dot(
        selection.astype(rows.dtype), rows, precision=PRECISE, preferred_element_type=jnp.float32
    ).astype(rows.dtype)


def pick(table, places):
    return jnp.stack(
        [lax.dynamic_index_in_dim(table, places[i], 0, keepdims=False) for i in range(2)]
    )


def accumulate(previous, update):
    return (
        update
        if previous is None
        else tuple((left + right for left, right in zip(previous, update)))
    )


def general_device(
    inputs,
    out_grad,
    pair_index,
    norm_gain,
    query_weight,
    key_weight,
    value_weight,
    score_kernel,
    head_mixing,
    group_gain,
    output_weight,
    second_gain,
    gate_weight,
    up_weight,
    down_weight,
):
    micro_count = inputs.shape[0]
    local_rows = inputs.shape[2]
    block_rows = local_rows // 2
    model_width = inputs.shape[3]
    head_count = score_kernel.shape[0]
    head_dim = model_width // head_count
    groups = head_count // 2
    halo_rows = score_kernel.shape[1] - 1
    key_reach = (score_kernel.shape[2] - 1) // 2
    block_count = 2 * lax.axis_size("ctx")
    seq_length = block_count * block_rows
    key_block = min(512, seq_length)
    layout = (block_rows, halo_rows, key_reach, key_block, groups, head_dim ** (-0.5))
    extended = block_rows + halo_rows
    my_index = lax.axis_index("ctx")
    slot_ids = jnp.arange(block_count, dtype=jnp.int32)
    mix_table = head_mixing.reshape(groups, 2, 2)
    pad_width = ((2 * key_reach, 2 * key_reach), (0, 0))
    layer_rows = []
    input_rows = []
    feed_sums = None
    attention_sums = None
    kernel_total = jnp.zeros(score_kernel.shape, jnp.float32)
    mixing_total = jnp.zeros(head_mixing.shape, jnp.float32)
    for batch_index in range(micro_count):
        gain_first, query_full, key_full, value_full, gain_group, out_full = (
            lax.all_gather(norm_gain, ("seq", "ctx"), axis=0, tiled=True),
            lax.all_gather(query_weight, ("seq", "ctx"), axis=0, tiled=True),
            lax.all_gather(key_weight, ("seq", "ctx"), axis=0, tiled=True),
            lax.all_gather(value_weight, ("seq", "ctx"), axis=0, tiled=True),
            lax.all_gather(group_gain, ("seq", "ctx"), axis=0, tiled=True),
            lax.all_gather(output_weight, ("seq", "ctx"), axis=0, tiled=True),
        )
        tokens = inputs[batch_index, 0].astype(jnp.float32)
        normed_first, factor_first = normalize(tokens)
        hidden = (normed_first * gain_first.astype(jnp.float32)).astype(jnp.bfloat16)
        query_proj = jnp.dot(hidden, query_full, preferred_element_type=jnp.float32).astype(
            jnp.bfloat16
        )
        key_proj = jnp.dot(hidden, key_full, preferred_element_type=jnp.float32).astype(
            jnp.bfloat16
        )
        value_proj = jnp.dot(hidden, value_full, preferred_element_type=jnp.float32).astype(
            jnp.bfloat16
        )
        tail_rows = jnp.concatenate(
            [query_proj[block_rows - halo_rows : block_rows], query_proj[local_rows - halo_rows :]],
            axis=0,
        )
        key_dealt, value_dealt, tail_dealt = (
            lax.all_gather(key_proj, "ctx", axis=0, tiled=True),
            lax.all_gather(value_proj, "ctx", axis=0, tiled=True),
            lax.all_gather(tail_rows, "ctx", axis=0, tiled=True),
        )
        pairs_row = pair_index[batch_index]
        owner_pair = jnp.repeat(pairs_row, 2)
        block_of_slot = jnp.where(slot_ids % 2 == 0, owner_pair, block_count - 1 - owner_pair)
        to_natural = (block_of_slot[None, :] == slot_ids[:, None]).astype(jnp.float32)
        slot_of_block = jnp.sum(
            jnp.where(block_of_slot[None, :] == slot_ids[:, None], slot_ids[None, :], 0), axis=1
        )
        my_pair = lax.dynamic_index_in_dim(pairs_row, my_index, 0, keepdims=False)
        my_blocks = jnp.stack([my_pair, block_count - 1 - my_pair])
        key_pad = jnp.pad(
            reorder(to_natural, key_dealt.reshape(block_count, -1)).reshape(
                seq_length, model_width
            ),
            pad_width,
        ).reshape(-1, head_count, head_dim)
        value_pad = jnp.pad(
            reorder(to_natural, value_dealt.reshape(block_count, -1)).reshape(
                seq_length, model_width
            ),
            pad_width,
        )
        tail_blocks = reorder(to_natural, tail_dealt.reshape(block_count, -1)).reshape(
            block_count, halo_rows, model_width
        )
        previous = jnp.concatenate(
            [jnp.zeros((1, halo_rows, model_width), jnp.bfloat16), tail_blocks[:-1]], axis=0
        )
        query_ext = jnp.concatenate(
            [pick(previous, my_blocks), query_proj.reshape(2, block_rows, model_width)], axis=1
        ).reshape(2, extended, head_count, head_dim)
        row_pos = (
            my_blocks[:, None] * block_rows
            - halo_rows
            + jnp.arange(extended, dtype=jnp.int32)[None, :]
        )
        mixed_in, log_total = attend_forward(
            query_ext, row_pos, key_pad, value_pad, score_kernel, layout
        )
        mixed_six = mixed_in.reshape(2, groups, 2, block_rows, 2, head_dim)
        heads_out = jnp.einsum(
            "gqp,ngpiqd->nigqd", mix_table, mixed_six, precision=PRECISE
        ).reshape(local_rows, head_count, head_dim)
        group_normed, group_factor = normalize(heads_out)
        normed_low = (
            group_normed.reshape(local_rows, model_width) * gain_group.astype(jnp.float32)
        ).astype(jnp.bfloat16)
        residual = tokens + jnp.dot(normed_low, out_full, preferred_element_type=jnp.float32)
        gain_second, gate_full, up_full, down_full = (
            lax.all_gather(second_gain, ("seq", "ctx"), axis=0, tiled=True),
            lax.all_gather(gate_weight, ("seq", "ctx"), axis=0, tiled=True),
            lax.all_gather(up_weight, ("seq", "ctx"), axis=0, tiled=True),
            lax.all_gather(down_weight, ("seq", "ctx"), axis=0, tiled=True),
        )
        normed_second, factor_second = normalize(residual)
        second_hidden = (normed_second * gain_second.astype(jnp.float32)).astype(jnp.bfloat16)
        gate_proj = jnp.dot(second_hidden, gate_full, preferred_element_type=jnp.float32)
        up_proj = jnp.dot(second_hidden, up_full, preferred_element_type=jnp.float32)
        activated = (jax.nn.silu(gate_proj) * up_proj).astype(jnp.bfloat16)
        layer_rows.append(
            (residual + jnp.dot(activated, down_full, preferred_element_type=jnp.float32)).astype(
                jnp.bfloat16
            )
        )
        gain_second, gate_full, up_full, down_full = (
            lax.all_gather(second_gain, ("seq", "ctx"), axis=0, tiled=True),
            lax.all_gather(gate_weight, ("seq", "ctx"), axis=0, tiled=True),
            lax.all_gather(up_weight, ("seq", "ctx"), axis=0, tiled=True),
            lax.all_gather(down_weight, ("seq", "ctx"), axis=0, tiled=True),
        )
        grad_rows = out_grad[batch_index, 0]
        hid_grad = jnp.dot(grad_rows, down_full.T, preferred_element_type=jnp.float32)
        down_grad = jnp.dot(activated.T, grad_rows, preferred_element_type=jnp.float32)
        sigmoid_gate = jax.nn.sigmoid(gate_proj)
        up_low = (hid_grad * gate_proj * sigmoid_gate).astype(jnp.bfloat16)
        gate_low = (
            hid_grad * up_proj * sigmoid_gate * (1.0 + gate_proj * (1.0 - sigmoid_gate))
        ).astype(jnp.bfloat16)
        second_grad = jnp.dot(gate_low, gate_full.T, preferred_element_type=jnp.float32) + jnp.dot(
            up_low, up_full.T, preferred_element_type=jnp.float32
        )
        gate_grad = jnp.dot(second_hidden.T, gate_low, preferred_element_type=jnp.float32)
        up_grad = jnp.dot(second_hidden.T, up_low, preferred_element_type=jnp.float32)
        residual_part, gain_second_grad = normalize_back(
            normed_second, factor_second, gain_second.astype(jnp.float32), second_grad
        )
        residual_grad = grad_rows.astype(jnp.float32) + residual_part
        feed_shards = (
            lax.psum_scatter(gain_second_grad, ("seq", "ctx"), scatter_dimension=0, tiled=True),
            lax.psum_scatter(gate_grad, ("seq", "ctx"), scatter_dimension=0, tiled=True),
            lax.psum_scatter(up_grad, ("seq", "ctx"), scatter_dimension=0, tiled=True),
            lax.psum_scatter(down_grad, ("seq", "ctx"), scatter_dimension=0, tiled=True),
        )
        feed_sums = accumulate(feed_sums, feed_shards)
        gain_first, query_full, key_full, value_full, gain_group, out_full = (
            lax.all_gather(norm_gain, ("seq", "ctx"), axis=0, tiled=True),
            lax.all_gather(query_weight, ("seq", "ctx"), axis=0, tiled=True),
            lax.all_gather(key_weight, ("seq", "ctx"), axis=0, tiled=True),
            lax.all_gather(value_weight, ("seq", "ctx"), axis=0, tiled=True),
            lax.all_gather(group_gain, ("seq", "ctx"), axis=0, tiled=True),
            lax.all_gather(output_weight, ("seq", "ctx"), axis=0, tiled=True),
        )
        attended_low = residual_grad.astype(jnp.bfloat16)
        out_weight_grad = jnp.dot(normed_low.T, attended_low, preferred_element_type=jnp.float32)
        normed_grad = jnp.dot(attended_low, out_full.T, preferred_element_type=jnp.float32)
        heads_grad, gain_group_grad = normalize_back(
            group_normed,
            group_factor,
            gain_group.astype(jnp.float32).reshape(head_count, head_dim),
            normed_grad.reshape(local_rows, head_count, head_dim),
        )
        heads_five = heads_grad.reshape(2, block_rows, groups, 2, head_dim)
        mixing_total = mixing_total + jnp.einsum(
            "nigqd,ngpiqd->gqp", heads_five, mixed_six, precision=PRECISE
        ).reshape(head_count, 2)
        mixed_grad = jnp.einsum(
            "gqp,nigqd->ngpiqd", mix_table, heads_five, precision=PRECISE
        ).reshape(2, groups, 2, block_rows, 2 * head_dim)
        mixed_low = mixed_grad.astype(jnp.bfloat16)
        delta_rows = jnp.sum(mixed_low.astype(jnp.float32) * mixed_in, axis=-1).reshape(
            2, head_count, block_rows
        )
        key_acc = jnp.zeros((seq_length, model_width), jnp.float32)
        value_acc = jnp.zeros((seq_length, model_width), jnp.float32)
        query_grad, key_acc, value_acc, kernel_part = attend_backward(
            query_ext,
            row_pos,
            key_pad,
            value_pad,
            score_kernel,
            log_total,
            mixed_low,
            delta_rows,
            key_acc,
            value_acc,
            layout,
        )
        kernel_total = kernel_total + kernel_part
        halo_grad = query_grad[:, :halo_rows].reshape(2, halo_rows, model_width)
        own_grad = query_grad[:, halo_rows:].reshape(2, block_rows, model_width)
        target_slot = pick(slot_of_block, jnp.maximum(my_blocks - 1, 0))
        routing = ((slot_ids[None, :] == target_slot[:, None]) & (my_blocks > 0)[:, None]).astype(
            jnp.float32
        )
        tail_grad = jnp.einsum("ws,wrc->src", routing, halo_grad, precision=PRECISE).reshape(
            block_count * halo_rows, model_width
        )
        key_back = reorder(to_natural.T, key_acc.reshape(block_count, -1)).reshape(
            seq_length, model_width
        )
        value_back = reorder(to_natural.T, value_acc.reshape(block_count, -1)).reshape(
            seq_length, model_width
        )
        key_mine, value_mine, tail_mine = (
            lax.psum_scatter(
                key_back.astype(jnp.bfloat16), "ctx", scatter_dimension=0, tiled=True
            ).astype(jnp.float32),
            lax.psum_scatter(
                value_back.astype(jnp.bfloat16), "ctx", scatter_dimension=0, tiled=True
            ).astype(jnp.float32),
            lax.psum_scatter(
                tail_grad.astype(jnp.bfloat16), "ctx", scatter_dimension=0, tiled=True
            ).astype(jnp.float32),
        )
        tail_mine = tail_mine.reshape(2, halo_rows, model_width)
        query_total = jnp.concatenate(
            [
                own_grad[:, : block_rows - halo_rows],
                own_grad[:, block_rows - halo_rows :] + tail_mine,
            ],
            axis=1,
        ).reshape(local_rows, model_width)
        query_low = query_total.astype(jnp.bfloat16)
        key_low = key_mine.astype(jnp.bfloat16)
        value_low = value_mine.astype(jnp.bfloat16)
        query_w_grad = jnp.dot(hidden.T, query_low, preferred_element_type=jnp.float32)
        key_w_grad = jnp.dot(hidden.T, key_low, preferred_element_type=jnp.float32)
        value_w_grad = jnp.dot(hidden.T, value_low, preferred_element_type=jnp.float32)
        hidden_grad = (
            jnp.dot(query_low, query_full.T, preferred_element_type=jnp.float32)
            + jnp.dot(key_low, key_full.T, preferred_element_type=jnp.float32)
            + jnp.dot(value_low, value_full.T, preferred_element_type=jnp.float32)
        )
        token_part, gain_first_grad = normalize_back(
            normed_first, factor_first, gain_first.astype(jnp.float32), hidden_grad
        )
        input_rows.append((residual_grad + token_part).astype(jnp.bfloat16))
        attention_shards = (
            lax.psum_scatter(gain_first_grad, ("seq", "ctx"), scatter_dimension=0, tiled=True),
            lax.psum_scatter(query_w_grad, ("seq", "ctx"), scatter_dimension=0, tiled=True),
            lax.psum_scatter(key_w_grad, ("seq", "ctx"), scatter_dimension=0, tiled=True),
            lax.psum_scatter(value_w_grad, ("seq", "ctx"), scatter_dimension=0, tiled=True),
            lax.psum_scatter(
                gain_group_grad.reshape(model_width),
                ("seq", "ctx"),
                scatter_dimension=0,
                tiled=True,
            ),
            lax.psum_scatter(out_weight_grad, ("seq", "ctx"), scatter_dimension=0, tiled=True),
        )
        attention_sums = accumulate(attention_sums, attention_shards)
    kernel_sum, mixing_sum = lax.psum((kernel_total, mixing_total), ("seq", "ctx"))
    layer_out = jnp.stack(layer_rows)[:, None]
    input_grad = jnp.stack(input_rows)[:, None]
    return (
        layer_out,
        input_grad,
        attention_sums[0],
        attention_sums[1],
        attention_sums[2],
        attention_sums[3],
        kernel_sum,
        mixing_sum,
        attention_sums[4],
        attention_sums[5],
        feed_sums[0],
        feed_sums[1],
        feed_sums[2],
        feed_sums[3],
    )


def on_device(
    inputs,
    out_grad,
    pair_index,
    norm_gain,
    query_weight,
    key_weight,
    value_weight,
    score_kernel,
    head_mixing,
    group_gain,
    output_weight,
    second_gain,
    gate_weight,
    up_weight,
    down_weight,
):
    groups, planes = lax.axis_size("ctx"), lax.axis_size("seq")
    heads, width = score_kernel.shape[0], inputs.shape[3]
    if groups != 8 or heads != 2 * groups or (groups * inputs.shape[2]) % TILE:
        return general_device(
            inputs, out_grad, pair_index, norm_gain, query_weight, key_weight, value_weight,
            score_kernel, head_mixing, group_gain, output_weight, second_gain, gate_weight,
            up_weight, down_weight,
        )
    micro, local = inputs.shape[0], inputs.shape[2]
    blk, seq = local // 2, local * groups
    blocks = seq // blk
    pair = width // groups
    owned = width // (groups * planes)
    hidden = gate_weight.shape[1]
    chunk = hidden // (groups * planes)
    me = lax.axis_index("ctx")
    tokens_low = inputs.reshape(micro * local, width)
    grads_low = out_grad.reshape(micro * local, width)

    rows_all = micro * local
    qkv_shape = (groups, owned, 3 * pair)
    feed_shape = (groups, owned, 2 * planes * chunk)
    gain_rows = jnp.stack([norm_gain, group_gain, second_gain])
    spread_sems = [DMA((9,))] * 2
    feed_mine, qkv, gains, all_tokens, out_rows = communicate(
        functools.partial(enter_kernel, planes), "enter", 1, 50,
        [
            (feed_shape, BF16),
            ((planes,) + qkv_shape, BF16),
            ((planes, groups, 8, TILE), F32),
            ((groups, rows_all, width), BF16),
            ((planes, owned, width), BF16),
        ],
        [pltpu.VMEM((owned, width), BF16)] * 3 + [pltpu.VMEM((owned, hidden), BF16)] * 2
        + [pltpu.VMEM((3, owned), BF16), pltpu.VMEM((8, TILE), F32)]
        + [pltpu.VMEM(qkv_shape, BF16), pltpu.VMEM(feed_shape, BF16)]
        + [DMA((3, groups))] * 2 + spread_sems + [DMA((1, 2, planes))] * 2
        + [DMA((2, 2, planes))] * 2 + [DMA((11,))],
        (
            query_weight, key_weight, value_weight, gate_weight, up_weight, gain_rows, tokens_low,
            output_weight,
        ),
        ANYWHERE,
    )
    all_tokens, down_mine = lax.optimization_barrier((all_tokens, down_weight))
    feed = lax.all_gather(feed_mine.reshape(groups * owned, -1), "seq", axis=0, tiled=True)
    down = lax.all_gather(down_mine, "seq", axis=0, tiled=True)
    qkv = qkv.reshape(width, 3 * pair)
    hidden_all, heads_in, gains, gain_pair, out_rows, all_grads = communicate(
        functools.partial(heads_kernel, planes), "heads", 2, 20,
        [
            ((width, groups * rows_all), BF16),
            ((groups * rows_all, 3 * pair), BF16),
            ((8, width), F32),
            ((8, pair), F32),
            ((4, owned, width), BF16),
            ((groups, rows_all, width), BF16),
        ],
        [
            pltpu.VMEM((groups, rows_all, width), BF16),
            pltpu.VMEM((width, 3 * pair), BF16),
            pltpu.VMEM((width, groups * rows_all), BF16),
            pltpu.VMEM((groups * rows_all, 3 * pair), BF16),
        ]
        + [DMA((4,))] * 2 + spread_sems + [DMA((groups + 1,)), DMA((2, groups)), DMA((2,))],
        (all_tokens, qkv, gains, out_rows, grads_low),
        None, [ANYWHERE] * 2 + [ON_CHIP] + [ANYWHERE] * 2, (ANYWHERE,) * 2 + (ON_CHIP,) * 2 + (ANYWHERE,) * 2,
    )
    all_grads = all_grads.reshape(-1, width)
    out_rows = out_rows.reshape(pair, width)

    slots = jnp.arange(blocks, dtype=jnp.int32)
    owner = jnp.repeat(pair_index, 2, axis=1)
    block_of_slot = jnp.where(slots % 2 == 0, owner, blocks - 1 - owner)
    place = (
        (slots // 2)[None] * (2 * micro)
        + 2 * jnp.arange(micro, dtype=jnp.int32)[:, None]
        + (slots % 2)[None]
    )
    blk_table = jnp.sum(
        jnp.where(block_of_slot[:, None, :] == slots[None, :, None], place[:, None, :], 0), axis=2
    ).astype(jnp.int32)
    ker = lax.dynamic_slice_in_dim(score_kernel, 2 * me, 2, 0)
    mix = jnp.repeat(lax.dynamic_slice_in_dim(head_mixing, 2 * me, 2, 0), pair // 2, axis=0).T
    scale = (width // heads) ** (-0.5)

    mixed, y, prob = pair_forward(blk_table, ker, mix, gain_pair, heads_in, micro, seq, blk, scale)
    by_core = (groups // 2, 2, rows_all)
    sum_spec = sum_scratch(rows_all, width)
    residual, second_all = communicate(
        second_kernel, "second", 3, 40,
        [((rows_all, width), F32), ((groups, rows_all, width), BF16)],
        [
            pltpu.VMEM(by_core + (pair,), BF16),
            pltpu.VMEM((pair, width), BF16),
            pltpu.VMEM((rows_all, width), BF16),
            pltpu.VMEM((rows_all, width), F32),
            pltpu.VMEM((rows_all, width), BF16),
            DMA((5,)),
        ]
        + sum_spec + spread_sems,
        (mixed.reshape(by_core + (pair,)), out_rows, tokens_low, gains),
        None, [ANYWHERE] * 3 + [ON_CHIP], (ANYWHERE,) * 2,
    )
    second_all = second_all.reshape(-1, width)

    half = planes * chunk
    both = jnp.dot(second_all, feed, preferred_element_type=F32)
    gate, up = both[:, :half], both[:, half:]
    sigmoid = jax.nn.sigmoid(gate)
    active = (gate * sigmoid * up).astype(BF16)
    slopes = jnp.concatenate(
        [up * sigmoid * (1.0 + gate * (1.0 - sigmoid)), gate * sigmoid], axis=1
    )
    down_grad = lax.dot_general(active, all_grads, (((0,), (0,)), ((), ())), preferred_element_type=F32)
    all_grads, down_grad, slopes = lax.optimization_barrier((all_grads, down_grad.astype(BF16), slopes))
    hid_grad = lax.dot_general(all_grads, down, (((1,), (1,)), ((), ())), preferred_element_type=F32)
    lows = (jnp.concatenate([hid_grad, hid_grad], axis=1) * slopes).astype(BF16)
    feed_grad = lax.dot_general(second_all, lows, (((0,), (0,)), ((), ())), preferred_element_type=F32)
    lows, feed_grad = lax.optimization_barrier((lows, feed_grad.astype(BF16)))
    feed_sum = lax.psum_scatter(feed_grad, "seq", scatter_dimension=0, tiled=True)
    down_sum = lax.psum_scatter(down_grad, "seq", scatter_dimension=0, tiled=True)
    residual_grad, gain_second_grad, mixed_grad, out_w_grad = communicate(
        back_kernel, "back", 4, 42,
        [
            ((rows_all, width), F32),
            ((1, width), F32),
            ((groups, rows_all, pair), BF16),
            ((pair, width), BF16),
        ],
        [
            pltpu.VMEM(by_core + (2 * half,), BF16),
            pltpu.VMEM((width, 2 * half), BF16),
            pltpu.VMEM((rows_all, width), F32),
            pltpu.VMEM((rows_all, width), BF16),
            pltpu.VMEM((pair, width), BF16),
            pltpu.VMEM((groups, rows_all, pair), BF16),
            pltpu.VMEM((rows_all, width), F32),
            pltpu.VMEM((groups, rows_all, width), BF16),
            pltpu.VMEM((pair, width), F32),
            DMA((7,)),
        ]
        + sum_spec + spread_sems,
        (
            lows.reshape(by_core + (2 * half,)), feed, residual, grads_low, out_rows,
            mixed.reshape(groups, rows_all, pair), gains,
        ),
        None, [ANYWHERE] * 6 + [ON_CHIP], (ANYWHERE, ON_CHIP, ON_CHIP, ON_CHIP),
    )
    mixed_grad = mixed_grad.reshape(-1, pair)
    mixed_grad, down_sum = lax.optimization_barrier((mixed_grad, down_sum))
    qkv_low, misc = pair_backward(
        blk_table, ker, mix, gain_pair, heads_in, mixed_grad, y, prob, seq, blk, scale
    )
    small = (8, width)
    layer_out, row_grad = communicate(
        layer_kernel, "layer", 6, 18, [((rows_all, width), BF16), ((planes, owned, width), BF16)],
        [
            pltpu.VMEM(by_core + (half,), BF16),
            pltpu.VMEM((half, width), BF16),
            pltpu.VMEM((rows_all, width), F32),
            DMA((3,)),
        ]
        + sum_spec + [DMA((4,))] * 2 + [DMA],
        (
            active.reshape(by_core + (half,)), down, residual,
            out_w_grad.reshape(4, owned, width),
        ),
        None, [ANYWHERE] * 4, (ON_CHIP, ANYWHERE),
    )
    input_grad, sums, misc, qkv_back, feed_back, out_w_back = communicate(
        functools.partial(leave_kernel, planes), "leave", 5, 55,
        [
            ((rows_all, width), BF16),
            (small, F32),
            ((groups,) + misc.shape, F32),
            (qkv_shape, BF16),
            (feed_shape, BF16),
            ((1, owned, width), BF16),
        ],
        [
            pltpu.VMEM(by_core + (3 * pair,), BF16),
            pltpu.VMEM((width, 3 * pair), BF16),
            pltpu.VMEM(hidden_all.shape, BF16),
            pltpu.VMEM((rows_all, width), F32),
            pltpu.VMEM((rows_all, width), BF16),
            DMA((5,)),
            pltpu.VMEM((planes,) + misc.shape, F32),
            DMA((2, groups)),
            DMA((2, groups)),
        ]
        + sum_spec[:6]
        + [pltpu.VMEM((groups,) + small, F32), pltpu.VMEM((planes,) + small, F32)]
        + [pltpu.VMEM((planes, groups * owned, 4 * pair), BF16)]
        + [pltpu.VMEM((2, planes, groups * owned, 4 * pair), BF16)] * 2
        + [pltpu.VMEM(qkv_shape, BF16)]
        + sum_spec[6:]
        + [DMA((2, groups))] * 2
        + [DMA((2, 2, planes))] * 2
        + [DMA((2, groups))] * 2
        + [DMA((3,))],
        (
            qkv_low.reshape(by_core + (3 * pair,)), qkv, hidden_all,
            residual_grad, tokens_low, gains, gain_second_grad, misc,
            feed_sum.reshape(feed_shape), row_grad,
        ),
        None, [ANYWHERE] * 5 + [ON_CHIP] * 3 + [ANYWHERE, ON_CHIP],
        (ON_CHIP,) * 3 + (ANYWHERE,) * 2 + (ON_CHIP,),
    )
    plain = [(owned, width)] * 3 + [(owned, hidden)] * 2 + [(owned, width), (chunk, width)]
    landed = (qkv_back, feed_back, out_w_back, down_sum, input_grad, layer_out)
    out_shapes = [jax.ShapeDtypeStruct(shape, F32) for shape in plain]
    out_shapes += [jax.ShapeDtypeStruct((rows_all, width), BF16)] * 2
    row = jax.ShapeDtypeStruct((1, owned), F32)
    flat_index = (lax.axis_index("seq") * groups + me).astype(jnp.int32).reshape(1)
    results = pl.pallas_call(
        functools.partial(finish_kernel, len(out_shapes)),
        name="finish",
        out_shape=tuple(out_shapes)
        + (row, row, row)
        + (jax.ShapeDtypeStruct(score_kernel.shape[::-1], F32), jax.ShapeDtypeStruct((2, heads), F32)),
        in_specs=[pl.BlockSpec(memory_space=pltpu.SMEM)] + [ON_CHIP] * 2 + [ANYWHERE] * 6,
        out_specs=(ANYWHERE,) * len(out_shapes) + (ON_CHIP,) * 5,
        scratch_shapes=[pltpu.VMEM(value.shape, BF16) for value in landed]
        + [pltpu.VMEM(shape, F32) for shape in plain]
        + [DMA((6,)), DMA((len(out_shapes),))],
        compiler_params=pltpu.CompilerParams(vmem_limit_bytes=60 << 20),
    )(flat_index, sums, misc, *landed)
    q_back, k_back, v_back, gate_back, up_back, out_w_out, down_out, input_grad, layer_out = results[:9]
    gain_outs = [value.reshape(owned) for value in results[9:12]]
    ker_out, mix_out = jnp.transpose(results[12], (2, 1, 0)), results[13].T

    shape = inputs.shape
    return (
        layer_out.reshape(shape),
        input_grad.reshape(shape),
        gain_outs[0],
        q_back,
        k_back,
        v_back,
        ker_out,
        mix_out,
        gain_outs[1],
        out_w_out,
        gain_outs[2],
        gate_back,
        up_back,
        down_out,
    )


def solution(mesh):
    placed = (
        P(None, "seq", "ctx", None),
        P(None, "seq", "ctx", None),
        P(),
        P(("seq", "ctx")),
        P(("seq", "ctx"), None),
        P(("seq", "ctx"), None),
        P(("seq", "ctx"), None),
        P(),
        P(),
        P(("seq", "ctx")),
        P(("seq", "ctx"), None),
        P(("seq", "ctx")),
        P(("seq", "ctx"), None),
        P(("seq", "ctx"), None),
        P(("seq", "ctx"), None),
    )
    return jax.shard_map(
        on_device,
        mesh=mesh,
        in_specs=placed,
        out_specs=(
            P(None, "seq", "ctx", None),
            P(None, "seq", "ctx", None),
            P(("seq", "ctx")),
            P(("seq", "ctx"), None),
            P(("seq", "ctx"), None),
            P(("seq", "ctx"), None),
            P(),
            P(),
            P(("seq", "ctx")),
            P(("seq", "ctx"), None),
            P(("seq", "ctx")),
            P(("seq", "ctx"), None),
            P(("seq", "ctx"), None),
            P(("seq", "ctx"), None),
        ),
        check_vma=False,
    )
```

```python
import functools

import jax
import jax.numpy as jnp
from jax import lax
from jax.experimental import pallas as pl
from jax.experimental.pallas import tpu as pltpu
from jax.sharding import PartitionSpec as P

EPSILON = 1e-05
NEGATIVE = -1e30
F32 = jnp.float32
BF16 = jnp.bfloat16
TILE = 128


def nt(left, right):
    return lax.dot_general(left, right, (((1,), (1,)), ((), ())), preferred_element_type=F32)


def tn(left, right):
    return lax.dot_general(left, right, (((0,), (0,)), ((), ())), preferred_element_type=F32)


def nn(left, right):
    return lax.dot_general(left, right, (((1,), (0,)), ((), ())), preferred_element_type=F32)


def natural_rows(blk_ref, m, blk, seq):
    return [pl.multiple_of(blk_ref[m, b] * blk, blk) for b in range(seq // blk)]


def head_lanes(width):
    return lax.broadcasted_iota(jnp.int32, (1, width), 1) < width // 2


def load_heads(blk_ref, m, blk, seq, qkv_ref, qm, kf, ks, vn):
    width = vn.shape[1]
    first = head_lanes(width)
    kf[0:8, :] = jnp.zeros((8, width), F32)
    kf[seq : seq + TILE + 8, :] = jnp.zeros((TILE + 8, width), F32)
    for b, row in enumerate(natural_rows(blk_ref, m, blk, seq)):
        here = pl.ds(blk * b, blk)
        q = qkv_ref[pl.ds(row, blk), 0:width].astype(F32)
        qm[0, here, :] = jnp.where(first, q, 0.0).astype(BF16)
        qm[1, here, :] = jnp.where(first, 0.0, q).astype(BF16)
        kf[pl.ds(blk * b + 5, blk), :] = qkv_ref[pl.ds(row, blk), width : 2 * width].astype(F32)
        vn[here, :] = qkv_ref[pl.ds(row, blk), 2 * width : 3 * width]
    ks[...] = kf[0 : seq + TILE, :].astype(BF16)


def scores(qm, ks, h, rb, upto, scale):
    rows = pl.ds(TILE * rb, TILE)
    raw = nt(qm[h, rows, :], ks[0 : TILE * upto, :]) * scale
    key = lax.broadcasted_iota(jnp.int32, raw.shape, 1) - 5
    row = lax.broadcasted_iota(jnp.int32, raw.shape, 0) + TILE * rb
    return jnp.where((key >= 0) & (key <= row), raw, 0.0)


def head_factor(values, first, dim):
    squares = values * values
    own = jnp.sum(jnp.where(first, squares, 0.0), axis=1, keepdims=True)
    other = jnp.sum(jnp.where(first, 0.0, squares), axis=1, keepdims=True)
    return jnp.where(
        first, lax.rsqrt(own / dim + EPSILON), lax.rsqrt(other / dim + EPSILON)
    )


def forward_kernel(
    seq, blk, rows_tap, keys_tap, scale,
    blk_ref, ker_ref, mix_ref, gain_ref, qkv_ref,
    z_ref, y_ref, p_ref,
    qm, kf, ks, vn, shi, slo, thi, tlo, run, logit,
):
    m = pl.program_id(0)
    width = vn.shape[1]
    first = head_lanes(width)
    tiles = seq // TILE

    @pl.when(m == 0)
    def _():
        shi[...] = jnp.zeros(shi.shape, BF16)
        slo[...] = jnp.zeros(slo.shape, BF16)
        away = lax.broadcasted_iota(jnp.int32, (2 * TILE, TILE), 0) - lax.broadcasted_iota(
            jnp.int32, (2 * TILE, TILE), 1
        )
        for h in range(2):
            for a in range(rows_tap):
                band = jnp.zeros((2 * TILE, TILE), F32)
                for t in range(keys_tap):
                    band = jnp.where(away == keys_tap - 1 - t, ker_ref[h, a, t], band)
                high = band.astype(BF16)
                thi[h, :, TILE * a : TILE * (a + 1)] = high
                tlo[h, :, TILE * a : TILE * (a + 1)] = (band - high.astype(F32)).astype(BF16)

    load_heads(blk_ref, m, blk, seq, qkv_ref, qm, kf, ks, vn)
    for h in range(2):
        for rb in range(tiles):
            upto = min(rb + 2, tiles + 1)
            zeroed = scores(qm, ks, h, rb, upto, scale)
            high = zeroed.astype(BF16)
            shi[pl.ds(16 + TILE * rb, TILE), 0 : TILE * upto] = high
            slo[pl.ds(16 + TILE * rb, TILE), 0 : TILE * upto] = (zeroed - high.astype(F32)).astype(BF16)
        for b in range(tiles):
            count = seq - TILE * b
            rows = pl.ds(TILE * b, count + 16)
            lanes = pl.ds(TILE * b, 2 * TILE)
            high, low = shi[rows, lanes], slo[rows, lanes]
            run[0 : count + 16, :] = nn(high, thi[h]) + nn(low, thi[h]) + nn(high, tlo[h])
            total = run[16 : 16 + count, 0:TILE]
            for a in range(1, rows_tap):
                total = total + run[pl.ds(16 - a, count), TILE * a : TILE * (a + 1)]
            logit[pl.ds(TILE * b, count), TILE * b : TILE * (b + 1)] = total
        for rb in range(tiles):
            rows = pl.ds(TILE * rb, TILE)
            wide = TILE * (rb + 1)
            value = logit[rows, 0:wide]
            key = lax.broadcasted_iota(jnp.int32, value.shape, 1)
            row = lax.broadcasted_iota(jnp.int32, value.shape, 0) + TILE * rb
            value = jnp.where(key <= row, value, NEGATIVE)
            weight = jnp.exp(value - jnp.max(value, axis=1, keepdims=True))
            weight = weight / jnp.sum(weight, axis=1, keepdims=True)
            lowered = weight.astype(BF16)
            p_ref[0, h, rows, 0:wide] = lowered
            y_ref[0, h, rows, :] = nn(lowered, vn[0:wide, :])
    out = mix_ref[0:1, :] * y_ref[0, 0] + mix_ref[1:2, :] * y_ref[0, 1]
    normed = out * head_factor(out, first, width // 2)
    final = (normed * gain_ref[1:2, :]).astype(BF16)
    for b, row in enumerate(natural_rows(blk_ref, m, blk, seq)):
        z_ref[pl.ds(row, blk), :] = final[blk * b : blk * (b + 1), :]


def backward_kernel(
    seq, blk, rows_tap, keys_tap, scale,
    blk_ref, ker_ref, mix_ref, gain_ref, qkv_ref, zg_ref, y_ref, p_ref,
    low_ref, misc_ref,
    qm, kf, ks, vn, sb, up, zn, yl, cg, cs, eb, qa, ka, acc, taps,
):
    m = pl.program_id(0)
    width = vn.shape[1]
    first = head_lanes(width)
    tiles = seq // TILE
    wide_u = 3 * TILE
    span = keys_tap - 1
    lanes_all = rows_tap * TILE

    @pl.when(m == 0)
    def _():
        misc_ref[...] = jnp.zeros(misc_ref.shape, F32)
        taps[...] = jnp.zeros(taps.shape, F32)
        acc[...] = jnp.zeros(acc.shape, F32)
        cg[seq : seq + 8, :] = jnp.zeros((8, seq), F32)
        for b in range(1, tiles):
            start = TILE * b - 16
            cg[start : TILE * b, TILE * b : TILE * (b + 1)] = jnp.zeros((16, TILE), F32)
            cs[0:start, lanes_all * b : lanes_all * (b + 1)] = jnp.zeros((start, lanes_all), BF16)
        eb[...] = jnp.zeros(eb.shape, BF16)
        sb[...] = jnp.zeros(sb.shape, BF16)
        away = lax.broadcasted_iota(jnp.int32, (2 * TILE, TILE), 0) - lax.broadcasted_iota(
            jnp.int32, (2 * TILE, TILE), 1
        )
        none = jnp.zeros((TILE, TILE), BF16)
        for h in range(2):
            for a in range(rows_tap):
                band = jnp.zeros((2 * TILE, TILE), F32)
                for t in range(keys_tap):
                    band = jnp.where(away == TILE - span + t, ker_ref[h, a, t], band)
                band = band.astype(BF16)
                at = wide_u * a
                up[h, at : at + 2 * TILE, 0:TILE] = band
                up[h, at + 2 * TILE : at + wide_u, 0:TILE] = none
                up[h, at : at + TILE, TILE : 2 * TILE] = none
                up[h, at + TILE : at + wide_u, TILE : 2 * TILE] = band

    load_heads(blk_ref, m, blk, seq, qkv_ref, qm, kf, ks, vn)
    places = natural_rows(blk_ref, m, blk, seq)
    for b, row in enumerate(places):
        zn[pl.ds(blk * b, blk), :] = zg_ref[pl.ds(row, blk), :].astype(F32)
    dim = width // 2
    y0, y1 = y_ref[0, 0], y_ref[0, 1]
    out = mix_ref[0:1, :] * y0 + mix_ref[1:2, :] * y1
    factor = head_factor(out, first, dim)
    normed = out * factor
    upstream = zn[...]
    misc_ref[16:17, 0:width] += jnp.sum(upstream * normed, axis=0, keepdims=True)
    scaled = upstream * gain_ref[1:2, :]
    both = scaled * normed
    own = jnp.sum(jnp.where(first, both, 0.0), axis=1, keepdims=True) / dim
    other = jnp.sum(jnp.where(first, 0.0, both), axis=1, keepdims=True) / dim
    out_grad = factor * (scaled - normed * jnp.where(first, own, other))
    misc_ref[17:18, 0:width] += jnp.sum(out_grad * y0, axis=0, keepdims=True)
    misc_ref[18:19, 0:width] += jnp.sum(out_grad * y1, axis=0, keepdims=True)
    yl[0] = (mix_ref[0:1, :] * out_grad).astype(BF16)
    yl[1] = (mix_ref[1:2, :] * out_grad).astype(BF16)

    for b in range(tiles):
        rows = pl.ds(TILE * b, seq - TILE * b)
        lanes = pl.ds(TILE * b, TILE)
        part = tn(p_ref[0, 0, rows, lanes], yl[0, rows, :]) + tn(p_ref[0, 1, rows, lanes], yl[1, rows, :])
        part = part.astype(BF16)
        for i in range(TILE // blk):
            low_ref[pl.ds(places[b * (TILE // blk) + i], blk), 2 * width : 3 * width] = part[blk * i : blk * (i + 1), :]

    ka[...] = jnp.zeros(ka.shape, F32)
    for h in range(2):
        for rb in range(tiles):
            rows = pl.ds(TILE * rb, TILE)
            upto = min(rb + 2, tiles + 1)
            sb[rows, 0 : TILE * upto] = scores(qm, ks, h, rb, upto, scale).astype(BF16)
            wide = TILE * (rb + 1)
            prob = p_ref[0, h, rows, 0:wide].astype(F32)
            grad = nt(yl[h, rows, :], vn[0:wide, :])
            both = prob * grad
            cg[rows, 0:wide] = both - prob * jnp.sum(both, axis=1, keepdims=True)
        for b in range(tiles):
            start = max(0, TILE * b - 16)
            count = seq - start
            for a in range(rows_tap):
                cs[pl.ds(start, count), pl.ds(lanes_all * b + TILE * a, TILE)] = cg[
                    pl.ds(start + a, count), TILE * b : TILE * (b + 1)
                ].astype(BF16)
            acc[h] += tn(
                sb[pl.ds(start, count), pl.ds(TILE * b, TILE + 16)],
                cs[pl.ds(start, count), pl.ds(lanes_all * b, lanes_all)],
            )
        for b in range(0, tiles + 1, 2):
            start = max(0, TILE * b - 16)
            count = seq - start
            columns = min(2, tiles + 1 - b)
            left, right = [], []
            for a in range(rows_tap):
                for piece in range(columns + 1):
                    block = b - 1 + piece
                    if 0 <= block < tiles:
                        left.append(cs[pl.ds(start, count), pl.ds(lanes_all * block + TILE * a, TILE)])
                        right.append(
                            up[h, pl.ds(wide_u * a + TILE * piece, TILE), 0 : TILE * columns]
                        )
            grad = nn(jnp.concatenate(left, axis=1), jnp.concatenate(right, axis=0))
            key = lax.broadcasted_iota(jnp.int32, grad.shape, 1) + TILE * b - 5
            row = lax.broadcasted_iota(jnp.int32, grad.shape, 0) + start
            low = jnp.where((key >= 0) & (key <= row), grad, 0.0).astype(BF16)
            eb[pl.ds(start, count), pl.ds(TILE * b, TILE * columns)] = low
            ka[pl.ds(TILE * b, TILE * columns), :] += tn(low, qm[h, pl.ds(start, count), :])
        for rb in range(tiles):
            rows = pl.ds(TILE * rb, TILE)
            upto = min(rb + 2, tiles + 1)
            part = nn(eb[rows, 0 : TILE * upto], ks[0 : TILE * upto, :]) * scale
            if h == 0:
                qa[rows, :] = part
            else:
                qa[rows, :] = jnp.where(first, qa[rows, :], part)
    for b, row in enumerate(places):
        low_ref[pl.ds(row, blk), 0:width] = qa[pl.ds(blk * b, blk), :].astype(BF16)
        low_ref[pl.ds(row, blk), width : 2 * width] = (ka[pl.ds(blk * b + 5, blk), :] * scale).astype(BF16)

    @pl.when(m == pl.num_programs(0) - 1)
    def _():
        away = lax.broadcasted_iota(jnp.int32, (TILE + 16, TILE), 0) - lax.broadcasted_iota(
            jnp.int32, (TILE + 16, TILE), 1
        )
        for h in range(2):
            for a in range(rows_tap):
                table = acc[h, :, TILE * a : TILE * (a + 1)]
                for t in range(keys_tap):
                    at = a * keys_tap + t
                    taps[at : at + 1, :] = jnp.sum(
                        jnp.where(away == span - t, table, 0.0), axis=0, keepdims=True
                    )
            count = taps.shape[0]
            tap = lax.broadcasted_iota(jnp.int32, (8, count), 1) - keys_tap * lax.broadcasted_iota(
                jnp.int32, (8, count), 0
            )
            rows = ((tap >= 0) & (tap < keys_tap)).astype(F32)
            at = lax.broadcasted_iota(jnp.int32, (count, TILE), 0)
            lane = lax.broadcasted_iota(jnp.int32, (count, TILE), 1)
            value = jnp.sum(taps[...], axis=1, keepdims=True)
            lanes = jnp.zeros((count, TILE), F32)
            for a in range(rows_tap):
                lanes = jnp.where((at == keys_tap * a + lane) & (lane < keys_tap), value, lanes)
            misc_ref[8 * h : 8 * h + 8, 0:TILE] = lax.dot_general(
                rows, lanes, (((1,), (0,)), ((), ())),
                precision=lax.Precision.HIGHEST, preferred_element_type=F32,
            )


def whole(shape):
    return pl.BlockSpec(shape, lambda m: (0,) * len(shape))


def pair_forward(blk_table, ker, mix, gain, qkv, micro, seq, blk, scale):
    width = qkv.shape[1] // 3
    mixed = (qkv.shape[0], width)
    rows_tap, keys_tap = ker.shape[1:]
    smem = pl.BlockSpec(memory_space=pltpu.SMEM)
    per = lambda shape: pl.BlockSpec((1,) + shape, lambda m: (m,) + (0,) * len(shape))
    return pl.pallas_call(
        functools.partial(forward_kernel, seq, blk, rows_tap, keys_tap, scale),
        name="pair_forward",
        grid=(micro,),
        out_shape=(
            jax.ShapeDtypeStruct(mixed, BF16),
            jax.ShapeDtypeStruct((micro, 2, seq, width), F32),
            jax.ShapeDtypeStruct((micro, 2, seq, seq), BF16),
        ),
        in_specs=[smem, smem, whole(mix.shape), whole(gain.shape), whole(qkv.shape)],
        out_specs=(whole(mixed), per((2, seq, width)), per((2, seq, seq))),
        scratch_shapes=[
            pltpu.VMEM((2, seq, width), BF16),
            pltpu.VMEM((seq + TILE + 8, width), F32),
            pltpu.VMEM((seq + TILE, width), BF16),
            pltpu.VMEM((seq, width), BF16),
            pltpu.VMEM((seq + 16, seq + TILE), BF16),
            pltpu.VMEM((seq + 16, seq + TILE), BF16),
            pltpu.VMEM((2, 2 * TILE, rows_tap * TILE), BF16),
            pltpu.VMEM((2, 2 * TILE, rows_tap * TILE), BF16),
            pltpu.VMEM((seq + 16, rows_tap * TILE), F32),
            pltpu.VMEM((seq, seq), F32),
        ],
        compiler_params=pltpu.CompilerParams(vmem_limit_bytes=56 << 20),
        cost_estimate=pl.CostEstimate(flops=20 * 10**9, transcendentals=10**6, bytes_accessed=8 << 20),
    )(blk_table, ker, mix, gain, qkv)


def pair_backward(blk_table, ker, mix, gain, qkv, zg, y, p, seq, blk, scale):
    width = qkv.shape[1] // 3
    micro = y.shape[0]
    rows_tap, keys_tap = ker.shape[1:]
    tiles = seq // TILE
    smem = pl.BlockSpec(memory_space=pltpu.SMEM)
    per = lambda shape: pl.BlockSpec((1,) + shape, lambda m: (m,) + (0,) * len(shape))
    taps = -(-rows_tap * keys_tap // 8) * 8
    return pl.pallas_call(
        functools.partial(backward_kernel, seq, blk, rows_tap, keys_tap, scale),
        name="pair_backward",
        grid=(micro,),
        out_shape=(
            jax.ShapeDtypeStruct(qkv.shape, BF16),
            jax.ShapeDtypeStruct((24, 2 * TILE), F32),
        ),
        in_specs=[smem, smem, whole(mix.shape), whole(gain.shape), whole(qkv.shape), whole(zg.shape)]
        + [per((2, seq, width)), per((2, seq, seq))],
        out_specs=(whole(qkv.shape), whole((24, 2 * TILE))),
        scratch_shapes=[
            pltpu.VMEM((2, seq, width), BF16),
            pltpu.VMEM((seq + TILE + 8, width), F32),
            pltpu.VMEM((seq + TILE, width), BF16),
            pltpu.VMEM((seq, width), BF16),
            pltpu.VMEM((seq, seq + TILE), BF16),
            pltpu.VMEM((2, rows_tap * 3 * TILE, 2 * TILE), BF16),
            pltpu.VMEM((seq, width), F32),
            pltpu.VMEM((2, seq, width), BF16),
            pltpu.VMEM((seq + 8, seq), F32),
            pltpu.VMEM((seq, tiles * rows_tap * TILE), BF16),
            pltpu.VMEM((seq, seq + TILE), BF16),
            pltpu.VMEM((seq, width), F32),
            pltpu.VMEM((seq + TILE, width), F32),
            pltpu.VMEM((2, TILE + 16, rows_tap * TILE), F32),
            pltpu.VMEM((taps, TILE), F32),
        ],
        compiler_params=pltpu.CompilerParams(vmem_limit_bytes=56 << 20),
        cost_estimate=pl.CostEstimate(flops=30 * 10**9, transcendentals=10**5, bytes_accessed=12 << 20),
    )(blk_table, ker, mix, gain, qkv, zg, y, p)


MESH = pl.DeviceIdType.MESH


def peer(offset):
    mine = lax.axis_index("ctx")
    y = (mine // 4 + offset // 4) % 2
    x = ((mine // 2) % 2 + (offset // 2) % 2) % 2
    core = (mine % 2 + offset % 2) % 2
    return y * 4 + x * 2 + core


def greet(places):
    barrier = pltpu.get_barrier_semaphore()
    for place in places:
        pl.semaphore_signal(barrier, inc=1, device_id=place, device_id_type=MESH)
    return lambda: pl.semaphore_wait(barrier, len(places))


def remote(source, target, send, receive, place):
    return pltpu.make_async_remote_copy(
        src_ref=source, dst_ref=target, send_sem=send, recv_sem=receive,
        device_id=place, device_id_type=MESH,
    )


def exchange_start(plane, mine, source, target, sends, receives):
    copies = [
        remote(source.at[peer(d)], target.at[mine], sends.at[d], receives.at[d], (plane, peer(d)))
        for d in (6, 7, 2, 3, 4, 5, 1)
    ]
    for copy in copies:
        copy.start()
    return copies


class Spread:
    def __init__(self, source, target, sends, receives):
        self.plane, self.mine = lax.axis_index("seq"), lax.axis_index("ctx")
        self.source, self.target, self.sends, self.receives = source, target, sends, receives
        self.copies = {}
        half = target.shape[1] // 2
        self.first, self.second = pl.ds(0, half), pl.ds(half, half)

    def send(self, key, source, target, offset):
        copy = remote(source, target, self.sends.at[key], self.receives.at[key], (self.plane, peer(offset)))
        copy.start()
        self.copies[key] = copy

    def hand_on(self, key, block, offset, rows=None):
        piece = self.target.at[block] if rows is None else self.target.at[block, rows]
        self.send(key, piece, piece, offset)

    def start(self):
        for d in (2, 4, 1):
            self.send(d, self.source, self.target.at[self.mine], d)

    def near(self):
        self.copies[2].wait_recv()
        self.hand_on(6, peer(2), 4, self.first)
        self.hand_on(3, peer(2), 1)
        self.copies[4].wait_recv()
        self.hand_on(0, peer(4), 2, self.second)
        self.hand_on(5, peer(4), 1)

    def across(self):
        self.copies[6].wait_recv()
        self.hand_on(7, peer(6), 1, self.first)
        self.copies[0].wait_recv()
        self.hand_on(8, peer(6), 1, self.second)

    def finish(self):
        for key in (1, 3, 5, 7, 8):
            self.copies[key].wait_recv()
        for copy in self.copies.values():
            copy.wait_send()


class PlaneSum:
    def __init__(self, terms, part, own, near, stage, far, hop, sends, receives):
        self.plane, self.mine = lax.axis_index("seq"), lax.axis_index("ctx")
        self.terms, self.part, self.own = terms, part, own
        self.near, self.stage, self.far, self.hop = near, stage, far, hop
        self.sends, self.receives = sends, receives
        self.copies = {}
        half = part.shape[1] // 2
        self.first, self.second = pl.ds(0, half), pl.ds(half, half)

    def send(self, key, source, target, offset):
        copy = remote(source, target, self.sends.at[key], self.receives.at[key], (self.plane, peer(offset)))
        copy.start()
        self.copies[key] = copy

    def start(self, met):
        self.part[...] = self.terms(1 - self.mine % 2).astype(BF16)
        met()
        for d in (6, 2, 4, 0):
            self.send(d, self.part.at[peer(d) // 2], self.near.at[d // 2], 1)

    def prepare(self):
        self.own[...] = self.terms(self.mine % 2)

    def chip_sum(self, d):
        self.copies[d].wait_recv()
        self.stage[d // 2] = (self.own[peer(d) // 2] + self.near[d // 2].astype(F32)).astype(BF16)

    def add_hop(self, slot, rows, hop):
        self.stage[slot, rows, :] = (
            self.stage[slot, rows, :].astype(F32) + self.hop[hop].astype(F32)
        ).astype(BF16)

    def run(self):
        first, second = self.first, self.second
        self.chip_sum(6)
        self.send(1, self.stage.at[3, first], self.hop.at[0], 2)
        self.send(3, self.stage.at[3, second], self.hop.at[1], 4)
        self.chip_sum(2)
        self.send(5, self.stage.at[1, first], self.far.at[0, first], 2)
        self.chip_sum(4)
        self.send(7, self.stage.at[2, second], self.far.at[1, second], 4)
        self.copies[1].wait_recv()
        self.add_hop(2, first, 0)
        self.send(8, self.stage.at[2, first], self.far.at[1, first], 4)
        self.copies[3].wait_recv()
        self.add_hop(1, second, 1)
        self.send(9, self.stage.at[1, second], self.far.at[0, second], 2)

    def total(self):
        self.copies[0].wait_recv()
        value = self.own[self.mine // 2] + self.near[0].astype(F32)
        for key in (5, 7, 8, 9):
            self.copies[key].wait_recv()
        return value + self.far[0].astype(F32) + self.far[1].astype(F32)

    def finish(self):
        for copy in self.copies.values():
            copy.wait_send()


class Fetch:
    def __init__(self, source, buffer, sem):
        self.copy, self.buffer, self.ready = pltpu.make_async_copy(source, buffer, sem), buffer, False
        self.copy.start()

    def get(self):
        if not self.ready:
            self.copy.wait()
            self.ready = True
        return self.buffer


def fetch(sources, buffers, sems):
    return [Fetch(source, buffer, sems.at[i]) for i, (source, buffer) in enumerate(zip(sources, buffers))]


def put(buffer, out, sem):
    copy = pltpu.make_async_copy(buffer, out, sem)
    copy.start()
    return copy


def terms_of(values, product):
    chips, _, rows, width = values.buffer.shape

    def terms(core):
        left = values.get()[:, core].reshape(chips * rows, width)
        return product(left).reshape(chips, rows, -1)

    return terms


class Line:
    def __init__(self, sources, targets, planes, sends, receives):
        self.sources, self.targets, self.planes = sources, targets, planes
        self.sends, self.receives = sends, receives
        self.plane, self.mine = lax.axis_index("seq"), lax.axis_index("ctx")

    def copy(self, i, up, step):
        block = jnp.clip(self.plane - step if up else self.plane + step, 0, self.planes - 1)
        next_plane = jnp.clip(self.plane + 1 if up else self.plane - 1, 0, self.planes - 1)
        at = (i, int(up), step)
        target = self.targets[i].at[block]
        source = target if step else self.sources[i]
        return remote(source, target, self.sends.at[at], self.receives.at[at], (next_plane, self.mine))

    def arrived(self, i, up, step):
        block = jnp.clip(self.plane - 1 - step if up else self.plane + 1 + step, 0, self.planes - 1)
        at = (i, int(up), step)
        target = self.targets[i].at[block]
        from_plane = jnp.clip(self.plane - 1 if up else self.plane + 1, 0, self.planes - 1)
        return remote(target, target, self.sends.at[at], self.receives.at[at], (from_plane, self.mine))

    def step(self, step):
        for up in (True, False):
            have = self.plane >= step if up else self.plane + step < self.planes
            more = self.plane + 1 < self.planes if up else self.plane > 0
            for i in range(len(self.targets)):
                if step:
                    @pl.when(have)
                    def _(i=i, up=up):
                        self.arrived(i, up, step - 1).wait_recv()

                if step < self.planes - 1:
                    @pl.when(have & more)
                    def _(i=i, up=up):
                        self.copy(i, up, step).start()

    def finish(self):
        for step in range(self.planes - 1):
            for up in (True, False):
                have = self.plane >= step if up else self.plane + step < self.planes
                more = self.plane + 1 < self.planes if up else self.plane > 0
                for i in range(len(self.targets)):
                    @pl.when(have & more)
                    def _(i=i, up=up, step=step):
                        self.copy(i, up, step).wait_send()


def plane_peers(plane, offsets):
    return [(plane, peer(d)) for d in offsets]


def other_planes(plane, mine, planes):
    return [((plane + d) % planes, mine) for d in range(1, planes)]


class RowDeal:
    def __init__(self, gathered, dealt, sends, receives, local):
        self.plane, self.mine = lax.axis_index("seq"), lax.axis_index("ctx")
        self.gathered, self.dealt, self.sends, self.receives, self.local = gathered, dealt, sends, receives, local

    def out(self, s, back):
        if back:
            target = 4 * (self.mine % 2) + s
            source, place = self.dealt.at[s], self.gathered.at[self.mine // 2]
        else:
            target = 2 * s + self.mine // 4
            source, place = self.gathered.at[s], self.dealt.at[self.mine % 4]
        slot = self.mine // 2 if back else self.mine % 4
        copy = remote(source, place, self.sends.at[s], self.receives.at[slot], (self.plane, target))
        keep = pltpu.make_async_copy(source, place, self.local)
        return target == self.mine, copy, keep

    def into(self, r, back):
        if back:
            origin = 2 * r + self.mine // 4
            place = self.gathered.at[r]
        else:
            origin = 4 * (self.mine % 2) + r
            place = self.dealt.at[r]
        return origin == self.mine, remote(place, place, self.sends.at[r], self.receives.at[r], (self.plane, origin))

    def start(self, back):
        for s in range(4):
            here, copy, keep = self.out(s, back)

            @pl.when(here)
            def _():
                keep.start()

            @pl.when(jnp.logical_not(here))
            def _():
                copy.start()

    def wait(self, back):
        for s in range(4):
            here, copy, keep = self.out(s, back)

            @pl.when(here)
            def _():
                keep.wait()

            @pl.when(jnp.logical_not(here))
            def _():
                copy.wait_send()

        for r in range(4):
            here, copy = self.into(r, back)

            @pl.when(jnp.logical_not(here))
            def _():
                copy.wait_recv()


def enter_kernel(
    planes, q, k, v, gate, up, norm_gain, group_gain, second_gain, tokens, out_w,
    feed_out, qkv_out, gains_out, tokens_out, out_w_out,
    q_near, k_near, v_near, gate_near, up_near, norm_near, group_near, second_near, packed, qkv, feed,
    deal_sends, deal_receives, sends, receives, row_sends, row_receives, line_sends, line_receives, local,
):
    plane, mine = lax.axis_index("seq"), lax.axis_index("ctx")
    loads = [
        pltpu.make_async_copy(source, place, local.at[5 + i])
        for i, (source, place) in enumerate(
            (
                (norm_gain, norm_near), (group_gain, group_near), (second_gain, second_near),
                (q, q_near), (k, k_near), (v, v_near), (gate, gate_near), (up, up_near),
            )
        )
    ]
    keep = [
        pltpu.make_async_copy(qkv.at[mine], qkv_out.at[plane, mine], local.at[0]),
        pltpu.make_async_copy(packed, gains_out.at[plane, mine], local.at[1]),
        pltpu.make_async_copy(feed.at[mine], feed_out.at[mine], local.at[2]),
        pltpu.make_async_copy(tokens, tokens_out.at[mine], local.at[3]),
        pltpu.make_async_copy(out_w, out_w_out.at[plane], local.at[4]),
    ]
    for copy in loads + keep[3:]:
        copy.start()
    met = greet(plane_peers(plane, range(1, 8)) + other_planes(plane, mine, planes))
    groups, _, three = qkv.shape
    pair = three // 3
    half = feed.shape[2] // 2
    for copy in loads[:6]:
        copy.wait()
    packed[...] = jnp.zeros(packed.shape, F32)
    for i, gain in enumerate((norm_near, group_near, second_near)):
        packed[i : i + 1, 0 : gain.shape[0]] = gain[...].astype(F32).reshape(1, -1)
    for c in range(groups):
        for i, weight in enumerate((q_near, k_near, v_near)):
            qkv[c, :, pair * i : pair * (i + 1)] = weight[:, pair * c : pair * (c + 1)]
    for copy in keep[:2]:
        copy.start()
    met()
    first = exchange_start(plane, mine, qkv, qkv_out.at[plane], deal_sends.at[0], deal_receives.at[0])
    for d in (6, 7, 2, 3, 4, 5, 1):
        copy = remote(packed, gains_out.at[plane, mine], deal_sends.at[1, d], deal_receives.at[1, d], (plane, peer(d)))
        copy.start()
        first.append(copy)
    rows = Line([out_w], [out_w_out], planes, row_sends, row_receives)
    rows.step(0)
    for copy in loads[6:]:
        copy.wait()
    for c in range(groups):
        for i, weight in enumerate((gate_near, up_near)):
            for s in range(half // TILE):
                at = TILE * (groups * s + c)
                feed[c, :, half * i + TILE * s : half * i + TILE * (s + 1)] = weight[:, at : at + TILE]
    keep[2].start()
    keep[0].wait()
    keep[1].wait()
    for copy in first:
        copy.wait_recv()
    line = Line(
        [qkv_out.at[plane], gains_out.at[plane]], [qkv_out, gains_out], planes, line_sends, line_receives
    )
    line.step(0)
    spread = Spread(tokens, tokens_out, sends, receives)
    spread.start()
    rows.step(1)
    line.step(1)
    spread.near()
    deals = exchange_start(plane, mine, feed, feed_out, deal_sends.at[2], deal_receives.at[2])
    rows.step(2)
    line.step(2)
    spread.across()
    for step in range(3, planes):
        rows.step(step)
        line.step(step)
    spread.finish()
    for copy in first:
        copy.wait_send()
    for copy in deals:
        copy.wait()
    for copy in keep[2:]:
        copy.wait()
    line.finish()
    rows.finish()


def heads_kernel(
    planes, tokens, qkv, gains, out_w, grads, hidden, heads, gains_out, pair_gain, out_w_out, grads_out,
    tokens_near, qkv_near, hidden_near, heads_near,
    row_sends, row_receives, sends, receives, loads, stores, local,
):
    plane, mine = lax.axis_index("seq"), lax.axis_index("ctx")
    groups = tokens.shape[0]
    weight = Fetch(qkv, qkv_near, loads.at[groups])
    blocks = [Fetch(tokens.at[i], tokens_near.at[i], loads.at[i]) for i in range(groups)]
    keep = pltpu.make_async_copy(grads, grads_out.at[mine], local.at[1])
    keep.start()
    greet(plane_peers(plane, range(1, 8)))()
    spread = Spread(grads, grads_out, sends, receives)
    spread.start()
    deal = RowDeal(out_w, out_w_out, row_sends, row_receives, local.at[0])
    deal.start(False)
    owned = out_w.shape[1]
    for s in range(planes):
        for c in range(groups):
            at = owned * (groups * s + c)
            gains_out[:, at : at + owned] = gains[s, c, :, 0:owned]
    for r in range(4):
        pair_gain[:, owned * r : owned * (r + 1)] = gains[mine // 2, 4 * (mine % 2) + r, :, 0:owned]
    gain = gains_out[0:1, :]
    out = []
    for i in range(groups):
        value = blocks[i].get()[...].astype(F32)
        low = (value * inverse_root(value) * gain).astype(BF16)
        rows = pl.ds(value.shape[0] * i, value.shape[0])
        hidden_near[:, rows] = low.T
        out.append(put(hidden_near.at[:, rows], hidden.at[:, rows], stores.at[0, i]))
        heads_near[rows, :] = nn(low, weight.get()[...]).astype(BF16)
        out.append(put(heads_near.at[rows], heads.at[rows], stores.at[1, i]))
        if i == groups - 3:
            spread.near()
    deal.wait(False)
    spread.across()
    for copy in out:
        copy.wait()
    spread.finish()
    keep.wait()


def inverse_root(values):
    return lax.rsqrt(jnp.mean(values * values, axis=1, keepdims=True) + EPSILON)


def second_kernel(
    mixed, out_w, tokens, gains, residual, spread_out,
    mixed_near, out_w_near, tokens_near, residual_near, own_near, loads,
    part, own, near, stage, far, hop, sum_sends, sum_receives, sends, receives,
):
    plane, mine = lax.axis_index("seq"), lax.axis_index("ctx")
    left, weight, rows_in = fetch(
        (mixed, out_w, tokens), (mixed_near, out_w_near, tokens_near), loads
    )
    met = greet(plane_peers(plane, (1, 2, 4)))
    rows = PlaneSum(
        terms_of(left, lambda value: nn(value, weight.get()[...])), part, own, near, stage, far, hop,
        sum_sends, sum_receives,
    )
    rows.start(met)
    rows.prepare()
    rows.run()
    value = rows_in.get()[...].astype(F32) + rows.total()
    own_near[...] = (value * inverse_root(value) * gains[2:3, :]).astype(BF16)
    spread = Spread(own_near, spread_out, sends, receives)
    spread.start()
    keep = put(own_near, spread_out.at[mine], loads.at[3])
    residual_near[...] = value
    out = put(residual_near, residual, loads.at[4])
    rows.finish()
    spread.near()
    spread.across()
    keep.wait()
    out.wait()
    spread.finish()


def back_through_norm(upstream, values, gain):
    factor = inverse_root(values)
    normed = values * factor
    scaled = upstream * gain
    grad = factor * (scaled - normed * jnp.mean(scaled * normed, axis=1, keepdims=True))
    return grad, jnp.sum(upstream * normed, axis=0, keepdims=True)


def back_kernel(
    lows, feed, residual, grads, out_w, mixed, gains, residual_grad, gain_grad, mixed_grad, out_w_grad,
    lows_near, feed_near, residual_near, grads_near, out_w_near, mixed_near, residual_grad_near, gathered, total, loads,
    part, own, near, stage, far, hop, sum_sends, sum_receives, sends, receives,
):
    plane, mine = lax.axis_index("seq"), lax.axis_index("ctx")
    weight, left, before, upstream, out_rows, taken = fetch(
        (feed, lows, residual, grads, out_w, mixed),
        (feed_near, lows_near, residual_near, grads_near, out_w_near, mixed_near),
        loads,
    )
    met = greet(plane_peers(plane, (1, 2, 4)))
    rows = PlaneSum(
        terms_of(left, lambda value: nt(value, weight.get()[...])), part, own, near, stage, far, hop,
        sum_sends, sum_receives,
    )
    rows.start(met)
    rows.prepare()
    rows.run()
    grad, gain_part = back_through_norm(rows.total(), before.get()[...], gains[2:3, :])
    grad = grad + upstream.get()[...].astype(F32)
    gathered[mine] = grad.astype(BF16)
    spread = Spread(gathered.at[mine], gathered, sends, receives)
    spread.start()
    gain_grad[...] = gain_part
    residual_grad_near[...] = grad
    out = put(residual_grad_near, residual_grad, loads.at[6])
    taken.get()

    def use(d):
        block = peer(d) if d else mine
        value = gathered[block]
        mixed_grad[block] = nt(value, out_rows.get()[...]).astype(BF16)
        term = tn(mixed_near[block], value)
        total[...] = total[...] + term if d else term

    use(0)
    rows.finish()
    spread.near()
    use(2)
    use(4)
    spread.copies[1].wait_recv()
    use(1)
    spread.across()
    use(6)
    for keys, d in (((3,), 3), ((5,), 5), ((7, 8), 7)):
        for key in keys:
            spread.copies[key].wait_recv()
        use(d)
    out_w_grad[...] = total[...].astype(BF16)
    for copy in spread.copies.values():
        copy.wait_send()
    out.wait()


class Fold:
    def __init__(self, own, stage, landed, planes, sends, receives):
        self.own, self.stage, self.landed, self.planes = own, stage, landed, planes
        self.sends, self.receives = sends, receives
        self.plane, self.mine = lax.axis_index("seq"), lax.axis_index("ctx")

    def copy(self, j, up):
        place = jnp.clip(self.plane + 1 if up else self.plane - 1, 0, self.planes - 1)
        at = (int(up), j)
        return remote(self.stage.at[at], self.landed.at[at], self.sends.at[at], self.receives.at[at], (place, self.mine))

    def advance(self, j, up):
        active = self.plane < j if up else self.plane > j
        inner = self.plane > 0 if up else self.plane < self.planes - 1

        @pl.when(active & inner)
        def _():
            self.copy(j, up).wait_recv()
            self.stage[int(up), j] = (
                self.own[j].astype(F32) + self.landed[int(up), j].astype(F32)
            ).astype(BF16)

        @pl.when(active & jnp.logical_not(inner))
        def _():
            self.stage[int(up), j] = self.own[j]

        @pl.when(active)
        def _():
            self.copy(j, up).start()

    def round(self, i):
        self.advance(self.planes - 1 - i, True)
        self.advance(i, False)

    def total(self, store):
        for j in range(self.planes):
            @pl.when(self.plane == j)
            def _():
                value = self.own[j].astype(F32)
                if j > 0:
                    self.copy(j, True).wait_recv()
                    value = value + self.landed[1, j].astype(F32)
                if j < self.planes - 1:
                    self.copy(j, False).wait_recv()
                    value = value + self.landed[0, j].astype(F32)
                store(value.astype(BF16))

    def finish(self):
        for j in range(self.planes):
            for up in (True, False):
                @pl.when(self.plane < j if up else self.plane > j)
                def _():
                    self.copy(j, up).wait_send()


def layer_kernel(
    active, down, residual, out_w_grad, layer_out, row_grad,
    active_near, down_near, residual_near, loads,
    part, own, near, stage, far, hop, sum_sends, sum_receives, row_sends, row_receives, local,
):
    plane, mine = lax.axis_index("seq"), lax.axis_index("ctx")
    left, weight, before = fetch(
        (active, down, residual), (active_near, down_near, residual_near), loads
    )
    met = greet(plane_peers(plane, range(1, 8)))
    rows = PlaneSum(
        terms_of(left, lambda value: nn(value, weight.get()[...])), part, own, near, stage, far, hop,
        sum_sends, sum_receives,
    )
    rows.start(met)
    deal = RowDeal(row_grad, out_w_grad, row_sends, row_receives, local)
    deal.start(True)
    rows.prepare()
    rows.run()
    layer_out[...] = (before.get()[...] + rows.total()).astype(BF16)
    deal.wait(True)
    rows.finish()


def leave_kernel(
    planes, qkv_low_in, qkv_in, hidden_in, residual_grad_in, tokens_in,
    gains, second_grad, misc, feed_grad, row_grad,
    input_grad, small_out, misc_out, qkv_out, feed_out, out_w_out,
    qkv_low_near, qkv_near, hidden_near, residual_grad_near, tokens_near, loads,
    misc_all, misc_sends, misc_receives,
    part, own, near, stage, far, hop, small_plane, small_all,
    grads, fold_stage, fold_landed, qkv_sum,
    sum_sends, sum_receives, small_sends, small_receives,
    fold_sends, fold_receives, deal_sends, deal_receives, local,
):
    plane, mine = lax.axis_index("seq"), lax.axis_index("ctx")
    qkv_low, qkv, hidden, residual_grad, tokens = fetch(
        (qkv_low_in, qkv_in, hidden_in, residual_grad_in, tokens_in),
        (qkv_low_near, qkv_near, hidden_near, residual_grad_near, tokens_near),
        loads,
    )
    keep_feed = pltpu.make_async_copy(feed_grad.at[mine], feed_out.at[mine], local.at[0])
    keep_feed.start()
    misc_all[plane] = misc[...]
    met = greet(plane_peers(plane, range(1, 8)) + other_planes(plane, mine, planes))
    misc_copies = [
        remote(misc_all.at[plane], misc_all.at[plane], misc_sends.at[0, d], misc_receives.at[0, d], ((plane + d) % planes, mine))
        for d in range(1, planes)
    ]
    rows = PlaneSum(
        terms_of(qkv_low, lambda left: nt(left, qkv.get()[...])), part, own, near, stage, far, hop,
        sum_sends, sum_receives,
    )
    halves = [pl.ds(grads.shape[1] // 2 * k, grads.shape[1] // 2) for k in range(2)]
    folds = [
        Fold(
            grads.at[:, rows], fold_stage.at[:, :, rows], fold_landed.at[:, :, rows], planes,
            fold_sends.at[k], fold_receives.at[k],
        )
        for k, rows in enumerate(halves)
    ]
    ends = (plane == 0) | (plane == planes - 1)
    block, owned = grads.shape[1], row_grad.shape[1]
    three = qkv_low_in.shape[3]
    pair = three // 3

    def project(i):
        j = jnp.where(plane < planes // 2, planes - 1 - i, i)
        lows = qkv_low.get()[...].reshape(hidden_near.shape[1], three)
        columns = hidden.get()[pl.ds(pl.multiple_of(block * j, block), block), :]
        grads[j, :, 0:three] = nn(columns, lows).astype(BF16)
        for p in range(block // owned):
            grads[j, owned * p : owned * (p + 1), three : three + pair] = row_grad[
                j, :, pair * p : pair * (p + 1)
            ]

    def rounds(outer, inner):
        for here, i in ((ends, outer), (jnp.logical_not(ends), inner)):
            if 0 <= i < planes - 1:
                @pl.when(here)
                def _():
                    for fold in folds:
                        fold.round(i)

    rows.start(met)
    for copy in misc_copies:
        copy.start()
    project(0)
    rounds(0, -1)
    rows.prepare()
    for i in range(1, planes):
        project(i)
    rounds(1, -1)
    rows.run()
    rounds(2, 0)
    for copy in misc_copies:
        copy.wait()
    total = misc_all[0]
    for i in range(1, planes):
        total = total + misc_all[i]
    misc_out[mine] = total
    misc_copies = [
        remote(misc_out.at[mine], misc_out.at[mine], misc_sends.at[1, d], misc_receives.at[1, d], (plane, peer(d)))
        for d in range(1, 8)
    ]
    for copy in misc_copies:
        copy.start()
    grad, gain_part = back_through_norm(rows.total(), tokens.get()[...].astype(F32), gains[0:1, :])
    small_plane[mine] = jnp.zeros(small_plane.shape[1:], F32)
    small_plane[mine, 0:1, :] = gain_part
    small_plane[mine, 1:2, :] = second_grad[...]
    near_copies = [
        remote(small_plane.at[mine], small_plane.at[mine], small_sends.at[0, d], small_receives.at[0, d], (plane, peer(d)))
        for d in range(1, 8)
    ]
    for copy in near_copies:
        copy.start()
    input_grad[...] = (residual_grad.get()[...] + grad).astype(BF16)
    deals = exchange_start(plane, mine, feed_grad, feed_out, deal_sends.at[0], deal_receives.at[0])
    rounds(-1, 1)
    for copy in near_copies:
        copy.wait()
    total = small_plane[0]
    for i in range(1, 8):
        total = total + small_plane[i]
    small_all[plane] = total
    far_copies = [
        remote(small_all.at[plane], small_all.at[plane], small_sends.at[1, d], small_receives.at[1, d], ((plane + d) % planes, mine))
        for d in range(1, planes)
    ]
    for copy in far_copies:
        copy.start()
    rounds(-1, 2)
    keep_qkv = pltpu.make_async_copy(qkv_sum.at[mine], qkv_out.at[mine], local.at[2])
    handed = [
        remote(
            qkv_sum.at[peer(d)], qkv_out.at[mine], deal_sends.at[1, d], deal_receives.at[1, d], (plane, peer(d))
        )
        for d in range(1, 8)
    ]
    for k, fold in enumerate(folds):
        def store(value, k=k):
            count = value.shape[0] // owned
            for p in range(count):
                piece = value[owned * p : owned * (p + 1), :]
                qkv_sum[count * k + p] = piece[:, 0:three]
                at = pair * (count * k + p)
                out_w_out[0, :, at : at + pair] = piece[:, three : three + pair]

        fold.total(store)
        same = mine // 4 == k
        for d in range(1, 8):
            @pl.when(same if d < 4 else jnp.logical_not(same))
            def _():
                handed[d - 1].start()

        @pl.when(same)
        def _():
            keep_qkv.start()

    deals += handed
    rows.finish()
    for copy in far_copies:
        copy.wait()
    total = small_all[0]
    for i in range(1, planes):
        total = total + small_all[i]
    small_out[...] = total
    for copy in deals + misc_copies:
        copy.wait()
    keep_feed.wait()
    keep_qkv.wait()
    for fold in folds:
        fold.finish()


def finish_kernel(count, place, small, misc, *refs):
    ins, outs = refs[:6], refs[6 : 6 + count]
    norm_out, group_out, second_out, ker_out, mix_out = refs[6 + count : 11 + count]
    near, made = refs[11 + count : 17 + count], refs[17 + count : 17 + 2 * count - 2]
    loads, stores = refs[-2:]
    moves = [pltpu.make_async_copy(ins[i], near[i], loads.at[i]) for i in range(6)]
    for move in moves:
        move.start()
    qkv, feed, out_w, down, grad, layer = near
    groups, owned, three = qkv.shape
    pair = three // 3
    half = feed.shape[2] // 2
    results = list(made) + [grad, layer]
    out = [pltpu.make_async_copy(results[i], outs[i], stores.at[i]) for i in range(count)]
    moves[3].wait()
    made[6][...] = down[...].astype(F32)
    out[6].start()
    moves[2].wait()
    made[5][...] = out_w[0].astype(F32)
    out[5].start()
    for i in (4, 5):
        moves[i].wait()
        out[i + 3].start()
    moves[1].wait()
    for i in range(2):
        for c in range(groups):
            for s in range(half // TILE):
                at = TILE * (groups * s + c)
                made[3 + i][:, at : at + TILE] = feed[
                    c, :, half * i + TILE * s : half * i + TILE * (s + 1)
                ].astype(F32)
        out[3 + i].start()
    moves[0].wait()
    for i in range(3):
        for c in range(groups):
            made[i][:, pair * c : pair * (c + 1)] = qkv[c, :, pair * i : pair * (i + 1)].astype(F32)
        out[i].start()
    flat = place[0]
    width = small.shape[1]
    turned = pltpu.roll(small[...], (width - owned * flat) % width, 1)
    norm_out[...] = turned[0:1, 0:owned]
    second_out[...] = turned[1:2, 0:owned]
    rows = misc[flat // 4]
    wide = rows.shape[1]
    turned = pltpu.roll(rows, (wide - owned * (flat % 4)) % wide, 1)
    group_out[...] = turned[16:17, 0:owned]
    heads = [(c, h) for c in range(groups) for h in range(2)]
    for a in range(ker_out.shape[1]):
        rows = jnp.concatenate([misc[c, 8 * h + a : 8 * h + a + 1, 0:TILE] for c, h in heads], axis=0)
        ker_out[:, a, :] = rows.T[0 : ker_out.shape[0], :]
    for p in range(2):
        sums = [
            jnp.sum(misc[c, 17 + p : 18 + p, pair // 2 * h : pair // 2 * (h + 1)], axis=1, keepdims=True)
            for c, h in heads
        ]
        mix_out[p : p + 1, :] = jnp.broadcast_to(jnp.concatenate(sums, axis=0), (len(heads), TILE)).T[0:1, :]
    for copy in out:
        copy.wait()


DMA = pltpu.SemaphoreType.DMA
ANYWHERE = pl.BlockSpec(memory_space=pl.ANY)
ON_CHIP = pl.BlockSpec(memory_space=pltpu.VMEM)


def communicate(kernel, name, number, micros, outs, scratch, args, spec, specs=None, out_specs=None):
    return pl.pallas_call(
        kernel,
        name=name,
        out_shape=tuple(jax.ShapeDtypeStruct(shape, kind) for shape, kind in outs),
        in_specs=specs or [spec] * len(args),
        out_specs=out_specs or (spec,) * len(outs),
        scratch_shapes=scratch,
        compiler_params=pltpu.CompilerParams(
            collective_id=number, has_side_effects=True, vmem_limit_bytes=56 << 20
        ),
        cost_estimate=pl.CostEstimate(flops=0, transcendentals=0, bytes_accessed=micros * 3500000),
    )(*args)


def sum_scratch(rows, width):
    return [
        pltpu.VMEM((4, rows, width), BF16),
        pltpu.VMEM((4, rows, width), F32),
        pltpu.VMEM((4, rows, width), BF16),
        pltpu.VMEM((4, rows, width), BF16),
        pltpu.VMEM((2, rows, width), BF16),
        pltpu.VMEM((2, rows // 2, width), BF16),
        DMA((10,)),
        DMA((10,)),
    ]


PRECISE = lax.Precision.HIGHEST


def normalize(values):
    factor = lax.rsqrt(jnp.mean(values * values, axis=-1, keepdims=True) + EPSILON)
    return (values * factor, factor)


def normalize_back(normed, factor, gain, upstream):
    gain_grad = jnp.sum(upstream * normed, axis=0)
    scaled = upstream * gain
    return (
        factor * (scaled - normed * jnp.mean(scaled * normed, axis=-1, keepdims=True)),
        gain_grad,
    )


def add_rows(target, update, offset):
    current = lax.dynamic_slice_in_dim(target, offset, update.shape[0], 0)
    return lax.dynamic_update_slice_in_dim(target, current + update, offset, 0)


def masked_scores(query_ext, key_pad, offset, row_pos, layout):
    block_rows, halo_rows, key_reach, key_block, groups, score_scale = layout
    extent = key_block + 4 * key_reach
    key_slab = lax.dynamic_slice_in_dim(key_pad, offset, extent, 0)
    raw_scores = (
        jnp.einsum("nrhd,khd->nhrk", query_ext, key_slab, preferred_element_type=jnp.float32)
        * score_scale
    )
    key_pos = offset - 2 * key_reach + jnp.arange(extent, dtype=jnp.int32)
    keep_mask = (key_pos[None, None, :] <= row_pos[:, :, None]) & (key_pos >= 0)[None, None, :]
    return jnp.where(keep_mask[:, None], raw_scores, 0.0)


def convolve(zeroed, kernel, shift, extent, layout):
    block_rows, halo_rows, key_reach = (layout[0], layout[1], layout[2])
    result = jnp.zeros(zeroed.shape[:2] + (block_rows, extent), jnp.float32)
    for row_tap in range(halo_rows + 1):
        for key_tap in range(2 * key_reach + 1):
            column = shift + 3 * key_reach - key_tap
            result = (
                result
                + kernel[:, row_tap, key_tap][None, :, None, None]
                * zeroed[
                    :,
                    :,
                    halo_rows - row_tap : halo_rows - row_tap + block_rows,
                    column : column + extent,
                ]
            )
    return result


def attend_forward(query_ext, row_pos, key_pad, value_pad, kernel, layout):
    block_rows, halo_rows, key_reach, key_block, groups, score_scale = layout
    members = query_ext.shape[0]
    head_count = query_ext.shape[2]
    pair_width = value_pad.shape[1] // groups
    block_count = jnp.max(row_pos) // key_block + 1

    def advance(position, carried):
        running_max, running_sum, gathered = carried
        offset = position * key_block
        zeroed = masked_scores(query_ext, key_pad, offset, row_pos, layout)
        logits = convolve(zeroed, kernel, 0, key_block, layout)
        key_pos = offset + jnp.arange(key_block, dtype=jnp.int32)
        valid_mask = key_pos[None, None, :] <= row_pos[:, halo_rows:, None]
        logits = jnp.where(valid_mask[:, None], logits, NEGATIVE)
        new_max = jnp.maximum(running_max, jnp.max(logits, axis=-1))
        shrink = jnp.exp(running_max - new_max)
        weights = jnp.exp(logits - new_max[..., None])
        running_sum = running_sum * shrink + jnp.sum(weights, axis=-1)
        value_slab = lax.dynamic_slice_in_dim(
            value_pad, offset + 2 * key_reach, key_block, 0
        ).reshape(key_block, groups, pair_width)
        low_weights = weights.astype(jnp.bfloat16).reshape(
            members, groups, 2, block_rows, key_block
        )
        gathered = gathered * shrink.reshape(members, groups, 2, block_rows, 1) + jnp.einsum(
            "ngpik,kgc->ngpic", low_weights, value_slab, preferred_element_type=jnp.float32
        )
        return (new_max, running_sum, gathered)

    initial = (
        jnp.full((members, head_count, block_rows), NEGATIVE, jnp.float32),
        jnp.zeros((members, head_count, block_rows), jnp.float32),
        jnp.zeros((members, groups, 2, block_rows, pair_width), jnp.float32),
    )
    running_max, running_sum, gathered = lax.fori_loop(0, block_count, advance, initial)
    mixed_in = gathered / running_sum.reshape(members, groups, 2, block_rows, 1)
    return (mixed_in, running_max + jnp.log(running_sum))


def attend_backward(
    query_ext,
    row_pos,
    key_pad,
    value_pad,
    kernel,
    log_total,
    mixed_low,
    delta_rows,
    key_acc,
    value_acc,
    layout,
):
    block_rows, halo_rows, key_reach, key_block, groups, score_scale = layout
    members = query_ext.shape[0]
    ext_rows = query_ext.shape[1]
    head_count = query_ext.shape[2]
    model_width = value_pad.shape[1]
    pair_width = model_width // groups
    extent = key_block + 2 * key_reach
    block_count = jnp.max(row_pos) // key_block + 1

    def advance(position, carried):
        query_grad, key_acc, value_acc, kernel_grad = carried
        offset = position * key_block
        zeroed = masked_scores(query_ext, key_pad, offset, row_pos, layout)
        logits = convolve(zeroed, kernel, -key_reach, extent, layout)
        key_pos = offset - key_reach + jnp.arange(extent, dtype=jnp.int32)
        valid_mask = (key_pos[None, None, :] <= row_pos[:, halo_rows:, None]) & (key_pos >= 0)[
            None, None, :
        ]
        probability = jnp.where(valid_mask[:, None], jnp.exp(logits - log_total[..., None]), 0.0)
        value_slab = lax.dynamic_slice_in_dim(value_pad, offset + key_reach, extent, 0).reshape(
            extent, groups, pair_width
        )
        prob_grad = jnp.einsum(
            "ngpic,kgc->ngpik", mixed_low, value_slab, preferred_element_type=jnp.float32
        ).reshape(members, head_count, block_rows, extent)
        logit_grad = probability * (prob_grad - delta_rows[..., None])
        central = (
            probability[..., key_reach : key_reach + key_block]
            .astype(jnp.bfloat16)
            .reshape(members, groups, 2, block_rows, key_block)
        )
        value_part = jnp.einsum(
            "ngpik,ngpic->kgc", central, mixed_low, preferred_element_type=jnp.float32
        ).reshape(key_block, model_width)
        value_acc = add_rows(value_acc, value_part, offset)
        middle = logit_grad[..., key_reach : key_reach + key_block]
        tap_sums = []
        for row_tap in range(halo_rows + 1):
            for key_tap in range(2 * key_reach + 1):
                column = 3 * key_reach - key_tap
                tap_sums.append(
                    jnp.sum(
                        middle
                        * zeroed[
                            :,
                            :,
                            halo_rows - row_tap : halo_rows - row_tap + block_rows,
                            column : column + key_block,
                        ],
                        axis=(0, 2, 3),
                    )
                )
        kernel_grad = kernel_grad + jnp.stack(tap_sums, axis=1).reshape(
            head_count, halo_rows + 1, 2 * key_reach + 1
        )
        padded = jnp.pad(logit_grad, ((0, 0), (0, 0), (halo_rows, halo_rows), (0, 0)))
        score_grad = jnp.zeros((members, head_count, ext_rows, key_block), jnp.float32)
        for row_tap in range(halo_rows + 1):
            for key_tap in range(2 * key_reach + 1):
                score_grad = (
                    score_grad
                    + kernel[:, row_tap, key_tap][None, :, None, None]
                    * padded[:, :, row_tap : row_tap + ext_rows, key_tap : key_tap + key_block]
                )
        key_central = offset + jnp.arange(key_block, dtype=jnp.int32)
        keep_mask = (key_central[None, None, :] <= row_pos[:, :, None]) & (key_central >= 0)[
            None, None, :
        ]
        score_low = jnp.where(keep_mask[:, None], score_grad, 0.0).astype(jnp.bfloat16)
        key_slab = lax.dynamic_slice_in_dim(key_pad, offset + 2 * key_reach, key_block, 0)
        query_grad = (
            query_grad
            + jnp.einsum("nhrk,khd->nrhd", score_low, key_slab, preferred_element_type=jnp.float32)
            * score_scale
        )
        key_part = (
            jnp.einsum(
                "nhrk,nrhd->khd", score_low, query_ext, preferred_element_type=jnp.float32
            ).reshape(key_block, model_width)
            * score_scale
        )
        key_acc = add_rows(key_acc, key_part, offset)
        return (query_grad, key_acc, value_acc, kernel_grad)

    initial = (
        jnp.zeros(query_ext.shape, jnp.float32),
        key_acc,
        value_acc,
        jnp.zeros(kernel.shape, jnp.float32),
    )
    return lax.fori_loop(0, block_count, advance, initial)


def reorder(selection, rows):
    return jnp.dot(
        selection.astype(rows.dtype), rows, precision=PRECISE, preferred_element_type=jnp.float32
    ).astype(rows.dtype)


def pick(table, places):
    return jnp.stack(
        [lax.dynamic_index_in_dim(table, places[i], 0, keepdims=False) for i in range(2)]
    )


def accumulate(previous, update):
    return (
        update
        if previous is None
        else tuple((left + right for left, right in zip(previous, update)))
    )


def general_device(
    inputs,
    out_grad,
    pair_index,
    norm_gain,
    query_weight,
    key_weight,
    value_weight,
    score_kernel,
    head_mixing,
    group_gain,
    output_weight,
    second_gain,
    gate_weight,
    up_weight,
    down_weight,
):
    micro_count = inputs.shape[0]
    local_rows = inputs.shape[2]
    block_rows = local_rows // 2
    model_width = inputs.shape[3]
    head_count = score_kernel.shape[0]
    head_dim = model_width // head_count
    groups = head_count // 2
    halo_rows = score_kernel.shape[1] - 1
    key_reach = (score_kernel.shape[2] - 1) // 2
    block_count = 2 * lax.axis_size("ctx")
    seq_length = block_count * block_rows
    key_block = min(512, seq_length)
    layout = (block_rows, halo_rows, key_reach, key_block, groups, head_dim ** (-0.5))
    extended = block_rows + halo_rows
    my_index = lax.axis_index("ctx")
    slot_ids = jnp.arange(block_count, dtype=jnp.int32)
    mix_table = head_mixing.reshape(groups, 2, 2)
    pad_width = ((2 * key_reach, 2 * key_reach), (0, 0))
    layer_rows = []
    input_rows = []
    feed_sums = None
    attention_sums = None
    kernel_total = jnp.zeros(score_kernel.shape, jnp.float32)
    mixing_total = jnp.zeros(head_mixing.shape, jnp.float32)
    for batch_index in range(micro_count):
        gain_first, query_full, key_full, value_full, gain_group, out_full = (
            lax.all_gather(norm_gain, ("seq", "ctx"), axis=0, tiled=True),
            lax.all_gather(query_weight, ("seq", "ctx"), axis=0, tiled=True),
            lax.all_gather(key_weight, ("seq", "ctx"), axis=0, tiled=True),
            lax.all_gather(value_weight, ("seq", "ctx"), axis=0, tiled=True),
            lax.all_gather(group_gain, ("seq", "ctx"), axis=0, tiled=True),
            lax.all_gather(output_weight, ("seq", "ctx"), axis=0, tiled=True),
        )
        tokens = inputs[batch_index, 0].astype(jnp.float32)
        normed_first, factor_first = normalize(tokens)
        hidden = (normed_first * gain_first.astype(jnp.float32)).astype(jnp.bfloat16)
        query_proj = jnp.dot(hidden, query_full, preferred_element_type=jnp.float32).astype(
            jnp.bfloat16
        )
        key_proj = jnp.dot(hidden, key_full, preferred_element_type=jnp.float32).astype(
            jnp.bfloat16
        )
        value_proj = jnp.dot(hidden, value_full, preferred_element_type=jnp.float32).astype(
            jnp.bfloat16
        )
        tail_rows = jnp.concatenate(
            [query_proj[block_rows - halo_rows : block_rows], query_proj[local_rows - halo_rows :]],
            axis=0,
        )
        key_dealt, value_dealt, tail_dealt = (
            lax.all_gather(key_proj, "ctx", axis=0, tiled=True),
            lax.all_gather(value_proj, "ctx", axis=0, tiled=True),
            lax.all_gather(tail_rows, "ctx", axis=0, tiled=True),
        )
        pairs_row = pair_index[batch_index]
        owner_pair = jnp.repeat(pairs_row, 2)
        block_of_slot = jnp.where(slot_ids % 2 == 0, owner_pair, block_count - 1 - owner_pair)
        to_natural = (block_of_slot[None, :] == slot_ids[:, None]).astype(jnp.float32)
        slot_of_block = jnp.sum(
            jnp.where(block_of_slot[None, :] == slot_ids[:, None], slot_ids[None, :], 0), axis=1
        )
        my_pair = lax.dynamic_index_in_dim(pairs_row, my_index, 0, keepdims=False)
        my_blocks = jnp.stack([my_pair, block_count - 1 - my_pair])
        key_pad = jnp.pad(
            reorder(to_natural, key_dealt.reshape(block_count, -1)).reshape(
                seq_length, model_width
            ),
            pad_width,
        ).reshape(-1, head_count, head_dim)
        value_pad = jnp.pad(
            reorder(to_natural, value_dealt.reshape(block_count, -1)).reshape(
                seq_length, model_width
            ),
            pad_width,
        )
        tail_blocks = reorder(to_natural, tail_dealt.reshape(block_count, -1)).reshape(
            block_count, halo_rows, model_width
        )
        previous = jnp.concatenate(
            [jnp.zeros((1, halo_rows, model_width), jnp.bfloat16), tail_blocks[:-1]], axis=0
        )
        query_ext = jnp.concatenate(
            [pick(previous, my_blocks), query_proj.reshape(2, block_rows, model_width)], axis=1
        ).reshape(2, extended, head_count, head_dim)
        row_pos = (
            my_blocks[:, None] * block_rows
            - halo_rows
            + jnp.arange(extended, dtype=jnp.int32)[None, :]
        )
        mixed_in, log_total = attend_forward(
            query_ext, row_pos, key_pad, value_pad, score_kernel, layout
        )
        mixed_six = mixed_in.reshape(2, groups, 2, block_rows, 2, head_dim)
        heads_out = jnp.einsum(
            "gqp,ngpiqd->nigqd", mix_table, mixed_six, precision=PRECISE
        ).reshape(local_rows, head_count, head_dim)
        group_normed, group_factor = normalize(heads_out)
        normed_low = (
            group_normed.reshape(local_rows, model_width) * gain_group.astype(jnp.float32)
        ).astype(jnp.bfloat16)
        residual = tokens + jnp.dot(normed_low, out_full, preferred_element_type=jnp.float32)
        gain_second, gate_full, up_full, down_full = (
            lax.all_gather(second_gain, ("seq", "ctx"), axis=0, tiled=True),
            lax.all_gather(gate_weight, ("seq", "ctx"), axis=0, tiled=True),
            lax.all_gather(up_weight, ("seq", "ctx"), axis=0, tiled=True),
            lax.all_gather(down_weight, ("seq", "ctx"), axis=0, tiled=True),
        )
        normed_second, factor_second = normalize(residual)
        second_hidden = (normed_second * gain_second.astype(jnp.float32)).astype(jnp.bfloat16)
        gate_proj = jnp.dot(second_hidden, gate_full, preferred_element_type=jnp.float32)
        up_proj = jnp.dot(second_hidden, up_full, preferred_element_type=jnp.float32)
        activated = (jax.nn.silu(gate_proj) * up_proj).astype(jnp.bfloat16)
        layer_rows.append(
            (residual + jnp.dot(activated, down_full, preferred_element_type=jnp.float32)).astype(
                jnp.bfloat16
            )
        )
        gain_second, gate_full, up_full, down_full = (
            lax.all_gather(second_gain, ("seq", "ctx"), axis=0, tiled=True),
            lax.all_gather(gate_weight, ("seq", "ctx"), axis=0, tiled=True),
            lax.all_gather(up_weight, ("seq", "ctx"), axis=0, tiled=True),
            lax.all_gather(down_weight, ("seq", "ctx"), axis=0, tiled=True),
        )
        grad_rows = out_grad[batch_index, 0]
        hid_grad = jnp.dot(grad_rows, down_full.T, preferred_element_type=jnp.float32)
        down_grad = jnp.dot(activated.T, grad_rows, preferred_element_type=jnp.float32)
        sigmoid_gate = jax.nn.sigmoid(gate_proj)
        up_low = (hid_grad * gate_proj * sigmoid_gate).astype(jnp.bfloat16)
        gate_low = (
            hid_grad * up_proj * sigmoid_gate * (1.0 + gate_proj * (1.0 - sigmoid_gate))
        ).astype(jnp.bfloat16)
        second_grad = jnp.dot(gate_low, gate_full.T, preferred_element_type=jnp.float32) + jnp.dot(
            up_low, up_full.T, preferred_element_type=jnp.float32
        )
        gate_grad = jnp.dot(second_hidden.T, gate_low, preferred_element_type=jnp.float32)
        up_grad = jnp.dot(second_hidden.T, up_low, preferred_element_type=jnp.float32)
        residual_part, gain_second_grad = normalize_back(
            normed_second, factor_second, gain_second.astype(jnp.float32), second_grad
        )
        residual_grad = grad_rows.astype(jnp.float32) + residual_part
        feed_shards = (
            lax.psum_scatter(gain_second_grad, ("seq", "ctx"), scatter_dimension=0, tiled=True),
            lax.psum_scatter(gate_grad, ("seq", "ctx"), scatter_dimension=0, tiled=True),
            lax.psum_scatter(up_grad, ("seq", "ctx"), scatter_dimension=0, tiled=True),
            lax.psum_scatter(down_grad, ("seq", "ctx"), scatter_dimension=0, tiled=True),
        )
        feed_sums = accumulate(feed_sums, feed_shards)
        gain_first, query_full, key_full, value_full, gain_group, out_full = (
            lax.all_gather(norm_gain, ("seq", "ctx"), axis=0, tiled=True),
            lax.all_gather(query_weight, ("seq", "ctx"), axis=0, tiled=True),
            lax.all_gather(key_weight, ("seq", "ctx"), axis=0, tiled=True),
            lax.all_gather(value_weight, ("seq", "ctx"), axis=0, tiled=True),
            lax.all_gather(group_gain, ("seq", "ctx"), axis=0, tiled=True),
            lax.all_gather(output_weight, ("seq", "ctx"), axis=0, tiled=True),
        )
        attended_low = residual_grad.astype(jnp.bfloat16)
        out_weight_grad = jnp.dot(normed_low.T, attended_low, preferred_element_type=jnp.float32)
        normed_grad = jnp.dot(attended_low, out_full.T, preferred_element_type=jnp.float32)
        heads_grad, gain_group_grad = normalize_back(
            group_normed,
            group_factor,
            gain_group.astype(jnp.float32).reshape(head_count, head_dim),
            normed_grad.reshape(local_rows, head_count, head_dim),
        )
        heads_five = heads_grad.reshape(2, block_rows, groups, 2, head_dim)
        mixing_total = mixing_total + jnp.einsum(
            "nigqd,ngpiqd->gqp", heads_five, mixed_six, precision=PRECISE
        ).reshape(head_count, 2)
        mixed_grad = jnp.einsum(
            "gqp,nigqd->ngpiqd", mix_table, heads_five, precision=PRECISE
        ).reshape(2, groups, 2, block_rows, 2 * head_dim)
        mixed_low = mixed_grad.astype(jnp.bfloat16)
        delta_rows = jnp.sum(mixed_low.astype(jnp.float32) * mixed_in, axis=-1).reshape(
            2, head_count, block_rows
        )
        key_acc = jnp.zeros((seq_length, model_width), jnp.float32)
        value_acc = jnp.zeros((seq_length, model_width), jnp.float32)
        query_grad, key_acc, value_acc, kernel_part = attend_backward(
            query_ext,
            row_pos,
            key_pad,
            value_pad,
            score_kernel,
            log_total,
            mixed_low,
            delta_rows,
            key_acc,
            value_acc,
            layout,
        )
        kernel_total = kernel_total + kernel_part
        halo_grad = query_grad[:, :halo_rows].reshape(2, halo_rows, model_width)
        own_grad = query_grad[:, halo_rows:].reshape(2, block_rows, model_width)
        target_slot = pick(slot_of_block, jnp.maximum(my_blocks - 1, 0))
        routing = ((slot_ids[None, :] == target_slot[:, None]) & (my_blocks > 0)[:, None]).astype(
            jnp.float32
        )
        tail_grad = jnp.einsum("ws,wrc->src", routing, halo_grad, precision=PRECISE).reshape(
            block_count * halo_rows, model_width
        )
        key_back = reorder(to_natural.T, key_acc.reshape(block_count, -1)).reshape(
            seq_length, model_width
        )
        value_back = reorder(to_natural.T, value_acc.reshape(block_count, -1)).reshape(
            seq_length, model_width
        )
        key_mine, value_mine, tail_mine = (
            lax.psum_scatter(
                key_back.astype(jnp.bfloat16), "ctx", scatter_dimension=0, tiled=True
            ).astype(jnp.float32),
            lax.psum_scatter(
                value_back.astype(jnp.bfloat16), "ctx", scatter_dimension=0, tiled=True
            ).astype(jnp.float32),
            lax.psum_scatter(
                tail_grad.astype(jnp.bfloat16), "ctx", scatter_dimension=0, tiled=True
            ).astype(jnp.float32),
        )
        tail_mine = tail_mine.reshape(2, halo_rows, model_width)
        query_total = jnp.concatenate(
            [
                own_grad[:, : block_rows - halo_rows],
                own_grad[:, block_rows - halo_rows :] + tail_mine,
            ],
            axis=1,
        ).reshape(local_rows, model_width)
        query_low = query_total.astype(jnp.bfloat16)
        key_low = key_mine.astype(jnp.bfloat16)
        value_low = value_mine.astype(jnp.bfloat16)
        query_w_grad = jnp.dot(hidden.T, query_low, preferred_element_type=jnp.float32)
        key_w_grad = jnp.dot(hidden.T, key_low, preferred_element_type=jnp.float32)
        value_w_grad = jnp.dot(hidden.T, value_low, preferred_element_type=jnp.float32)
        hidden_grad = (
            jnp.dot(query_low, query_full.T, preferred_element_type=jnp.float32)
            + jnp.dot(key_low, key_full.T, preferred_element_type=jnp.float32)
            + jnp.dot(value_low, value_full.T, preferred_element_type=jnp.float32)
        )
        token_part, gain_first_grad = normalize_back(
            normed_first, factor_first, gain_first.astype(jnp.float32), hidden_grad
        )
        input_rows.append((residual_grad + token_part).astype(jnp.bfloat16))
        attention_shards = (
            lax.psum_scatter(gain_first_grad, ("seq", "ctx"), scatter_dimension=0, tiled=True),
            lax.psum_scatter(query_w_grad, ("seq", "ctx"), scatter_dimension=0, tiled=True),
            lax.psum_scatter(key_w_grad, ("seq", "ctx"), scatter_dimension=0, tiled=True),
            lax.psum_scatter(value_w_grad, ("seq", "ctx"), scatter_dimension=0, tiled=True),
            lax.psum_scatter(
                gain_group_grad.reshape(model_width),
                ("seq", "ctx"),
                scatter_dimension=0,
                tiled=True,
            ),
            lax.psum_scatter(out_weight_grad, ("seq", "ctx"), scatter_dimension=0, tiled=True),
        )
        attention_sums = accumulate(attention_sums, attention_shards)
    kernel_sum, mixing_sum = lax.psum((kernel_total, mixing_total), ("seq", "ctx"))
    layer_out = jnp.stack(layer_rows)[:, None]
    input_grad = jnp.stack(input_rows)[:, None]
    return (
        layer_out,
        input_grad,
        attention_sums[0],
        attention_sums[1],
        attention_sums[2],
        attention_sums[3],
        kernel_sum,
        mixing_sum,
        attention_sums[4],
        attention_sums[5],
        feed_sums[0],
        feed_sums[1],
        feed_sums[2],
        feed_sums[3],
    )


def on_device(
    inputs,
    out_grad,
    pair_index,
    norm_gain,
    query_weight,
    key_weight,
    value_weight,
    score_kernel,
    head_mixing,
    group_gain,
    output_weight,
    second_gain,
    gate_weight,
    up_weight,
    down_weight,
):
    groups, planes = lax.axis_size("ctx"), lax.axis_size("seq")
    heads, width = score_kernel.shape[0], inputs.shape[3]
    if groups != 8 or heads != 2 * groups or (groups * inputs.shape[2]) % TILE:
        return general_device(
            inputs, out_grad, pair_index, norm_gain, query_weight, key_weight, value_weight,
            score_kernel, head_mixing, group_gain, output_weight, second_gain, gate_weight,
            up_weight, down_weight,
        )
    micro, local = inputs.shape[0], inputs.shape[2]
    blk, seq = local // 2, local * groups
    blocks = seq // blk
    pair = width // groups
    owned = width // (groups * planes)
    hidden = gate_weight.shape[1]
    chunk = hidden // (groups * planes)
    me = lax.axis_index("ctx")
    tokens_low = inputs.reshape(micro * local, width)
    grads_low = out_grad.reshape(micro * local, width)

    rows_all = micro * local
    qkv_shape = (groups, owned, 3 * pair)
    feed_shape = (groups, owned, 2 * planes * chunk)
    spread_sems = [DMA((9,))] * 2
    feed_mine, qkv, gains, all_tokens, out_rows = communicate(
        functools.partial(enter_kernel, planes), "enter", 1, 50,
        [
            (feed_shape, BF16),
            ((planes,) + qkv_shape, BF16),
            ((planes, groups, 8, TILE), F32),
            ((groups, rows_all, width), BF16),
            ((planes, owned, width), BF16),
        ],
        [pltpu.VMEM((owned, width), BF16)] * 3 + [pltpu.VMEM((owned, hidden), BF16)] * 2
        + [pltpu.VMEM((owned,), BF16)] * 3 + [pltpu.VMEM((8, TILE), F32)]
        + [pltpu.VMEM(qkv_shape, BF16), pltpu.VMEM(feed_shape, BF16)]
        + [DMA((3, groups))] * 2 + spread_sems + [DMA((1, 2, planes))] * 2
        + [DMA((2, 2, planes))] * 2 + [DMA((13,))],
        (
            query_weight, key_weight, value_weight, gate_weight, up_weight, norm_gain, group_gain,
            second_gain, tokens_low, output_weight,
        ),
        ANYWHERE,
    )
    all_tokens, down_mine = lax.optimization_barrier((all_tokens, down_weight))
    feed = lax.all_gather(feed_mine.reshape(groups * owned, -1), "seq", axis=0, tiled=True)
    down = lax.all_gather(down_mine, "seq", axis=0, tiled=True)
    qkv = qkv.reshape(width, 3 * pair)
    hidden_all, heads_in, gains, gain_pair, out_rows, all_grads = communicate(
        functools.partial(heads_kernel, planes), "heads", 2, 20,
        [
            ((width, groups * rows_all), BF16),
            ((groups * rows_all, 3 * pair), BF16),
            ((8, width), F32),
            ((8, pair), F32),
            ((4, owned, width), BF16),
            ((groups, rows_all, width), BF16),
        ],
        [
            pltpu.VMEM((groups, rows_all, width), BF16),
            pltpu.VMEM((width, 3 * pair), BF16),
            pltpu.VMEM((width, groups * rows_all), BF16),
            pltpu.VMEM((groups * rows_all, 3 * pair), BF16),
        ]
        + [DMA((4,))] * 2 + spread_sems + [DMA((groups + 1,)), DMA((2, groups)), DMA((2,))],
        (all_tokens, qkv, gains, out_rows, grads_low),
        None, [ANYWHERE] * 2 + [ON_CHIP] + [ANYWHERE] * 2, (ANYWHERE,) * 2 + (ON_CHIP,) * 2 + (ANYWHERE,) * 2,
    )
    all_grads = all_grads.reshape(-1, width)
    out_rows = out_rows.reshape(pair, width)

    slots = jnp.arange(blocks, dtype=jnp.int32)
    owner = jnp.repeat(pair_index, 2, axis=1)
    block_of_slot = jnp.where(slots % 2 == 0, owner, blocks - 1 - owner)
    place = (
        (slots // 2)[None] * (2 * micro)
        + 2 * jnp.arange(micro, dtype=jnp.int32)[:, None]
        + (slots % 2)[None]
    )
    blk_table = jnp.sum(
        jnp.where(block_of_slot[:, None, :] == slots[None, :, None], place[:, None, :], 0), axis=2
    ).astype(jnp.int32)
    ker = lax.dynamic_slice_in_dim(score_kernel, 2 * me, 2, 0)
    mix = jnp.repeat(lax.dynamic_slice_in_dim(head_mixing, 2 * me, 2, 0), pair // 2, axis=0).T
    scale = (width // heads) ** (-0.5)

    mixed, y, prob = pair_forward(blk_table, ker, mix, gain_pair, heads_in, micro, seq, blk, scale)
    by_core = (groups // 2, 2, rows_all)
    sum_spec = sum_scratch(rows_all, width)
    residual, second_all = communicate(
        second_kernel, "second", 3, 40,
        [((rows_all, width), F32), ((groups, rows_all, width), BF16)],
        [
            pltpu.VMEM(by_core + (pair,), BF16),
            pltpu.VMEM((pair, width), BF16),
            pltpu.VMEM((rows_all, width), BF16),
            pltpu.VMEM((rows_all, width), F32),
            pltpu.VMEM((rows_all, width), BF16),
            DMA((5,)),
        ]
        + sum_spec + spread_sems,
        (mixed.reshape(by_core + (pair,)), out_rows, tokens_low, gains),
        None, [ANYWHERE] * 3 + [ON_CHIP], (ANYWHERE,) * 2,
    )
    second_all = second_all.reshape(-1, width)

    half = planes * chunk
    both = jnp.dot(second_all, feed, preferred_element_type=F32)
    gate, up = both[:, :half], both[:, half:]
    sigmoid = jax.nn.sigmoid(gate)
    active = (gate * sigmoid * up).astype(BF16)
    slopes = jnp.concatenate(
        [up * sigmoid * (1.0 + gate * (1.0 - sigmoid)), gate * sigmoid], axis=1
    )
    down_grad = lax.dot_general(active, all_grads, (((0,), (0,)), ((), ())), preferred_element_type=F32)
    all_grads, down_grad, slopes = lax.optimization_barrier((all_grads, down_grad.astype(BF16), slopes))
    hid_grad = lax.dot_general(all_grads, down, (((1,), (1,)), ((), ())), preferred_element_type=F32)
    lows = (jnp.concatenate([hid_grad, hid_grad], axis=1) * slopes).astype(BF16)
    feed_grad = lax.dot_general(second_all, lows, (((0,), (0,)), ((), ())), preferred_element_type=F32)
    lows, feed_grad = lax.optimization_barrier((lows, feed_grad.astype(BF16)))
    feed_sum = lax.psum_scatter(feed_grad, "seq", scatter_dimension=0, tiled=True)
    down_sum = lax.psum_scatter(down_grad, "seq", scatter_dimension=0, tiled=True)
    residual_grad, gain_second_grad, mixed_grad, out_w_grad = communicate(
        back_kernel, "back", 4, 42,
        [
            ((rows_all, width), F32),
            ((1, width), F32),
            ((groups, rows_all, pair), BF16),
            ((pair, width), BF16),
        ],
        [
            pltpu.VMEM(by_core + (2 * half,), BF16),
            pltpu.VMEM((width, 2 * half), BF16),
            pltpu.VMEM((rows_all, width), F32),
            pltpu.VMEM((rows_all, width), BF16),
            pltpu.VMEM((pair, width), BF16),
            pltpu.VMEM((groups, rows_all, pair), BF16),
            pltpu.VMEM((rows_all, width), F32),
            pltpu.VMEM((groups, rows_all, width), BF16),
            pltpu.VMEM((pair, width), F32),
            DMA((7,)),
        ]
        + sum_spec + spread_sems,
        (
            lows.reshape(by_core + (2 * half,)), feed, residual, grads_low, out_rows,
            mixed.reshape(groups, rows_all, pair), gains,
        ),
        None, [ANYWHERE] * 6 + [ON_CHIP], (ANYWHERE, ON_CHIP, ON_CHIP, ON_CHIP),
    )
    mixed_grad = mixed_grad.reshape(-1, pair)
    qkv_low, misc = pair_backward(
        blk_table, ker, mix, gain_pair, heads_in, mixed_grad, y, prob, seq, blk, scale
    )
    small = (8, width)
    layer_out, row_grad = communicate(
        layer_kernel, "layer", 6, 18, [((rows_all, width), BF16), ((planes, owned, width), BF16)],
        [
            pltpu.VMEM(by_core + (half,), BF16),
            pltpu.VMEM((half, width), BF16),
            pltpu.VMEM((rows_all, width), F32),
            DMA((3,)),
        ]
        + sum_spec + [DMA((4,))] * 2 + [DMA],
        (
            active.reshape(by_core + (half,)), down, residual,
            out_w_grad.reshape(4, owned, width),
        ),
        None, [ANYWHERE] * 4, (ON_CHIP, ANYWHERE),
    )
    input_grad, sums, misc, qkv_back, feed_back, out_w_back = communicate(
        functools.partial(leave_kernel, planes), "leave", 5, 55,
        [
            ((rows_all, width), BF16),
            (small, F32),
            ((groups,) + misc.shape, F32),
            (qkv_shape, BF16),
            (feed_shape, BF16),
            ((1, owned, width), BF16),
        ],
        [
            pltpu.VMEM(by_core + (3 * pair,), BF16),
            pltpu.VMEM((width, 3 * pair), BF16),
            pltpu.VMEM(hidden_all.shape, BF16),
            pltpu.VMEM((rows_all, width), F32),
            pltpu.VMEM((rows_all, width), BF16),
            DMA((5,)),
            pltpu.VMEM((planes,) + misc.shape, F32),
            DMA((2, groups)),
            DMA((2, groups)),
        ]
        + sum_spec[:6]
        + [pltpu.VMEM((groups,) + small, F32), pltpu.VMEM((planes,) + small, F32)]
        + [pltpu.VMEM((planes, groups * owned, 4 * pair), BF16)]
        + [pltpu.VMEM((2, planes, groups * owned, 4 * pair), BF16)] * 2
        + [pltpu.VMEM(qkv_shape, BF16)]
        + sum_spec[6:]
        + [DMA((2, groups))] * 2
        + [DMA((2, 2, planes))] * 2
        + [DMA((2, groups))] * 2
        + [DMA((3,))],
        (
            qkv_low.reshape(by_core + (3 * pair,)), qkv, hidden_all,
            residual_grad, tokens_low, gains, gain_second_grad, misc,
            feed_sum.reshape(feed_shape), row_grad,
        ),
        None, [ANYWHERE] * 5 + [ON_CHIP] * 3 + [ANYWHERE, ON_CHIP],
        (ON_CHIP,) * 3 + (ANYWHERE,) * 2 + (ON_CHIP,),
    )
    plain = [(owned, width)] * 3 + [(owned, hidden)] * 2 + [(owned, width), (chunk, width)]
    landed = (qkv_back, feed_back, out_w_back, down_sum, input_grad, layer_out)
    out_shapes = [jax.ShapeDtypeStruct(shape, F32) for shape in plain]
    out_shapes += [jax.ShapeDtypeStruct((rows_all, width), BF16)] * 2
    row = jax.ShapeDtypeStruct((1, owned), F32)
    flat_index = (lax.axis_index("seq") * groups + me).astype(jnp.int32).reshape(1)
    results = pl.pallas_call(
        functools.partial(finish_kernel, len(out_shapes)),
        name="finish",
        out_shape=tuple(out_shapes)
        + (row, row, row)
        + (jax.ShapeDtypeStruct(score_kernel.shape[::-1], F32), jax.ShapeDtypeStruct((2, heads), F32)),
        in_specs=[pl.BlockSpec(memory_space=pltpu.SMEM)] + [ON_CHIP] * 2 + [ANYWHERE] * 6,
        out_specs=(ANYWHERE,) * len(out_shapes) + (ON_CHIP,) * 5,
        scratch_shapes=[pltpu.VMEM(value.shape, BF16) for value in landed]
        + [pltpu.VMEM(shape, F32) for shape in plain]
        + [DMA((6,)), DMA((len(out_shapes),))],
        compiler_params=pltpu.CompilerParams(vmem_limit_bytes=60 << 20),
    )(flat_index, sums, misc, *landed)
    q_back, k_back, v_back, gate_back, up_back, out_w_out, down_out, input_grad, layer_out = results[:9]
    gain_outs = [value.reshape(owned) for value in results[9:12]]
    ker_out, mix_out = jnp.transpose(results[12], (2, 1, 0)), results[13].T

    shape = inputs.shape
    return (
        layer_out.reshape(shape),
        input_grad.reshape(shape),
        gain_outs[0],
        q_back,
        k_back,
        v_back,
        ker_out,
        mix_out,
        gain_outs[1],
        out_w_out,
        gain_outs[2],
        gate_back,
        up_back,
        down_out,
    )


def solution(mesh):
    placed = (
        P(None, "seq", "ctx", None),
        P(None, "seq", "ctx", None),
        P(),
        P(("seq", "ctx")),
        P(("seq", "ctx"), None),
        P(("seq", "ctx"), None),
        P(("seq", "ctx"), None),
        P(),
        P(),
        P(("seq", "ctx")),
        P(("seq", "ctx"), None),
        P(("seq", "ctx")),
        P(("seq", "ctx"), None),
        P(("seq", "ctx"), None),
        P(("seq", "ctx"), None),
    )
    return jax.shard_map(
        on_device,
        mesh=mesh,
        in_specs=placed,
        out_specs=(
            P(None, "seq", "ctx", None),
            P(None, "seq", "ctx", None),
            P(("seq", "ctx")),
            P(("seq", "ctx"), None),
            P(("seq", "ctx"), None),
            P(("seq", "ctx"), None),
            P(),
            P(),
            P(("seq", "ctx")),
            P(("seq", "ctx"), None),
            P(("seq", "ctx")),
            P(("seq", "ctx"), None),
            P(("seq", "ctx"), None),
            P(("seq", "ctx"), None),
        ),
        check_vma=False,
    )
```

```python
import functools

import jax
import jax.numpy as jnp
from jax import lax
from jax.experimental import pallas as pl
from jax.experimental.pallas import tpu as pltpu
from jax.sharding import PartitionSpec as P

EPSILON = 1e-05
NEGATIVE = -1e30
F32 = jnp.float32
BF16 = jnp.bfloat16
TILE = 128


def nt(left, right):
    return lax.dot_general(left, right, (((1,), (1,)), ((), ())), preferred_element_type=F32)


def tn(left, right):
    return lax.dot_general(left, right, (((0,), (0,)), ((), ())), preferred_element_type=F32)


def nn(left, right):
    return lax.dot_general(left, right, (((1,), (0,)), ((), ())), preferred_element_type=F32)


def natural_rows(blk_ref, m, blk, seq):
    return [pl.multiple_of(blk_ref[m, b] * blk, blk) for b in range(seq // blk)]


def head_lanes(width):
    return lax.broadcasted_iota(jnp.int32, (1, width), 1) < width // 2


def load_heads(blk_ref, m, blk, seq, qkv_ref, qm, kf, ks, vn):
    width = vn.shape[1]
    first = head_lanes(width)
    kf[0:8, :] = jnp.zeros((8, width), F32)
    kf[seq : seq + TILE + 8, :] = jnp.zeros((TILE + 8, width), F32)
    for b, row in enumerate(natural_rows(blk_ref, m, blk, seq)):
        here = pl.ds(blk * b, blk)
        q = qkv_ref[pl.ds(row, blk), 0:width].astype(F32)
        qm[0, here, :] = jnp.where(first, q, 0.0).astype(BF16)
        qm[1, here, :] = jnp.where(first, 0.0, q).astype(BF16)
        kf[pl.ds(blk * b + 5, blk), :] = qkv_ref[pl.ds(row, blk), width : 2 * width].astype(F32)
        vn[here, :] = qkv_ref[pl.ds(row, blk), 2 * width : 3 * width]
    ks[...] = kf[0 : seq + TILE, :].astype(BF16)


def scores(qm, ks, h, rb, upto, scale):
    rows = pl.ds(TILE * rb, TILE)
    raw = nt(qm[h, rows, :], ks[0 : TILE * upto, :]) * scale
    key = lax.broadcasted_iota(jnp.int32, raw.shape, 1) - 5
    row = lax.broadcasted_iota(jnp.int32, raw.shape, 0) + TILE * rb
    return jnp.where((key >= 0) & (key <= row), raw, 0.0)


def head_factor(values, first, dim):
    squares = values * values
    own = jnp.sum(jnp.where(first, squares, 0.0), axis=1, keepdims=True)
    other = jnp.sum(jnp.where(first, 0.0, squares), axis=1, keepdims=True)
    return jnp.where(
        first, lax.rsqrt(own / dim + EPSILON), lax.rsqrt(other / dim + EPSILON)
    )


def forward_kernel(
    seq, blk, rows_tap, keys_tap, scale,
    blk_ref, ker_ref, mix_ref, gain_ref, qkv_ref,
    z_ref, y_ref, p_ref,
    qm, kf, ks, vn, shi, slo, thi, tlo, run, logit,
):
    m = pl.program_id(0)
    width = vn.shape[1]
    first = head_lanes(width)
    tiles = seq // TILE

    @pl.when(m == 0)
    def _():
        shi[...] = jnp.zeros(shi.shape, BF16)
        slo[...] = jnp.zeros(slo.shape, BF16)
        away = lax.broadcasted_iota(jnp.int32, (2 * TILE, TILE), 0) - lax.broadcasted_iota(
            jnp.int32, (2 * TILE, TILE), 1
        )
        for h in range(2):
            for a in range(rows_tap):
                band = jnp.zeros((2 * TILE, TILE), F32)
                for t in range(keys_tap):
                    band = jnp.where(away == keys_tap - 1 - t, ker_ref[h, a, t], band)
                high = band.astype(BF16)
                thi[h, :, TILE * a : TILE * (a + 1)] = high
                tlo[h, :, TILE * a : TILE * (a + 1)] = (band - high.astype(F32)).astype(BF16)

    load_heads(blk_ref, m, blk, seq, qkv_ref, qm, kf, ks, vn)
    for h in range(2):
        for rb in range(tiles):
            upto = min(rb + 2, tiles + 1)
            zeroed = scores(qm, ks, h, rb, upto, scale)
            high = zeroed.astype(BF16)
            shi[pl.ds(16 + TILE * rb, TILE), 0 : TILE * upto] = high
            slo[pl.ds(16 + TILE * rb, TILE), 0 : TILE * upto] = (zeroed - high.astype(F32)).astype(BF16)
        for b in range(tiles):
            count = seq - TILE * b
            rows = pl.ds(TILE * b, count + 16)
            lanes = pl.ds(TILE * b, 2 * TILE)
            high, low = shi[rows, lanes], slo[rows, lanes]
            run[0 : count + 16, :] = nn(high, thi[h]) + nn(low, thi[h]) + nn(high, tlo[h])
            total = run[16 : 16 + count, 0:TILE]
            for a in range(1, rows_tap):
                total = total + run[pl.ds(16 - a, count), TILE * a : TILE * (a + 1)]
            logit[pl.ds(TILE * b, count), TILE * b : TILE * (b + 1)] = total
        for rb in range(tiles):
            rows = pl.ds(TILE * rb, TILE)
            wide = TILE * (rb + 1)
            value = logit[rows, 0:wide]
            key = lax.broadcasted_iota(jnp.int32, value.shape, 1)
            row = lax.broadcasted_iota(jnp.int32, value.shape, 0) + TILE * rb
            value = jnp.where(key <= row, value, NEGATIVE)
            weight = jnp.exp(value - jnp.max(value, axis=1, keepdims=True))
            weight = weight / jnp.sum(weight, axis=1, keepdims=True)
            lowered = weight.astype(BF16)
            p_ref[0, h, rows, 0:wide] = lowered
            y_ref[0, h, rows, :] = nn(lowered, vn[0:wide, :])
    out = mix_ref[0:1, :] * y_ref[0, 0] + mix_ref[1:2, :] * y_ref[0, 1]
    normed = out * head_factor(out, first, width // 2)
    final = (normed * gain_ref[1:2, :]).astype(BF16)
    for b, row in enumerate(natural_rows(blk_ref, m, blk, seq)):
        z_ref[pl.ds(row, blk), :] = final[blk * b : blk * (b + 1), :]


def backward_kernel(
    seq, blk, rows_tap, keys_tap, scale,
    blk_ref, ker_ref, mix_ref, gain_ref, qkv_ref, zg_ref, y_ref, p_ref,
    low_ref, misc_ref,
    qm, kf, ks, vn, sb, up, zn, yl, cg, cs, eb, qa, ka, acc, taps,
):
    m = pl.program_id(0)
    width = vn.shape[1]
    first = head_lanes(width)
    tiles = seq // TILE
    wide_u = 3 * TILE
    span = keys_tap - 1
    lanes_all = rows_tap * TILE

    @pl.when(m == 0)
    def _():
        misc_ref[...] = jnp.zeros(misc_ref.shape, F32)
        taps[...] = jnp.zeros(taps.shape, F32)
        acc[...] = jnp.zeros(acc.shape, F32)
        cg[seq : seq + 8, :] = jnp.zeros((8, seq), F32)
        for b in range(1, tiles):
            start = TILE * b - 16
            cg[start : TILE * b, TILE * b : TILE * (b + 1)] = jnp.zeros((16, TILE), F32)
            cs[0:start, lanes_all * b : lanes_all * (b + 1)] = jnp.zeros((start, lanes_all), BF16)
        eb[...] = jnp.zeros(eb.shape, BF16)
        sb[...] = jnp.zeros(sb.shape, BF16)
        away = lax.broadcasted_iota(jnp.int32, (2 * TILE, TILE), 0) - lax.broadcasted_iota(
            jnp.int32, (2 * TILE, TILE), 1
        )
        none = jnp.zeros((TILE, TILE), BF16)
        for h in range(2):
            for a in range(rows_tap):
                band = jnp.zeros((2 * TILE, TILE), F32)
                for t in range(keys_tap):
                    band = jnp.where(away == TILE - span + t, ker_ref[h, a, t], band)
                band = band.astype(BF16)
                at = wide_u * a
                up[h, at : at + 2 * TILE, 0:TILE] = band
                up[h, at + 2 * TILE : at + wide_u, 0:TILE] = none
                up[h, at : at + TILE, TILE : 2 * TILE] = none
                up[h, at + TILE : at + wide_u, TILE : 2 * TILE] = band

    load_heads(blk_ref, m, blk, seq, qkv_ref, qm, kf, ks, vn)
    places = natural_rows(blk_ref, m, blk, seq)
    for b, row in enumerate(places):
        zn[pl.ds(blk * b, blk), :] = zg_ref[pl.ds(row, blk), :].astype(F32)
    dim = width // 2
    y0, y1 = y_ref[0, 0], y_ref[0, 1]
    out = mix_ref[0:1, :] * y0 + mix_ref[1:2, :] * y1
    factor = head_factor(out, first, dim)
    normed = out * factor
    upstream = zn[...]
    misc_ref[16:17, 0:width] += jnp.sum(upstream * normed, axis=0, keepdims=True)
    scaled = upstream * gain_ref[1:2, :]
    both = scaled * normed
    own = jnp.sum(jnp.where(first, both, 0.0), axis=1, keepdims=True) / dim
    other = jnp.sum(jnp.where(first, 0.0, both), axis=1, keepdims=True) / dim
    out_grad = factor * (scaled - normed * jnp.where(first, own, other))
    misc_ref[17:18, 0:width] += jnp.sum(out_grad * y0, axis=0, keepdims=True)
    misc_ref[18:19, 0:width] += jnp.sum(out_grad * y1, axis=0, keepdims=True)
    yl[0] = (mix_ref[0:1, :] * out_grad).astype(BF16)
    yl[1] = (mix_ref[1:2, :] * out_grad).astype(BF16)

    for b in range(tiles):
        rows = pl.ds(TILE * b, seq - TILE * b)
        lanes = pl.ds(TILE * b, TILE)
        part = tn(p_ref[0, 0, rows, lanes], yl[0, rows, :]) + tn(p_ref[0, 1, rows, lanes], yl[1, rows, :])
        part = part.astype(BF16)
        for i in range(TILE // blk):
            low_ref[pl.ds(places[b * (TILE // blk) + i], blk), 2 * width : 3 * width] = part[blk * i : blk * (i + 1), :]

    ka[...] = jnp.zeros(ka.shape, F32)
    for h in range(2):
        for rb in range(tiles):
            rows = pl.ds(TILE * rb, TILE)
            upto = min(rb + 2, tiles + 1)
            sb[rows, 0 : TILE * upto] = scores(qm, ks, h, rb, upto, scale).astype(BF16)
            wide = TILE * (rb + 1)
            prob = p_ref[0, h, rows, 0:wide].astype(F32)
            grad = nt(yl[h, rows, :], vn[0:wide, :])
            both = prob * grad
            cg[rows, 0:wide] = both - prob * jnp.sum(both, axis=1, keepdims=True)
        for b in range(tiles):
            start = max(0, TILE * b - 16)
            count = seq - start
            for a in range(rows_tap):
                cs[pl.ds(start, count), pl.ds(lanes_all * b + TILE * a, TILE)] = cg[
                    pl.ds(start + a, count), TILE * b : TILE * (b + 1)
                ].astype(BF16)
            acc[h] += tn(
                sb[pl.ds(start, count), pl.ds(TILE * b, TILE + 16)],
                cs[pl.ds(start, count), pl.ds(lanes_all * b, lanes_all)],
            )
        for b in range(0, tiles + 1, 2):
            start = max(0, TILE * b - 16)
            count = seq - start
            columns = min(2, tiles + 1 - b)
            left, right = [], []
            for a in range(rows_tap):
                for piece in range(columns + 1):
                    block = b - 1 + piece
                    if 0 <= block < tiles:
                        left.append(cs[pl.ds(start, count), pl.ds(lanes_all * block + TILE * a, TILE)])
                        right.append(
                            up[h, pl.ds(wide_u * a + TILE * piece, TILE), 0 : TILE * columns]
                        )
            grad = nn(jnp.concatenate(left, axis=1), jnp.concatenate(right, axis=0))
            key = lax.broadcasted_iota(jnp.int32, grad.shape, 1) + TILE * b - 5
            row = lax.broadcasted_iota(jnp.int32, grad.shape, 0) + start
            low = jnp.where((key >= 0) & (key <= row), grad, 0.0).astype(BF16)
            eb[pl.ds(start, count), pl.ds(TILE * b, TILE * columns)] = low
            ka[pl.ds(TILE * b, TILE * columns), :] += tn(low, qm[h, pl.ds(start, count), :])
        for rb in range(tiles):
            rows = pl.ds(TILE * rb, TILE)
            upto = min(rb + 2, tiles + 1)
            part = nn(eb[rows, 0 : TILE * upto], ks[0 : TILE * upto, :]) * scale
            if h == 0:
                qa[rows, :] = part
            else:
                qa[rows, :] = jnp.where(first, qa[rows, :], part)
    for b, row in enumerate(places):
        low_ref[pl.ds(row, blk), 0:width] = qa[pl.ds(blk * b, blk), :].astype(BF16)
        low_ref[pl.ds(row, blk), width : 2 * width] = (ka[pl.ds(blk * b + 5, blk), :] * scale).astype(BF16)

    @pl.when(m == pl.num_programs(0) - 1)
    def _():
        away = lax.broadcasted_iota(jnp.int32, (TILE + 16, TILE), 0) - lax.broadcasted_iota(
            jnp.int32, (TILE + 16, TILE), 1
        )
        for h in range(2):
            for a in range(rows_tap):
                table = acc[h, :, TILE * a : TILE * (a + 1)]
                for t in range(keys_tap):
                    at = a * keys_tap + t
                    taps[at : at + 1, :] = jnp.sum(
                        jnp.where(away == span - t, table, 0.0), axis=0, keepdims=True
                    )
            count = taps.shape[0]
            tap = lax.broadcasted_iota(jnp.int32, (8, count), 1) - keys_tap * lax.broadcasted_iota(
                jnp.int32, (8, count), 0
            )
            rows = ((tap >= 0) & (tap < keys_tap)).astype(F32)
            at = lax.broadcasted_iota(jnp.int32, (count, TILE), 0)
            lane = lax.broadcasted_iota(jnp.int32, (count, TILE), 1)
            value = jnp.sum(taps[...], axis=1, keepdims=True)
            lanes = jnp.zeros((count, TILE), F32)
            for a in range(rows_tap):
                lanes = jnp.where((at == keys_tap * a + lane) & (lane < keys_tap), value, lanes)
            misc_ref[8 * h : 8 * h + 8, 0:TILE] = lax.dot_general(
                rows, lanes, (((1,), (0,)), ((), ())),
                precision=lax.Precision.HIGHEST, preferred_element_type=F32,
            )


def whole(shape):
    return pl.BlockSpec(shape, lambda m: (0,) * len(shape))


def pair_forward(blk_table, ker, mix, gain, qkv, micro, seq, blk, scale):
    width = qkv.shape[1] // 3
    mixed = (qkv.shape[0], width)
    rows_tap, keys_tap = ker.shape[1:]
    smem = pl.BlockSpec(memory_space=pltpu.SMEM)
    per = lambda shape: pl.BlockSpec((1,) + shape, lambda m: (m,) + (0,) * len(shape))
    return pl.pallas_call(
        functools.partial(forward_kernel, seq, blk, rows_tap, keys_tap, scale),
        name="pair_forward",
        grid=(micro,),
        out_shape=(
            jax.ShapeDtypeStruct(mixed, BF16),
            jax.ShapeDtypeStruct((micro, 2, seq, width), F32),
            jax.ShapeDtypeStruct((micro, 2, seq, seq), BF16),
        ),
        in_specs=[smem, smem, whole(mix.shape), whole(gain.shape), whole(qkv.shape)],
        out_specs=(whole(mixed), per((2, seq, width)), per((2, seq, seq))),
        scratch_shapes=[
            pltpu.VMEM((2, seq, width), BF16),
            pltpu.VMEM((seq + TILE + 8, width), F32),
            pltpu.VMEM((seq + TILE, width), BF16),
            pltpu.VMEM((seq, width), BF16),
            pltpu.VMEM((seq + 16, seq + TILE), BF16),
            pltpu.VMEM((seq + 16, seq + TILE), BF16),
            pltpu.VMEM((2, 2 * TILE, rows_tap * TILE), BF16),
            pltpu.VMEM((2, 2 * TILE, rows_tap * TILE), BF16),
            pltpu.VMEM((seq + 16, rows_tap * TILE), F32),
            pltpu.VMEM((seq, seq), F32),
        ],
        compiler_params=pltpu.CompilerParams(vmem_limit_bytes=56 << 20),
        cost_estimate=pl.CostEstimate(flops=20 * 10**9, transcendentals=10**6, bytes_accessed=8 << 20),
    )(blk_table, ker, mix, gain, qkv)


def pair_backward(blk_table, ker, mix, gain, qkv, zg, y, p, seq, blk, scale):
    width = qkv.shape[1] // 3
    micro = y.shape[0]
    rows_tap, keys_tap = ker.shape[1:]
    tiles = seq // TILE
    smem = pl.BlockSpec(memory_space=pltpu.SMEM)
    per = lambda shape: pl.BlockSpec((1,) + shape, lambda m: (m,) + (0,) * len(shape))
    taps = -(-rows_tap * keys_tap // 8) * 8
    return pl.pallas_call(
        functools.partial(backward_kernel, seq, blk, rows_tap, keys_tap, scale),
        name="pair_backward",
        grid=(micro,),
        out_shape=(
            jax.ShapeDtypeStruct(qkv.shape, BF16),
            jax.ShapeDtypeStruct((24, 2 * TILE), F32),
        ),
        in_specs=[smem, smem, whole(mix.shape), whole(gain.shape), whole(qkv.shape), whole(zg.shape)]
        + [per((2, seq, width)), per((2, seq, seq))],
        out_specs=(whole(qkv.shape), whole((24, 2 * TILE))),
        scratch_shapes=[
            pltpu.VMEM((2, seq, width), BF16),
            pltpu.VMEM((seq + TILE + 8, width), F32),
            pltpu.VMEM((seq + TILE, width), BF16),
            pltpu.VMEM((seq, width), BF16),
            pltpu.VMEM((seq, seq + TILE), BF16),
            pltpu.VMEM((2, rows_tap * 3 * TILE, 2 * TILE), BF16),
            pltpu.VMEM((seq, width), F32),
            pltpu.VMEM((2, seq, width), BF16),
            pltpu.VMEM((seq + 8, seq), F32),
            pltpu.VMEM((seq, tiles * rows_tap * TILE), BF16),
            pltpu.VMEM((seq, seq + TILE), BF16),
            pltpu.VMEM((seq, width), F32),
            pltpu.VMEM((seq + TILE, width), F32),
            pltpu.VMEM((2, TILE + 16, rows_tap * TILE), F32),
            pltpu.VMEM((taps, TILE), F32),
        ],
        compiler_params=pltpu.CompilerParams(vmem_limit_bytes=56 << 20),
        cost_estimate=pl.CostEstimate(flops=30 * 10**9, transcendentals=10**5, bytes_accessed=12 << 20),
    )(blk_table, ker, mix, gain, qkv, zg, y, p)


MESH = pl.DeviceIdType.MESH


def peer(offset):
    mine = lax.axis_index("ctx")
    y = (mine // 4 + offset // 4) % 2
    x = ((mine // 2) % 2 + (offset // 2) % 2) % 2
    core = (mine % 2 + offset % 2) % 2
    return y * 4 + x * 2 + core


def greet(places):
    barrier = pltpu.get_barrier_semaphore()
    for place in places:
        pl.semaphore_signal(barrier, inc=1, device_id=place, device_id_type=MESH)
    return lambda: pl.semaphore_wait(barrier, len(places))


def remote(source, target, send, receive, place):
    return pltpu.make_async_remote_copy(
        src_ref=source, dst_ref=target, send_sem=send, recv_sem=receive,
        device_id=place, device_id_type=MESH,
    )


def exchange_start(plane, mine, source, target, sends, receives):
    copies = [
        remote(source.at[peer(d)], target.at[mine], sends.at[d], receives.at[d], (plane, peer(d)))
        for d in (6, 7, 2, 3, 4, 5, 1)
    ]
    for copy in copies:
        copy.start()
    return copies


class Spread:
    def __init__(self, source, target, sends, receives):
        self.plane, self.mine = lax.axis_index("seq"), lax.axis_index("ctx")
        self.source, self.target, self.sends, self.receives = source, target, sends, receives
        self.copies = {}
        half = target.shape[1] // 2
        self.first, self.second = pl.ds(0, half), pl.ds(half, half)

    def send(self, key, source, target, offset):
        copy = remote(source, target, self.sends.at[key], self.receives.at[key], (self.plane, peer(offset)))
        copy.start()
        self.copies[key] = copy

    def hand_on(self, key, block, offset, rows=None):
        piece = self.target.at[block] if rows is None else self.target.at[block, rows]
        self.send(key, piece, piece, offset)

    def start(self):
        for d in (2, 4, 1):
            self.send(d, self.source, self.target.at[self.mine], d)

    def near(self):
        self.copies[2].wait_recv()
        self.hand_on(6, peer(2), 4, self.first)
        self.hand_on(3, peer(2), 1)
        self.copies[4].wait_recv()
        self.hand_on(0, peer(4), 2, self.second)
        self.hand_on(5, peer(4), 1)

    def across(self):
        self.copies[6].wait_recv()
        self.hand_on(7, peer(6), 1, self.first)
        self.copies[0].wait_recv()
        self.hand_on(8, peer(6), 1, self.second)

    def finish(self):
        for key in (1, 3, 5, 7, 8):
            self.copies[key].wait_recv()
        for copy in self.copies.values():
            copy.wait_send()


class PlaneSum:
    def __init__(self, terms, part, own, near, stage, far, hop, sends, receives):
        self.plane, self.mine = lax.axis_index("seq"), lax.axis_index("ctx")
        self.terms, self.part, self.own = terms, part, own
        self.near, self.stage, self.far, self.hop = near, stage, far, hop
        self.sends, self.receives = sends, receives
        self.copies = {}
        half = part.shape[1] // 2
        self.first, self.second = pl.ds(0, half), pl.ds(half, half)

    def send(self, key, source, target, offset):
        copy = remote(source, target, self.sends.at[key], self.receives.at[key], (self.plane, peer(offset)))
        copy.start()
        self.copies[key] = copy

    def start(self, met):
        self.part[...] = self.terms(1 - self.mine % 2).astype(BF16)
        met()
        for d in (6, 2, 4, 0):
            self.send(d, self.part.at[peer(d) // 2], self.near.at[d // 2], 1)

    def prepare(self):
        self.own[...] = self.terms(self.mine % 2)

    def chip_sum(self, d):
        self.copies[d].wait_recv()
        self.stage[d // 2] = (self.own[peer(d) // 2] + self.near[d // 2].astype(F32)).astype(BF16)

    def add_hop(self, slot, rows, hop):
        self.stage[slot, rows, :] = (
            self.stage[slot, rows, :].astype(F32) + self.hop[hop].astype(F32)
        ).astype(BF16)

    def run(self):
        first, second = self.first, self.second
        self.chip_sum(6)
        self.send(1, self.stage.at[3, first], self.hop.at[0], 2)
        self.send(3, self.stage.at[3, second], self.hop.at[1], 4)
        self.chip_sum(2)
        self.send(5, self.stage.at[1, first], self.far.at[0, first], 2)
        self.chip_sum(4)
        self.send(7, self.stage.at[2, second], self.far.at[1, second], 4)
        self.copies[1].wait_recv()
        self.add_hop(2, first, 0)
        self.send(8, self.stage.at[2, first], self.far.at[1, first], 4)
        self.copies[3].wait_recv()
        self.add_hop(1, second, 1)
        self.send(9, self.stage.at[1, second], self.far.at[0, second], 2)

    def total(self):
        self.copies[0].wait_recv()
        value = self.own[self.mine // 2] + self.near[0].astype(F32)
        for key in (5, 7, 8, 9):
            self.copies[key].wait_recv()
        return value + self.far[0].astype(F32) + self.far[1].astype(F32)

    def finish(self):
        for copy in self.copies.values():
            copy.wait_send()


class Fetch:
    def __init__(self, source, buffer, sem):
        self.copy, self.buffer, self.ready = pltpu.make_async_copy(source, buffer, sem), buffer, False
        self.copy.start()

    def get(self):
        if not self.ready:
            self.copy.wait()
            self.ready = True
        return self.buffer


def fetch(sources, buffers, sems):
    return [Fetch(source, buffer, sems.at[i]) for i, (source, buffer) in enumerate(zip(sources, buffers))]


def put(buffer, out, sem):
    copy = pltpu.make_async_copy(buffer, out, sem)
    copy.start()
    return copy


def terms_of(values, product):
    chips, _, rows, width = values.buffer.shape

    def terms(core):
        left = values.get()[:, core].reshape(chips * rows, width)
        return product(left).reshape(chips, rows, -1)

    return terms


class Line:
    def __init__(self, sources, targets, planes, sends, receives):
        self.sources, self.targets, self.planes = sources, targets, planes
        self.sends, self.receives = sends, receives
        self.plane, self.mine = lax.axis_index("seq"), lax.axis_index("ctx")

    def copy(self, i, up, step):
        block = jnp.clip(self.plane - step if up else self.plane + step, 0, self.planes - 1)
        next_plane = jnp.clip(self.plane + 1 if up else self.plane - 1, 0, self.planes - 1)
        at = (i, int(up), step)
        target = self.targets[i].at[block]
        source = target if step else self.sources[i]
        return remote(source, target, self.sends.at[at], self.receives.at[at], (next_plane, self.mine))

    def arrived(self, i, up, step):
        block = jnp.clip(self.plane - 1 - step if up else self.plane + 1 + step, 0, self.planes - 1)
        at = (i, int(up), step)
        target = self.targets[i].at[block]
        from_plane = jnp.clip(self.plane - 1 if up else self.plane + 1, 0, self.planes - 1)
        return remote(target, target, self.sends.at[at], self.receives.at[at], (from_plane, self.mine))

    def step(self, step):
        for up in (True, False):
            have = self.plane >= step if up else self.plane + step < self.planes
            more = self.plane + 1 < self.planes if up else self.plane > 0
            for i in range(len(self.targets)):
                if step:
                    @pl.when(have)
                    def _(i=i, up=up):
                        self.arrived(i, up, step - 1).wait_recv()

                if step < self.planes - 1:
                    @pl.when(have & more)
                    def _(i=i, up=up):
                        self.copy(i, up, step).start()

    def finish(self):
        for step in range(self.planes - 1):
            for up in (True, False):
                have = self.plane >= step if up else self.plane + step < self.planes
                more = self.plane + 1 < self.planes if up else self.plane > 0
                for i in range(len(self.targets)):
                    @pl.when(have & more)
                    def _(i=i, up=up, step=step):
                        self.copy(i, up, step).wait_send()


def plane_peers(plane, offsets):
    return [(plane, peer(d)) for d in offsets]


def other_planes(plane, mine, planes):
    return [((plane + d) % planes, mine) for d in range(1, planes)]


class RowDeal:
    def __init__(self, gathered, dealt, sends, receives, local):
        self.plane, self.mine = lax.axis_index("seq"), lax.axis_index("ctx")
        self.gathered, self.dealt, self.sends, self.receives, self.local = gathered, dealt, sends, receives, local

    def out(self, s, back):
        if back:
            target = 4 * (self.mine % 2) + s
            source, place = self.dealt.at[s], self.gathered.at[self.mine // 2]
        else:
            target = 2 * s + self.mine // 4
            source, place = self.gathered.at[s], self.dealt.at[self.mine % 4]
        slot = self.mine // 2 if back else self.mine % 4
        copy = remote(source, place, self.sends.at[s], self.receives.at[slot], (self.plane, target))
        keep = pltpu.make_async_copy(source, place, self.local)
        return target == self.mine, copy, keep

    def into(self, r, back):
        if back:
            origin = 2 * r + self.mine // 4
            place = self.gathered.at[r]
        else:
            origin = 4 * (self.mine % 2) + r
            place = self.dealt.at[r]
        return origin == self.mine, remote(place, place, self.sends.at[r], self.receives.at[r], (self.plane, origin))

    def start(self, back):
        for s in range(4):
            here, copy, keep = self.out(s, back)

            @pl.when(here)
            def _():
                keep.start()

            @pl.when(jnp.logical_not(here))
            def _():
                copy.start()

    def wait(self, back):
        for s in range(4):
            here, copy, keep = self.out(s, back)

            @pl.when(here)
            def _():
                keep.wait()

            @pl.when(jnp.logical_not(here))
            def _():
                copy.wait_send()

        for r in range(4):
            here, copy = self.into(r, back)

            @pl.when(jnp.logical_not(here))
            def _():
                copy.wait_recv()


def enter_kernel(
    planes, q, k, v, gate, up, norm_gain, group_gain, second_gain, tokens, out_w,
    feed_out, qkv_out, gains_out, tokens_out, out_w_out,
    q_near, k_near, v_near, gate_near, up_near, norm_near, group_near, second_near, packed, qkv, feed,
    deal_sends, deal_receives, sends, receives, row_sends, row_receives, line_sends, line_receives, local,
):
    plane, mine = lax.axis_index("seq"), lax.axis_index("ctx")
    loads = [
        pltpu.make_async_copy(source, place, local.at[5 + i])
        for i, (source, place) in enumerate(
            (
                (norm_gain, norm_near), (group_gain, group_near), (second_gain, second_near),
                (q, q_near), (k, k_near), (v, v_near), (gate, gate_near), (up, up_near),
            )
        )
    ]
    keep = [
        pltpu.make_async_copy(qkv.at[mine], qkv_out.at[plane, mine], local.at[0]),
        pltpu.make_async_copy(packed, gains_out.at[plane, mine], local.at[1]),
        pltpu.make_async_copy(feed.at[mine], feed_out.at[mine], local.at[2]),
        pltpu.make_async_copy(tokens, tokens_out.at[mine], local.at[3]),
        pltpu.make_async_copy(out_w, out_w_out.at[plane], local.at[4]),
    ]
    for copy in loads + keep[3:]:
        copy.start()
    met = greet(plane_peers(plane, range(1, 8)) + other_planes(plane, mine, planes))
    groups, _, three = qkv.shape
    pair = three // 3
    half = feed.shape[2] // 2
    for copy in loads[:6]:
        copy.wait()
    packed[...] = jnp.zeros(packed.shape, F32)
    for i, gain in enumerate((norm_near, group_near, second_near)):
        packed[i : i + 1, 0 : gain.shape[0]] = gain[...].astype(F32).reshape(1, -1)
    for c in range(groups):
        for i, weight in enumerate((q_near, k_near, v_near)):
            qkv[c, :, pair * i : pair * (i + 1)] = weight[:, pair * c : pair * (c + 1)]
    for copy in keep[:2]:
        copy.start()
    met()
    first = exchange_start(plane, mine, qkv, qkv_out.at[plane], deal_sends.at[0], deal_receives.at[0])
    for d in (6, 7, 2, 3, 4, 5, 1):
        copy = remote(packed, gains_out.at[plane, mine], deal_sends.at[1, d], deal_receives.at[1, d], (plane, peer(d)))
        copy.start()
        first.append(copy)
    rows = Line([out_w], [out_w_out], planes, row_sends, row_receives)
    rows.step(0)
    for copy in loads[6:]:
        copy.wait()
    for c in range(groups):
        for i, weight in enumerate((gate_near, up_near)):
            for s in range(half // TILE):
                at = TILE * (groups * s + c)
                feed[c, :, half * i + TILE * s : half * i + TILE * (s + 1)] = weight[:, at : at + TILE]
    keep[2].start()
    keep[0].wait()
    keep[1].wait()
    for copy in first:
        copy.wait_recv()
    line = Line(
        [qkv_out.at[plane], gains_out.at[plane]], [qkv_out, gains_out], planes, line_sends, line_receives
    )
    line.step(0)
    spread = Spread(tokens, tokens_out, sends, receives)
    spread.start()
    rows.step(1)
    line.step(1)
    spread.near()
    deals = exchange_start(plane, mine, feed, feed_out, deal_sends.at[2], deal_receives.at[2])
    rows.step(2)
    line.step(2)
    spread.across()
    for step in range(3, planes):
        rows.step(step)
        line.step(step)
    spread.finish()
    for copy in first:
        copy.wait_send()
    for copy in deals:
        copy.wait()
    for copy in keep[2:]:
        copy.wait()
    line.finish()
    rows.finish()


def heads_kernel(
    planes, tokens, qkv, gains, out_w, grads, hidden, heads, gains_out, pair_gain, out_w_out, grads_out,
    tokens_near, qkv_near, hidden_near, heads_near,
    row_sends, row_receives, sends, receives, loads, stores, local,
):
    plane, mine = lax.axis_index("seq"), lax.axis_index("ctx")
    groups = tokens.shape[0]
    weight = Fetch(qkv, qkv_near, loads.at[groups])
    blocks = [Fetch(tokens.at[i], tokens_near.at[i], loads.at[i]) for i in range(groups)]
    keep = pltpu.make_async_copy(grads, grads_out.at[mine], local.at[1])
    keep.start()
    greet(plane_peers(plane, range(1, 8)))()
    spread = Spread(grads, grads_out, sends, receives)
    spread.start()
    deal = RowDeal(out_w, out_w_out, row_sends, row_receives, local.at[0])
    deal.start(False)
    owned = out_w.shape[1]
    for s in range(planes):
        for c in range(groups):
            at = owned * (groups * s + c)
            gains_out[:, at : at + owned] = gains[s, c, :, 0:owned]
    for r in range(4):
        pair_gain[:, owned * r : owned * (r + 1)] = gains[mine // 2, 4 * (mine % 2) + r, :, 0:owned]
    gain = gains_out[0:1, :]
    out = []
    for i in range(groups):
        value = blocks[i].get()[...].astype(F32)
        low = (value * inverse_root(value) * gain).astype(BF16)
        rows = pl.ds(value.shape[0] * i, value.shape[0])
        hidden_near[:, rows] = low.T
        out.append(put(hidden_near.at[:, rows], hidden.at[:, rows], stores.at[0, i]))
        heads_near[rows, :] = nn(low, weight.get()[...]).astype(BF16)
        out.append(put(heads_near.at[rows], heads.at[rows], stores.at[1, i]))
        if i == groups - 3:
            spread.near()
    deal.wait(False)
    spread.across()
    for copy in out:
        copy.wait()
    spread.finish()
    keep.wait()


def inverse_root(values):
    return lax.rsqrt(jnp.mean(values * values, axis=1, keepdims=True) + EPSILON)


def second_kernel(
    mixed, out_w, tokens, gains, residual, spread_out,
    mixed_near, out_w_near, tokens_near, residual_near, own_near, loads,
    part, own, near, stage, far, hop, sum_sends, sum_receives, sends, receives,
):
    plane, mine = lax.axis_index("seq"), lax.axis_index("ctx")
    left, weight, rows_in = fetch(
        (mixed, out_w, tokens), (mixed_near, out_w_near, tokens_near), loads
    )
    met = greet(plane_peers(plane, (1, 2, 4)))
    rows = PlaneSum(
        terms_of(left, lambda value: nn(value, weight.get()[...])), part, own, near, stage, far, hop,
        sum_sends, sum_receives,
    )
    rows.start(met)
    rows.prepare()
    rows.run()
    value = rows_in.get()[...].astype(F32) + rows.total()
    own_near[...] = (value * inverse_root(value) * gains[2:3, :]).astype(BF16)
    spread = Spread(own_near, spread_out, sends, receives)
    spread.start()
    keep = put(own_near, spread_out.at[mine], loads.at[3])
    residual_near[...] = value
    out = put(residual_near, residual, loads.at[4])
    rows.finish()
    spread.near()
    spread.across()
    keep.wait()
    out.wait()
    spread.finish()


def back_through_norm(upstream, values, gain):
    factor = inverse_root(values)
    normed = values * factor
    scaled = upstream * gain
    grad = factor * (scaled - normed * jnp.mean(scaled * normed, axis=1, keepdims=True))
    return grad, jnp.sum(upstream * normed, axis=0, keepdims=True)


def back_kernel(
    lows, feed, residual, grads, out_w, mixed, gains, residual_grad, gain_grad, mixed_grad, out_w_grad,
    lows_near, feed_near, residual_near, grads_near, out_w_near, mixed_near, residual_grad_near, gathered, total, loads,
    part, own, near, stage, far, hop, sum_sends, sum_receives, sends, receives,
):
    plane, mine = lax.axis_index("seq"), lax.axis_index("ctx")
    weight, left, before, upstream, out_rows, taken = fetch(
        (feed, lows, residual, grads, out_w, mixed),
        (feed_near, lows_near, residual_near, grads_near, out_w_near, mixed_near),
        loads,
    )
    met = greet(plane_peers(plane, (1, 2, 4)))
    rows = PlaneSum(
        terms_of(left, lambda value: nt(value, weight.get()[...])), part, own, near, stage, far, hop,
        sum_sends, sum_receives,
    )
    rows.start(met)
    rows.prepare()
    rows.run()
    grad, gain_part = back_through_norm(rows.total(), before.get()[...], gains[2:3, :])
    grad = grad + upstream.get()[...].astype(F32)
    gathered[mine] = grad.astype(BF16)
    spread = Spread(gathered.at[mine], gathered, sends, receives)
    spread.start()
    gain_grad[...] = gain_part
    residual_grad_near[...] = grad
    out = put(residual_grad_near, residual_grad, loads.at[6])
    taken.get()

    def use(d):
        block = peer(d) if d else mine
        value = gathered[block]
        mixed_grad[block] = nt(value, out_rows.get()[...]).astype(BF16)
        term = tn(mixed_near[block], value)
        total[...] = total[...] + term if d else term

    use(0)
    rows.finish()
    spread.near()
    use(2)
    use(4)
    spread.copies[1].wait_recv()
    use(1)
    spread.across()
    use(6)
    for keys, d in (((3,), 3), ((5,), 5), ((7, 8), 7)):
        for key in keys:
            spread.copies[key].wait_recv()
        use(d)
    out_w_grad[...] = total[...].astype(BF16)
    for copy in spread.copies.values():
        copy.wait_send()
    out.wait()


class Fold:
    def __init__(self, own, stage, landed, planes, sends, receives):
        self.own, self.stage, self.landed, self.planes = own, stage, landed, planes
        self.sends, self.receives = sends, receives
        self.plane, self.mine = lax.axis_index("seq"), lax.axis_index("ctx")

    def copy(self, j, up):
        place = jnp.clip(self.plane + 1 if up else self.plane - 1, 0, self.planes - 1)
        at = (int(up), j)
        return remote(self.stage.at[at], self.landed.at[at], self.sends.at[at], self.receives.at[at], (place, self.mine))

    def advance(self, j, up):
        active = self.plane < j if up else self.plane > j
        inner = self.plane > 0 if up else self.plane < self.planes - 1

        @pl.when(active & inner)
        def _():
            self.copy(j, up).wait_recv()
            self.stage[int(up), j] = (
                self.own[j].astype(F32) + self.landed[int(up), j].astype(F32)
            ).astype(BF16)

        @pl.when(active & jnp.logical_not(inner))
        def _():
            self.stage[int(up), j] = self.own[j]

        @pl.when(active)
        def _():
            self.copy(j, up).start()

    def round(self, i):
        self.advance(self.planes - 1 - i, True)
        self.advance(i, False)

    def total(self, store):
        for j in range(self.planes):
            @pl.when(self.plane == j)
            def _():
                value = self.own[j].astype(F32)
                if j > 0:
                    self.copy(j, True).wait_recv()
                    value = value + self.landed[1, j].astype(F32)
                if j < self.planes - 1:
                    self.copy(j, False).wait_recv()
                    value = value + self.landed[0, j].astype(F32)
                store(value.astype(BF16))

    def finish(self):
        for j in range(self.planes):
            for up in (True, False):
                @pl.when(self.plane < j if up else self.plane > j)
                def _():
                    self.copy(j, up).wait_send()


def layer_kernel(
    active, down, residual, out_w_grad, layer_out, row_grad,
    active_near, down_near, residual_near, loads,
    part, own, near, stage, far, hop, sum_sends, sum_receives, row_sends, row_receives, local,
):
    plane, mine = lax.axis_index("seq"), lax.axis_index("ctx")
    left, weight, before = fetch(
        (active, down, residual), (active_near, down_near, residual_near), loads
    )
    met = greet(plane_peers(plane, range(1, 8)))
    rows = PlaneSum(
        terms_of(left, lambda value: nn(value, weight.get()[...])), part, own, near, stage, far, hop,
        sum_sends, sum_receives,
    )
    met()
    deal = RowDeal(row_grad, out_w_grad, row_sends, row_receives, local)
    deal.start(True)
    rows.start(lambda: None)
    rows.prepare()
    rows.run()
    layer_out[...] = (before.get()[...] + rows.total()).astype(BF16)
    deal.wait(True)
    rows.finish()


def leave_kernel(
    planes, qkv_low_in, qkv_in, hidden_in, residual_grad_in, tokens_in,
    gains, second_grad, misc, feed_grad, row_grad,
    input_grad, small_out, misc_out, qkv_out, feed_out, out_w_out,
    qkv_low_near, qkv_near, hidden_near, residual_grad_near, tokens_near, loads,
    misc_all, misc_sends, misc_receives,
    part, own, near, stage, far, hop, small_plane, small_all,
    grads, fold_stage, fold_landed, qkv_sum,
    sum_sends, sum_receives, small_sends, small_receives,
    fold_sends, fold_receives, deal_sends, deal_receives, local,
):
    plane, mine = lax.axis_index("seq"), lax.axis_index("ctx")
    qkv_low, qkv, hidden, residual_grad, tokens = fetch(
        (qkv_low_in, qkv_in, hidden_in, residual_grad_in, tokens_in),
        (qkv_low_near, qkv_near, hidden_near, residual_grad_near, tokens_near),
        loads,
    )
    keep_feed = pltpu.make_async_copy(feed_grad.at[mine], feed_out.at[mine], local.at[0])
    keep_feed.start()
    misc_all[plane] = misc[...]
    met = greet(plane_peers(plane, range(1, 8)) + other_planes(plane, mine, planes))
    misc_copies = [
        remote(misc_all.at[plane], misc_all.at[plane], misc_sends.at[0, d], misc_receives.at[0, d], ((plane + d) % planes, mine))
        for d in range(1, planes)
    ]
    rows = PlaneSum(
        terms_of(qkv_low, lambda left: nt(left, qkv.get()[...])), part, own, near, stage, far, hop,
        sum_sends, sum_receives,
    )
    halves = [pl.ds(grads.shape[1] // 2 * k, grads.shape[1] // 2) for k in range(2)]
    folds = [
        Fold(
            grads.at[:, rows], fold_stage.at[:, :, rows], fold_landed.at[:, :, rows], planes,
            fold_sends.at[k], fold_receives.at[k],
        )
        for k, rows in enumerate(halves)
    ]
    ends = (plane == 0) | (plane == planes - 1)
    block, owned = grads.shape[1], row_grad.shape[1]
    three = qkv_low_in.shape[3]
    pair = three // 3

    def project(i):
        j = jnp.where(plane < planes // 2, planes - 1 - i, i)
        lows = qkv_low.get()[...].reshape(hidden_near.shape[1], three)
        columns = hidden.get()[pl.ds(pl.multiple_of(block * j, block), block), :]
        grads[j, :, 0:three] = nn(columns, lows).astype(BF16)
        for p in range(block // owned):
            grads[j, owned * p : owned * (p + 1), three : three + pair] = row_grad[
                j, :, pair * p : pair * (p + 1)
            ]

    def rounds(outer, inner):
        for here, i in ((ends, outer), (jnp.logical_not(ends), inner)):
            if 0 <= i < planes - 1:
                @pl.when(here)
                def _():
                    for fold in folds:
                        fold.round(i)

    rows.start(met)
    for copy in misc_copies:
        copy.start()
    project(0)
    rounds(0, -1)
    rows.prepare()
    for i in range(1, planes):
        project(i)
    rounds(1, -1)
    rows.run()
    rounds(2, 0)
    for copy in misc_copies:
        copy.wait()
    total = misc_all[0]
    for i in range(1, planes):
        total = total + misc_all[i]
    misc_out[mine] = total
    misc_copies = [
        remote(misc_out.at[mine], misc_out.at[mine], misc_sends.at[1, d], misc_receives.at[1, d], (plane, peer(d)))
        for d in range(1, 8)
    ]
    for copy in misc_copies:
        copy.start()
    grad, gain_part = back_through_norm(rows.total(), tokens.get()[...].astype(F32), gains[0:1, :])
    small_plane[mine] = jnp.zeros(small_plane.shape[1:], F32)
    small_plane[mine, 0:1, :] = gain_part
    small_plane[mine, 1:2, :] = second_grad[...]
    near_copies = [
        remote(small_plane.at[mine], small_plane.at[mine], small_sends.at[0, d], small_receives.at[0, d], (plane, peer(d)))
        for d in range(1, 8)
    ]
    for copy in near_copies:
        copy.start()
    input_grad[...] = (residual_grad.get()[...] + grad).astype(BF16)
    deals = exchange_start(plane, mine, feed_grad, feed_out, deal_sends.at[0], deal_receives.at[0])
    rounds(-1, 1)
    for copy in near_copies:
        copy.wait()
    total = small_plane[0]
    for i in range(1, 8):
        total = total + small_plane[i]
    small_all[plane] = total
    far_copies = [
        remote(small_all.at[plane], small_all.at[plane], small_sends.at[1, d], small_receives.at[1, d], ((plane + d) % planes, mine))
        for d in range(1, planes)
    ]
    for copy in far_copies:
        copy.start()
    rounds(-1, 2)
    keep_qkv = pltpu.make_async_copy(qkv_sum.at[mine], qkv_out.at[mine], local.at[2])
    handed = [
        remote(
            qkv_sum.at[peer(d)], qkv_out.at[mine], deal_sends.at[1, d], deal_receives.at[1, d], (plane, peer(d))
        )
        for d in range(1, 8)
    ]
    for k, fold in enumerate(folds):
        def store(value, k=k):
            count = value.shape[0] // owned
            for p in range(count):
                piece = value[owned * p : owned * (p + 1), :]
                qkv_sum[count * k + p] = piece[:, 0:three]
                at = pair * (count * k + p)
                out_w_out[0, :, at : at + pair] = piece[:, three : three + pair]

        fold.total(store)
        same = mine // 4 == k
        for d in range(1, 8):
            @pl.when(same if d < 4 else jnp.logical_not(same))
            def _():
                handed[d - 1].start()

        @pl.when(same)
        def _():
            keep_qkv.start()

    deals += handed
    rows.finish()
    for copy in far_copies:
        copy.wait()
    total = small_all[0]
    for i in range(1, planes):
        total = total + small_all[i]
    small_out[...] = total
    for copy in deals + misc_copies:
        copy.wait()
    keep_feed.wait()
    keep_qkv.wait()
    for fold in folds:
        fold.finish()


def finish_kernel(count, place, small, misc, *refs):
    ins, outs = refs[:6], refs[6 : 6 + count]
    norm_out, group_out, second_out, ker_out, mix_out = refs[6 + count : 11 + count]
    near, made = refs[11 + count : 17 + count], refs[17 + count : 17 + 2 * count - 2]
    loads, stores = refs[-2:]
    moves = [pltpu.make_async_copy(ins[i], near[i], loads.at[i]) for i in range(6)]
    for move in moves:
        move.start()
    qkv, feed, out_w, down, grad, layer = near
    groups, owned, three = qkv.shape
    pair = three // 3
    half = feed.shape[2] // 2
    results = list(made) + [grad, layer]
    out = [pltpu.make_async_copy(results[i], outs[i], stores.at[i]) for i in range(count)]
    moves[3].wait()
    made[6][...] = down[...].astype(F32)
    out[6].start()
    moves[2].wait()
    made[5][...] = out_w[0].astype(F32)
    out[5].start()
    for i in (4, 5):
        moves[i].wait()
        out[i + 3].start()
    moves[1].wait()
    for i in range(2):
        for c in range(groups):
            for s in range(half // TILE):
                at = TILE * (groups * s + c)
                made[3 + i][:, at : at + TILE] = feed[
                    c, :, half * i + TILE * s : half * i + TILE * (s + 1)
                ].astype(F32)
        out[3 + i].start()
    moves[0].wait()
    for i in range(3):
        for c in range(groups):
            made[i][:, pair * c : pair * (c + 1)] = qkv[c, :, pair * i : pair * (i + 1)].astype(F32)
        out[i].start()
    flat = place[0]
    width = small.shape[1]
    turned = pltpu.roll(small[...], (width - owned * flat) % width, 1)
    norm_out[...] = turned[0:1, 0:owned]
    second_out[...] = turned[1:2, 0:owned]
    rows = misc[flat // 4]
    wide = rows.shape[1]
    turned = pltpu.roll(rows, (wide - owned * (flat % 4)) % wide, 1)
    group_out[...] = turned[16:17, 0:owned]
    heads = [(c, h) for c in range(groups) for h in range(2)]
    for a in range(ker_out.shape[1]):
        rows = jnp.concatenate([misc[c, 8 * h + a : 8 * h + a + 1, 0:TILE] for c, h in heads], axis=0)
        ker_out[:, a, :] = rows.T[0 : ker_out.shape[0], :]
    for p in range(2):
        sums = [
            jnp.sum(misc[c, 17 + p : 18 + p, pair // 2 * h : pair // 2 * (h + 1)], axis=1, keepdims=True)
            for c, h in heads
        ]
        mix_out[p : p + 1, :] = jnp.broadcast_to(jnp.concatenate(sums, axis=0), (len(heads), TILE)).T[0:1, :]
    for copy in out:
        copy.wait()


DMA = pltpu.SemaphoreType.DMA
ANYWHERE = pl.BlockSpec(memory_space=pl.ANY)
ON_CHIP = pl.BlockSpec(memory_space=pltpu.VMEM)


def communicate(kernel, name, number, micros, outs, scratch, args, spec, specs=None, out_specs=None):
    return pl.pallas_call(
        kernel,
        name=name,
        out_shape=tuple(jax.ShapeDtypeStruct(shape, kind) for shape, kind in outs),
        in_specs=specs or [spec] * len(args),
        out_specs=out_specs or (spec,) * len(outs),
        scratch_shapes=scratch,
        compiler_params=pltpu.CompilerParams(
            collective_id=number, has_side_effects=True, vmem_limit_bytes=56 << 20
        ),
        cost_estimate=pl.CostEstimate(flops=0, transcendentals=0, bytes_accessed=micros * 3500000),
    )(*args)


def sum_scratch(rows, width):
    return [
        pltpu.VMEM((4, rows, width), BF16),
        pltpu.VMEM((4, rows, width), F32),
        pltpu.VMEM((4, rows, width), BF16),
        pltpu.VMEM((4, rows, width), BF16),
        pltpu.VMEM((2, rows, width), BF16),
        pltpu.VMEM((2, rows // 2, width), BF16),
        DMA((10,)),
        DMA((10,)),
    ]


PRECISE = lax.Precision.HIGHEST


def normalize(values):
    factor = lax.rsqrt(jnp.mean(values * values, axis=-1, keepdims=True) + EPSILON)
    return (values * factor, factor)


def normalize_back(normed, factor, gain, upstream):
    gain_grad = jnp.sum(upstream * normed, axis=0)
    scaled = upstream * gain
    return (
        factor * (scaled - normed * jnp.mean(scaled * normed, axis=-1, keepdims=True)),
        gain_grad,
    )


def add_rows(target, update, offset):
    current = lax.dynamic_slice_in_dim(target, offset, update.shape[0], 0)
    return lax.dynamic_update_slice_in_dim(target, current + update, offset, 0)


def masked_scores(query_ext, key_pad, offset, row_pos, layout):
    block_rows, halo_rows, key_reach, key_block, groups, score_scale = layout
    extent = key_block + 4 * key_reach
    key_slab = lax.dynamic_slice_in_dim(key_pad, offset, extent, 0)
    raw_scores = (
        jnp.einsum("nrhd,khd->nhrk", query_ext, key_slab, preferred_element_type=jnp.float32)
        * score_scale
    )
    key_pos = offset - 2 * key_reach + jnp.arange(extent, dtype=jnp.int32)
    keep_mask = (key_pos[None, None, :] <= row_pos[:, :, None]) & (key_pos >= 0)[None, None, :]
    return jnp.where(keep_mask[:, None], raw_scores, 0.0)


def convolve(zeroed, kernel, shift, extent, layout):
    block_rows, halo_rows, key_reach = (layout[0], layout[1], layout[2])
    result = jnp.zeros(zeroed.shape[:2] + (block_rows, extent), jnp.float32)
    for row_tap in range(halo_rows + 1):
        for key_tap in range(2 * key_reach + 1):
            column = shift + 3 * key_reach - key_tap
            result = (
                result
                + kernel[:, row_tap, key_tap][None, :, None, None]
                * zeroed[
                    :,
                    :,
                    halo_rows - row_tap : halo_rows - row_tap + block_rows,
                    column : column + extent,
                ]
            )
    return result


def attend_forward(query_ext, row_pos, key_pad, value_pad, kernel, layout):
    block_rows, halo_rows, key_reach, key_block, groups, score_scale = layout
    members = query_ext.shape[0]
    head_count = query_ext.shape[2]
    pair_width = value_pad.shape[1] // groups
    block_count = jnp.max(row_pos) // key_block + 1

    def advance(position, carried):
        running_max, running_sum, gathered = carried
        offset = position * key_block
        zeroed = masked_scores(query_ext, key_pad, offset, row_pos, layout)
        logits = convolve(zeroed, kernel, 0, key_block, layout)
        key_pos = offset + jnp.arange(key_block, dtype=jnp.int32)
        valid_mask = key_pos[None, None, :] <= row_pos[:, halo_rows:, None]
        logits = jnp.where(valid_mask[:, None], logits, NEGATIVE)
        new_max = jnp.maximum(running_max, jnp.max(logits, axis=-1))
        shrink = jnp.exp(running_max - new_max)
        weights = jnp.exp(logits - new_max[..., None])
        running_sum = running_sum * shrink + jnp.sum(weights, axis=-1)
        value_slab = lax.dynamic_slice_in_dim(
            value_pad, offset + 2 * key_reach, key_block, 0
        ).reshape(key_block, groups, pair_width)
        low_weights = weights.astype(jnp.bfloat16).reshape(
            members, groups, 2, block_rows, key_block
        )
        gathered = gathered * shrink.reshape(members, groups, 2, block_rows, 1) + jnp.einsum(
            "ngpik,kgc->ngpic", low_weights, value_slab, preferred_element_type=jnp.float32
        )
        return (new_max, running_sum, gathered)

    initial = (
        jnp.full((members, head_count, block_rows), NEGATIVE, jnp.float32),
        jnp.zeros((members, head_count, block_rows), jnp.float32),
        jnp.zeros((members, groups, 2, block_rows, pair_width), jnp.float32),
    )
    running_max, running_sum, gathered = lax.fori_loop(0, block_count, advance, initial)
    mixed_in = gathered / running_sum.reshape(members, groups, 2, block_rows, 1)
    return (mixed_in, running_max + jnp.log(running_sum))


def attend_backward(
    query_ext,
    row_pos,
    key_pad,
    value_pad,
    kernel,
    log_total,
    mixed_low,
    delta_rows,
    key_acc,
    value_acc,
    layout,
):
    block_rows, halo_rows, key_reach, key_block, groups, score_scale = layout
    members = query_ext.shape[0]
    ext_rows = query_ext.shape[1]
    head_count = query_ext.shape[2]
    model_width = value_pad.shape[1]
    pair_width = model_width // groups
    extent = key_block + 2 * key_reach
    block_count = jnp.max(row_pos) // key_block + 1

    def advance(position, carried):
        query_grad, key_acc, value_acc, kernel_grad = carried
        offset = position * key_block
        zeroed = masked_scores(query_ext, key_pad, offset, row_pos, layout)
        logits = convolve(zeroed, kernel, -key_reach, extent, layout)
        key_pos = offset - key_reach + jnp.arange(extent, dtype=jnp.int32)
        valid_mask = (key_pos[None, None, :] <= row_pos[:, halo_rows:, None]) & (key_pos >= 0)[
            None, None, :
        ]
        probability = jnp.where(valid_mask[:, None], jnp.exp(logits - log_total[..., None]), 0.0)
        value_slab = lax.dynamic_slice_in_dim(value_pad, offset + key_reach, extent, 0).reshape(
            extent, groups, pair_width
        )
        prob_grad = jnp.einsum(
            "ngpic,kgc->ngpik", mixed_low, value_slab, preferred_element_type=jnp.float32
        ).reshape(members, head_count, block_rows, extent)
        logit_grad = probability * (prob_grad - delta_rows[..., None])
        central = (
            probability[..., key_reach : key_reach + key_block]
            .astype(jnp.bfloat16)
            .reshape(members, groups, 2, block_rows, key_block)
        )
        value_part = jnp.einsum(
            "ngpik,ngpic->kgc", central, mixed_low, preferred_element_type=jnp.float32
        ).reshape(key_block, model_width)
        value_acc = add_rows(value_acc, value_part, offset)
        middle = logit_grad[..., key_reach : key_reach + key_block]
        tap_sums = []
        for row_tap in range(halo_rows + 1):
            for key_tap in range(2 * key_reach + 1):
                column = 3 * key_reach - key_tap
                tap_sums.append(
                    jnp.sum(
                        middle
                        * zeroed[
                            :,
                            :,
                            halo_rows - row_tap : halo_rows - row_tap + block_rows,
                            column : column + key_block,
                        ],
                        axis=(0, 2, 3),
                    )
                )
        kernel_grad = kernel_grad + jnp.stack(tap_sums, axis=1).reshape(
            head_count, halo_rows + 1, 2 * key_reach + 1
        )
        padded = jnp.pad(logit_grad, ((0, 0), (0, 0), (halo_rows, halo_rows), (0, 0)))
        score_grad = jnp.zeros((members, head_count, ext_rows, key_block), jnp.float32)
        for row_tap in range(halo_rows + 1):
            for key_tap in range(2 * key_reach + 1):
                score_grad = (
                    score_grad
                    + kernel[:, row_tap, key_tap][None, :, None, None]
                    * padded[:, :, row_tap : row_tap + ext_rows, key_tap : key_tap + key_block]
                )
        key_central = offset + jnp.arange(key_block, dtype=jnp.int32)
        keep_mask = (key_central[None, None, :] <= row_pos[:, :, None]) & (key_central >= 0)[
            None, None, :
        ]
        score_low = jnp.where(keep_mask[:, None], score_grad, 0.0).astype(jnp.bfloat16)
        key_slab = lax.dynamic_slice_in_dim(key_pad, offset + 2 * key_reach, key_block, 0)
        query_grad = (
            query_grad
            + jnp.einsum("nhrk,khd->nrhd", score_low, key_slab, preferred_element_type=jnp.float32)
            * score_scale
        )
        key_part = (
            jnp.einsum(
                "nhrk,nrhd->khd", score_low, query_ext, preferred_element_type=jnp.float32
            ).reshape(key_block, model_width)
            * score_scale
        )
        key_acc = add_rows(key_acc, key_part, offset)
        return (query_grad, key_acc, value_acc, kernel_grad)

    initial = (
        jnp.zeros(query_ext.shape, jnp.float32),
        key_acc,
        value_acc,
        jnp.zeros(kernel.shape, jnp.float32),
    )
    return lax.fori_loop(0, block_count, advance, initial)


def reorder(selection, rows):
    return jnp.dot(
        selection.astype(rows.dtype), rows, precision=PRECISE, preferred_element_type=jnp.float32
    ).astype(rows.dtype)


def pick(table, places):
    return jnp.stack(
        [lax.dynamic_index_in_dim(table, places[i], 0, keepdims=False) for i in range(2)]
    )


def accumulate(previous, update):
    return (
        update
        if previous is None
        else tuple((left + right for left, right in zip(previous, update)))
    )


def general_device(
    inputs,
    out_grad,
    pair_index,
    norm_gain,
    query_weight,
    key_weight,
    value_weight,
    score_kernel,
    head_mixing,
    group_gain,
    output_weight,
    second_gain,
    gate_weight,
    up_weight,
    down_weight,
):
    micro_count = inputs.shape[0]
    local_rows = inputs.shape[2]
    block_rows = local_rows // 2
    model_width = inputs.shape[3]
    head_count = score_kernel.shape[0]
    head_dim = model_width // head_count
    groups = head_count // 2
    halo_rows = score_kernel.shape[1] - 1
    key_reach = (score_kernel.shape[2] - 1) // 2
    block_count = 2 * lax.axis_size("ctx")
    seq_length = block_count * block_rows
    key_block = min(512, seq_length)
    layout = (block_rows, halo_rows, key_reach, key_block, groups, head_dim ** (-0.5))
    extended = block_rows + halo_rows
    my_index = lax.axis_index("ctx")
    slot_ids = jnp.arange(block_count, dtype=jnp.int32)
    mix_table = head_mixing.reshape(groups, 2, 2)
    pad_width = ((2 * key_reach, 2 * key_reach), (0, 0))
    layer_rows = []
    input_rows = []
    feed_sums = None
    attention_sums = None
    kernel_total = jnp.zeros(score_kernel.shape, jnp.float32)
    mixing_total = jnp.zeros(head_mixing.shape, jnp.float32)
    for batch_index in range(micro_count):
        gain_first, query_full, key_full, value_full, gain_group, out_full = (
            lax.all_gather(norm_gain, ("seq", "ctx"), axis=0, tiled=True),
            lax.all_gather(query_weight, ("seq", "ctx"), axis=0, tiled=True),
            lax.all_gather(key_weight, ("seq", "ctx"), axis=0, tiled=True),
            lax.all_gather(value_weight, ("seq", "ctx"), axis=0, tiled=True),
            lax.all_gather(group_gain, ("seq", "ctx"), axis=0, tiled=True),
            lax.all_gather(output_weight, ("seq", "ctx"), axis=0, tiled=True),
        )
        tokens = inputs[batch_index, 0].astype(jnp.float32)
        normed_first, factor_first = normalize(tokens)
        hidden = (normed_first * gain_first.astype(jnp.float32)).astype(jnp.bfloat16)
        query_proj = jnp.dot(hidden, query_full, preferred_element_type=jnp.float32).astype(
            jnp.bfloat16
        )
        key_proj = jnp.dot(hidden, key_full, preferred_element_type=jnp.float32).astype(
            jnp.bfloat16
        )
        value_proj = jnp.dot(hidden, value_full, preferred_element_type=jnp.float32).astype(
            jnp.bfloat16
        )
        tail_rows = jnp.concatenate(
            [query_proj[block_rows - halo_rows : block_rows], query_proj[local_rows - halo_rows :]],
            axis=0,
        )
        key_dealt, value_dealt, tail_dealt = (
            lax.all_gather(key_proj, "ctx", axis=0, tiled=True),
            lax.all_gather(value_proj, "ctx", axis=0, tiled=True),
            lax.all_gather(tail_rows, "ctx", axis=0, tiled=True),
        )
        pairs_row = pair_index[batch_index]
        owner_pair = jnp.repeat(pairs_row, 2)
        block_of_slot = jnp.where(slot_ids % 2 == 0, owner_pair, block_count - 1 - owner_pair)
        to_natural = (block_of_slot[None, :] == slot_ids[:, None]).astype(jnp.float32)
        slot_of_block = jnp.sum(
            jnp.where(block_of_slot[None, :] == slot_ids[:, None], slot_ids[None, :], 0), axis=1
        )
        my_pair = lax.dynamic_index_in_dim(pairs_row, my_index, 0, keepdims=False)
        my_blocks = jnp.stack([my_pair, block_count - 1 - my_pair])
        key_pad = jnp.pad(
            reorder(to_natural, key_dealt.reshape(block_count, -1)).reshape(
                seq_length, model_width
            ),
            pad_width,
        ).reshape(-1, head_count, head_dim)
        value_pad = jnp.pad(
            reorder(to_natural, value_dealt.reshape(block_count, -1)).reshape(
                seq_length, model_width
            ),
            pad_width,
        )
        tail_blocks = reorder(to_natural, tail_dealt.reshape(block_count, -1)).reshape(
            block_count, halo_rows, model_width
        )
        previous = jnp.concatenate(
            [jnp.zeros((1, halo_rows, model_width), jnp.bfloat16), tail_blocks[:-1]], axis=0
        )
        query_ext = jnp.concatenate(
            [pick(previous, my_blocks), query_proj.reshape(2, block_rows, model_width)], axis=1
        ).reshape(2, extended, head_count, head_dim)
        row_pos = (
            my_blocks[:, None] * block_rows
            - halo_rows
            + jnp.arange(extended, dtype=jnp.int32)[None, :]
        )
        mixed_in, log_total = attend_forward(
            query_ext, row_pos, key_pad, value_pad, score_kernel, layout
        )
        mixed_six = mixed_in.reshape(2, groups, 2, block_rows, 2, head_dim)
        heads_out = jnp.einsum(
            "gqp,ngpiqd->nigqd", mix_table, mixed_six, precision=PRECISE
        ).reshape(local_rows, head_count, head_dim)
        group_normed, group_factor = normalize(heads_out)
        normed_low = (
            group_normed.reshape(local_rows, model_width) * gain_group.astype(jnp.float32)
        ).astype(jnp.bfloat16)
        residual = tokens + jnp.dot(normed_low, out_full, preferred_element_type=jnp.float32)
        gain_second, gate_full, up_full, down_full = (
            lax.all_gather(second_gain, ("seq", "ctx"), axis=0, tiled=True),
            lax.all_gather(gate_weight, ("seq", "ctx"), axis=0, tiled=True),
            lax.all_gather(up_weight, ("seq", "ctx"), axis=0, tiled=True),
            lax.all_gather(down_weight, ("seq", "ctx"), axis=0, tiled=True),
        )
        normed_second, factor_second = normalize(residual)
        second_hidden = (normed_second * gain_second.astype(jnp.float32)).astype(jnp.bfloat16)
        gate_proj = jnp.dot(second_hidden, gate_full, preferred_element_type=jnp.float32)
        up_proj = jnp.dot(second_hidden, up_full, preferred_element_type=jnp.float32)
        activated = (jax.nn.silu(gate_proj) * up_proj).astype(jnp.bfloat16)
        layer_rows.append(
            (residual + jnp.dot(activated, down_full, preferred_element_type=jnp.float32)).astype(
                jnp.bfloat16
            )
        )
        gain_second, gate_full, up_full, down_full = (
            lax.all_gather(second_gain, ("seq", "ctx"), axis=0, tiled=True),
            lax.all_gather(gate_weight, ("seq", "ctx"), axis=0, tiled=True),
            lax.all_gather(up_weight, ("seq", "ctx"), axis=0, tiled=True),
            lax.all_gather(down_weight, ("seq", "ctx"), axis=0, tiled=True),
        )
        grad_rows = out_grad[batch_index, 0]
        hid_grad = jnp.dot(grad_rows, down_full.T, preferred_element_type=jnp.float32)
        down_grad = jnp.dot(activated.T, grad_rows, preferred_element_type=jnp.float32)
        sigmoid_gate = jax.nn.sigmoid(gate_proj)
        up_low = (hid_grad * gate_proj * sigmoid_gate).astype(jnp.bfloat16)
        gate_low = (
            hid_grad * up_proj * sigmoid_gate * (1.0 + gate_proj * (1.0 - sigmoid_gate))
        ).astype(jnp.bfloat16)
        second_grad = jnp.dot(gate_low, gate_full.T, preferred_element_type=jnp.float32) + jnp.dot(
            up_low, up_full.T, preferred_element_type=jnp.float32
        )
        gate_grad = jnp.dot(second_hidden.T, gate_low, preferred_element_type=jnp.float32)
        up_grad = jnp.dot(second_hidden.T, up_low, preferred_element_type=jnp.float32)
        residual_part, gain_second_grad = normalize_back(
            normed_second, factor_second, gain_second.astype(jnp.float32), second_grad
        )
        residual_grad = grad_rows.astype(jnp.float32) + residual_part
        feed_shards = (
            lax.psum_scatter(gain_second_grad, ("seq", "ctx"), scatter_dimension=0, tiled=True),
            lax.psum_scatter(gate_grad, ("seq", "ctx"), scatter_dimension=0, tiled=True),
            lax.psum_scatter(up_grad, ("seq", "ctx"), scatter_dimension=0, tiled=True),
            lax.psum_scatter(down_grad, ("seq", "ctx"), scatter_dimension=0, tiled=True),
        )
        feed_sums = accumulate(feed_sums, feed_shards)
        gain_first, query_full, key_full, value_full, gain_group, out_full = (
            lax.all_gather(norm_gain, ("seq", "ctx"), axis=0, tiled=True),
            lax.all_gather(query_weight, ("seq", "ctx"), axis=0, tiled=True),
            lax.all_gather(key_weight, ("seq", "ctx"), axis=0, tiled=True),
            lax.all_gather(value_weight, ("seq", "ctx"), axis=0, tiled=True),
            lax.all_gather(group_gain, ("seq", "ctx"), axis=0, tiled=True),
            lax.all_gather(output_weight, ("seq", "ctx"), axis=0, tiled=True),
        )
        attended_low = residual_grad.astype(jnp.bfloat16)
        out_weight_grad = jnp.dot(normed_low.T, attended_low, preferred_element_type=jnp.float32)
        normed_grad = jnp.dot(attended_low, out_full.T, preferred_element_type=jnp.float32)
        heads_grad, gain_group_grad = normalize_back(
            group_normed,
            group_factor,
            gain_group.astype(jnp.float32).reshape(head_count, head_dim),
            normed_grad.reshape(local_rows, head_count, head_dim),
        )
        heads_five = heads_grad.reshape(2, block_rows, groups, 2, head_dim)
        mixing_total = mixing_total + jnp.einsum(
            "nigqd,ngpiqd->gqp", heads_five, mixed_six, precision=PRECISE
        ).reshape(head_count, 2)
        mixed_grad = jnp.einsum(
            "gqp,nigqd->ngpiqd", mix_table, heads_five, precision=PRECISE
        ).reshape(2, groups, 2, block_rows, 2 * head_dim)
        mixed_low = mixed_grad.astype(jnp.bfloat16)
        delta_rows = jnp.sum(mixed_low.astype(jnp.float32) * mixed_in, axis=-1).reshape(
            2, head_count, block_rows
        )
        key_acc = jnp.zeros((seq_length, model_width), jnp.float32)
        value_acc = jnp.zeros((seq_length, model_width), jnp.float32)
        query_grad, key_acc, value_acc, kernel_part = attend_backward(
            query_ext,
            row_pos,
            key_pad,
            value_pad,
            score_kernel,
            log_total,
            mixed_low,
            delta_rows,
            key_acc,
            value_acc,
            layout,
        )
        kernel_total = kernel_total + kernel_part
        halo_grad = query_grad[:, :halo_rows].reshape(2, halo_rows, model_width)
        own_grad = query_grad[:, halo_rows:].reshape(2, block_rows, model_width)
        target_slot = pick(slot_of_block, jnp.maximum(my_blocks - 1, 0))
        routing = ((slot_ids[None, :] == target_slot[:, None]) & (my_blocks > 0)[:, None]).astype(
            jnp.float32
        )
        tail_grad = jnp.einsum("ws,wrc->src", routing, halo_grad, precision=PRECISE).reshape(
            block_count * halo_rows, model_width
        )
        key_back = reorder(to_natural.T, key_acc.reshape(block_count, -1)).reshape(
            seq_length, model_width
        )
        value_back = reorder(to_natural.T, value_acc.reshape(block_count, -1)).reshape(
            seq_length, model_width
        )
        key_mine, value_mine, tail_mine = (
            lax.psum_scatter(
                key_back.astype(jnp.bfloat16), "ctx", scatter_dimension=0, tiled=True
            ).astype(jnp.float32),
            lax.psum_scatter(
                value_back.astype(jnp.bfloat16), "ctx", scatter_dimension=0, tiled=True
            ).astype(jnp.float32),
            lax.psum_scatter(
                tail_grad.astype(jnp.bfloat16), "ctx", scatter_dimension=0, tiled=True
            ).astype(jnp.float32),
        )
        tail_mine = tail_mine.reshape(2, halo_rows, model_width)
        query_total = jnp.concatenate(
            [
                own_grad[:, : block_rows - halo_rows],
                own_grad[:, block_rows - halo_rows :] + tail_mine,
            ],
            axis=1,
        ).reshape(local_rows, model_width)
        query_low = query_total.astype(jnp.bfloat16)
        key_low = key_mine.astype(jnp.bfloat16)
        value_low = value_mine.astype(jnp.bfloat16)
        query_w_grad = jnp.dot(hidden.T, query_low, preferred_element_type=jnp.float32)
        key_w_grad = jnp.dot(hidden.T, key_low, preferred_element_type=jnp.float32)
        value_w_grad = jnp.dot(hidden.T, value_low, preferred_element_type=jnp.float32)
        hidden_grad = (
            jnp.dot(query_low, query_full.T, preferred_element_type=jnp.float32)
            + jnp.dot(key_low, key_full.T, preferred_element_type=jnp.float32)
            + jnp.dot(value_low, value_full.T, preferred_element_type=jnp.float32)
        )
        token_part, gain_first_grad = normalize_back(
            normed_first, factor_first, gain_first.astype(jnp.float32), hidden_grad
        )
        input_rows.append((residual_grad + token_part).astype(jnp.bfloat16))
        attention_shards = (
            lax.psum_scatter(gain_first_grad, ("seq", "ctx"), scatter_dimension=0, tiled=True),
            lax.psum_scatter(query_w_grad, ("seq", "ctx"), scatter_dimension=0, tiled=True),
            lax.psum_scatter(key_w_grad, ("seq", "ctx"), scatter_dimension=0, tiled=True),
            lax.psum_scatter(value_w_grad, ("seq", "ctx"), scatter_dimension=0, tiled=True),
            lax.psum_scatter(
                gain_group_grad.reshape(model_width),
                ("seq", "ctx"),
                scatter_dimension=0,
                tiled=True,
            ),
            lax.psum_scatter(out_weight_grad, ("seq", "ctx"), scatter_dimension=0, tiled=True),
        )
        attention_sums = accumulate(attention_sums, attention_shards)
    kernel_sum, mixing_sum = lax.psum((kernel_total, mixing_total), ("seq", "ctx"))
    layer_out = jnp.stack(layer_rows)[:, None]
    input_grad = jnp.stack(input_rows)[:, None]
    return (
        layer_out,
        input_grad,
        attention_sums[0],
        attention_sums[1],
        attention_sums[2],
        attention_sums[3],
        kernel_sum,
        mixing_sum,
        attention_sums[4],
        attention_sums[5],
        feed_sums[0],
        feed_sums[1],
        feed_sums[2],
        feed_sums[3],
    )


def on_device(
    inputs,
    out_grad,
    pair_index,
    norm_gain,
    query_weight,
    key_weight,
    value_weight,
    score_kernel,
    head_mixing,
    group_gain,
    output_weight,
    second_gain,
    gate_weight,
    up_weight,
    down_weight,
):
    groups, planes = lax.axis_size("ctx"), lax.axis_size("seq")
    heads, width = score_kernel.shape[0], inputs.shape[3]
    if groups != 8 or heads != 2 * groups or (groups * inputs.shape[2]) % TILE:
        return general_device(
            inputs, out_grad, pair_index, norm_gain, query_weight, key_weight, value_weight,
            score_kernel, head_mixing, group_gain, output_weight, second_gain, gate_weight,
            up_weight, down_weight,
        )
    micro, local = inputs.shape[0], inputs.shape[2]
    blk, seq = local // 2, local * groups
    blocks = seq // blk
    pair = width // groups
    owned = width // (groups * planes)
    hidden = gate_weight.shape[1]
    chunk = hidden // (groups * planes)
    me = lax.axis_index("ctx")
    tokens_low = inputs.reshape(micro * local, width)
    grads_low = out_grad.reshape(micro * local, width)

    rows_all = micro * local
    qkv_shape = (groups, owned, 3 * pair)
    feed_shape = (groups, owned, 2 * planes * chunk)
    spread_sems = [DMA((9,))] * 2
    feed_mine, qkv, gains, all_tokens, out_rows = communicate(
        functools.partial(enter_kernel, planes), "enter", 1, 50,
        [
            (feed_shape, BF16),
            ((planes,) + qkv_shape, BF16),
            ((planes, groups, 8, TILE), F32),
            ((groups, rows_all, width), BF16),
            ((planes, owned, width), BF16),
        ],
        [pltpu.VMEM((owned, width), BF16)] * 3 + [pltpu.VMEM((owned, hidden), BF16)] * 2
        + [pltpu.VMEM((owned,), BF16)] * 3 + [pltpu.VMEM((8, TILE), F32)]
        + [pltpu.VMEM(qkv_shape, BF16), pltpu.VMEM(feed_shape, BF16)]
        + [DMA((3, groups))] * 2 + spread_sems + [DMA((1, 2, planes))] * 2
        + [DMA((2, 2, planes))] * 2 + [DMA((13,))],
        (
            query_weight, key_weight, value_weight, gate_weight, up_weight, norm_gain, group_gain,
            second_gain, tokens_low, output_weight,
        ),
        ANYWHERE,
    )
    all_tokens, down_mine = lax.optimization_barrier((all_tokens, down_weight))
    feed = lax.all_gather(feed_mine.reshape(groups * owned, -1), "seq", axis=0, tiled=True)
    down = lax.all_gather(down_mine, "seq", axis=0, tiled=True)
    qkv = qkv.reshape(width, 3 * pair)
    hidden_all, heads_in, gains, gain_pair, out_rows, all_grads = communicate(
        functools.partial(heads_kernel, planes), "heads", 2, 20,
        [
            ((width, groups * rows_all), BF16),
            ((groups * rows_all, 3 * pair), BF16),
            ((8, width), F32),
            ((8, pair), F32),
            ((4, owned, width), BF16),
            ((groups, rows_all, width), BF16),
        ],
        [
            pltpu.VMEM((groups, rows_all, width), BF16),
            pltpu.VMEM((width, 3 * pair), BF16),
            pltpu.VMEM((width, groups * rows_all), BF16),
            pltpu.VMEM((groups * rows_all, 3 * pair), BF16),
        ]
        + [DMA((4,))] * 2 + spread_sems + [DMA((groups + 1,)), DMA((2, groups)), DMA((2,))],
        (all_tokens, qkv, gains, out_rows, grads_low),
        None, [ANYWHERE] * 2 + [ON_CHIP] + [ANYWHERE] * 2, (ANYWHERE,) * 2 + (ON_CHIP,) * 2 + (ANYWHERE,) * 2,
    )
    all_grads = all_grads.reshape(-1, width)
    out_rows = out_rows.reshape(pair, width)

    slots = jnp.arange(blocks, dtype=jnp.int32)
    owner = jnp.repeat(pair_index, 2, axis=1)
    block_of_slot = jnp.where(slots % 2 == 0, owner, blocks - 1 - owner)
    place = (
        (slots // 2)[None] * (2 * micro)
        + 2 * jnp.arange(micro, dtype=jnp.int32)[:, None]
        + (slots % 2)[None]
    )
    blk_table = jnp.sum(
        jnp.where(block_of_slot[:, None, :] == slots[None, :, None], place[:, None, :], 0), axis=2
    ).astype(jnp.int32)
    ker = lax.dynamic_slice_in_dim(score_kernel, 2 * me, 2, 0)
    mix = jnp.repeat(lax.dynamic_slice_in_dim(head_mixing, 2 * me, 2, 0), pair // 2, axis=0).T
    scale = (width // heads) ** (-0.5)

    mixed, y, prob = pair_forward(blk_table, ker, mix, gain_pair, heads_in, micro, seq, blk, scale)
    by_core = (groups // 2, 2, rows_all)
    sum_spec = sum_scratch(rows_all, width)
    residual, second_all = communicate(
        second_kernel, "second", 3, 40,
        [((rows_all, width), F32), ((groups, rows_all, width), BF16)],
        [
            pltpu.VMEM(by_core + (pair,), BF16),
            pltpu.VMEM((pair, width), BF16),
            pltpu.VMEM((rows_all, width), BF16),
            pltpu.VMEM((rows_all, width), F32),
            pltpu.VMEM((rows_all, width), BF16),
            DMA((5,)),
        ]
        + sum_spec + spread_sems,
        (mixed.reshape(by_core + (pair,)), out_rows, tokens_low, gains),
        None, [ANYWHERE] * 3 + [ON_CHIP], (ANYWHERE,) * 2,
    )
    second_all = second_all.reshape(-1, width)

    half = planes * chunk
    both = jnp.dot(second_all, feed, preferred_element_type=F32)
    gate, up = both[:, :half], both[:, half:]
    sigmoid = jax.nn.sigmoid(gate)
    active = (gate * sigmoid * up).astype(BF16)
    slopes = jnp.concatenate(
        [up * sigmoid * (1.0 + gate * (1.0 - sigmoid)), gate * sigmoid], axis=1
    )
    down_grad = lax.dot_general(active, all_grads, (((0,), (0,)), ((), ())), preferred_element_type=F32)
    all_grads, down_grad, slopes = lax.optimization_barrier((all_grads, down_grad.astype(BF16), slopes))
    hid_grad = lax.dot_general(all_grads, down, (((1,), (1,)), ((), ())), preferred_element_type=F32)
    lows = (jnp.concatenate([hid_grad, hid_grad], axis=1) * slopes).astype(BF16)
    feed_grad = lax.dot_general(second_all, lows, (((0,), (0,)), ((), ())), preferred_element_type=F32)
    lows, feed_grad = lax.optimization_barrier((lows, feed_grad.astype(BF16)))
    feed_sum = lax.psum_scatter(feed_grad, "seq", scatter_dimension=0, tiled=True)
    down_sum = lax.psum_scatter(down_grad, "seq", scatter_dimension=0, tiled=True)
    residual_grad, gain_second_grad, mixed_grad, out_w_grad = communicate(
        back_kernel, "back", 4, 42,
        [
            ((rows_all, width), F32),
            ((1, width), F32),
            ((groups, rows_all, pair), BF16),
            ((pair, width), BF16),
        ],
        [
            pltpu.VMEM(by_core + (2 * half,), BF16),
            pltpu.VMEM((width, 2 * half), BF16),
            pltpu.VMEM((rows_all, width), F32),
            pltpu.VMEM((rows_all, width), BF16),
            pltpu.VMEM((pair, width), BF16),
            pltpu.VMEM((groups, rows_all, pair), BF16),
            pltpu.VMEM((rows_all, width), F32),
            pltpu.VMEM((groups, rows_all, width), BF16),
            pltpu.VMEM((pair, width), F32),
            DMA((7,)),
        ]
        + sum_spec + spread_sems,
        (
            lows.reshape(by_core + (2 * half,)), feed, residual, grads_low, out_rows,
            mixed.reshape(groups, rows_all, pair), gains,
        ),
        None, [ANYWHERE] * 6 + [ON_CHIP], (ANYWHERE, ON_CHIP, ON_CHIP, ON_CHIP),
    )
    mixed_grad = mixed_grad.reshape(-1, pair)
    qkv_low, misc = pair_backward(
        blk_table, ker, mix, gain_pair, heads_in, mixed_grad, y, prob, seq, blk, scale
    )
    small = (8, width)
    layer_out, row_grad = communicate(
        layer_kernel, "layer", 6, 18, [((rows_all, width), BF16), ((planes, owned, width), BF16)],
        [
            pltpu.VMEM(by_core + (half,), BF16),
            pltpu.VMEM((half, width), BF16),
            pltpu.VMEM((rows_all, width), F32),
            DMA((3,)),
        ]
        + sum_spec + [DMA((4,))] * 2 + [DMA],
        (
            active.reshape(by_core + (half,)), down, residual,
            out_w_grad.reshape(4, owned, width),
        ),
        None, [ANYWHERE] * 4, (ON_CHIP, ANYWHERE),
    )
    input_grad, sums, misc, qkv_back, feed_back, out_w_back = communicate(
        functools.partial(leave_kernel, planes), "leave", 5, 55,
        [
            ((rows_all, width), BF16),
            (small, F32),
            ((groups,) + misc.shape, F32),
            (qkv_shape, BF16),
            (feed_shape, BF16),
            ((1, owned, width), BF16),
        ],
        [
            pltpu.VMEM(by_core + (3 * pair,), BF16),
            pltpu.VMEM((width, 3 * pair), BF16),
            pltpu.VMEM(hidden_all.shape, BF16),
            pltpu.VMEM((rows_all, width), F32),
            pltpu.VMEM((rows_all, width), BF16),
            DMA((5,)),
            pltpu.VMEM((planes,) + misc.shape, F32),
            DMA((2, groups)),
            DMA((2, groups)),
        ]
        + sum_spec[:6]
        + [pltpu.VMEM((groups,) + small, F32), pltpu.VMEM((planes,) + small, F32)]
        + [pltpu.VMEM((planes, groups * owned, 4 * pair), BF16)]
        + [pltpu.VMEM((2, planes, groups * owned, 4 * pair), BF16)] * 2
        + [pltpu.VMEM(qkv_shape, BF16)]
        + sum_spec[6:]
        + [DMA((2, groups))] * 2
        + [DMA((2, 2, planes))] * 2
        + [DMA((2, groups))] * 2
        + [DMA((3,))],
        (
            qkv_low.reshape(by_core + (3 * pair,)), qkv, hidden_all,
            residual_grad, tokens_low, gains, gain_second_grad, misc,
            feed_sum.reshape(feed_shape), row_grad,
        ),
        None, [ANYWHERE] * 5 + [ON_CHIP] * 3 + [ANYWHERE, ON_CHIP],
        (ON_CHIP,) * 3 + (ANYWHERE,) * 2 + (ON_CHIP,),
    )
    plain = [(owned, width)] * 3 + [(owned, hidden)] * 2 + [(owned, width), (chunk, width)]
    landed = (qkv_back, feed_back, out_w_back, down_sum, input_grad, layer_out)
    out_shapes = [jax.ShapeDtypeStruct(shape, F32) for shape in plain]
    out_shapes += [jax.ShapeDtypeStruct((rows_all, width), BF16)] * 2
    row = jax.ShapeDtypeStruct((1, owned), F32)
    flat_index = (lax.axis_index("seq") * groups + me).astype(jnp.int32).reshape(1)
    results = pl.pallas_call(
        functools.partial(finish_kernel, len(out_shapes)),
        name="finish",
        out_shape=tuple(out_shapes)
        + (row, row, row)
        + (jax.ShapeDtypeStruct(score_kernel.shape[::-1], F32), jax.ShapeDtypeStruct((2, heads), F32)),
        in_specs=[pl.BlockSpec(memory_space=pltpu.SMEM)] + [ON_CHIP] * 2 + [ANYWHERE] * 6,
        out_specs=(ANYWHERE,) * len(out_shapes) + (ON_CHIP,) * 5,
        scratch_shapes=[pltpu.VMEM(value.shape, BF16) for value in landed]
        + [pltpu.VMEM(shape, F32) for shape in plain]
        + [DMA((6,)), DMA((len(out_shapes),))],
        compiler_params=pltpu.CompilerParams(vmem_limit_bytes=60 << 20),
    )(flat_index, sums, misc, *landed)
    q_back, k_back, v_back, gate_back, up_back, out_w_out, down_out, input_grad, layer_out = results[:9]
    gain_outs = [value.reshape(owned) for value in results[9:12]]
    ker_out, mix_out = jnp.transpose(results[12], (2, 1, 0)), results[13].T

    shape = inputs.shape
    return (
        layer_out.reshape(shape),
        input_grad.reshape(shape),
        gain_outs[0],
        q_back,
        k_back,
        v_back,
        ker_out,
        mix_out,
        gain_outs[1],
        out_w_out,
        gain_outs[2],
        gate_back,
        up_back,
        down_out,
    )


def solution(mesh):
    placed = (
        P(None, "seq", "ctx", None),
        P(None, "seq", "ctx", None),
        P(),
        P(("seq", "ctx")),
        P(("seq", "ctx"), None),
        P(("seq", "ctx"), None),
        P(("seq", "ctx"), None),
        P(),
        P(),
        P(("seq", "ctx")),
        P(("seq", "ctx"), None),
        P(("seq", "ctx")),
        P(("seq", "ctx"), None),
        P(("seq", "ctx"), None),
        P(("seq", "ctx"), None),
    )
    return jax.shard_map(
        on_device,
        mesh=mesh,
        in_specs=placed,
        out_specs=(
            P(None, "seq", "ctx", None),
            P(None, "seq", "ctx", None),
            P(("seq", "ctx")),
            P(("seq", "ctx"), None),
            P(("seq", "ctx"), None),
            P(("seq", "ctx"), None),
            P(),
            P(),
            P(("seq", "ctx")),
            P(("seq", "ctx"), None),
            P(("seq", "ctx")),
            P(("seq", "ctx"), None),
            P(("seq", "ctx"), None),
            P(("seq", "ctx"), None),
        ),
        check_vma=False,
    )
```
